32 devices in a mesh: dp: 2 (over core), row: 4 (over y, x), col: 4 (over z).
Axes of the slice: x: 2, y: 2, z: 4, core: 2. Of those that a mesh axis runs over, the one named last changes fastest.
Arguments:
- block_input: bfloat16 [8192, 2048], P(('dp', 'row')), may hold values from -6 to 6
- segment_ids: int32 [8192], P(('dp', 'row')), may hold values from 0 to 3, as said below
- positions: int32 [8192], P(('dp', 'row')), may hold values from 0 to 1023, as said below
- w_query: bfloat16 [2048, 2048], P('row', 'col'), as said below
- w_key: bfloat16 [2048, 2048], P('row', 'col'), as said below
- w_value: bfloat16 [2048, 2048], P('row', 'col'), may hold values from -0.125 to 0.125
- w_out: bfloat16 [2048, 2048], P('col', 'row'), may hold values from -0.125 to 0.125
- w_gate: bfloat16 [2048, 8192], P('row', 'col'), may hold values from -0.125 to 0.125
- w_up: bfloat16 [2048, 8192], P('row', 'col'), may hold values from -0.125 to 0.125
- w_down: bfloat16 [8192, 2048], P('col', 'row'), may hold values from -0.0625 to 0.0625
- query_gain: float32 [2048], P('col'), may hold values from 0.25 to 1.75
- key_gain: float32 [2048], P('col'), may hold values from 0.25 to 1.75
- attn_gain: float32 [2048], replicated, may hold values from 0.25 to 1.75
- mlp_gain: float32 [2048], replicated, may hold values from 0.25 to 1.75
- grad_output: bfloat16 [8192, 2048], P(('dp', 'row')), as said below
Outputs:
- block_output: bfloat16 [8192, 2048], P(('dp', 'row'))
- grad_input: float32 [8192, 2048], P(('dp', 'row'))
- grad_w_query: float32 [2048, 2048], P('row', 'col')
- grad_w_key: float32 [2048, 2048], P('row', 'col')
- grad_w_value: float32 [2048, 2048], P('row', 'col')
- grad_w_out: float32 [2048, 2048], P('col', 'row')
- grad_w_gate: float32 [2048, 8192], P('row', 'col')
- grad_w_up: float32 [2048, 8192], P('row', 'col')
- grad_w_down: float32 [8192, 2048], P('col', 'row')
- grad_query_gain: float32 [2048], P('col')
- grad_key_gain: float32 [2048], P('col')
- grad_attn_gain: float32 [2048], replicated
- grad_mlp_gain: float32 [2048], replicated
The draws below stay inside these ranges and needn't reach their ends.
Inputs may be any that keep to these rules, and one draw needn't show every extreme that they name: `segment_ids`: within each sequence of 1024 tokens the ids never fall. `positions`: the index of a token counted from the first token with the same id in its sequence. `w_query`: scaled to the fan-in 2048. `w_key`: scaled to the fan-in 2048. `grad_output`: of order one in every row.
All inputs are finite; a program needn't handle non-finite values.
Results may differ from the reference program's by a relative error of at most 0.02.
Values may be sent and summed in bfloat16 or wider, within the bound.
No kernel may reach another device: no remote copies, remote signals or barrier semaphores. Data moves between devices by JAX's collectives and lax.ppermute only.
A program may use at most 320 MiB of HBM per device.

```python
import jax
import jax.numpy as jnp
from jax import lax

D = 2048
HEADS = 16
HD = 128
FF = 8192
LEN = 1024
TOKENS = 8192


def document_cuts(key):
    seq_count = TOKENS // LEN
    loose = jax.random.randint(jax.random.fold_in(key, 11), (seq_count, 3), 1, LEN + LEN // 2)
    inner = jax.random.randint(jax.random.fold_in(key, 12), (seq_count, 3), 1, LEN)
    row_index = jnp.arange(seq_count)[:, None]
    return jnp.where(row_index == 0, LEN, jnp.where(row_index == 1, inner, loose)).astype(jnp.int32)


def draw_segment_ids(key, part):
    cut_points = document_cuts(key)
    place = jnp.arange(LEN, dtype=jnp.int32)
    crossed = (place[None, :, None] >= cut_points[:, None, :]).astype(jnp.int32)
    return jnp.sum(crossed, axis=-1).reshape(TOKENS).astype(jnp.int32)


def draw_positions(key, part):
    cut_points = document_cuts(key)
    place = jnp.arange(LEN, dtype=jnp.int32)
    begins = jnp.where(place[None, :, None] >= cut_points[:, None, :], cut_points[:, None, :], 0)
    return (place[None, :] - jnp.max(begins, axis=-1)).reshape(TOKENS).astype(jnp.int32)


def projection_draw(key):
    base = jnp.clip(jax.random.normal(key, (D, D), jnp.float32), -6.0, 6.0)
    column = jnp.arange(D, dtype=jnp.float32)
    jitter = jnp.exp(jax.random.uniform(jax.random.fold_in(key, 5), (D,), jnp.float32, -0.35, 0.35))
    scales = (0.5 + column / D) * jitter
    return base * scales[None, :] * D ** (-0.5)


def draw_w_query(key, part):
    return projection_draw(jax.random.fold_in(key, 21)).astype(jnp.bfloat16)


def draw_w_key(key, part):
    return projection_draw(jax.random.fold_in(key, 22)).astype(jnp.bfloat16)


def draw_grad_output(key, part):
    base = jnp.clip(jax.random.normal(key, (TOKENS, D), jnp.float32), -6.0, 6.0)
    place = jnp.arange(TOKENS, dtype=jnp.float32) / TOKENS
    jitter = jnp.exp(jax.random.uniform(jax.random.fold_in(key, 3), (TOKENS,), jnp.float32, -0.4, 0.4))
    scales = 0.6 * jnp.power(3.0, place) * jitter
    return (base * scales[:, None]).astype(jnp.bfloat16)


def shard_levels(own_key, extent, cuts, least, top_value):
    loudness, own = 1.0, jax.random.fold_in(own_key, 6)
    for dim, shards_of in cuts:
        steps = jnp.exp(jax.random.uniform(jax.random.fold_in(own, dim), (shards_of,), jnp.float32, least / len(cuts), top_value / len(cuts)))
        loudness = loudness * jnp.repeat(steps, extent[dim] // shards_of).reshape([-1 if axis == dim else 1 for axis in range(len(extent))])
    return loudness


def gaussian(own_key, dims, deviation, bound, shards=(), kind=jnp.bfloat16):
    factor_of = shard_levels(own_key, dims, shards, -0.22, 0.18) if shards else 1.0
    values = jax.random.normal(own_key, dims, jnp.float32) * deviation * factor_of
    return jnp.minimum(jnp.maximum(values, -bound), bound).astype(kind)


def setup_inputs(seed: int = 0) -> dict:
    keys = jax.random.split(jax.random.key(seed), 16)
    block_input = gaussian(keys[0], (TOKENS, D), 1.0, 6.0, ((0, 8),))
    segment_ids = draw_segment_ids(jax.random.fold_in(keys[15], 71), 0)
    positions = draw_positions(jax.random.fold_in(keys[15], 71), 0)
    w_query = draw_w_query(jax.random.fold_in(keys[15], 71), 0)
    w_key = draw_w_key(jax.random.fold_in(keys[15], 71), 0)
    w_value = gaussian(keys[5], (D, D), D ** -0.5, 0.125, ((0, 4), (1, 4)))
    w_out = gaussian(keys[6], (D, D), D ** -0.5, 0.125, ((0, 4), (1, 4)))
    w_gate = gaussian(keys[7], (D, FF), D ** -0.5, 0.125, ((0, 4), (1, 4)))
    w_up = gaussian(keys[8], (D, FF), D ** -0.5, 0.125, ((0, 4), (1, 4)))
    w_down = gaussian(keys[9], (FF, D), FF ** -0.5, 0.0625, ((0, 4), (1, 4)))
    query_gain = jnp.clip(1.0 + 0.15 * jax.random.normal(keys[10], (D,), jnp.float32), 0.25, 1.75)
    key_gain = jnp.clip(1.0 + 0.15 * jax.random.normal(keys[11], (D,), jnp.float32), 0.25, 1.75)
    attn_gain = jnp.clip(1.0 + 0.15 * jax.random.normal(keys[12], (D,), jnp.float32), 0.25, 1.75)
    mlp_gain = jnp.clip(1.0 + 0.15 * jax.random.normal(keys[13], (D,), jnp.float32), 0.25, 1.75)
    grad_output = draw_grad_output(jax.random.fold_in(keys[15], 71), 0)
    return dict(block_input=block_input, segment_ids=segment_ids, positions=positions, w_query=w_query, w_key=w_key, w_value=w_value, w_out=w_out, w_gate=w_gate, w_up=w_up, w_down=w_down, query_gain=query_gain, key_gain=key_gain, attn_gain=attn_gain, mlp_gain=mlp_gain, grad_output=grad_output)


EPS = 1e-06
THETA = 500000.0
NEG_FILL = -1e+30

def rms_scale(values):
    return lax.rsqrt(lax.optimization_barrier(jnp.mean(values * values, axis=-1, keepdims=True)) + EPS)

def rms_back(grad_unit, unit_vals, scale_vals):
    return scale_vals * (grad_unit - unit_vals * lax.optimization_barrier(jnp.mean(grad_unit * unit_vals, axis=-1, keepdims=True)))

def rope_tables(positions):
    half_dim = HD // 2
    inv_freq = THETA ** (-(jnp.arange(half_dim, dtype=jnp.float32) * 2.0) / HD)
    angles = positions.astype(jnp.float32)[:, None] * inv_freq[None, :]
    cosine = jnp.concatenate([jnp.cos(angles), jnp.cos(angles)], axis=-1)
    sine_tab = jnp.concatenate([jnp.sin(angles), jnp.sin(angles)], axis=-1)
    return (cosine, sine_tab)

def rotate(values):
    first_half = values[..., :HD // 2]
    second_half = values[..., HD // 2:]
    return jnp.concatenate([-second_half, first_half], axis=-1)

def rotate_back(values):
    first_half = values[..., :HD // 2]
    second_half = values[..., HD // 2:]
    return jnp.concatenate([second_half, -first_half], axis=-1)

def plain_dot(left_mat, right_mat):
    return jnp.dot(left_mat, right_mat, preferred_element_type=jnp.float32)

def times_transposed(left_mat, right_mat):
    return lax.dot_general(left_mat, right_mat, (((1,), (1,)), ((), ())), preferred_element_type=jnp.float32)

def left_transposed(left_mat, right_mat):
    return lax.dot_general(left_mat, right_mat, (((0,), (0,)), ((), ())), preferred_element_type=jnp.float32)

def one_sequence(x_seq, grad_seq, seg_seq, pos_seq, weights, gains):
    w_query, w_key, w_value, w_out, w_gate, w_up, w_down = weights
    query_gain, key_gain, attn_gain, mlp_gain = gains
    length = x_seq.shape[0]
    score_scale = HD ** (-0.5)
    query_raw = plain_dot(x_seq, w_query)
    key_raw = plain_dot(x_seq, w_key)
    value_raw = plain_dot(x_seq, w_value)
    query_scale = rms_scale(query_raw)
    query_unit = query_raw * query_scale
    key_scale = rms_scale(key_raw)
    key_unit = key_raw * key_scale
    cosine, sine_tab = rope_tables(pos_seq)

    def turn(values):
        head_view = values.reshape(length, HEADS, HD)
        return head_view * cosine[:, None, :] + rotate(head_view) * sine_tab[:, None, :]

    def unturn(values):
        back = values * cosine[:, None, :] + rotate_back(values * sine_tab[:, None, :])
        return back.reshape(length, D)
    query_rot = turn(query_unit * query_gain).astype(jnp.bfloat16)
    key_rot = turn(key_unit * key_gain).astype(jnp.bfloat16)
    value_heads = value_raw.astype(jnp.bfloat16).reshape(length, HEADS, HD)
    index_vec = jnp.arange(length)
    allowed = ((seg_seq[:, None] == seg_seq[None, :]) & (index_vec[None, :] <= index_vec[:, None]))[None]
    scores = jnp.einsum('qhd,khd->hqk', query_rot.astype(jnp.float32), key_rot.astype(jnp.float32)) * score_scale
    masked = jnp.where(allowed, scores, NEG_FILL)
    row_peak = lax.optimization_barrier(jnp.max(masked, axis=-1, keepdims=True))
    row_total = lax.optimization_barrier(jnp.sum(jnp.exp(masked - row_peak), axis=-1, keepdims=True))
    log_total = row_peak + jnp.log(row_total)
    probs = jnp.where(allowed, jnp.exp(scores - log_total), 0.0)
    probs_b = probs.astype(jnp.bfloat16)
    attended_heads = jnp.einsum('hqk,khd->qhd', probs_b.astype(jnp.float32), value_heads.astype(jnp.float32)).astype(jnp.bfloat16)
    attended = attended_heads.reshape(length, D)
    attn_raw = plain_dot(attended, w_out)
    attn_scale = rms_scale(attn_raw)
    attn_unit = attn_raw * attn_scale
    hidden = x_seq.astype(jnp.float32) + attn_unit * attn_gain
    hidden_b = hidden.astype(jnp.bfloat16)
    gate_proj = plain_dot(hidden_b, w_gate)
    up_proj = plain_dot(hidden_b, w_up)
    gate_sig = jax.nn.sigmoid(gate_proj)
    gate_act = gate_proj * gate_sig
    mixed_act = (gate_act * up_proj).astype(jnp.bfloat16)
    down_raw = plain_dot(mixed_act, w_down)
    down_scale = rms_scale(down_raw)
    down_unit = down_raw * down_scale
    block_out = (hidden + down_unit * mlp_gain).astype(jnp.bfloat16)
    grad_y = grad_seq.astype(jnp.float32)
    grad_mlp_gain = lax.optimization_barrier(jnp.sum(grad_y * down_unit, axis=0))
    grad_down_in = rms_back(grad_y * mlp_gain, down_unit, down_scale).astype(jnp.bfloat16)
    grad_w_down = left_transposed(mixed_act, grad_down_in)
    grad_mixed = times_transposed(grad_down_in, w_down)
    grad_gate_in = (grad_mixed * up_proj * gate_sig * (1.0 + gate_proj * (1.0 - gate_sig))).astype(jnp.bfloat16)
    grad_up_in = (grad_mixed * gate_act).astype(jnp.bfloat16)
    grad_w_gate = left_transposed(hidden_b, grad_gate_in)
    grad_w_up = left_transposed(hidden_b, grad_up_in)
    grad_hidden = grad_y + times_transposed(grad_gate_in, w_gate) + times_transposed(grad_up_in, w_up)
    grad_attn_gain = lax.optimization_barrier(jnp.sum(grad_hidden * attn_unit, axis=0))
    grad_attn_in = rms_back(grad_hidden * attn_gain, attn_unit, attn_scale).astype(jnp.bfloat16)
    grad_w_out = left_transposed(attended, grad_attn_in)
    grad_att = times_transposed(grad_attn_in, w_out).astype(jnp.bfloat16).reshape(length, HEADS, HD)
    grad_att_f = grad_att.astype(jnp.float32)
    delta = lax.optimization_barrier(jnp.sum(grad_att_f * attended_heads.astype(jnp.float32), axis=-1))
    grad_probs = jnp.einsum('qhd,khd->hqk', grad_att_f, value_heads.astype(jnp.float32))
    grad_scores = (probs * (grad_probs - jnp.transpose(delta)[:, :, None]) * score_scale).astype(jnp.bfloat16)
    grad_scores_f = grad_scores.astype(jnp.float32)
    grad_query_rot = jnp.einsum('hqk,khd->qhd', grad_scores_f, key_rot.astype(jnp.float32))
    grad_key_rot = jnp.einsum('hqk,qhd->khd', grad_scores_f, query_rot.astype(jnp.float32))
    grad_value_heads = jnp.einsum('hqk,qhd->khd', probs_b.astype(jnp.float32), grad_att_f)
    grad_query_norm = unturn(grad_query_rot)
    grad_key_norm = unturn(grad_key_rot)
    grad_query_gain = lax.optimization_barrier(jnp.sum(grad_query_norm * query_unit, axis=0))
    grad_key_gain = lax.optimization_barrier(jnp.sum(grad_key_norm * key_unit, axis=0))
    grad_query_in = rms_back(grad_query_norm * query_gain, query_unit, query_scale).astype(jnp.bfloat16)
    grad_key_in = rms_back(grad_key_norm * key_gain, key_unit, key_scale).astype(jnp.bfloat16)
    grad_value_in = grad_value_heads.reshape(length, D).astype(jnp.bfloat16)
    grad_input = grad_hidden + times_transposed(grad_query_in, w_query) + times_transposed(grad_key_in, w_key) + times_transposed(grad_value_in, w_value)
    grad_w_query = left_transposed(x_seq, grad_query_in)
    grad_w_key = left_transposed(x_seq, grad_key_in)
    grad_w_value = left_transposed(x_seq, grad_value_in)
    weight_grads = (grad_w_query, grad_w_key, grad_w_value, grad_w_out, grad_w_gate, grad_w_up, grad_w_down)
    gain_grads = (grad_query_gain, grad_key_gain, grad_attn_gain, grad_mlp_gain)
    return (block_out, grad_input, weight_grads, gain_grads)

def reference(block_input, segment_ids, positions, w_query, w_key, w_value, w_out, w_gate, w_up, w_down, query_gain, key_gain, attn_gain, mlp_gain, grad_output):
    seq_count = block_input.shape[0] // LEN
    weights = (w_query, w_key, w_value, w_out, w_gate, w_up, w_down)
    gains = (query_gain, key_gain, attn_gain, mlp_gain)

    def step_fn(running, seq_item):
        x_seq, grad_seq, seg_seq, pos_seq = seq_item
        block_out, grad_in, weight_grads, gain_grads = one_sequence(x_seq, grad_seq, seg_seq, pos_seq, weights, gains)
        running = jax.tree.map(lambda acc_val, new_val: acc_val + new_val, running, (weight_grads, gain_grads))
        return (running, (block_out, grad_in))
    initial = (tuple((jnp.zeros(one_w.shape, jnp.float32) for one_w in weights)), tuple((jnp.zeros(one_g.shape, jnp.float32) for one_g in gains)))
    stacked = (block_input.reshape(seq_count, LEN, D), grad_output.reshape(seq_count, LEN, D), segment_ids.reshape(seq_count, LEN), positions.reshape(seq_count, LEN))
    totals, results = lax.scan(step_fn, initial, stacked)
    weight_grads, gain_grads = totals
    block_out, grad_in = results
    return (block_out.reshape(-1, D), grad_in.reshape(-1, D), weight_grads[0], weight_grads[1], weight_grads[2], weight_grads[3], weight_grads[4], weight_grads[5], weight_grads[6], gain_grads[0], gain_grads[1], gain_grads[2], gain_grads[3])
```

```python
import functools

import jax
import jax.numpy as jnp
from jax import lax
from jax.experimental import pallas as pl
from jax.experimental.pallas import tpu as pltpu
from jax.sharding import PartitionSpec as P

HD = 128
LEN = 1024
BQ = 256

EPS = 1e-06
THETA = 500000.0
NEG_FILL = -1e30
SCORE_SCALE = HD ** (-0.5)
F32 = jnp.float32
BF16 = jnp.bfloat16


def plain_dot(left_mat, right_mat):
    return jnp.dot(left_mat, right_mat, preferred_element_type=F32)


def times_transposed(left_mat, right_mat):
    return lax.dot_general(
        left_mat, right_mat, (((1,), (1,)), ((), ())), preferred_element_type=F32
    )


def left_transposed(left_mat, right_mat):
    return lax.dot_general(
        left_mat, right_mat, (((0,), (0,)), ((), ())), preferred_element_type=F32
    )


def rope_tables(positions):
    half_dim = HD // 2
    inv_freq = THETA ** (-(jnp.arange(half_dim, dtype=F32) * 2.0) / HD)
    angles = positions.astype(F32)[:, None] * inv_freq[None, :]
    cos_half, sin_half = jnp.cos(angles), jnp.sin(angles)
    cosine = jnp.concatenate([cos_half, cos_half], axis=-1)
    sine_signed = jnp.concatenate([-sin_half, sin_half], axis=-1)
    return cosine, sine_signed


def allowed_block(seg_col_ref, seg_row_ref, first, keys):
    rows = seg_col_ref[pl.ds(first, BQ), :]
    cols = seg_row_ref[:, :keys]
    query_index = first + lax.broadcasted_iota(jnp.int32, (BQ, keys), 0)
    key_index = lax.broadcasted_iota(jnp.int32, (BQ, keys), 1)
    return (rows == cols) & (key_index <= query_index)


def attend_forward_kernel(
    q_ref, k_ref, v_ref, qs_ref, ks_ref, qg_ref, kg_ref, cos_ref, sin_ref, segc_ref, segr_ref,
    qrot_ref, krot_ref, vb_ref, att_ref, log_ref,
):
    cosine, sine = cos_ref[...], sin_ref[...]

    def turned(raw, scale, gain):
        norm = raw * scale * gain
        return (norm * cosine + pltpu.roll(norm, HD // 2, 1) * sine).astype(BF16)

    qrot_ref[...] = turned(q_ref[...], qs_ref[...], qg_ref[...])
    krot_ref[...] = turned(k_ref[...], ks_ref[...], kg_ref[...])
    vb_ref[...] = v_ref[...].astype(BF16)
    for first in range(0, LEN, BQ):
        keys = first + BQ
        scores = times_transposed(qrot_ref[first:keys, :], krot_ref[:keys, :]) * SCORE_SCALE
        allowed = allowed_block(segc_ref, segr_ref, first, keys)
        masked = jnp.where(allowed, scores, NEG_FILL)
        peak = jnp.max(masked, axis=1, keepdims=True)
        weight = jnp.exp(masked - peak)
        total = jnp.sum(weight, axis=1, keepdims=True)
        probs = (weight * (1.0 / total)).astype(BF16)
        att_ref[first:keys, :] = plain_dot(probs, vb_ref[:keys, :]).astype(BF16)
        log_ref[0, first:keys, :] = peak + jnp.log(total)


def attend_backward_kernel(
    q_ref, k_ref, qs_ref, ks_ref, qg_ref, kg_ref, cos_ref, sin_ref, segc_ref, segr_ref,
    qrot_ref, krot_ref, vb_ref, att_ref, log_ref, grad_ref,
    dzq_ref, dzk_ref, gv_ref, dotq_ref, dotk_ref, gainq_ref, gaink_ref,
    dq_acc, dk_acc, dv_acc,
):
    dk_acc[...] = jnp.zeros_like(dk_acc)
    dv_acc[...] = jnp.zeros_like(dv_acc)
    for first in range(0, LEN, BQ):
        keys = first + BQ
        queries = qrot_ref[first:keys, :]
        grads = grad_ref[first:keys, :]
        scores = times_transposed(queries, krot_ref[:keys, :]) * SCORE_SCALE
        allowed = allowed_block(segc_ref, segr_ref, first, keys)
        probs = jnp.where(allowed, jnp.exp(scores - log_ref[0, first:keys, :]), 0.0)
        delta = jnp.sum(
            grads.astype(F32) * att_ref[first:keys, :].astype(F32), axis=1, keepdims=True
        )
        grad_probs = times_transposed(grads, vb_ref[:keys, :])
        grad_scores = (probs * (grad_probs - delta) * SCORE_SCALE).astype(BF16)
        dq_acc[first:keys, :] = plain_dot(grad_scores, krot_ref[:keys, :])
        dk_acc[:keys, :] += left_transposed(grad_scores, queries)
        dv_acc[:keys, :] += left_transposed(probs.astype(BF16), grads)
    gv_ref[...] = dv_acc[...].astype(BF16)
    cosine, sine = cos_ref[...], sin_ref[...]

    def finish(acc, raw_ref, scale_ref, gain_ref, dz_ref, dot_ref, gain_grad_ref):
        grad_rot = acc[...]
        grad_norm = grad_rot * cosine - pltpu.roll(grad_rot, HD // 2, 1) * sine
        unit = raw_ref[...] * scale_ref[...]
        gain_grad_ref[...] = jnp.sum(grad_norm * unit, axis=0, keepdims=True)
        grad_unit = grad_norm * gain_ref[...]
        dz_ref[...] = grad_unit
        part = jnp.sum(grad_unit * unit, axis=1, keepdims=True)

        @pl.when(pl.program_id(0) == 0)
        def _():
            dot_ref[...] = part

        @pl.when(pl.program_id(0) > 0)
        def _():
            dot_ref[...] += part

    finish(dq_acc, q_ref, qs_ref, qg_ref, dzq_ref, dotq_ref, gainq_ref)
    finish(dk_acc, k_ref, ks_ref, kg_ref, dzk_ref, dotk_ref, gaink_ref)


def head_spec(offset):
    return pl.BlockSpec((LEN, HD), lambda h: (0, offset + h))


def whole_spec(shape):
    return pl.BlockSpec(shape, lambda h: (0,) * len(shape))


def gain_spec():
    return pl.BlockSpec((1, HD), lambda h: (0, h))


LOG_SPEC = pl.BlockSpec((1, LEN, 1), lambda h: (h, 0, 0))
COLUMN = (LEN, 1)
TABLE = (LEN, HD)


def attend_forward(qkv, scales, gains, tables, seg_col, seg_row, heads):
    width = heads * HD
    piece = jax.ShapeDtypeStruct((LEN, width), BF16)
    return pl.pallas_call(
        attend_forward_kernel,
        grid=(heads,),
        in_specs=[
            head_spec(0), head_spec(heads), head_spec(2 * heads),
            whole_spec(COLUMN), whole_spec(COLUMN), gain_spec(), gain_spec(),
            whole_spec(TABLE), whole_spec(TABLE), whole_spec(COLUMN), whole_spec((1, LEN)),
        ],
        out_specs=[head_spec(0)] * 4 + [LOG_SPEC],
        out_shape=[piece] * 4 + [jax.ShapeDtypeStruct((heads, LEN, 1), F32)],
        compiler_params=pltpu.CompilerParams(vmem_limit_bytes=48 << 20),
        cost_estimate=pl.CostEstimate(
            flops=heads * 4 * LEN * LEN * HD, bytes_accessed=LEN * width * 20, transcendentals=0
        ),
        name="attend_forward",
    )(qkv, qkv, qkv, *scales, *gains, *tables, seg_col, seg_row)


def attend_backward(qkv, scales, gains, tables, seg_col, seg_row, saved, grad_att, heads):
    width = heads * HD
    full = jax.ShapeDtypeStruct((LEN, width), F32)
    column = jax.ShapeDtypeStruct(COLUMN, F32)
    gain_row = jax.ShapeDtypeStruct((1, width), F32)
    return pl.pallas_call(
        attend_backward_kernel,
        grid=(heads,),
        in_specs=[
            head_spec(0), head_spec(heads),
            whole_spec(COLUMN), whole_spec(COLUMN), gain_spec(), gain_spec(),
            whole_spec(TABLE), whole_spec(TABLE), whole_spec(COLUMN), whole_spec((1, LEN)),
            head_spec(0), head_spec(0), head_spec(0), head_spec(0), LOG_SPEC, head_spec(0),
        ],
        out_specs=[
            head_spec(0), head_spec(0), head_spec(0),
            whole_spec(COLUMN), whole_spec(COLUMN), gain_spec(), gain_spec(),
        ],
        out_shape=[
            full, full, jax.ShapeDtypeStruct((LEN, width), BF16), column, column, gain_row, gain_row,
        ],
        scratch_shapes=[pltpu.VMEM((LEN, HD), F32)] * 3,
        compiler_params=pltpu.CompilerParams(vmem_limit_bytes=48 << 20),
        cost_estimate=pl.CostEstimate(
            flops=heads * 10 * LEN * LEN * HD, bytes_accessed=LEN * width * 40, transcendentals=0
        ),
        name="attend_backward",
    )(qkv, qkv, *scales, *gains, *tables, seg_col, seg_row, *saved, grad_att)


def shards(
    sizes,
    block_input,
    segment_ids,
    positions,
    w_query,
    w_key,
    w_value,
    w_out,
    w_gate,
    w_up,
    w_down,
    query_gain,
    key_gain,
    attn_gain,
    mlp_gain,
    grad_output,
):
    cores, rows, cols = sizes
    tokens_here, width = block_input.shape
    assert tokens_here == LEN and cores == 2
    local_width = w_query.shape[1]
    heads = local_width // HD
    core = lax.axis_index("dp")
    swap = [(0, 1), (1, 0)]

    def own_half(array, axis):
        half = array.shape[axis] // 2
        return lax.dynamic_slice_in_dim(array, core * half, half, axis)

    def other_half(array, axis):
        half = array.shape[axis] // 2
        return lax.dynamic_slice_in_dim(array, (1 - core) * half, half, axis)

    def gather(weight, axis):
        return lax.all_gather(own_half(weight, axis), ("row", "dp"), axis=axis, tiled=True)

    def sum_over_col(partial):
        piece = lax.psum_scatter(partial.astype(BF16), "col", scatter_dimension=0, tiled=True)
        whole = lax.all_gather(piece, ("dp", "col"), axis=0, tiled=True)
        return lax.dynamic_slice_in_dim(whole, core * tokens_here, tokens_here, 0).astype(F32)

    def both_cores(half, axis):
        other = lax.ppermute(half, "dp", swap)
        first = jnp.where(core == 0, half, other)
        second = jnp.where(core == 0, other, half)
        return jnp.concatenate([first, second], axis=axis).astype(F32)

    def summed(left_mat, right_own, right_other):
        sent = left_transposed(left_mat, right_other).astype(BF16)
        got = lax.ppermute(sent, "dp", swap)
        total = (left_transposed(left_mat, right_own) + got.astype(F32)).astype(BF16)
        return lax.psum_scatter(total, "row", scatter_dimension=0, tiled=True)

    full_qkv = gather(jnp.concatenate([w_query, w_key, w_value], axis=1), 0)
    full_out = gather(w_out, 1)
    full_gate = gather(w_gate, 0)
    full_up = gather(w_up, 0)
    full_down = gather(w_down, 1)

    qkv = plain_dot(block_input, full_qkv)
    query_raw, key_raw = qkv[:, :local_width], qkv[:, local_width : 2 * local_width]
    query_sq, key_sq = lax.psum(
        (jnp.sum(query_raw * query_raw, axis=1), jnp.sum(key_raw * key_raw, axis=1)), "col"
    )
    query_scale = lax.rsqrt(query_sq / width + EPS)[:, None]
    key_scale = lax.rsqrt(key_sq / width + EPS)[:, None]
    scales = (query_scale, key_scale)
    gains = (query_gain[None, :], key_gain[None, :])
    tables = rope_tables(positions)
    seg_col, seg_row = segment_ids[:, None], segment_ids[None, :]
    query_rot, key_rot, value_heads, attended, log_total = attend_forward(
        qkv, scales, gains, tables, seg_col, seg_row, heads
    )
    attn_raw = sum_over_col(plain_dot(attended, full_out))
    attn_scale = lax.rsqrt(jnp.mean(attn_raw * attn_raw, axis=1, keepdims=True) + EPS)
    attn_unit = attn_raw * attn_scale
    hidden = block_input.astype(F32) + attn_unit * attn_gain
    hidden_b = hidden.astype(BF16)
    gate_proj = plain_dot(hidden_b, full_gate)
    up_proj = plain_dot(hidden_b, full_up)
    gate_sig = jax.nn.sigmoid(gate_proj)
    gate_act = gate_proj * gate_sig
    mixed_act = (gate_act * up_proj).astype(BF16)
    down_raw = sum_over_col(plain_dot(mixed_act, full_down))
    down_scale = lax.rsqrt(jnp.mean(down_raw * down_raw, axis=1, keepdims=True) + EPS)
    down_unit = down_raw * down_scale
    block_output = (hidden + down_unit * mlp_gain).astype(BF16)

    grad_y = grad_output.astype(F32)
    grad_mlp_gain = jnp.sum(grad_y * down_unit, axis=0)
    down_dz = grad_y * mlp_gain
    grad_down_in = (
        down_scale * (down_dz - down_unit * jnp.mean(down_dz * down_unit, axis=1, keepdims=True))
    ).astype(BF16)
    grad_mixed = times_transposed(grad_down_in, full_down)
    grad_gate_in = (grad_mixed * up_proj * gate_sig * (1.0 + gate_proj * (1.0 - gate_sig))).astype(BF16)
    grad_up_in = (grad_mixed * gate_act).astype(BF16)
    mlp_part = times_transposed(grad_gate_in, full_gate) + times_transposed(grad_up_in, full_up)
    grad_hidden = grad_y + sum_over_col(mlp_part)
    down_block = summed(grad_down_in, own_half(mixed_act, 1), other_half(mixed_act, 1))
    gate_block = summed(hidden_b, own_half(grad_gate_in, 1), other_half(grad_gate_in, 1))
    up_block = summed(hidden_b, own_half(grad_up_in, 1), other_half(grad_up_in, 1))

    grad_attn_gain = jnp.sum(grad_hidden * attn_unit, axis=0)
    attn_dz = grad_hidden * attn_gain
    grad_attn_in = (
        attn_scale * (attn_dz - attn_unit * jnp.mean(attn_dz * attn_unit, axis=1, keepdims=True))
    ).astype(BF16)
    grad_att = times_transposed(grad_attn_in, full_out).astype(BF16)
    query_dz, key_dz, grad_value_in, query_dot, key_dot, grad_query_gain, grad_key_gain = attend_backward(
        qkv, scales, gains, tables, seg_col, seg_row,
        (query_rot, key_rot, value_heads, attended, log_total), grad_att, heads,
    )
    query_dot, key_dot = lax.psum((query_dot[:, 0], key_dot[:, 0]), "col")
    grad_query_in = (
        query_scale * (query_dz - query_raw * query_scale * (query_dot / width)[:, None])
    ).astype(BF16)
    grad_key_in = (
        key_scale * (key_dz - key_raw * key_scale * (key_dot / width)[:, None])
    ).astype(BF16)
    grad_qkv = jnp.concatenate([grad_query_in, grad_key_in, grad_value_in], axis=1)
    grad_input = grad_hidden + sum_over_col(times_transposed(grad_qkv, full_qkv))

    def interleaved(picker):
        return jnp.concatenate(
            [picker(one, 1) for one in (grad_query_in, grad_key_in, grad_value_in)], axis=1
        )

    qkv_block = summed(block_input, interleaved(own_half), interleaved(other_half))
    out_block = summed(grad_attn_in, own_half(attended, 1), other_half(attended, 1))
    qkv_pair = both_cores(qkv_block[None], 0)
    quarter = local_width // 2

    def projection(index):
        part = qkv_pair[:, :, index * quarter : (index + 1) * quarter]
        return jnp.concatenate([part[0], part[1]], axis=1)

    gain_grads = lax.psum(
        (grad_query_gain[0], grad_key_gain[0], grad_attn_gain, grad_mlp_gain), ("dp", "row")
    )
    return (
        block_output,
        grad_input,
        projection(0),
        projection(1),
        projection(2),
        jnp.transpose(both_cores(out_block, 1)),
        both_cores(gate_block, 1),
        both_cores(up_block, 1),
        jnp.transpose(both_cores(down_block, 1)),
        gain_grads[0],
        gain_grads[1],
        gain_grads[2],
        gain_grads[3],
    )


def solution(mesh):
    in_specs = (
        P(("dp", "row"), None),
        P(("dp", "row")),
        P(("dp", "row")),
        P("row", "col"),
        P("row", "col"),
        P("row", "col"),
        P("col", "row"),
        P("row", "col"),
        P("row", "col"),
        P("col", "row"),
        P("col"),
        P("col"),
        P(),
        P(),
        P(("dp", "row"), None),
    )
    out_specs = (
        P(("dp", "row"), None),
        P(("dp", "row"), None),
        P("row", "col"),
        P("row", "col"),
        P("row", "col"),
        P("col", "row"),
        P("row", "col"),
        P("row", "col"),
        P("col", "row"),
        P("col"),
        P("col"),
        P(),
        P(),
    )
    sizes = (mesh.shape["dp"], mesh.shape["row"], mesh.shape["col"])
    return jax.shard_map(
        functools.partial(shards, sizes), mesh=mesh, in_specs=in_specs, out_specs=out_specs, check_vma=False
    )
```

```python
import functools

import jax
import jax.numpy as jnp
from jax import lax
from jax.experimental import pallas as pl
from jax.experimental.pallas import tpu as pltpu
from jax.sharding import PartitionSpec as P

HD = 128
LEN = 1024
BQ = 256

EPS = 1e-06
THETA = 500000.0
NEG_FILL = -1e30
SCORE_SCALE = HD ** (-0.5)
F32 = jnp.float32
BF16 = jnp.bfloat16


def plain_dot(left_mat, right_mat):
    return jnp.dot(left_mat, right_mat, preferred_element_type=F32)


def times_transposed(left_mat, right_mat):
    return lax.dot_general(
        left_mat, right_mat, (((1,), (1,)), ((), ())), preferred_element_type=F32
    )


def left_transposed(left_mat, right_mat):
    return lax.dot_general(
        left_mat, right_mat, (((0,), (0,)), ((), ())), preferred_element_type=F32
    )


def rope_tables(positions):
    half_dim = HD // 2
    inv_freq = THETA ** (-(jnp.arange(half_dim, dtype=F32) * 2.0) / HD)
    angles = positions.astype(F32)[:, None] * inv_freq[None, :]
    cos_half, sin_half = jnp.cos(angles), jnp.sin(angles)
    cosine = jnp.concatenate([cos_half, cos_half], axis=-1)
    sine_signed = jnp.concatenate([-sin_half, sin_half], axis=-1)
    return cosine, sine_signed


def allowed_block(seg_col_ref, seg_row_ref, first, keys):
    rows = seg_col_ref[pl.ds(first, BQ), :]
    cols = seg_row_ref[:, :keys]
    query_index = first + lax.broadcasted_iota(jnp.int32, (BQ, keys), 0)
    key_index = lax.broadcasted_iota(jnp.int32, (BQ, keys), 1)
    return (rows == cols) & (key_index <= query_index)


def attend_forward_kernel(
    q_ref, k_ref, v_ref, qs_ref, ks_ref, qg_ref, kg_ref, cos_ref, sin_ref, segc_ref, segr_ref,
    qrot_ref, krot_ref, vb_ref, att_ref, log_ref,
):
    cosine, sine = cos_ref[...], sin_ref[...]

    def turned(raw, scale, gain):
        norm = raw * scale * gain
        return (norm * cosine + pltpu.roll(norm, HD // 2, 1) * sine).astype(BF16)

    qrot_ref[...] = turned(q_ref[...], qs_ref[...], qg_ref[...])
    krot_ref[...] = turned(k_ref[...], ks_ref[...], kg_ref[...])
    vb_ref[...] = v_ref[...].astype(BF16)
    for first in range(0, LEN, BQ):
        keys = first + BQ
        scores = times_transposed(qrot_ref[first:keys, :], krot_ref[:keys, :]) * SCORE_SCALE
        allowed = allowed_block(segc_ref, segr_ref, first, keys)
        masked = jnp.where(allowed, scores, NEG_FILL)
        peak = jnp.max(masked, axis=1, keepdims=True)
        weight = jnp.exp(masked - peak)
        total = jnp.sum(weight, axis=1, keepdims=True)
        probs = (weight * (1.0 / total)).astype(BF16)
        att_ref[first:keys, :] = plain_dot(probs, vb_ref[:keys, :]).astype(BF16)
        log_ref[0, first:keys, :] = peak + jnp.log(total)


def attend_backward_kernel(
    q_ref, k_ref, qs_ref, ks_ref, qg_ref, kg_ref, cos_ref, sin_ref, segc_ref, segr_ref,
    qrot_ref, krot_ref, vb_ref, att_ref, log_ref, grad_ref,
    dzq_ref, dzk_ref, gv_ref, dotq_ref, dotk_ref, gainq_ref, gaink_ref,
    dq_acc, dk_acc, dv_acc,
):
    dk_acc[...] = jnp.zeros_like(dk_acc)
    dv_acc[...] = jnp.zeros_like(dv_acc)
    for first in range(0, LEN, BQ):
        keys = first + BQ
        queries = qrot_ref[first:keys, :]
        grads = grad_ref[first:keys, :]
        scores = times_transposed(queries, krot_ref[:keys, :]) * SCORE_SCALE
        allowed = allowed_block(segc_ref, segr_ref, first, keys)
        probs = jnp.where(allowed, jnp.exp(scores - log_ref[0, first:keys, :]), 0.0)
        delta = jnp.sum(
            grads.astype(F32) * att_ref[first:keys, :].astype(F32), axis=1, keepdims=True
        )
        grad_probs = times_transposed(grads, vb_ref[:keys, :])
        grad_scores = (probs * (grad_probs - delta) * SCORE_SCALE).astype(BF16)
        dq_acc[first:keys, :] = plain_dot(grad_scores, krot_ref[:keys, :])
        dk_acc[:keys, :] += left_transposed(grad_scores, queries)
        dv_acc[:keys, :] += left_transposed(probs.astype(BF16), grads)
    gv_ref[...] = dv_acc[...].astype(BF16)
    cosine, sine = cos_ref[...], sin_ref[...]

    def finish(acc, raw_ref, scale_ref, gain_ref, dz_ref, dot_ref, gain_grad_ref):
        grad_rot = acc[...]
        grad_norm = grad_rot * cosine - pltpu.roll(grad_rot, HD // 2, 1) * sine
        unit = raw_ref[...] * scale_ref[...]
        gain_grad_ref[...] = jnp.sum(grad_norm * unit, axis=0, keepdims=True)
        grad_unit = grad_norm * gain_ref[...]
        dz_ref[...] = grad_unit
        part = jnp.sum(grad_unit * unit, axis=1, keepdims=True)

        @pl.when(pl.program_id(0) == 0)
        def _():
            dot_ref[...] = part

        @pl.when(pl.program_id(0) > 0)
        def _():
            dot_ref[...] += part

    finish(dq_acc, q_ref, qs_ref, qg_ref, dzq_ref, dotq_ref, gainq_ref)
    finish(dk_acc, k_ref, ks_ref, kg_ref, dzk_ref, dotk_ref, gaink_ref)


def head_spec(offset):
    return pl.BlockSpec((LEN, HD), lambda h: (0, offset + h))


def whole_spec(shape):
    return pl.BlockSpec(shape, lambda h: (0,) * len(shape))


def gain_spec():
    return pl.BlockSpec((1, HD), lambda h: (0, h))


LOG_SPEC = pl.BlockSpec((1, LEN, 1), lambda h: (h, 0, 0))
COLUMN = (LEN, 1)
TABLE = (LEN, HD)


def attend_forward(qkv, scales, gains, tables, seg_col, seg_row, heads):
    width = heads * HD
    piece = jax.ShapeDtypeStruct((LEN, width), BF16)
    return pl.pallas_call(
        attend_forward_kernel,
        grid=(heads,),
        in_specs=[
            head_spec(0), head_spec(heads), head_spec(2 * heads),
            whole_spec(COLUMN), whole_spec(COLUMN), gain_spec(), gain_spec(),
            whole_spec(TABLE), whole_spec(TABLE), whole_spec(COLUMN), whole_spec((1, LEN)),
        ],
        out_specs=[head_spec(0)] * 4 + [LOG_SPEC],
        out_shape=[piece] * 4 + [jax.ShapeDtypeStruct((heads, LEN, 1), F32)],
        compiler_params=pltpu.CompilerParams(vmem_limit_bytes=48 << 20),
        cost_estimate=pl.CostEstimate(
            flops=heads * 4 * LEN * LEN * HD, bytes_accessed=LEN * width * 20, transcendentals=0
        ),
        name="attend_forward",
    )(qkv, qkv, qkv, *scales, *gains, *tables, seg_col, seg_row)


def attend_backward(qkv, scales, gains, tables, seg_col, seg_row, saved, grad_att, heads):
    width = heads * HD
    full = jax.ShapeDtypeStruct((LEN, width), F32)
    column = jax.ShapeDtypeStruct(COLUMN, F32)
    gain_row = jax.ShapeDtypeStruct((1, width), F32)
    return pl.pallas_call(
        attend_backward_kernel,
        grid=(heads,),
        in_specs=[
            head_spec(0), head_spec(heads),
            whole_spec(COLUMN), whole_spec(COLUMN), gain_spec(), gain_spec(),
            whole_spec(TABLE), whole_spec(TABLE), whole_spec(COLUMN), whole_spec((1, LEN)),
            head_spec(0), head_spec(0), head_spec(0), head_spec(0), LOG_SPEC, head_spec(0),
        ],
        out_specs=[
            head_spec(0), head_spec(0), head_spec(0),
            whole_spec(COLUMN), whole_spec(COLUMN), gain_spec(), gain_spec(),
        ],
        out_shape=[
            full, full, jax.ShapeDtypeStruct((LEN, width), BF16), column, column, gain_row, gain_row,
        ],
        scratch_shapes=[pltpu.VMEM((LEN, HD), F32)] * 3,
        compiler_params=pltpu.CompilerParams(vmem_limit_bytes=48 << 20),
        cost_estimate=pl.CostEstimate(
            flops=heads * 10 * LEN * LEN * HD, bytes_accessed=LEN * width * 40, transcendentals=0
        ),
        name="attend_backward",
    )(qkv, qkv, *scales, *gains, *tables, seg_col, seg_row, *saved, grad_att)


def shards(
    sizes,
    block_input,
    segment_ids,
    positions,
    w_query,
    w_key,
    w_value,
    w_out,
    w_gate,
    w_up,
    w_down,
    query_gain,
    key_gain,
    attn_gain,
    mlp_gain,
    grad_output,
):
    cores, rows, cols = sizes
    tokens_here, width = block_input.shape
    assert tokens_here == LEN and cores == 2 and cols == 4
    local_width = w_query.shape[1]
    heads = local_width // HD
    chunk = tokens_here // cols
    core = lax.axis_index("dp")
    col = lax.axis_index("col")
    swap = [(0, 1), (1, 0)]

    def own_half(array, axis):
        half = array.shape[axis] // 2
        return lax.dynamic_slice_in_dim(array, core * half, half, axis)

    def other_half(array, axis):
        half = array.shape[axis] // 2
        return lax.dynamic_slice_in_dim(array, (1 - core) * half, half, axis)

    def gather(weight, axis):
        return lax.all_gather(own_half(weight, axis), ("row", "dp"), axis=axis, tiled=True)

    def line_step(from_left, from_right, step):
        from_left = lax.ppermute(from_left, "col", [(i, i + 1) for i in range(step - 1, cols - 1)])
        from_right = lax.ppermute(from_right, "col", [(i + 1, i) for i in range(cols - step)])
        return from_left, from_right

    def line_gather(own):
        lefts, rights = [own], [own]
        for step in range(1, cols):
            left, right = line_step(lefts[-1], rights[-1], step)
            lefts.append(left)
            rights.append(right)
        return lefts, rights

    def pick(at_zero, at_one, at_two, at_three):
        low = jnp.where(col == 0, at_zero, at_one)
        high = jnp.where(col == 2, at_two, at_three)
        return jnp.where(col < 2, low, high)

    slot_chunk = (
        pick(3, 3, 0, 0),
        pick(2, 2, 1, 1),
        pick(1, 0, 3, 2),
        col,
    )

    def slot_rows(array, slot):
        return lax.dynamic_slice_in_dim(array, slot_chunk[slot] * chunk, chunk, 0)

    def place(whole, slot, rows_of):
        return lax.dynamic_update_slice_in_dim(whole, rows_of, slot_chunk[slot] * chunk, 0)

    def gather_slots(own):
        lefts, rights = line_gather(own)
        return (
            pick(rights[3], rights[2], lefts[2], lefts[3]),
            pick(rights[2], rights[1], lefts[1], lefts[2]),
            jnp.where(col % 2 == 0, rights[1], lefts[1]),
            own,
        )

    def sum_slots(parts):
        up = lax.ppermute(parts[0], "col", [(0, 1)])
        down = lax.ppermute(parts[0], "col", [(3, 2)])
        up = jnp.where(col == 0, parts[1], parts[0]) + up
        down = jnp.where(col == 3, parts[1], parts[0]) + down
        up = lax.ppermute(up, "col", [(0, 1), (1, 2)])
        down = lax.ppermute(down, "col", [(3, 2), (2, 1)])
        up = jnp.where(col == 1, parts[1], parts[2]) + up
        down = jnp.where(col == 2, parts[1], parts[2]) + down
        up = lax.ppermute(up, "col", [(0, 1), (1, 2), (2, 3)])
        down = lax.ppermute(down, "col", [(3, 2), (2, 1), (1, 0)])
        return parts[3].astype(F32) + up.astype(F32) + down.astype(F32)

    def both_cores(half, axis):
        other = lax.ppermute(half, "dp", swap)
        first = jnp.where(core == 0, half, other)
        second = jnp.where(core == 0, other, half)
        return jnp.concatenate([first, second], axis=axis).astype(F32)

    def summed(left_mat, right_own, right_other):
        sent = left_transposed(left_mat, right_other).astype(BF16)
        got = lax.ppermute(sent, "dp", swap)
        total = (left_transposed(left_mat, right_own) + got.astype(F32)).astype(BF16)
        return lax.psum_scatter(total, "row", scatter_dimension=0, tiled=True)

    full_qkv = gather(jnp.concatenate([w_query, w_key, w_value], axis=1), 0)
    out_half = own_half(w_out, 0)
    out_pieces = [out_half] + [
        lax.ppermute(out_half, "col", [(i, (i - step) % cols) for i in range(cols)])
        for step in range(1, cols)
    ]
    full_out = lax.all_gather(jnp.stack(out_pieces), ("row", "dp"), axis=0, tiled=False)
    full_out = full_out.reshape(rows, cores, cols, local_width // 2, width // rows)
    full_out = jnp.transpose(full_out, (2, 1, 3, 0, 4)).reshape(cols * local_width, width)
    full_gate = gather(w_gate, 0)
    full_up = gather(w_up, 0)
    full_down = gather(w_down, 1)

    qkv = plain_dot(block_input, full_qkv)
    query_raw, key_raw = qkv[:, :local_width], qkv[:, local_width : 2 * local_width]
    query_sq, key_sq = lax.psum(
        (jnp.sum(query_raw * query_raw, axis=1), jnp.sum(key_raw * key_raw, axis=1)), "col"
    )
    query_scale = lax.rsqrt(query_sq / width + EPS)[:, None]
    key_scale = lax.rsqrt(key_sq / width + EPS)[:, None]
    scales = (query_scale, key_scale)
    gains = (query_gain[None, :], key_gain[None, :])
    tables = rope_tables(positions)
    seg_col, seg_row = segment_ids[:, None], segment_ids[None, :]
    query_rot, key_rot, value_heads, attended, log_total = attend_forward(
        qkv, scales, gains, tables, seg_col, seg_row, heads
    )
    lefts, rights = line_gather(attended)
    attended_all = jnp.concatenate(
        [attended] + [rights[step] + lefts[cols - step] for step in range(1, cols)], axis=1
    )

    saved = []
    down_parts = []
    for slot in range(cols):
        attn_raw = plain_dot(slot_rows(attended_all, slot), full_out)
        attn_scale = lax.rsqrt(jnp.mean(attn_raw * attn_raw, axis=1, keepdims=True) + EPS)
        attn_unit = attn_raw * attn_scale
        hidden = slot_rows(block_input, slot).astype(F32) + attn_unit * attn_gain
        hidden_b = hidden.astype(BF16)
        gate_proj = plain_dot(hidden_b, full_gate)
        up_proj = plain_dot(hidden_b, full_up)
        gate_sig = jax.nn.sigmoid(gate_proj)
        gate_act = gate_proj * gate_sig
        mixed_act = (gate_act * up_proj).astype(BF16)
        down_parts.append(plain_dot(mixed_act, full_down).astype(BF16))
        saved.append((attn_scale, attn_raw, hidden, hidden_b, gate_proj, up_proj, mixed_act))
    down_slots = gather_slots(sum_slots(down_parts).astype(BF16))

    block_output = jnp.zeros((tokens_here, width), BF16)
    grad_mlp_gain = 0.0
    mlp_parts = [None] * cols
    grads = [None] * cols
    for slot in reversed(range(cols)):
        attn_scale, attn_raw, hidden, hidden_b, gate_proj, up_proj, mixed_act = saved[slot]
        down_raw = down_slots[slot].astype(F32)
        down_scale = lax.rsqrt(jnp.mean(down_raw * down_raw, axis=1, keepdims=True) + EPS)
        down_unit = down_raw * down_scale
        block_output = place(block_output, slot, (hidden + down_unit * mlp_gain).astype(BF16))
        grad_y = slot_rows(grad_output, slot).astype(F32)
        grad_mlp_gain = grad_mlp_gain + jnp.sum(grad_y * down_unit, axis=0)
        down_dz = grad_y * mlp_gain
        grad_down_in = (
            down_scale * (down_dz - down_unit * jnp.mean(down_dz * down_unit, axis=1, keepdims=True))
        ).astype(BF16)
        grad_mixed = times_transposed(grad_down_in, full_down)
        gate_sig = jax.nn.sigmoid(gate_proj)
        grad_gate_in = (
            grad_mixed * up_proj * gate_sig * (1.0 + gate_proj * (1.0 - gate_sig))
        ).astype(BF16)
        grad_up_in = (grad_mixed * (gate_proj * gate_sig)).astype(BF16)
        mlp_parts[slot] = (
            times_transposed(grad_gate_in, full_gate) + times_transposed(grad_up_in, full_up)
        ).astype(BF16)
        grads[slot] = (grad_down_in, grad_gate_in, grad_up_in)
    mlp_slots = gather_slots(sum_slots(mlp_parts).astype(BF16))

    def stacked(pieces):
        return jnp.concatenate(pieces, axis=0)

    hidden_all = stacked([one[3] for one in saved])
    mixed_all = stacked([one[6] for one in saved])
    grad_down_all, grad_gate_all, grad_up_all = (stacked([one[i] for one in grads]) for i in range(3))
    down_block = summed(grad_down_all, own_half(mixed_all, 1), other_half(mixed_all, 1))
    gate_block = summed(hidden_all, own_half(grad_gate_all, 1), other_half(grad_gate_all, 1))
    up_block = summed(hidden_all, own_half(grad_up_all, 1), other_half(grad_up_all, 1))

    grad_attn_gain = 0.0
    grad_att = jnp.zeros((tokens_here, local_width), BF16)
    attn_ins = [None] * cols
    for slot in reversed(range(cols)):
        attn_scale, attn_raw = saved[slot][:2]
        attn_unit = attn_raw * attn_scale
        grad_hidden = slot_rows(grad_output, slot).astype(F32) + mlp_slots[slot].astype(F32)
        grad_attn_gain = grad_attn_gain + jnp.sum(grad_hidden * attn_unit, axis=0)
        attn_dz = grad_hidden * attn_gain
        grad_attn_in = (
            attn_scale * (attn_dz - attn_unit * jnp.mean(attn_dz * attn_unit, axis=1, keepdims=True))
        ).astype(BF16)
        grad_att = place(
            grad_att, slot, times_transposed(grad_attn_in, full_out[:local_width]).astype(BF16)
        )
        attn_ins[slot] = grad_attn_in
    own_grad_hidden = (
        slot_rows(grad_output, 3).astype(F32) + mlp_slots[3].astype(F32)
    )

    query_dz, key_dz, grad_value_in, query_dot, key_dot, grad_query_gain, grad_key_gain = attend_backward(
        qkv, scales, gains, tables, seg_col, seg_row,
        (query_rot, key_rot, value_heads, attended, log_total), grad_att, heads,
    )
    query_dot, key_dot = lax.psum((query_dot[:, 0], key_dot[:, 0]), "col")
    grad_query_in = (
        query_scale * (query_dz - query_raw * query_scale * (query_dot / width)[:, None])
    ).astype(BF16)
    grad_key_in = (
        key_scale * (key_dz - key_raw * key_scale * (key_dot / width)[:, None])
    ).astype(BF16)
    grad_qkv = jnp.concatenate([grad_query_in, grad_key_in, grad_value_in], axis=1)
    input_parts = [
        times_transposed(slot_rows(grad_qkv, slot), full_qkv).astype(BF16) for slot in range(cols)
    ]
    input_slots = gather_slots((own_grad_hidden + sum_slots(input_parts)).astype(BF16))
    grad_input = jnp.zeros((tokens_here, width), F32)
    for slot in reversed(range(cols)):
        grad_input = place(grad_input, slot, input_slots[slot].astype(F32))

    def interleaved(picker):
        return jnp.concatenate(
            [picker(one, 1) for one in (grad_query_in, grad_key_in, grad_value_in)], axis=1
        )

    qkv_block = summed(block_input, interleaved(own_half), interleaved(other_half))
    attended_slots = stacked([slot_rows(attended, slot) for slot in range(cols)])
    out_block = summed(
        stacked(attn_ins), own_half(attended_slots, 1), other_half(attended_slots, 1)
    )
    qkv_pair = both_cores(qkv_block[None], 0)
    quarter = local_width // 2

    def projection(index):
        part = qkv_pair[:, :, index * quarter : (index + 1) * quarter]
        return jnp.concatenate([part[0], part[1]], axis=1)

    gain_grads = (grad_query_gain[0], grad_key_gain[0], grad_attn_gain, grad_mlp_gain)
    for axis in ("dp", "row"):
        gain_grads = lax.psum(gain_grads, axis)
    return (
        block_output,
        grad_input,
        projection(0),
        projection(1),
        projection(2),
        jnp.transpose(both_cores(out_block, 1)),
        both_cores(gate_block, 1),
        both_cores(up_block, 1),
        jnp.transpose(both_cores(down_block, 1)),
        gain_grads[0],
        gain_grads[1],
        gain_grads[2],
        gain_grads[3],
    )


def solution(mesh):
    in_specs = (
        P(("dp", "row"), None),
        P(("dp", "row")),
        P(("dp", "row")),
        P("row", "col"),
        P("row", "col"),
        P("row", "col"),
        P("col", "row"),
        P("row", "col"),
        P("row", "col"),
        P("col", "row"),
        P("col"),
        P("col"),
        P(),
        P(),
        P(("dp", "row"), None),
    )
    out_specs = (
        P(("dp", "row"), None),
        P(("dp", "row"), None),
        P("row", "col"),
        P("row", "col"),
        P("row", "col"),
        P("col", "row"),
        P("row", "col"),
        P("row", "col"),
        P("col", "row"),
        P("col"),
        P("col"),
        P(),
        P(),
    )
    sizes = (mesh.shape["dp"], mesh.shape["row"], mesh.shape["col"])
    return jax.shard_map(
        functools.partial(shards, sizes), mesh=mesh, in_specs=in_specs, out_specs=out_specs, check_vma=False
    )
```

```python
import functools

import jax
import jax.numpy as jnp
from jax import lax
from jax.experimental import pallas as pl
from jax.experimental.pallas import tpu as pltpu
from jax.sharding import PartitionSpec as P

HD = 128
LEN = 1024
BQ = 256

EPS = 1e-06
THETA = 500000.0
NEG_FILL = -1e30
SCORE_SCALE = HD ** (-0.5)
F32 = jnp.float32
BF16 = jnp.bfloat16


def plain_dot(left_mat, right_mat):
    return jnp.dot(left_mat, right_mat, preferred_element_type=F32)


def times_transposed(left_mat, right_mat):
    return lax.dot_general(
        left_mat, right_mat, (((1,), (1,)), ((), ())), preferred_element_type=F32
    )


def left_transposed(left_mat, right_mat):
    return lax.dot_general(
        left_mat, right_mat, (((0,), (0,)), ((), ())), preferred_element_type=F32
    )


def rope_tables(positions):
    half_dim = HD // 2
    inv_freq = THETA ** (-(jnp.arange(half_dim, dtype=F32) * 2.0) / HD)
    angles = positions.astype(F32)[:, None] * inv_freq[None, :]
    cos_half, sin_half = jnp.cos(angles), jnp.sin(angles)
    cosine = jnp.concatenate([cos_half, cos_half], axis=-1)
    sine_signed = jnp.concatenate([-sin_half, sin_half], axis=-1)
    return cosine, sine_signed


def fill_mask(bias_ref, seg_col_ref, seg_row_ref):
    @pl.when(pl.program_id(0) == 0)
    def _():
        for first in range(0, LEN, BQ):
            keys = first + BQ
            rows = seg_col_ref[first:keys, :]
            cols = seg_row_ref[:, :keys]
            query_index = first + lax.broadcasted_iota(jnp.int32, (BQ, keys), 0)
            key_index = lax.broadcasted_iota(jnp.int32, (BQ, keys), 1)
            allowed = (rows == cols) & (key_index <= query_index)
            bias_ref[first:keys, :keys] = jnp.where(allowed, 0.0, NEG_FILL)


def attend_forward_kernel(
    q_ref, k_ref, v_ref, qs_ref, ks_ref, qg_ref, kg_ref, cos_ref, sin_ref, segc_ref, segr_ref,
    qrot_ref, krot_ref, vb_ref, att_ref, log_ref, bias_ref,
):
    fill_mask(bias_ref, segc_ref, segr_ref)
    cosine, sine = cos_ref[...], sin_ref[...]

    def turned(raw, scale, gain):
        norm = raw * scale * gain
        return (norm * cosine + pltpu.roll(norm, HD // 2, 1) * sine).astype(BF16)

    qrot_ref[...] = turned(q_ref[...], qs_ref[...], qg_ref[...])
    krot_ref[...] = turned(k_ref[...], ks_ref[...], kg_ref[...])
    vb_ref[...] = v_ref[...].astype(BF16)
    for first in range(0, LEN, BQ):
        keys = first + BQ
        scores = times_transposed(qrot_ref[first:keys, :], krot_ref[:keys, :]) * SCORE_SCALE
        masked = scores + bias_ref[first:keys, :keys]
        peak = jnp.max(masked, axis=1, keepdims=True)
        weight = jnp.exp(masked - peak)
        total = jnp.sum(weight, axis=1, keepdims=True)
        probs = (weight * (1.0 / total)).astype(BF16)
        att_ref[first:keys, :] = plain_dot(probs, vb_ref[:keys, :]).astype(BF16)
        log_ref[0, first:keys, :] = peak + jnp.log(total)


def attend_backward_kernel(
    q_ref, k_ref, qs_ref, ks_ref, qg_ref, kg_ref, cos_ref, sin_ref, segc_ref, segr_ref,
    qrot_ref, krot_ref, vb_ref, att_ref, log_ref, grad_ref,
    dzq_ref, dzk_ref, gv_ref, dotq_ref, dotk_ref, gainq_ref, gaink_ref,
    dq_acc, dk_acc, dv_acc, bias_ref,
):
    fill_mask(bias_ref, segc_ref, segr_ref)
    dk_acc[...] = jnp.zeros_like(dk_acc)
    dv_acc[...] = jnp.zeros_like(dv_acc)
    for first in range(0, LEN, BQ):
        keys = first + BQ
        queries = qrot_ref[first:keys, :]
        grads = grad_ref[first:keys, :]
        scores = times_transposed(queries, krot_ref[:keys, :]) * SCORE_SCALE
        probs = jnp.exp(scores + bias_ref[first:keys, :keys] - log_ref[0, first:keys, :])
        delta = jnp.sum(
            grads.astype(F32) * att_ref[first:keys, :].astype(F32), axis=1, keepdims=True
        )
        grad_probs = times_transposed(grads, vb_ref[:keys, :])
        grad_scores = (probs * (grad_probs - delta) * SCORE_SCALE).astype(BF16)
        dq_acc[first:keys, :] = plain_dot(grad_scores, krot_ref[:keys, :])
        dk_acc[:keys, :] += left_transposed(grad_scores, queries)
        dv_acc[:keys, :] += left_transposed(probs.astype(BF16), grads)
    gv_ref[...] = dv_acc[...].astype(BF16)
    cosine, sine = cos_ref[...], sin_ref[...]

    def finish(acc, raw_ref, scale_ref, gain_ref, dz_ref, dot_ref, gain_grad_ref):
        grad_rot = acc[...]
        grad_norm = grad_rot * cosine - pltpu.roll(grad_rot, HD // 2, 1) * sine
        unit = raw_ref[...] * scale_ref[...]
        gain_grad_ref[...] = jnp.sum(grad_norm * unit, axis=0, keepdims=True)
        grad_unit = grad_norm * gain_ref[...]
        dz_ref[...] = grad_unit
        part = jnp.sum(grad_unit * unit, axis=1, keepdims=True)

        @pl.when(pl.program_id(0) == 0)
        def _():
            dot_ref[...] = part

        @pl.when(pl.program_id(0) > 0)
        def _():
            dot_ref[...] += part

    finish(dq_acc, q_ref, qs_ref, qg_ref, dzq_ref, dotq_ref, gainq_ref)
    finish(dk_acc, k_ref, ks_ref, kg_ref, dzk_ref, dotk_ref, gaink_ref)


def head_spec(offset):
    return pl.BlockSpec((LEN, HD), lambda h: (0, offset + h))


def whole_spec(shape):
    return pl.BlockSpec(shape, lambda h: (0,) * len(shape))


def gain_spec():
    return pl.BlockSpec((1, HD), lambda h: (0, h))


LOG_SPEC = pl.BlockSpec((1, LEN, 1), lambda h: (h, 0, 0))
COLUMN = (LEN, 1)
TABLE = (LEN, HD)


def attend_forward(qkv, scales, gains, tables, seg_col, seg_row, heads):
    width = heads * HD
    piece = jax.ShapeDtypeStruct((LEN, width), BF16)
    return pl.pallas_call(
        attend_forward_kernel,
        grid=(heads,),
        in_specs=[
            head_spec(0), head_spec(heads), head_spec(2 * heads),
            whole_spec(COLUMN), whole_spec(COLUMN), gain_spec(), gain_spec(),
            whole_spec(TABLE), whole_spec(TABLE), whole_spec(COLUMN), whole_spec((1, LEN)),
        ],
        out_specs=[head_spec(0)] * 4 + [LOG_SPEC],
        out_shape=[piece] * 4 + [jax.ShapeDtypeStruct((heads, LEN, 1), F32)],
        scratch_shapes=[pltpu.VMEM((LEN, LEN), F32)],
        compiler_params=pltpu.CompilerParams(vmem_limit_bytes=48 << 20),
        cost_estimate=pl.CostEstimate(
            flops=heads * 4 * LEN * LEN * HD, bytes_accessed=LEN * width * 20, transcendentals=0
        ),
        name="attend_forward",
    )(qkv, qkv, qkv, *scales, *gains, *tables, seg_col, seg_row)


def attend_backward(qkv, scales, gains, tables, seg_col, seg_row, saved, grad_att, heads):
    width = heads * HD
    full = jax.ShapeDtypeStruct((LEN, width), F32)
    column = jax.ShapeDtypeStruct(COLUMN, F32)
    gain_row = jax.ShapeDtypeStruct((1, width), F32)
    return pl.pallas_call(
        attend_backward_kernel,
        grid=(heads,),
        in_specs=[
            head_spec(0), head_spec(heads),
            whole_spec(COLUMN), whole_spec(COLUMN), gain_spec(), gain_spec(),
            whole_spec(TABLE), whole_spec(TABLE), whole_spec(COLUMN), whole_spec((1, LEN)),
            head_spec(0), head_spec(0), head_spec(0), head_spec(0), LOG_SPEC, head_spec(0),
        ],
        out_specs=[
            head_spec(0), head_spec(0), head_spec(0),
            whole_spec(COLUMN), whole_spec(COLUMN), gain_spec(), gain_spec(),
        ],
        out_shape=[
            full, full, jax.ShapeDtypeStruct((LEN, width), BF16), column, column, gain_row, gain_row,
        ],
        scratch_shapes=[pltpu.VMEM((LEN, HD), F32)] * 3 + [pltpu.VMEM((LEN, LEN), F32)],
        compiler_params=pltpu.CompilerParams(vmem_limit_bytes=48 << 20),
        cost_estimate=pl.CostEstimate(
            flops=heads * 10 * LEN * LEN * HD, bytes_accessed=LEN * width * 40, transcendentals=0
        ),
        name="attend_backward",
    )(qkv, qkv, *scales, *gains, *tables, seg_col, seg_row, *saved, grad_att)


def project_out_kernel(slot_ref, att_ref, w_ref, x_ref, gain_ref, raw_ref, hidden_ref, hidden_b_ref, scale_ref):
    block = w_ref.shape[2]
    step = pl.program_id(0)
    raw_ref[:, pl.ds(pl.multiple_of(step * block, block), block)] = plain_dot(att_ref[...], w_ref[0])

    @pl.when(step == pl.num_programs(0) - 1)
    def _():
        raw = raw_ref[...]
        scale = lax.rsqrt(jnp.mean(raw * raw, axis=1, keepdims=True) + EPS)
        scale_ref[...] = scale
        hidden = x_ref[...].astype(F32) + raw * scale * gain_ref[...]
        hidden_ref[...] = hidden
        hidden_b_ref[...] = hidden.astype(BF16)


def project_out(slot_index, attended, weight, block_input, gain, chunk):
    blocks, depth, block = weight.shape
    width = blocks * block
    rows = pl.BlockSpec((chunk, width), lambda j, idx: (idx[0], 0))
    out = pl.BlockSpec((chunk, width), lambda j, idx: (0, 0))
    return pl.pallas_call(
        project_out_kernel,
        grid_spec=pltpu.PrefetchScalarGridSpec(
            num_scalar_prefetch=1,
            grid=(blocks,),
            in_specs=[
                pl.BlockSpec((chunk, depth), lambda j, idx: (idx[0], 0)),
                pl.BlockSpec((1, depth, block), lambda j, idx: (j, 0, 0)),
                rows,
                pl.BlockSpec((1, width), lambda j, idx: (0, 0)),
            ],
            out_specs=[out, out, out, pl.BlockSpec((chunk, 1), lambda j, idx: (0, 0))],
        ),
        out_shape=[
            jax.ShapeDtypeStruct((chunk, width), F32),
            jax.ShapeDtypeStruct((chunk, width), F32),
            jax.ShapeDtypeStruct((chunk, width), BF16),
            jax.ShapeDtypeStruct((chunk, 1), F32),
        ],
        compiler_params=pltpu.CompilerParams(vmem_limit_bytes=40 << 20),
        cost_estimate=pl.CostEstimate(
            flops=2 * chunk * depth * width, bytes_accessed=2 * depth * width + 16 * chunk * width, transcendentals=0
        ),
        name="project_out",
    )(slot_index, attended, weight, block_input, gain)


def after(value, *tokens):
    return lax.optimization_barrier((value, tokens))[0]


def shards(
    sizes,
    block_input,
    segment_ids,
    positions,
    w_query,
    w_key,
    w_value,
    w_out,
    w_gate,
    w_up,
    w_down,
    query_gain,
    key_gain,
    attn_gain,
    mlp_gain,
    grad_output,
):
    cores, rows, cols = sizes
    tokens_here, width = block_input.shape
    assert tokens_here == LEN and cores == 2 and cols == 4
    local_width = w_query.shape[1]
    heads = local_width // HD
    chunk = tokens_here // cols
    core = lax.axis_index("dp")
    col = lax.axis_index("col")
    swap = [(0, 1), (1, 0)]

    def own_half(array, axis):
        half = array.shape[axis] // 2
        return lax.dynamic_slice_in_dim(array, core * half, half, axis)

    def other_half(array, axis):
        half = array.shape[axis] // 2
        return lax.dynamic_slice_in_dim(array, (1 - core) * half, half, axis)

    def gather(weight, axis):
        return lax.all_gather(own_half(weight, axis), ("row", "dp"), axis=axis, tiled=True)

    def line_step(from_left, from_right, step):
        from_left = lax.ppermute(from_left, "col", [(i, i + 1) for i in range(step - 1, cols - 1)])
        from_right = lax.ppermute(from_right, "col", [(i + 1, i) for i in range(cols - step)])
        return from_left, from_right

    def line_gather(own):
        lefts, rights = [own], [own]
        for step in range(1, cols):
            left, right = line_step(lefts[-1], rights[-1], step)
            lefts.append(left)
            rights.append(right)
        return lefts, rights

    def pick(at_zero, at_one, at_two, at_three):
        low = jnp.where(col == 0, at_zero, at_one)
        high = jnp.where(col == 2, at_two, at_three)
        return jnp.where(col < 2, low, high)

    slot_chunk = (
        pick(3, 3, 0, 0),
        pick(2, 2, 1, 1),
        pick(1, 0, 3, 2),
        col,
    )

    def slot_rows(array, slot):
        return lax.dynamic_slice_in_dim(array, slot_chunk[slot] * chunk, chunk, 0)

    def place(whole, slot, rows_of):
        return lax.dynamic_update_slice_in_dim(whole, rows_of, slot_chunk[slot] * chunk, 0)

    def gather_slots(own, work):
        left1, right1 = line_step(own, own, 1)
        token = work(3, own)
        left1, right1 = after((left1, right1), token)
        left2, right2 = line_step(left1, right1, 2)
        token = work(2, jnp.where(col % 2 == 0, right1, left1))
        left2, right2 = after((left2, right2), token)
        left3, right3 = line_step(left2, right2, 3)
        token = work(1, pick(right2, right1, left1, left2))
        left3, right3 = after((left3, right3), token)
        return work(0, pick(right3, right2, left2, left3))

    def sum_slots(make, window=lambda step, gate: ()):
        first = make(0, ())
        up = lax.ppermute(first, "col", [(0, 1)])
        down = lax.ppermute(first, "col", [(3, 2)])
        second = make(1, first)
        up, down = after((up, down), second, window(1, first))
        up = jnp.where(col == 0, second, first) + up
        down = jnp.where(col == 3, second, first) + down
        gate = (up, down)
        up = lax.ppermute(up, "col", [(0, 1), (1, 2)])
        down = lax.ppermute(down, "col", [(3, 2), (2, 1)])
        third = make(2, gate)
        up, down = after((up, down), third, window(2, gate))
        up = jnp.where(col == 1, second, third) + up
        down = jnp.where(col == 2, second, third) + down
        gate = (up, down)
        up = lax.ppermute(up, "col", [(0, 1), (1, 2), (2, 3)])
        down = lax.ppermute(down, "col", [(3, 2), (2, 1), (1, 0)])
        fourth = make(3, gate)
        up, down = after((up, down), fourth, window(3, gate))
        return fourth.astype(F32) + up.astype(F32) + down.astype(F32)

    def both_cores(half, axis):
        other = lax.ppermute(half, "dp", swap)
        first = jnp.where(core == 0, half, other)
        second = jnp.where(core == 0, other, half)
        return jnp.concatenate([first, second], axis=axis).astype(F32)

    def summed(left_mat, right_own, right_other):
        sent = left_transposed(left_mat, right_other).astype(BF16)
        got = lax.ppermute(sent, "dp", swap)
        total = (left_transposed(left_mat, right_own) + got.astype(F32)).astype(BF16)
        return total, lax.psum_scatter(total, "row", scatter_dimension=0, tiled=True)

    full_qkv = gather(jnp.concatenate([w_query, w_key, w_value], axis=1), 0)
    out_half = own_half(w_out, 0)
    out_pieces = [out_half] + [
        lax.ppermute(out_half, "col", [(i, (i - step) % cols) for i in range(cols)])
        for step in range(1, cols)
    ]
    half_width = local_width // 2
    gathered_out = lax.all_gather(jnp.stack(out_pieces), ("row", "dp"), axis=0, tiled=False)
    gathered_out = gathered_out.reshape(rows, cores, cols, half_width, width // rows)
    full_out = gathered_out.reshape(rows, cols * local_width, width // rows)
    own_out = jnp.transpose(gathered_out[:, :, 0], (1, 2, 0, 3)).reshape(local_width, width)
    full_gate = gather(w_gate, 0)
    full_up = gather(w_up, 0)
    full_down = gather(w_down, 1)

    qkv = plain_dot(block_input, full_qkv)
    query_raw, key_raw = qkv[:, :local_width], qkv[:, local_width : 2 * local_width]
    query_sq, key_sq = lax.psum(
        (jnp.sum(query_raw * query_raw, axis=1), jnp.sum(key_raw * key_raw, axis=1)), "col"
    )
    query_scale = lax.rsqrt(query_sq / width + EPS)[:, None]
    key_scale = lax.rsqrt(key_sq / width + EPS)[:, None]
    scales = (query_scale, key_scale)
    gains = (query_gain[None, :], key_gain[None, :])
    tables = rope_tables(positions)
    seg_col, seg_row = segment_ids[:, None], segment_ids[None, :]
    query_rot, key_rot, value_heads, attended, log_total = attend_forward(
        qkv, scales, gains, tables, seg_col, seg_row, heads
    )
    lefts, rights = line_gather(attended)
    pieces = [attended] + [rights[step] + lefts[cols - step] for step in range(1, cols)]
    attended_all = jnp.concatenate(
        [one[:, half * half_width : (half + 1) * half_width] for half in range(cores) for one in pieces],
        axis=1,
    )

    saved = [None] * cols
    down_parts = [None] * cols

    def forward_chunk(slot, gate):
        rows_in = after(attended_all, gate)
        attn_raw, hidden, hidden_b, attn_scale = project_out(
            slot_chunk[slot].astype(jnp.int32)[None],
            rows_in, full_out, block_input, attn_gain[None, :], chunk,
        )
        gate_proj = plain_dot(hidden_b, full_gate)
        up_proj = plain_dot(hidden_b, full_up)
        mixed_act = (gate_proj * jax.nn.sigmoid(gate_proj) * up_proj).astype(BF16)
        down_parts[slot] = plain_dot(mixed_act, full_down).astype(BF16)
        saved[slot] = (attn_scale, attn_raw, hidden, hidden_b, gate_proj, up_proj, mixed_act)
        return down_parts[slot]

    down_own = sum_slots(forward_chunk).astype(BF16)

    state = dict(
        block_output=jnp.zeros((tokens_here, width), BF16),
        grad_att=jnp.zeros((tokens_here, local_width), BF16),
        grad_input=jnp.zeros((tokens_here, width), F32),
        mlp_gain=0.0,
        attn_gain=0.0,
    )
    grads = [None] * cols
    mlp_parts = [None] * cols

    def backward_chunk(slot, down_rows):
        attn_scale, attn_raw, hidden, hidden_b, gate_proj, up_proj, mixed_act = saved[slot]
        down_raw = down_rows.astype(F32)
        down_scale = lax.rsqrt(jnp.mean(down_raw * down_raw, axis=1, keepdims=True) + EPS)
        down_unit = down_raw * down_scale
        state["block_output"] = place(
            state["block_output"], slot, (hidden + down_unit * mlp_gain).astype(BF16)
        )
        grad_y = slot_rows(grad_output, slot).astype(F32)
        state["mlp_gain"] = state["mlp_gain"] + jnp.sum(grad_y * down_unit, axis=0)
        down_dz = grad_y * mlp_gain
        grad_down_in = (
            down_scale * (down_dz - down_unit * jnp.mean(down_dz * down_unit, axis=1, keepdims=True))
        ).astype(BF16)
        grad_mixed = times_transposed(grad_down_in, full_down)
        gate_sig = jax.nn.sigmoid(gate_proj)
        grad_gate_in = (
            grad_mixed * up_proj * gate_sig * (1.0 + gate_proj * (1.0 - gate_sig))
        ).astype(BF16)
        grad_up_in = (grad_mixed * (gate_proj * gate_sig)).astype(BF16)
        mlp_parts[slot] = (
            times_transposed(grad_gate_in, full_gate) + times_transposed(grad_up_in, full_up)
        ).astype(BF16)
        grads[slot] = (grad_down_in, grad_gate_in, grad_up_in)
        return mlp_parts[slot]

    gather_slots(down_own, backward_chunk)

    def stacked(pieces):
        return jnp.concatenate(pieces, axis=0)

    blocks = {}

    def mlp_window(step, gate):
        if step == 1:
            left_all, right_all = after(
                (stacked([one[0] for one in grads]), stacked([one[6] for one in saved])), gate
            )
            blocks["down"] = summed(left_all, own_half(right_all, 1), other_half(right_all, 1))
            return blocks["down"][0]
        kind = ("gate", "up")[step - 2]
        grad_all, hidden_all = after(
            (stacked([one[step - 1] for one in grads]), stacked([one[3] for one in saved])), gate
        )
        blocks[kind] = summed(hidden_all, own_half(grad_all, 1), other_half(grad_all, 1))
        return blocks[kind][0]

    mlp_own = sum_slots(lambda slot, gate: mlp_parts[slot], mlp_window).astype(BF16)

    attn_ins = [None] * cols

    def attention_chunk(slot, mlp_rows):
        attn_scale, attn_raw = saved[slot][:2]
        attn_unit = attn_raw * attn_scale
        grad_hidden = slot_rows(grad_output, slot).astype(F32) + mlp_rows.astype(F32)
        state["attn_gain"] = state["attn_gain"] + jnp.sum(grad_hidden * attn_unit, axis=0)
        attn_dz = grad_hidden * attn_gain
        grad_attn_in = (
            attn_scale * (attn_dz - attn_unit * jnp.mean(attn_dz * attn_unit, axis=1, keepdims=True))
        ).astype(BF16)
        state["grad_att"] = place(
            state["grad_att"], slot, times_transposed(grad_attn_in, own_out).astype(BF16)
        )
        attn_ins[slot] = grad_attn_in
        return state["grad_att"]

    gather_slots(mlp_own, attention_chunk)
    own_grad_hidden = slot_rows(grad_output, 3).astype(F32) + mlp_own.astype(F32)

    query_dz, key_dz, grad_value_in, query_dot, key_dot, grad_query_gain, grad_key_gain = attend_backward(
        qkv, scales, gains, tables, seg_col, seg_row,
        (query_rot, key_rot, value_heads, attended, log_total), state["grad_att"], heads,
    )
    query_dot, key_dot = lax.psum((query_dot[:, 0], key_dot[:, 0]), "col")
    grad_query_in = (
        query_scale * (query_dz - query_raw * query_scale * (query_dot / width)[:, None])
    ).astype(BF16)
    grad_key_in = (
        key_scale * (key_dz - key_raw * key_scale * (key_dot / width)[:, None])
    ).astype(BF16)
    grad_qkv = jnp.concatenate([grad_query_in, grad_key_in, grad_value_in], axis=1)

    def interleaved(picker):
        return jnp.concatenate(
            [picker(one, 1) for one in (grad_query_in, grad_key_in, grad_value_in)], axis=1
        )

    def input_window(step, gate):
        if step == 1:
            own, other, tokens_in = after(
                (interleaved(own_half), interleaved(other_half), block_input), gate
            )
            blocks["qkv"] = summed(tokens_in, own, other)
            return blocks["qkv"][0]
        if step == 2:
            attended_slots, left_all = after(
                (stacked([slot_rows(attended, slot) for slot in range(cols)]), stacked(attn_ins)), gate
            )
            blocks["out"] = summed(left_all, own_half(attended_slots, 1), other_half(attended_slots, 1))
            return blocks["out"][0]
        gain_grads = after(
            (grad_query_gain[0], grad_key_gain[0], state["attn_gain"], state["mlp_gain"]), gate
        )
        for axis in ("dp", "row"):
            gain_grads = lax.psum(gain_grads, axis)
        blocks["gains"] = gain_grads
        return gain_grads

    input_own = sum_slots(
        lambda slot, gate: times_transposed(after(slot_rows(grad_qkv, slot), gate), full_qkv).astype(BF16),
        input_window,
    )

    results = {}

    def output_chunk(slot, rows_in):
        state["grad_input"] = place(state["grad_input"], slot, rows_in.astype(F32))
        if slot == 3:
            results["down"] = jnp.transpose(both_cores(blocks["down"][1], 1))
            results["gate"] = both_cores(blocks["gate"][1], 1)
            return state["grad_input"], results["down"], results["gate"]
        if slot == 2:
            results["up"] = both_cores(blocks["up"][1], 1)
            return state["grad_input"], results["up"]
        if slot == 1:
            results["out"] = jnp.transpose(both_cores(blocks["out"][1], 1))
            results["qkv"] = [projection(index) for index in range(3)]
            return state["grad_input"], results["out"], results["qkv"]
        return state["grad_input"]

    quarter = local_width // 2

    def projection(index):
        pair = both_cores(blocks["qkv"][1][None, :, index * quarter : (index + 1) * quarter], 0)
        return jnp.concatenate([pair[0], pair[1]], axis=1)

    gather_slots((own_grad_hidden + input_own).astype(BF16), output_chunk)
    gain_grads = blocks["gains"]
    return (
        state["block_output"],
        state["grad_input"],
        *results["qkv"],
        results["out"],
        results["gate"],
        results["up"],
        results["down"],
        *gain_grads,
    )


def solution(mesh):
    in_specs = (
        P(("dp", "row"), None),
        P(("dp", "row")),
        P(("dp", "row")),
        P("row", "col"),
        P("row", "col"),
        P("row", "col"),
        P("col", "row"),
        P("row", "col"),
        P("row", "col"),
        P("col", "row"),
        P("col"),
        P("col"),
        P(),
        P(),
        P(("dp", "row"), None),
    )
    out_specs = (
        P(("dp", "row"), None),
        P(("dp", "row"), None),
        P("row", "col"),
        P("row", "col"),
        P("row", "col"),
        P("col", "row"),
        P("row", "col"),
        P("row", "col"),
        P("col", "row"),
        P("col"),
        P("col"),
        P(),
        P(),
    )
    sizes = (mesh.shape["dp"], mesh.shape["row"], mesh.shape["col"])
    return jax.shard_map(
        functools.partial(shards, sizes), mesh=mesh, in_specs=in_specs, out_specs=out_specs, check_vma=False
    )
```

```python
import functools

import jax
import jax.numpy as jnp
from jax import lax
from jax.experimental import pallas as pl
from jax.experimental.pallas import tpu as pltpu
from jax.sharding import PartitionSpec as P


HD = 128
LEN = 1024
BQ = 256

EPS = 1e-06
THETA = 500000.0
NEG_FILL = -1e30
SCORE_SCALE = HD ** (-0.5)
F32 = jnp.float32
BF16 = jnp.bfloat16


def plain_dot(left_mat, right_mat):
    return jnp.dot(left_mat, right_mat, preferred_element_type=F32)


def times_transposed(left_mat, right_mat):
    return lax.dot_general(
        left_mat, right_mat, (((1,), (1,)), ((), ())), preferred_element_type=F32
    )


def left_transposed(left_mat, right_mat):
    return lax.dot_general(
        left_mat, right_mat, (((0,), (0,)), ((), ())), preferred_element_type=F32
    )


def rope_tables(positions):
    half_dim = HD // 2
    inv_freq = THETA ** (-(jnp.arange(half_dim, dtype=F32) * 2.0) / HD)
    angles = positions.astype(F32)[:, None] * inv_freq[None, :]
    cos_half, sin_half = jnp.cos(angles), jnp.sin(angles)
    cosine = jnp.concatenate([cos_half, cos_half], axis=-1)
    sine_signed = jnp.concatenate([-sin_half, sin_half], axis=-1)
    return cosine, sine_signed


def fill_mask(bias_ref, seg_col_ref, seg_row_ref):
    @pl.when(pl.program_id(0) == 0)
    def _():
        for first in range(0, LEN, BQ):
            keys = first + BQ
            rows = seg_col_ref[first:keys, :]
            cols = seg_row_ref[:, :keys]
            query_index = first + lax.broadcasted_iota(jnp.int32, (BQ, keys), 0)
            key_index = lax.broadcasted_iota(jnp.int32, (BQ, keys), 1)
            allowed = (rows == cols) & (key_index <= query_index)
            bias_ref[first:keys, :keys] = jnp.where(allowed, 0.0, NEG_FILL)


def attend_forward_kernel(
    q_ref, k_ref, v_ref, qs_ref, ks_ref, qg_ref, kg_ref, cos_ref, sin_ref, segc_ref, segr_ref,
    qrot_ref, krot_ref, vb_ref, att_ref, log_ref, bias_ref,
):
    fill_mask(bias_ref, segc_ref, segr_ref)
    cosine, sine = cos_ref[...], sin_ref[...]

    def turned(raw, scale, gain):
        norm = raw * scale * gain
        return (norm * cosine + pltpu.roll(norm, HD // 2, 1) * sine).astype(BF16)

    qrot_ref[...] = turned(q_ref[...], qs_ref[...], qg_ref[...])
    krot_ref[...] = turned(k_ref[...], ks_ref[...], kg_ref[...])
    vb_ref[...] = v_ref[...].astype(BF16)
    for first in range(0, LEN, BQ):
        keys = first + BQ
        scores = times_transposed(qrot_ref[first:keys, :], krot_ref[:keys, :]) * SCORE_SCALE
        masked = scores + bias_ref[first:keys, :keys]
        peak = jnp.max(masked, axis=1, keepdims=True)
        weight = jnp.exp(masked - peak)
        total = jnp.sum(weight, axis=1, keepdims=True)
        probs = (weight * (1.0 / total)).astype(BF16)
        att_ref[first:keys, :] = plain_dot(probs, vb_ref[:keys, :]).astype(BF16)
        log_ref[0, first:keys, :] = peak + jnp.log(total)


def attend_backward_kernel(
    q_ref, k_ref, qs_ref, ks_ref, qg_ref, kg_ref, cos_ref, sin_ref, segc_ref, segr_ref,
    qrot_ref, krot_ref, vb_ref, att_ref, log_ref, grad_ref,
    dzq_ref, dzk_ref, gv_ref, dotq_ref, dotk_ref, gainq_ref, gaink_ref,
    dq_acc, dk_acc, dv_acc, bias_ref,
):
    fill_mask(bias_ref, segc_ref, segr_ref)
    dk_acc[...] = jnp.zeros_like(dk_acc)
    dv_acc[...] = jnp.zeros_like(dv_acc)
    for first in range(0, LEN, BQ):
        keys = first + BQ
        queries = qrot_ref[first:keys, :]
        grads = grad_ref[first:keys, :]
        scores = times_transposed(queries, krot_ref[:keys, :]) * SCORE_SCALE
        probs = jnp.exp(scores + bias_ref[first:keys, :keys] - log_ref[0, first:keys, :])
        delta = jnp.sum(
            grads.astype(F32) * att_ref[first:keys, :].astype(F32), axis=1, keepdims=True
        )
        grad_probs = times_transposed(grads, vb_ref[:keys, :])
        grad_scores = (probs * (grad_probs - delta) * SCORE_SCALE).astype(BF16)
        dq_acc[first:keys, :] = plain_dot(grad_scores, krot_ref[:keys, :])
        dk_acc[:keys, :] += left_transposed(grad_scores, queries)
        dv_acc[:keys, :] += left_transposed(probs.astype(BF16), grads)
    gv_ref[...] = dv_acc[...].astype(BF16)
    cosine, sine = cos_ref[...], sin_ref[...]

    def finish(acc, raw_ref, scale_ref, gain_ref, dz_ref, dot_ref, gain_grad_ref):
        grad_rot = acc[...]
        grad_norm = grad_rot * cosine - pltpu.roll(grad_rot, HD // 2, 1) * sine
        unit = raw_ref[...] * scale_ref[...]
        gain_grad_ref[...] = jnp.sum(grad_norm * unit, axis=0, keepdims=True)
        grad_unit = grad_norm * gain_ref[...]
        dz_ref[...] = grad_unit
        part = jnp.sum(grad_unit * unit, axis=1, keepdims=True)

        @pl.when(pl.program_id(0) == 0)
        def _():
            dot_ref[...] = part

        @pl.when(pl.program_id(0) > 0)
        def _():
            dot_ref[...] += part

    finish(dq_acc, q_ref, qs_ref, qg_ref, dzq_ref, dotq_ref, gainq_ref)
    finish(dk_acc, k_ref, ks_ref, kg_ref, dzk_ref, dotk_ref, gaink_ref)


def head_spec(offset):
    return pl.BlockSpec((LEN, HD), lambda h: (0, offset + h))


def whole_spec(shape):
    return pl.BlockSpec(shape, lambda h: (0,) * len(shape))


def gain_spec():
    return pl.BlockSpec((1, HD), lambda h: (0, h))


LOG_SPEC = pl.BlockSpec((1, LEN, 1), lambda h: (h, 0, 0))
COLUMN = (LEN, 1)
TABLE = (LEN, HD)


def attend_forward(qkv, scales, gains, tables, seg_col, seg_row, heads):
    width = heads * HD
    piece = jax.ShapeDtypeStruct((LEN, width), BF16)
    return pl.pallas_call(
        attend_forward_kernel,
        grid=(heads,),
        in_specs=[
            head_spec(0), head_spec(heads), head_spec(2 * heads),
            whole_spec(COLUMN), whole_spec(COLUMN), gain_spec(), gain_spec(),
            whole_spec(TABLE), whole_spec(TABLE), whole_spec(COLUMN), whole_spec((1, LEN)),
        ],
        out_specs=[head_spec(0)] * 4 + [LOG_SPEC],
        out_shape=[piece] * 4 + [jax.ShapeDtypeStruct((heads, LEN, 1), F32)],
        scratch_shapes=[pltpu.VMEM((LEN, LEN), F32)],
        compiler_params=pltpu.CompilerParams(vmem_limit_bytes=28 << 20),
        cost_estimate=pl.CostEstimate(
            flops=heads * 4 * LEN * LEN * HD, bytes_accessed=LEN * width * 20, transcendentals=0
        ),
        name="attend_forward",
    )(qkv, qkv, qkv, *scales, *gains, *tables, seg_col, seg_row)


def attend_backward(qkv, scales, gains, tables, seg_col, seg_row, saved, grad_att, heads):
    width = heads * HD
    full = jax.ShapeDtypeStruct((LEN, width), F32)
    column = jax.ShapeDtypeStruct(COLUMN, F32)
    gain_row = jax.ShapeDtypeStruct((1, width), F32)
    return pl.pallas_call(
        attend_backward_kernel,
        grid=(heads,),
        in_specs=[
            head_spec(0), head_spec(heads),
            whole_spec(COLUMN), whole_spec(COLUMN), gain_spec(), gain_spec(),
            whole_spec(TABLE), whole_spec(TABLE), whole_spec(COLUMN), whole_spec((1, LEN)),
            head_spec(0), head_spec(0), head_spec(0), head_spec(0), LOG_SPEC, head_spec(0),
        ],
        out_specs=[
            head_spec(0), head_spec(0), head_spec(0),
            whole_spec(COLUMN), whole_spec(COLUMN), gain_spec(), gain_spec(),
        ],
        out_shape=[
            full, full, jax.ShapeDtypeStruct((LEN, width), BF16), column, column, gain_row, gain_row,
        ],
        scratch_shapes=[pltpu.VMEM((LEN, HD), F32)] * 3 + [pltpu.VMEM((LEN, LEN), F32)],
        compiler_params=pltpu.CompilerParams(vmem_limit_bytes=28 << 20),
        cost_estimate=pl.CostEstimate(
            flops=heads * 10 * LEN * LEN * HD, bytes_accessed=LEN * width * 40, transcendentals=0
        ),
        name="attend_backward",
    )(qkv, qkv, *scales, *gains, *tables, seg_col, seg_row, *saved, grad_att)


def half_tile(step, core, tiles):
    per_half = tiles // 2
    return ((core + step // per_half) % 2) * per_half + step % per_half


def forward_chunk_kernel(
    idx_ref, att_ref, wo_own_ref, wo_oth_ref, x_ref, gain_ref, wg_ref, wu_ref, wd_own_ref, wd_oth_ref, *refs,
    blocks, tiles,
):
    raw_ref, scale_ref, hb_ref, gate_ref, up_ref, mixed_ref, part_ref, acc_ref = refs[-8:]
    block = wo_own_ref.shape[2]
    depth = wo_own_ref.shape[1]
    step = pl.program_id(0)
    core = idx_ref[1]

    @pl.when(step < blocks)
    def _():
        own = att_ref[:, pl.ds(pl.multiple_of(core * depth, depth), depth)]
        other = att_ref[:, pl.ds(pl.multiple_of((1 - core) * depth, depth), depth)]
        raw_ref[:, pl.ds(pl.multiple_of(step * block, block), block)] = plain_dot(
            own, wo_own_ref[0]
        ) + plain_dot(other, wo_oth_ref[0])

    @pl.when(step == blocks - 1)
    def _():
        raw = raw_ref[...]
        scale = lax.rsqrt(jnp.mean(raw * raw, axis=1, keepdims=True) + EPS)
        scale_ref[...] = scale
        hb_ref[...] = (x_ref[...].astype(F32) + raw * scale * gain_ref[...]).astype(BF16)
        acc_ref[...] = jnp.zeros_like(acc_ref)

    def tile_work(wd_ref):
        hidden_b = hb_ref[...]
        gate = plain_dot(hidden_b, wg_ref[...])
        up = plain_dot(hidden_b, wu_ref[...])
        mixed = (gate * jax.nn.sigmoid(gate) * up).astype(BF16)
        gate_ref[...] = gate.astype(BF16)
        up_ref[...] = up.astype(BF16)
        mixed_ref[...] = mixed
        for j in range(blocks):
            acc_ref[:, j * block : (j + 1) * block] += plain_dot(mixed, wd_ref[j])

    @pl.when((step >= blocks) & (step < blocks + tiles // 2))
    def _():
        tile_work(wd_own_ref)

    @pl.when(step >= blocks + tiles // 2)
    def _():
        tile_work(wd_oth_ref)

    @pl.when(step == blocks + tiles - 1)
    def _():
        part_ref[...] = acc_ref[...].astype(BF16)


TILE = 256


def forward_chunk(index, attended, out_halves, block_input, gain, w_gate, w_up, down_halves, chunk, before):
    tokens, width = block_input.shape
    hidden = w_gate.shape[1]
    blocks, depth, block = out_halves[0].shape
    tiles = hidden // TILE

    def tile_of(j, idx):
        return half_tile(jnp.maximum(j - blocks, 0), idx[1], tiles)

    rows = pl.BlockSpec((chunk, width), lambda j, idx: (idx[0], 0))
    out_half = pl.BlockSpec((1, depth, block), lambda j, idx: (jnp.minimum(j, blocks - 1), 0, 0))
    up_tile = pl.BlockSpec((width, TILE), lambda j, idx: (0, tile_of(j, idx)))
    down_own = pl.BlockSpec(
        (blocks, TILE, block), lambda j, idx: (0, jnp.clip(j - blocks, 0, tiles // 2 - 1), 0)
    )
    down_oth = pl.BlockSpec(
        (blocks, TILE, block), lambda j, idx: (0, jnp.maximum(j - blocks - tiles // 2, 0), 0)
    )
    act_tile = pl.BlockSpec((chunk, TILE), lambda j, idx: (idx[0], tile_of(j, idx)))
    before = tuple(before)
    return pl.pallas_call(
        functools.partial(forward_chunk_kernel, blocks=blocks, tiles=tiles),
        grid_spec=pltpu.PrefetchScalarGridSpec(
            num_scalar_prefetch=1,
            grid=(blocks + tiles,),
            in_specs=[
                pl.BlockSpec((chunk, attended.shape[1]), lambda j, idx: (idx[0], 0)),
                out_half, out_half, rows, pl.BlockSpec((1, width), lambda j, idx: (0, 0)),
                up_tile, up_tile, down_own, down_oth,
            ] + [pl.BlockSpec(memory_space=pl.ANY)] * len(before),
            out_specs=[
                rows, pl.BlockSpec((chunk, 1), lambda j, idx: (idx[0], 0)), rows, act_tile, act_tile, act_tile,
                pl.BlockSpec((chunk, width), lambda j, idx: (0, 0)),
            ],
            scratch_shapes=[pltpu.VMEM((chunk, width), F32)],
        ),
        out_shape=[
            jax.ShapeDtypeStruct((tokens, width), F32),
            jax.ShapeDtypeStruct((tokens, 1), F32),
            jax.ShapeDtypeStruct((tokens, width), BF16),
            jax.ShapeDtypeStruct((tokens, hidden), BF16),
            jax.ShapeDtypeStruct((tokens, hidden), BF16),
            jax.ShapeDtypeStruct((tokens, hidden), BF16),
            jax.ShapeDtypeStruct((chunk, width), BF16),
        ],
        input_output_aliases={10 + i: i for i in range(len(before))},
        compiler_params=pltpu.CompilerParams(vmem_limit_bytes=40 << 20),
        cost_estimate=pl.CostEstimate(
            flops=2 * chunk * width * (width + 3 * hidden),
            bytes_accessed=2 * width * (width + 3 * hidden),
            transcendentals=0,
        ),
        name="forward_chunk",
    )(index, attended, *out_halves, block_input, gain, w_gate, w_up, *down_halves, *before)


def backward_chunk_kernel(
    idx_ref, down_ref, raw_ref, scale_ref, x_ref, grad_ref, attn_gain_ref, mlp_gain_ref,
    gate_ref, up_ref, wg_ref, wu_ref, wd_own_ref, wd_oth_ref, *refs, blocks, tiles,
):
    out_ref, gdi_ref, gg_ref, gu_ref, part_ref, gain_grad_ref, acc_ref = refs[-7:]
    block = wd_own_ref.shape[2]
    step = pl.program_id(0)

    @pl.when(step == 0)
    def _():
        down_raw = down_ref[...].astype(F32)
        down_scale = lax.rsqrt(jnp.mean(down_raw * down_raw, axis=1, keepdims=True) + EPS)
        unit = down_raw * down_scale
        mlp_gain = mlp_gain_ref[...]
        hidden = x_ref[...].astype(F32) + raw_ref[...] * scale_ref[...] * attn_gain_ref[...]
        out_ref[...] = (hidden + unit * mlp_gain).astype(BF16)
        grad_y = grad_ref[...].astype(F32)
        gain_grad_ref[...] = jnp.sum(grad_y * unit, axis=0, keepdims=True)
        grad_unit = grad_y * mlp_gain
        mean = jnp.mean(grad_unit * unit, axis=1, keepdims=True)
        gdi_ref[...] = (down_scale * (grad_unit - unit * mean)).astype(BF16)
        acc_ref[...] = jnp.zeros_like(acc_ref)

    def tile_work(wd_ref):
        grad_mixed = times_transposed(gdi_ref[:, :block], wd_ref[0])
        for j in range(1, blocks):
            grad_mixed += times_transposed(gdi_ref[:, j * block : (j + 1) * block], wd_ref[j])
        gate = gate_ref[...].astype(F32)
        sig = jax.nn.sigmoid(gate)
        grad_gate = (grad_mixed * up_ref[...].astype(F32) * sig * (1.0 + gate * (1.0 - sig))).astype(BF16)
        grad_up = (grad_mixed * (gate * sig)).astype(BF16)
        gg_ref[...] = grad_gate
        gu_ref[...] = grad_up
        acc_ref[...] += times_transposed(grad_gate, wg_ref[...]) + times_transposed(grad_up, wu_ref[...])

    @pl.when(step < tiles // 2)
    def _():
        tile_work(wd_own_ref)

    @pl.when(step >= tiles // 2)
    def _():
        tile_work(wd_oth_ref)

    @pl.when(step == tiles - 1)
    def _():
        part_ref[...] = acc_ref[...].astype(BF16)


def backward_chunk(
    index, down_rows, raw, scale, block_input, grad_output, attn_gain, mlp_gain, gate, up, w_gate, w_up,
    down_halves, chunk, before,
):
    tokens, width = block_input.shape
    hidden = w_gate.shape[1]
    blocks, _, block = down_halves[0].shape
    tiles = hidden // TILE

    def tile_of(j, idx):
        return half_tile(j, idx[1], tiles)

    rows = pl.BlockSpec((chunk, width), lambda j, idx: (idx[0], 0))
    fixed = pl.BlockSpec((chunk, width), lambda j, idx: (0, 0))
    gain_row = pl.BlockSpec((1, width), lambda j, idx: (0, 0))
    up_tile = pl.BlockSpec((width, TILE), lambda j, idx: (0, tile_of(j, idx)))
    act_tile = pl.BlockSpec((chunk, TILE), lambda j, idx: (idx[0], tile_of(j, idx)))
    before = tuple(before)
    return pl.pallas_call(
        functools.partial(backward_chunk_kernel, blocks=blocks, tiles=tiles),
        grid_spec=pltpu.PrefetchScalarGridSpec(
            num_scalar_prefetch=1,
            grid=(tiles,),
            in_specs=[
                fixed, rows, pl.BlockSpec((chunk, 1), lambda j, idx: (idx[0], 0)), rows, rows, gain_row, gain_row,
                act_tile, act_tile, up_tile, up_tile,
                pl.BlockSpec((blocks, TILE, block), lambda j, idx: (0, jnp.minimum(j, tiles // 2 - 1), 0)),
                pl.BlockSpec((blocks, TILE, block), lambda j, idx: (0, jnp.maximum(j - tiles // 2, 0), 0)),
            ] + [pl.BlockSpec(memory_space=pl.ANY)] * len(before),
            out_specs=[rows, rows, act_tile, act_tile, fixed, gain_row],
            scratch_shapes=[pltpu.VMEM((chunk, width), F32)],
        ),
        out_shape=[
            jax.ShapeDtypeStruct((tokens, width), BF16),
            jax.ShapeDtypeStruct((tokens, width), BF16),
            jax.ShapeDtypeStruct((tokens, hidden), BF16),
            jax.ShapeDtypeStruct((tokens, hidden), BF16),
            jax.ShapeDtypeStruct((chunk, width), BF16),
            jax.ShapeDtypeStruct((1, width), F32),
        ],
        input_output_aliases={14 + i: i for i in range(len(before))},
        compiler_params=pltpu.CompilerParams(vmem_limit_bytes=40 << 20),
        cost_estimate=pl.CostEstimate(
            flops=6 * chunk * width * hidden, bytes_accessed=6 * width * hidden, transcendentals=0
        ),
        name="backward_chunk",
    )(
        index, down_rows, raw, scale, block_input, grad_output, attn_gain, mlp_gain, gate, up, w_gate, w_up,
        *down_halves, *before,
    )


def attention_chunk_kernel(
    idx_ref, mlp_ref, grad_ref, raw_ref, scale_ref, gain_ref, wo_own_ref, wo_oth_ref, *refs, blocks,
):
    gai_ref, gatt_ref, gain_grad_ref = refs[-3:]
    half, block = wo_own_ref.shape[1:]
    core = idx_ref[1]
    scale = scale_ref[...]
    unit = raw_ref[...] * scale
    grad_hidden = grad_ref[...].astype(F32) + mlp_ref[...].astype(F32)
    gain_grad_ref[...] = jnp.sum(grad_hidden * unit, axis=0, keepdims=True)
    grad_unit = grad_hidden * gain_ref[...]
    mean = jnp.mean(grad_unit * unit, axis=1, keepdims=True)
    gai_ref[...] = (scale * (grad_unit - unit * mean)).astype(BF16)
    for place, w_ref in ((core, wo_own_ref), (1 - core, wo_oth_ref)):
        total = times_transposed(gai_ref[:, :block], w_ref[0])
        for j in range(1, blocks):
            total += times_transposed(gai_ref[:, j * block : (j + 1) * block], w_ref[j])
        gatt_ref[:, pl.ds(pl.multiple_of(place * half, half), half)] = total.astype(BF16)


def attention_chunk(index, mlp_rows, grad_output, raw, scale, gain, out_halves, half, chunk, before):
    tokens, width = grad_output.shape
    blocks, _, block = out_halves[0].shape
    rows = pl.BlockSpec((chunk, width), lambda j, idx: (idx[0], 0))
    fixed = pl.BlockSpec((chunk, width), lambda j, idx: (0, 0))
    gain_row = pl.BlockSpec((1, width), lambda j, idx: (0, 0))
    own_heads = pl.BlockSpec((blocks, half, block), lambda j, idx: (0, 0, 0))
    before = tuple(before)
    return pl.pallas_call(
        functools.partial(attention_chunk_kernel, blocks=blocks),
        grid_spec=pltpu.PrefetchScalarGridSpec(
            num_scalar_prefetch=1,
            grid=(1,),
            in_specs=[
                fixed, rows, rows, pl.BlockSpec((chunk, 1), lambda j, idx: (idx[0], 0)), gain_row,
                own_heads, own_heads,
            ] + [pl.BlockSpec(memory_space=pl.ANY)] * len(before),
            out_specs=[rows, pl.BlockSpec((chunk, 2 * half), lambda j, idx: (idx[0], 0)), gain_row],
        ),
        out_shape=[
            jax.ShapeDtypeStruct((tokens, width), BF16),
            jax.ShapeDtypeStruct((tokens, 2 * half), BF16),
            jax.ShapeDtypeStruct((1, width), F32),
        ],
        input_output_aliases={8 + i: i for i in range(len(before))},
        compiler_params=pltpu.CompilerParams(vmem_limit_bytes=32 << 20),
        cost_estimate=pl.CostEstimate(
            flops=4 * chunk * width * half, bytes_accessed=16 * chunk * width, transcendentals=0
        ),
        name="attention_chunk",
    )(index, mlp_rows, grad_output, raw, scale, gain, *out_halves, *before)


def place_rows_kernel(idx_ref, rows_ref, *refs):
    refs[-1][...] = rows_ref[...].astype(refs[-1].dtype)


def place_rows(index, rows_in, tokens, dtype, before):
    chunk, width = rows_in.shape
    before = tuple(before)
    return pl.pallas_call(
        place_rows_kernel,
        grid_spec=pltpu.PrefetchScalarGridSpec(
            num_scalar_prefetch=1,
            grid=(2,),
            in_specs=[pl.BlockSpec((chunk // 2, width), lambda j, idx: (j, 0))]
            + [pl.BlockSpec(memory_space=pl.ANY)] * len(before),
            out_specs=pl.BlockSpec((chunk // 2, width), lambda j, idx: (2 * idx[0] + j, 0)),
        ),
        out_shape=jax.ShapeDtypeStruct((tokens, width), dtype),
        input_output_aliases={2: 0} if before else {},
        compiler_params=pltpu.CompilerParams(vmem_limit_bytes=16 << 20),
        cost_estimate=pl.CostEstimate(flops=0, bytes_accessed=6 * chunk * width, transcendentals=0),
        name="place_rows",
    )(index, rows_in, *before)


def after(value, *tokens):
    return lax.optimization_barrier((value, tokens))[0]


def unset_kernel(out_ref):
    pass


def unset(shape, dtype):
    return pl.pallas_call(
        unset_kernel,
        out_specs=pl.BlockSpec(memory_space=pl.ANY),
        out_shape=jax.ShapeDtypeStruct(shape, dtype),
        name="unset",
    )()


def shards(
    sizes,
    block_input,
    segment_ids,
    positions,
    w_query,
    w_key,
    w_value,
    w_out,
    w_gate,
    w_up,
    w_down,
    query_gain,
    key_gain,
    attn_gain,
    mlp_gain,
    grad_output,
):
    cores, rows, cols = sizes
    tokens_here, width = block_input.shape
    assert tokens_here == LEN and cores == 2 and cols == 4
    local_width = w_query.shape[1]
    half_width = local_width // 2
    heads = local_width // HD
    chunk = tokens_here // cols
    core = lax.axis_index("dp")
    row = lax.axis_index("row")
    col = lax.axis_index("col")
    swap = [(0, 1), (1, 0)]
    attn_row, mlp_row = attn_gain[None, :], mlp_gain[None, :]

    def own_half(array, axis):
        half = array.shape[axis] // 2
        return lax.dynamic_slice_in_dim(array, core * half, half, axis)

    def other_half(array, axis):
        half = array.shape[axis] // 2
        return lax.dynamic_slice_in_dim(array, (1 - core) * half, half, axis)

    def gather(weight, axis):
        return lax.all_gather(own_half(weight, axis), ("row", "dp"), axis=axis, tiled=True)

    def line_step(from_left, from_right, step):
        from_left = lax.ppermute(from_left, "col", [(i, i + 1) for i in range(step - 1, cols - 1)])
        from_right = lax.ppermute(from_right, "col", [(i + 1, i) for i in range(cols - step)])
        return from_left, from_right

    def sum_step(up, down, step):
        up = lax.ppermute(up, "col", [(i, i + 1) for i in range(step)])
        down = lax.ppermute(down, "col", [(cols - 1 - i, cols - 2 - i) for i in range(step)])
        return up, down

    def pick(at_zero, at_one, at_two, at_three):
        low = jnp.where(col == 0, at_zero, at_one)
        high = jnp.where(col == 2, at_two, at_three)
        return jnp.where(col < 2, low, high)

    slot_chunk = [pick(3, 3, 0, 0), pick(2, 2, 1, 1), pick(1, 0, 3, 2), col]
    slot_index = [jnp.stack([one, core]).astype(jnp.int32) for one in slot_chunk]

    def slot_rows(array, slot):
        return lax.dynamic_slice_in_dim(array, slot_chunk[slot] * chunk, chunk, 0)

    def gather_slots(own, work):
        left1, right1 = line_step(own, own, 1)
        left1, right1 = after((left1, right1), work(3, own))
        left2, right2 = line_step(left1, right1, 2)
        left2, right2 = after((left2, right2), work(2, jnp.where(col % 2 == 0, right1, left1)))
        left3, right3 = line_step(left2, right2, 3)
        left3, right3 = after((left3, right3), work(1, pick(right2, right1, left1, left2)))
        return work(0, pick(right3, right2, left2, left3))

    def sum_slots(make, window=lambda step, gate: ()):
        def at(step, gate):
            return make(step, gate), window(step, gate)

        first = make(0, ())
        up, down = sum_step(first, first, 1)
        second, extra = at(1, first)
        up, down = after((up, down), second, extra)
        up = jnp.where(col == 0, second, first) + up
        down = jnp.where(col == 3, second, first) + down
        gate = (up, down)
        up, down = sum_step(up, down, 2)
        third, extra = at(2, gate)
        up, down = after((up, down), third, extra)
        up = jnp.where(col == 1, second, third) + up
        down = jnp.where(col == 2, second, third) + down
        gate = (up, down)
        up, down = sum_step(up, down, 3)
        fourth, extra = at(3, gate)
        up, down = after((up, down), fourth, extra)
        return fourth.astype(F32) + up.astype(F32) + down.astype(F32)

    def both_cores(half, axis):
        other = lax.ppermute(half, "dp", swap)
        first = jnp.where(core == 0, half, other)
        second = jnp.where(core == 0, other, half)
        return jnp.concatenate([first, second], axis=axis).astype(F32)

    def sum_sent(left_mat, right_other):
        return lax.ppermute(left_transposed(left_mat, right_other).astype(BF16), "dp", swap)

    def sum_kept(left_mat, right_own, got):
        total = (left_transposed(left_mat, right_own) + got.astype(F32)).astype(BF16)
        return total, lax.psum_scatter(total, "row", scatter_dimension=0, tiled=True)

    by_x = [(0, 1), (1, 0), (2, 3), (3, 2)]
    by_y = [(0, 2), (2, 0), (1, 3), (3, 1)]

    def row_first(half):
        if rows != 4:
            return (half,)
        return half, lax.ppermute(half, "row", by_x), lax.ppermute(half, "row", by_y)

    def row_second(pieces):
        if rows != 4:
            return pieces
        middle = pieces[0].shape[0] // 2
        return (
            *pieces,
            lax.ppermute(pieces[1][:middle], "row", by_y),
            lax.ppermute(pieces[2][middle:], "row", by_x),
        )

    def row_blocks(pieces):
        if rows != 4:
            whole = lax.all_gather(pieces[0], ("row", "dp"), axis=0, tiled=False)
            whole = whole.reshape(rows, cores, *pieces[0].shape)
            return tuple(lax.dynamic_index_in_dim(whole, one, 1, keepdims=False) for one in (core, 1 - core))
        own, by_one, by_two, corner_top, corner_low = pieces
        middle = own.shape[0] // 2
        held = unset((rows, *own.shape), own.dtype)
        for piece, block, start in (
            (own, row, 0), (by_one, row ^ 1, 0), (by_two, row ^ 2, 0),
            (corner_top, row ^ 3, 0), (corner_low, row ^ 3, middle),
        ):
            held = lax.dynamic_update_slice(held, piece[None], (block, start, 0))
        return held, lax.ppermute(held, "dp", swap)

    full_qkv = gather(jnp.concatenate([w_query, w_key, w_value], axis=1), 0)
    full_gate = gather(w_gate, 0)
    full_up = gather(w_up, 0)
    down_pieces = row_first(own_half(w_down, 0))
    out_half = own_half(w_out, 0)
    out_stack = jnp.concatenate(
        [out_half]
        + [
            lax.ppermute(out_half, "col", [(i, (i - step) % cols) for i in range(cols)])
            for step in range(1, cols)
        ],
        axis=0,
    )

    qkv = plain_dot(after(block_input, down_pieces, out_stack), full_qkv)
    out_pieces = row_first(out_stack)
    down_pieces = row_second(down_pieces)
    query_raw, key_raw = qkv[:, :local_width], qkv[:, local_width : 2 * local_width]
    query_sq, key_sq = lax.psum(
        (jnp.sum(query_raw * query_raw, axis=1), jnp.sum(key_raw * key_raw, axis=1)), "col"
    )
    query_scale = lax.rsqrt(query_sq / width + EPS)[:, None]
    key_scale = lax.rsqrt(key_sq / width + EPS)[:, None]
    scales = (query_scale, key_scale)
    gains = (query_gain[None, :], key_gain[None, :])
    tables = rope_tables(positions)
    seg_col, seg_row = segment_ids[:, None], segment_ids[None, :]
    query_rot, key_rot, value_heads, attended, log_total = attend_forward(
        after(qkv, out_pieces, down_pieces), scales, gains, tables, seg_col, seg_row, heads
    )

    left1, right1 = line_step(attended, attended, 1)
    out_pieces = row_second(out_pieces)
    down_halves = row_blocks(down_pieces)
    left1, right1 = after((left1, right1), out_pieces, down_halves[0])
    left2, right2 = line_step(left1, right1, 2)
    out_halves = row_blocks(out_pieces)
    left2, right2 = after((left2, right2), out_halves[0], down_halves[1])
    left3, right3 = line_step(left2, right2, 3)
    pieces = [attended, right1 + left3, right2 + left2, right3 + left1]
    attended_all = jnp.concatenate(
        [one[:, half * half_width : (half + 1) * half_width] for half in range(cores) for one in pieces],
        axis=1,
    )

    held = dict(forward=(), backward=(), attention=(), output=())
    gain_sums = dict(mlp=0.0, attn=0.0)

    def forward_work(slot, gate):
        results = forward_chunk(
            slot_index[slot], after(attended_all, gate), out_halves, block_input, attn_row, full_gate, full_up,
            down_halves, chunk, held["forward"],
        )
        held["forward"] = results[:6]
        return results[6]

    down_own = sum_slots(forward_work).astype(BF16)
    attn_raw, attn_scale, hidden_b, gate_proj, up_proj, mixed_act = held["forward"]
    mlp_parts = [None] * cols

    def backward_work(slot, down_rows):
        results = backward_chunk(
            slot_index[slot], down_rows, attn_raw, attn_scale, block_input, grad_output, attn_row, mlp_row,
            gate_proj, up_proj, full_gate, full_up, down_halves, chunk, held["backward"],
        )
        held["backward"] = results[:4]
        mlp_parts[slot] = results[4]
        gain_sums["mlp"] = gain_sums["mlp"] + results[5]
        return results[4]

    gather_slots(down_own, backward_work)
    block_output, grad_down_in, grad_gate_in, grad_up_in = held["backward"]

    blocks = {}
    got = {}

    def mlp_window(step, gate):
        down_left, down_right, hidden_left, gate_right, up_right = after(
            (grad_down_in, mixed_act, hidden_b, grad_gate_in, grad_up_in), gate
        )
        if step == 1:
            got["down"] = sum_sent(down_left, other_half(down_right, 1))
            got["gate"] = sum_sent(hidden_left, other_half(gate_right, 1))
            return got["down"], got["gate"]
        if step == 2:
            blocks["down"] = sum_kept(down_left, own_half(down_right, 1), got["down"])
            got["up"] = sum_sent(hidden_left, other_half(up_right, 1))
            return blocks["down"][0], got["up"]
        blocks["gate"] = sum_kept(hidden_left, own_half(gate_right, 1), got["gate"])
        blocks["up"] = sum_kept(hidden_left, own_half(up_right, 1), got["up"])
        return blocks["gate"][0], blocks["up"][0]

    mlp_own = sum_slots(lambda slot, gate: mlp_parts[slot], mlp_window).astype(BF16)

    def attention_work(slot, mlp_rows):
        results = attention_chunk(
            slot_index[slot], mlp_rows, grad_output, attn_raw, attn_scale, attn_row, out_halves, half_width,
            chunk, held["attention"],
        )
        held["attention"] = results[:2]
        gain_sums["attn"] = gain_sums["attn"] + results[2]
        return results[1]

    gather_slots(mlp_own, attention_work)
    grad_attn_in, grad_att = held["attention"]
    own_grad_hidden = slot_rows(grad_output, 3).astype(F32) + mlp_own.astype(F32)

    query_dz, key_dz, grad_value_in, query_dot, key_dot, grad_query_gain, grad_key_gain = attend_backward(
        qkv, scales, gains, tables, seg_col, seg_row,
        (query_rot, key_rot, value_heads, attended, log_total), grad_att, heads,
    )
    query_dot, key_dot = lax.psum((query_dot[:, 0], key_dot[:, 0]), "col")
    grad_query_in = (
        query_scale * (query_dz - query_raw * query_scale * (query_dot / width)[:, None])
    ).astype(BF16)
    grad_key_in = (
        key_scale * (key_dz - key_raw * key_scale * (key_dot / width)[:, None])
    ).astype(BF16)
    grad_qkv = jnp.concatenate([grad_query_in, grad_key_in, grad_value_in], axis=1)
    gain_pack = jnp.concatenate([grad_query_gain, grad_key_gain, gain_sums["attn"], gain_sums["mlp"]], axis=1)

    def interleaved(picker, pieces_in):
        return jnp.concatenate([picker(one, 1) for one in pieces_in], axis=1)

    def input_window(step, gate):
        nonlocal gain_pack
        pack, *pieces_in, tokens_in, left_out, right_out = after(
            (gain_pack, grad_query_in, grad_key_in, grad_value_in, block_input, grad_attn_in, attended), gate
        )
        if step == 1:
            got["qkv"] = sum_sent(tokens_in, interleaved(other_half, pieces_in))
            got["out"] = sum_sent(left_out, other_half(right_out, 1))
            gain_pack = pack + lax.ppermute(pack, "dp", swap)
            return got["qkv"], got["out"], gain_pack
        if step == 2:
            blocks["qkv"] = sum_kept(tokens_in, interleaved(own_half, pieces_in), got["qkv"])
            if rows == 4:
                gain_pack = pack + lax.ppermute(pack, "row", by_x)
            return blocks["qkv"][0], gain_pack
        blocks["out"] = sum_kept(left_out, own_half(right_out, 1), got["out"])
        gain_pack = pack + lax.ppermute(pack, "row", by_y) if rows == 4 else lax.psum(pack, "row")
        return blocks["out"][0], gain_pack

    input_own = sum_slots(
        lambda slot, gate: times_transposed(after(slot_rows(grad_qkv, slot), gate), full_qkv).astype(BF16), input_window
    )

    results = {}
    quarter = local_width // 2

    def projection(index):
        pair = both_cores(blocks["qkv"][1][None, :, index * quarter : (index + 1) * quarter], 0)
        return jnp.concatenate([pair[0], pair[1]], axis=1)

    def output_work(slot, rows_in):
        held["output"] = (place_rows(slot_index[slot], rows_in, tokens_here, F32, held["output"]),)
        if slot == 3:
            results["down"] = jnp.transpose(both_cores(blocks["down"][1], 1))
            results["gate"] = both_cores(blocks["gate"][1], 1)
            return held["output"], results["down"], results["gate"]
        if slot == 2:
            results["up"] = both_cores(blocks["up"][1], 1)
            return held["output"], results["up"]
        if slot == 1:
            results["out"] = jnp.transpose(both_cores(blocks["out"][1], 1))
            results["qkv"] = [projection(index) for index in range(3)]
            return held["output"], results["out"], results["qkv"]
        return held["output"]

    gather_slots((own_grad_hidden + input_own).astype(BF16), output_work)
    ends = (local_width, 2 * local_width, 2 * local_width + width)
    gain_grads = jnp.split(gain_pack[0], ends)
    return (
        block_output,
        held["output"][0],
        *results["qkv"],
        results["out"],
        results["gate"],
        results["up"],
        results["down"],
        *gain_grads,
    )


def layer(sizes, *arrays):
    return shards(sizes, *arrays)


def solution(mesh):
    in_specs = (
        P(("dp", "row"), None),
        P(("dp", "row")),
        P(("dp", "row")),
        P("row", "col"),
        P("row", "col"),
        P("row", "col"),
        P("col", "row"),
        P("row", "col"),
        P("row", "col"),
        P("col", "row"),
        P("col"),
        P("col"),
        P(),
        P(),
        P(("dp", "row"), None),
    )
    out_specs = (
        P(("dp", "row"), None),
        P(("dp", "row"), None),
        P("row", "col"),
        P("row", "col"),
        P("row", "col"),
        P("col", "row"),
        P("row", "col"),
        P("row", "col"),
        P("col", "row"),
        P("col"),
        P("col"),
        P(),
        P(),
    )
    sizes = (mesh.shape["dp"], mesh.shape["row"], mesh.shape["col"])
    return jax.shard_map(
        functools.partial(layer, sizes), mesh=mesh, in_specs=in_specs, out_specs=out_specs, check_vma=False
    )
```

```python
import functools

import jax
import jax.numpy as jnp
from jax import lax
from jax.experimental import pallas as pl
from jax.experimental.pallas import tpu as pltpu
from jax.sharding import PartitionSpec as P


HD = 128
LEN = 1024
BQ = 256
VMEM = 60 << 20

EPS = 1e-06
THETA = 500000.0
NEG_FILL = -1e30
SCORE_SCALE = HD ** (-0.5)
F32 = jnp.float32
BF16 = jnp.bfloat16


def plain_dot(left_mat, right_mat):
    return jnp.dot(left_mat, right_mat, preferred_element_type=F32)


def times_transposed(left_mat, right_mat):
    return lax.dot_general(
        left_mat, right_mat, (((1,), (1,)), ((), ())), preferred_element_type=F32
    )


def left_transposed(left_mat, right_mat):
    return lax.dot_general(
        left_mat, right_mat, (((0,), (0,)), ((), ())), preferred_element_type=F32
    )


def rope_tables(positions):
    half_dim = HD // 2
    inv_freq = THETA ** (-(jnp.arange(half_dim, dtype=F32) * 2.0) / HD)
    angles = positions.astype(F32)[:, None] * inv_freq[None, :]
    cos_half, sin_half = jnp.cos(angles), jnp.sin(angles)
    cosine = jnp.concatenate([cos_half, cos_half], axis=-1)
    sine_signed = jnp.concatenate([-sin_half, sin_half], axis=-1)
    return cosine, sine_signed


def fill_mask(bias_ref, seg_col_ref, seg_row_ref):
    @pl.when(pl.program_id(0) == 0)
    def _():
        for first in range(0, LEN, BQ):
            keys = first + BQ
            rows = seg_col_ref[first:keys, :]
            cols = seg_row_ref[:, :keys]
            query_index = first + lax.broadcasted_iota(jnp.int32, (BQ, keys), 0)
            key_index = lax.broadcasted_iota(jnp.int32, (BQ, keys), 1)
            allowed = (rows == cols) & (key_index <= query_index)
            bias_ref[first:keys, :keys] = jnp.where(allowed, 0.0, NEG_FILL)


def attend_forward_kernel(
    q_ref, k_ref, v_ref, qs_ref, ks_ref, qg_ref, kg_ref, cos_ref, sin_ref, segc_ref, segr_ref,
    qrot_ref, krot_ref, vb_ref, att_ref, log_ref, bias_ref,
):
    fill_mask(bias_ref, segc_ref, segr_ref)
    cosine, sine = cos_ref[...], sin_ref[...]

    def turned(raw, scale, gain):
        norm = raw * scale * gain
        return (norm * cosine + pltpu.roll(norm, HD // 2, 1) * sine).astype(BF16)

    qrot_ref[...] = turned(q_ref[...], qs_ref[...], qg_ref[...])
    krot_ref[...] = turned(k_ref[...], ks_ref[...], kg_ref[...])
    vb_ref[...] = v_ref[...].astype(BF16)
    for first in range(0, LEN, BQ):
        keys = first + BQ
        scores = times_transposed(qrot_ref[first:keys, :], krot_ref[:keys, :]) * SCORE_SCALE
        masked = scores + bias_ref[first:keys, :keys]
        peak = jnp.max(masked, axis=1, keepdims=True)
        weight = jnp.exp(masked - peak)
        total = jnp.sum(weight, axis=1, keepdims=True)
        probs = (weight * (1.0 / total)).astype(BF16)
        att_ref[first:keys, :] = plain_dot(probs, vb_ref[:keys, :]).astype(BF16)
        log_ref[0, first:keys, :] = peak + jnp.log(total)


def attend_backward_kernel(
    q_ref, k_ref, qs_ref, ks_ref, qg_ref, kg_ref, cos_ref, sin_ref, segc_ref, segr_ref,
    qrot_ref, krot_ref, vb_ref, att_ref, log_ref, grad_ref,
    dzq_ref, dzk_ref, gv_ref, dotq_ref, dotk_ref, gainq_ref, gaink_ref,
    dq_acc, dk_acc, dv_acc, bias_ref,
):
    fill_mask(bias_ref, segc_ref, segr_ref)
    dk_acc[...] = jnp.zeros_like(dk_acc)
    dv_acc[...] = jnp.zeros_like(dv_acc)
    for first in range(0, LEN, BQ):
        keys = first + BQ
        queries = qrot_ref[first:keys, :]
        grads = grad_ref[first:keys, :]
        scores = times_transposed(queries, krot_ref[:keys, :]) * SCORE_SCALE
        probs = jnp.exp(scores + bias_ref[first:keys, :keys] - log_ref[0, first:keys, :])
        delta = jnp.sum(
            grads.astype(F32) * att_ref[first:keys, :].astype(F32), axis=1, keepdims=True
        )
        grad_probs = times_transposed(grads, vb_ref[:keys, :])
        grad_scores = (probs * (grad_probs - delta) * SCORE_SCALE).astype(BF16)
        dq_acc[first:keys, :] = plain_dot(grad_scores, krot_ref[:keys, :])
        dk_acc[:keys, :] += left_transposed(grad_scores, queries)
        dv_acc[:keys, :] += left_transposed(probs.astype(BF16), grads)
    gv_ref[...] = dv_acc[...].astype(BF16)
    cosine, sine = cos_ref[...], sin_ref[...]

    def finish(acc, raw_ref, scale_ref, gain_ref, dz_ref, dot_ref, gain_grad_ref):
        grad_rot = acc[...]
        grad_norm = grad_rot * cosine - pltpu.roll(grad_rot, HD // 2, 1) * sine
        unit = raw_ref[...] * scale_ref[...]
        gain_grad_ref[...] = jnp.sum(grad_norm * unit, axis=0, keepdims=True)
        grad_unit = grad_norm * gain_ref[...]
        dz_ref[...] = grad_unit
        part = jnp.sum(grad_unit * unit, axis=1, keepdims=True)

        @pl.when(pl.program_id(0) == 0)
        def _():
            dot_ref[...] = part

        @pl.when(pl.program_id(0) > 0)
        def _():
            dot_ref[...] += part

    finish(dq_acc, q_ref, qs_ref, qg_ref, dzq_ref, dotq_ref, gainq_ref)
    finish(dk_acc, k_ref, ks_ref, kg_ref, dzk_ref, dotk_ref, gaink_ref)


def head_spec(offset):
    return pl.BlockSpec((LEN, HD), lambda h: (0, offset + h))


def whole_spec(shape):
    return pl.BlockSpec(shape, lambda h: (0,) * len(shape))


def gain_spec():
    return pl.BlockSpec((1, HD), lambda h: (0, h))


LOG_SPEC = pl.BlockSpec((1, LEN, 1), lambda h: (h, 0, 0))
COLUMN = (LEN, 1)
TABLE = (LEN, HD)


def attend_forward(qkv, scales, gains, tables, seg_col, seg_row, heads):
    width = heads * HD
    piece = jax.ShapeDtypeStruct((LEN, width), BF16)
    return pl.pallas_call(
        attend_forward_kernel,
        grid=(heads,),
        in_specs=[
            head_spec(0), head_spec(heads), head_spec(2 * heads),
            whole_spec(COLUMN), whole_spec(COLUMN), gain_spec(), gain_spec(),
            whole_spec(TABLE), whole_spec(TABLE), whole_spec(COLUMN), whole_spec((1, LEN)),
        ],
        out_specs=[head_spec(0)] * 4 + [LOG_SPEC],
        out_shape=[piece] * 4 + [jax.ShapeDtypeStruct((heads, LEN, 1), F32)],
        scratch_shapes=[pltpu.VMEM((LEN, LEN), F32)],
        compiler_params=pltpu.CompilerParams(vmem_limit_bytes=VMEM),
        cost_estimate=pl.CostEstimate(
            flops=heads * 4 * LEN * LEN * HD, bytes_accessed=LEN * width * 20, transcendentals=0
        ),
        name="attend_forward",
    )(qkv, qkv, qkv, *scales, *gains, *tables, seg_col, seg_row)


def attend_backward(qkv, scales, gains, tables, seg_col, seg_row, saved, grad_att, heads):
    width = heads * HD
    full = jax.ShapeDtypeStruct((LEN, width), F32)
    column = jax.ShapeDtypeStruct(COLUMN, F32)
    gain_row = jax.ShapeDtypeStruct((1, width), F32)
    return pl.pallas_call(
        attend_backward_kernel,
        grid=(heads,),
        in_specs=[
            head_spec(0), head_spec(heads),
            whole_spec(COLUMN), whole_spec(COLUMN), gain_spec(), gain_spec(),
            whole_spec(TABLE), whole_spec(TABLE), whole_spec(COLUMN), whole_spec((1, LEN)),
            head_spec(0), head_spec(0), head_spec(0), head_spec(0), LOG_SPEC, head_spec(0),
        ],
        out_specs=[
            head_spec(0), head_spec(0), head_spec(0),
            whole_spec(COLUMN), whole_spec(COLUMN), gain_spec(), gain_spec(),
        ],
        out_shape=[
            full, full, jax.ShapeDtypeStruct((LEN, width), BF16), column, column, gain_row, gain_row,
        ],
        scratch_shapes=[pltpu.VMEM((LEN, HD), F32)] * 3 + [pltpu.VMEM((LEN, LEN), F32)],
        compiler_params=pltpu.CompilerParams(vmem_limit_bytes=VMEM),
        cost_estimate=pl.CostEstimate(
            flops=heads * 10 * LEN * LEN * HD, bytes_accessed=LEN * width * 40, transcendentals=0
        ),
        name="attend_backward",
    )(qkv, qkv, *scales, *gains, *tables, seg_col, seg_row, *saved, grad_att)


def half_tile(step, core, tiles):
    per_half = tiles // 2
    return ((core + step // per_half) % 2) * per_half + step % per_half


def forward_chunk_kernel(
    idx_ref, att_ref, wo_own_ref, wo_oth_ref, x_ref, gain_ref, wg_ref, wu_ref, wd_own_ref, wd_oth_ref, *refs,
    blocks, tiles,
):
    raw_ref, scale_ref, hb_ref, gate_ref, up_ref, mixed_ref, part_ref, acc_ref = refs[-8:]
    block = wo_own_ref.shape[2]
    depth = wo_own_ref.shape[1]
    step = pl.program_id(0)
    core = idx_ref[1]

    @pl.when(step < blocks)
    def _():
        own = att_ref[:, pl.ds(pl.multiple_of(core * depth, depth), depth)]
        other = att_ref[:, pl.ds(pl.multiple_of((1 - core) * depth, depth), depth)]
        raw_ref[:, pl.ds(pl.multiple_of(step * block, block), block)] = plain_dot(
            own, wo_own_ref[0]
        ) + plain_dot(other, wo_oth_ref[0])

    @pl.when(step == blocks - 1)
    def _():
        raw = raw_ref[...]
        scale = lax.rsqrt(jnp.mean(raw * raw, axis=1, keepdims=True) + EPS)
        scale_ref[...] = scale
        hb_ref[...] = (x_ref[...].astype(F32) + raw * scale * gain_ref[...]).astype(BF16)
        acc_ref[...] = jnp.zeros_like(acc_ref)

    def tile_work(wd_ref):
        hidden_b = hb_ref[...]
        gate = plain_dot(hidden_b, wg_ref[...])
        up = plain_dot(hidden_b, wu_ref[...])
        mixed = (gate * jax.nn.sigmoid(gate) * up).astype(BF16)
        gate_ref[...] = gate.astype(BF16)
        up_ref[...] = up.astype(BF16)
        mixed_ref[...] = mixed
        for j in range(blocks):
            acc_ref[:, j * block : (j + 1) * block] += plain_dot(mixed, wd_ref[j])

    @pl.when((step >= blocks) & (step < blocks + tiles // 2))
    def _():
        tile_work(wd_own_ref)

    @pl.when(step >= blocks + tiles // 2)
    def _():
        tile_work(wd_oth_ref)

    @pl.when(step == blocks + tiles - 1)
    def _():
        part_ref[...] = acc_ref[...].astype(BF16)


TILE = 256


def forward_chunk(index, attended, out_halves, block_input, gain, w_gate, w_up, down_halves, chunk, before):
    tokens, width = block_input.shape
    hidden = w_gate.shape[1]
    blocks, depth, block = out_halves[0].shape
    tiles = hidden // TILE

    def tile_of(j, idx):
        return half_tile(jnp.maximum(j - blocks, 0), idx[1], tiles)

    rows = pl.BlockSpec((chunk, width), lambda j, idx: (idx[0], 0))
    out_half = pl.BlockSpec((1, depth, block), lambda j, idx: (jnp.minimum(j, blocks - 1), 0, 0))
    up_tile = pl.BlockSpec((width, TILE), lambda j, idx: (0, tile_of(j, idx)))
    down_own = pl.BlockSpec(
        (blocks, TILE, block), lambda j, idx: (0, jnp.clip(j - blocks, 0, tiles // 2 - 1), 0)
    )
    down_oth = pl.BlockSpec(
        (blocks, TILE, block), lambda j, idx: (0, jnp.maximum(j - blocks - tiles // 2, 0), 0)
    )
    act_tile = pl.BlockSpec((chunk, TILE), lambda j, idx: (idx[0], tile_of(j, idx)))
    before = tuple(before)
    return pl.pallas_call(
        functools.partial(forward_chunk_kernel, blocks=blocks, tiles=tiles),
        grid_spec=pltpu.PrefetchScalarGridSpec(
            num_scalar_prefetch=1,
            grid=(blocks + tiles,),
            in_specs=[
                pl.BlockSpec((chunk, attended.shape[1]), lambda j, idx: (idx[0], 0)),
                out_half, out_half, rows, pl.BlockSpec((1, width), lambda j, idx: (0, 0)),
                up_tile, up_tile, down_own, down_oth,
            ] + [pl.BlockSpec(memory_space=pl.ANY)] * len(before),
            out_specs=[
                rows, pl.BlockSpec((chunk, 1), lambda j, idx: (idx[0], 0)), rows, act_tile, act_tile, act_tile,
                pl.BlockSpec((chunk, width), lambda j, idx: (0, 0)),
            ],
            scratch_shapes=[pltpu.VMEM((chunk, width), F32)],
        ),
        out_shape=[
            jax.ShapeDtypeStruct((tokens, width), F32),
            jax.ShapeDtypeStruct((tokens, 1), F32),
            jax.ShapeDtypeStruct((tokens, width), BF16),
            jax.ShapeDtypeStruct((tokens, hidden), BF16),
            jax.ShapeDtypeStruct((tokens, hidden), BF16),
            jax.ShapeDtypeStruct((tokens, hidden), BF16),
            jax.ShapeDtypeStruct((chunk, width), BF16),
        ],
        input_output_aliases={10 + i: i for i in range(len(before))},
        compiler_params=pltpu.CompilerParams(vmem_limit_bytes=VMEM),
        cost_estimate=pl.CostEstimate(
            flops=2 * chunk * width * (width + 3 * hidden),
            bytes_accessed=2 * width * (width + 3 * hidden),
            transcendentals=0,
        ),
        name="forward_chunk",
    )(index, attended, *out_halves, block_input, gain, w_gate, w_up, *down_halves, *before)


def backward_chunk_kernel(
    idx_ref, down_ref, raw_ref, scale_ref, x_ref, grad_ref, attn_gain_ref, mlp_gain_ref,
    gate_ref, up_ref, wg_ref, wu_ref, wd_own_ref, wd_oth_ref, *refs, blocks, tiles,
):
    out_ref, gdi_ref, gg_ref, gu_ref, part_ref, gain_grad_ref, acc_ref = refs[-7:]
    block = wd_own_ref.shape[2]
    step = pl.program_id(0)

    @pl.when(step == 0)
    def _():
        down_raw = down_ref[...].astype(F32)
        down_scale = lax.rsqrt(jnp.mean(down_raw * down_raw, axis=1, keepdims=True) + EPS)
        unit = down_raw * down_scale
        mlp_gain = mlp_gain_ref[...]
        hidden = x_ref[...].astype(F32) + raw_ref[...] * scale_ref[...] * attn_gain_ref[...]
        out_ref[...] = (hidden + unit * mlp_gain).astype(BF16)
        grad_y = grad_ref[...].astype(F32)
        gain_grad_ref[...] = jnp.sum(grad_y * unit, axis=0, keepdims=True)
        grad_unit = grad_y * mlp_gain
        mean = jnp.mean(grad_unit * unit, axis=1, keepdims=True)
        gdi_ref[...] = (down_scale * (grad_unit - unit * mean)).astype(BF16)
        acc_ref[...] = jnp.zeros_like(acc_ref)

    def tile_work(wd_ref):
        grad_mixed = times_transposed(gdi_ref[:, :block], wd_ref[0])
        for j in range(1, blocks):
            grad_mixed += times_transposed(gdi_ref[:, j * block : (j + 1) * block], wd_ref[j])
        gate = gate_ref[...].astype(F32)
        sig = jax.nn.sigmoid(gate)
        grad_gate = (grad_mixed * up_ref[...].astype(F32) * sig * (1.0 + gate * (1.0 - sig))).astype(BF16)
        grad_up = (grad_mixed * (gate * sig)).astype(BF16)
        gg_ref[...] = grad_gate
        gu_ref[...] = grad_up
        acc_ref[...] += times_transposed(grad_gate, wg_ref[...]) + times_transposed(grad_up, wu_ref[...])

    @pl.when(step < tiles // 2)
    def _():
        tile_work(wd_own_ref)

    @pl.when(step >= tiles // 2)
    def _():
        tile_work(wd_oth_ref)

    @pl.when(step == tiles - 1)
    def _():
        part_ref[...] = acc_ref[...].astype(BF16)


def backward_chunk(
    index, down_rows, raw, scale, block_input, grad_output, attn_gain, mlp_gain, gate, up, w_gate, w_up,
    down_halves, chunk, before,
):
    tokens, width = block_input.shape
    hidden = w_gate.shape[1]
    blocks, _, block = down_halves[0].shape
    tiles = hidden // TILE

    def tile_of(j, idx):
        return half_tile(j, idx[1], tiles)

    rows = pl.BlockSpec((chunk, width), lambda j, idx: (idx[0], 0))
    fixed = pl.BlockSpec((chunk, width), lambda j, idx: (0, 0))
    gain_row = pl.BlockSpec((1, width), lambda j, idx: (0, 0))
    up_tile = pl.BlockSpec((width, TILE), lambda j, idx: (0, tile_of(j, idx)))
    act_tile = pl.BlockSpec((chunk, TILE), lambda j, idx: (idx[0], tile_of(j, idx)))
    before = tuple(before)
    return pl.pallas_call(
        functools.partial(backward_chunk_kernel, blocks=blocks, tiles=tiles),
        grid_spec=pltpu.PrefetchScalarGridSpec(
            num_scalar_prefetch=1,
            grid=(tiles,),
            in_specs=[
                fixed, rows, pl.BlockSpec((chunk, 1), lambda j, idx: (idx[0], 0)), rows, rows, gain_row, gain_row,
                act_tile, act_tile, up_tile, up_tile,
                pl.BlockSpec((blocks, TILE, block), lambda j, idx: (0, jnp.minimum(j, tiles // 2 - 1), 0)),
                pl.BlockSpec((blocks, TILE, block), lambda j, idx: (0, jnp.maximum(j - tiles // 2, 0), 0)),
            ] + [pl.BlockSpec(memory_space=pl.ANY)] * len(before),
            out_specs=[rows, rows, act_tile, act_tile, fixed, gain_row],
            scratch_shapes=[pltpu.VMEM((chunk, width), F32)],
        ),
        out_shape=[
            jax.ShapeDtypeStruct((tokens, width), BF16),
            jax.ShapeDtypeStruct((tokens, width), BF16),
            jax.ShapeDtypeStruct((tokens, hidden), BF16),
            jax.ShapeDtypeStruct((tokens, hidden), BF16),
            jax.ShapeDtypeStruct((chunk, width), BF16),
            jax.ShapeDtypeStruct((1, width), F32),
        ],
        input_output_aliases={14 + i: i for i in range(len(before))},
        compiler_params=pltpu.CompilerParams(vmem_limit_bytes=VMEM),
        cost_estimate=pl.CostEstimate(
            flops=6 * chunk * width * hidden, bytes_accessed=6 * width * hidden, transcendentals=0
        ),
        name="backward_chunk",
    )(
        index, down_rows, raw, scale, block_input, grad_output, attn_gain, mlp_gain, gate, up, w_gate, w_up,
        *down_halves, *before,
    )


def attention_chunk_kernel(
    idx_ref, mlp_ref, grad_ref, raw_ref, scale_ref, gain_ref, wo_own_ref, wo_oth_ref, *refs, blocks,
):
    gai_ref, gatt_ref, gain_grad_ref = refs[-3:]
    half, block = wo_own_ref.shape[1:]
    core = idx_ref[1]
    scale = scale_ref[...]
    unit = raw_ref[...] * scale
    grad_hidden = grad_ref[...].astype(F32) + mlp_ref[...].astype(F32)
    gain_grad_ref[...] = jnp.sum(grad_hidden * unit, axis=0, keepdims=True)
    grad_unit = grad_hidden * gain_ref[...]
    mean = jnp.mean(grad_unit * unit, axis=1, keepdims=True)
    gai_ref[...] = (scale * (grad_unit - unit * mean)).astype(BF16)
    for place, w_ref in ((core, wo_own_ref), (1 - core, wo_oth_ref)):
        total = times_transposed(gai_ref[:, :block], w_ref[0])
        for j in range(1, blocks):
            total += times_transposed(gai_ref[:, j * block : (j + 1) * block], w_ref[j])
        gatt_ref[:, pl.ds(pl.multiple_of(place * half, half), half)] = total.astype(BF16)


def attention_chunk(index, mlp_rows, grad_output, raw, scale, gain, out_halves, half, chunk, before):
    tokens, width = grad_output.shape
    blocks, _, block = out_halves[0].shape
    rows = pl.BlockSpec((chunk, width), lambda j, idx: (idx[0], 0))
    fixed = pl.BlockSpec((chunk, width), lambda j, idx: (0, 0))
    gain_row = pl.BlockSpec((1, width), lambda j, idx: (0, 0))
    own_heads = pl.BlockSpec((blocks, half, block), lambda j, idx: (0, 0, 0))
    before = tuple(before)
    return pl.pallas_call(
        functools.partial(attention_chunk_kernel, blocks=blocks),
        grid_spec=pltpu.PrefetchScalarGridSpec(
            num_scalar_prefetch=1,
            grid=(1,),
            in_specs=[
                fixed, rows, rows, pl.BlockSpec((chunk, 1), lambda j, idx: (idx[0], 0)), gain_row,
                own_heads, own_heads,
            ] + [pl.BlockSpec(memory_space=pl.ANY)] * len(before),
            out_specs=[rows, pl.BlockSpec((chunk, 2 * half), lambda j, idx: (idx[0], 0)), gain_row],
        ),
        out_shape=[
            jax.ShapeDtypeStruct((tokens, width), BF16),
            jax.ShapeDtypeStruct((tokens, 2 * half), BF16),
            jax.ShapeDtypeStruct((1, width), F32),
        ],
        input_output_aliases={8 + i: i for i in range(len(before))},
        compiler_params=pltpu.CompilerParams(vmem_limit_bytes=VMEM),
        cost_estimate=pl.CostEstimate(
            flops=4 * chunk * width * half, bytes_accessed=16 * chunk * width, transcendentals=0
        ),
        name="attention_chunk",
    )(index, mlp_rows, grad_output, raw, scale, gain, *out_halves, *before)


def place_rows_kernel(idx_ref, rows_ref, *refs):
    refs[-1][...] = rows_ref[...].astype(refs[-1].dtype)


def place_rows(index, rows_in, tokens, dtype, before):
    chunk, width = rows_in.shape
    before = tuple(before)
    return pl.pallas_call(
        place_rows_kernel,
        grid_spec=pltpu.PrefetchScalarGridSpec(
            num_scalar_prefetch=1,
            grid=(2,),
            in_specs=[pl.BlockSpec((chunk // 2, width), lambda j, idx: (j, 0))]
            + [pl.BlockSpec(memory_space=pl.ANY)] * len(before),
            out_specs=pl.BlockSpec((chunk // 2, width), lambda j, idx: (2 * idx[0] + j, 0)),
        ),
        out_shape=jax.ShapeDtypeStruct((tokens, width), dtype),
        input_output_aliases={2: 0} if before else {},
        compiler_params=pltpu.CompilerParams(vmem_limit_bytes=VMEM),
        cost_estimate=pl.CostEstimate(flops=0, bytes_accessed=6 * chunk * width, transcendentals=0),
        name="place_rows",
    )(index, rows_in, *before)


def after(value, *tokens):
    return lax.optimization_barrier((value, tokens))[0]


def unset_kernel(out_ref):
    pass


def unset(shape, dtype):
    return pl.pallas_call(
        unset_kernel,
        out_specs=pl.BlockSpec(memory_space=pl.ANY),
        out_shape=jax.ShapeDtypeStruct(shape, dtype),
        name="unset",
    )()


def shards(
    sizes,
    block_input,
    segment_ids,
    positions,
    w_query,
    w_key,
    w_value,
    w_out,
    w_gate,
    w_up,
    w_down,
    query_gain,
    key_gain,
    attn_gain,
    mlp_gain,
    grad_output,
):
    cores, rows, cols = sizes
    tokens_here, width = block_input.shape
    assert tokens_here == LEN and cores == 2 and cols == 4
    local_width = w_query.shape[1]
    half_width = local_width // 2
    heads = local_width // HD
    chunk = tokens_here // cols
    core = lax.axis_index("dp")
    row = lax.axis_index("row")
    col = lax.axis_index("col")
    swap = [(0, 1), (1, 0)]
    attn_row, mlp_row = attn_gain[None, :], mlp_gain[None, :]

    def own_half(array, axis):
        half = array.shape[axis] // 2
        return lax.dynamic_slice_in_dim(array, core * half, half, axis)

    def other_half(array, axis):
        half = array.shape[axis] // 2
        return lax.dynamic_slice_in_dim(array, (1 - core) * half, half, axis)

    def gather(weight, axis):
        return lax.all_gather(own_half(weight, axis), ("row", "dp"), axis=axis, tiled=True)

    def line_step(from_left, from_right, step):
        from_left = lax.ppermute(from_left, "col", [(i, i + 1) for i in range(step - 1, cols - 1)])
        from_right = lax.ppermute(from_right, "col", [(i + 1, i) for i in range(cols - step)])
        return from_left, from_right

    def sum_step(up, down, step):
        up = lax.ppermute(up, "col", [(i, i + 1) for i in range(step)])
        down = lax.ppermute(down, "col", [(cols - 1 - i, cols - 2 - i) for i in range(step)])
        return up, down

    def pick(at_zero, at_one, at_two, at_three):
        low = jnp.where(col == 0, at_zero, at_one)
        high = jnp.where(col == 2, at_two, at_three)
        return jnp.where(col < 2, low, high)

    slot_chunk = [pick(3, 3, 0, 0), pick(2, 2, 1, 1), pick(1, 0, 3, 2), col]
    slot_index = [jnp.stack([one, core]).astype(jnp.int32) for one in slot_chunk]

    def slot_rows(array, slot):
        return lax.dynamic_slice_in_dim(array, slot_chunk[slot] * chunk, chunk, 0)

    def gather_slots(own, work):
        left1, right1 = line_step(own, own, 1)
        left1, right1 = after((left1, right1), work(3, own))
        left2, right2 = line_step(left1, right1, 2)
        left2, right2 = after((left2, right2), work(2, jnp.where(col % 2 == 0, right1, left1)))
        left3, right3 = line_step(left2, right2, 3)
        left3, right3 = after((left3, right3), work(1, pick(right2, right1, left1, left2)))
        return work(0, pick(right3, right2, left2, left3))

    def gather_halves(own, work):
        half = own.shape[1] // 2
        left, right, token = {}, {}, ()
        for part in range(2):
            left[part, 0] = right[part, 0] = own[:, part * half : (part + 1) * half]
        arrived = (
            lambda lefts, rights: lefts[0],
            lambda lefts, rights: jnp.where(col % 2 == 0, rights[1], lefts[1]),
            lambda lefts, rights: pick(rights[2], rights[1], lefts[1], lefts[2]),
            lambda lefts, rights: pick(rights[3], rights[2], lefts[2], lefts[3]),
        )

        def slot_of(step, token):
            halves = []
            for part in range(2):
                seen = tuple((left[part, k], right[part, k]) for k in range(step))
                seen = after(seen, token)
                halves.append(arrived[step - 1]([one[0] for one in seen], [one[1] for one in seen]))
            return jnp.concatenate(halves, axis=1)

        for step in range(1, cols):
            for part in range(2):
                sent = (left[part, step - 1], right[part, step - 1])
                left[part, step], right[part, step] = line_step(*sent, step)
            token = work(cols - step, slot_of(step, token))
        return work(0, slot_of(cols, token))

    def sum_slots(make, window=lambda step, gate: ()):
        def at(step, gate):
            return make(step, gate), window(step, gate)

        first = make(0, ())
        up, down = sum_step(first, first, 1)
        second, extra = at(1, first)
        up, down = after((up, down), second, extra)
        up = jnp.where(col == 0, second, first) + up
        down = jnp.where(col == 3, second, first) + down
        gate = (up, down)
        up, down = sum_step(up, down, 2)
        third, extra = at(2, gate)
        up, down = after((up, down), third, extra)
        up = jnp.where(col == 1, second, third) + up
        down = jnp.where(col == 2, second, third) + down
        gate = (up, down)
        up, down = sum_step(up, down, 3)
        fourth, extra = at(3, gate)
        up, down = after((up, down), fourth, extra)
        return fourth.astype(F32) + up.astype(F32) + down.astype(F32)

    def both_cores(half, axis):
        other = lax.ppermute(half, "dp", swap)
        first = jnp.where(core == 0, half, other)
        second = jnp.where(core == 0, other, half)
        return jnp.concatenate([first, second], axis=axis).astype(F32)

    def sum_sent(left_mat, right_other):
        return lax.ppermute(left_transposed(left_mat, right_other).astype(BF16), "dp", swap)

    def sum_kept(left_mat, right_own, got):
        total = (left_transposed(left_mat, right_own) + got.astype(F32)).astype(BF16)
        return total, lax.psum_scatter(total, "row", scatter_dimension=0, tiled=True)

    by_x = [(0, 1), (1, 0), (2, 3), (3, 2)]
    by_y = [(0, 2), (2, 0), (1, 3), (3, 1)]

    def row_first(half):
        if rows != 4:
            return (half,)
        return half, lax.ppermute(half, "row", by_x), lax.ppermute(half, "row", by_y)

    def row_second(pieces):
        if rows != 4:
            return pieces
        middle = pieces[0].shape[0] // 2
        return (
            *pieces,
            lax.ppermute(pieces[1][:middle], "row", by_y),
            lax.ppermute(pieces[2][middle:], "row", by_x),
        )

    def row_blocks(pieces):
        if rows != 4:
            whole = lax.all_gather(pieces[0], ("row", "dp"), axis=0, tiled=False)
            whole = whole.reshape(rows, cores, *pieces[0].shape)
            return tuple(lax.dynamic_index_in_dim(whole, one, 1, keepdims=False) for one in (core, 1 - core))
        own, by_one, by_two, corner_top, corner_low = pieces
        middle = own.shape[0] // 2
        held = unset((rows, *own.shape), own.dtype)
        for piece, block, start in (
            (own, row, 0), (by_one, row ^ 1, 0), (by_two, row ^ 2, 0),
            (corner_top, row ^ 3, 0), (corner_low, row ^ 3, middle),
        ):
            held = lax.dynamic_update_slice(held, piece[None], (block, start, 0))
        return held, lax.ppermute(held, "dp", swap)

    full_qkv = gather(jnp.concatenate([w_query, w_key, w_value], axis=1), 0)
    full_gate = gather(w_gate, 0)
    full_up = gather(w_up, 0)
    out_half = own_half(w_out, 0)
    out_stack = jnp.concatenate(
        [out_half]
        + [
            lax.ppermute(out_half, "col", [(i, (i - step) % cols) for i in range(cols)])
            for step in range(1, cols)
        ],
        axis=0,
    )
    down_start, out_start = after((own_half(w_down, 0), out_stack), full_qkv)
    down_pieces = row_first(down_start)
    out_pieces = row_first(out_start)

    qkv = plain_dot(block_input, full_qkv)
    query_raw, key_raw = qkv[:, :local_width], qkv[:, local_width : 2 * local_width]
    query_sq, key_sq = lax.psum(
        (jnp.sum(query_raw * query_raw, axis=1), jnp.sum(key_raw * key_raw, axis=1)), "col"
    )
    query_scale = lax.rsqrt(query_sq / width + EPS)[:, None]
    key_scale = lax.rsqrt(key_sq / width + EPS)[:, None]
    scales = (query_scale, key_scale)
    gains = (query_gain[None, :], key_gain[None, :])
    tables = rope_tables(positions)
    seg_col, seg_row = segment_ids[:, None], segment_ids[None, :]
    query_rot, key_rot, value_heads, attended, log_total = attend_forward(
        qkv, scales, gains, tables, seg_col, seg_row, heads
    )

    steps_from = {}
    for part in range(cores):
        steps_from[part] = [(attended[:, part * half_width : (part + 1) * half_width],) * 2]
    for step in range(1, cols):
        for part in range(cores):
            sent = steps_from[part][-1]
            steps_from[part].append(line_step(*sent, step))
        if step == 1:
            down_pieces = row_second(after(down_pieces, attended))
            out_pieces = row_second(after(out_pieces, attended))
            down_halves = row_blocks(down_pieces)
        if step == 2:
            out_halves = row_blocks(out_pieces)
    attended_all = jnp.concatenate(
        [
            steps_from[part][0][0] if step == 0 else steps_from[part][step][1] + steps_from[part][cols - step][0]
            for part in range(cores)
            for step in range(cols)
        ],
        axis=1,
    )

    held = dict(forward=(), backward=(), attention=(), output=())
    gain_sums = dict(mlp=0.0, attn=0.0)

    def forward_work(slot, gate):
        results = forward_chunk(
            slot_index[slot], after(attended_all, gate), out_halves, block_input, attn_row, full_gate, full_up,
            down_halves, chunk, held["forward"],
        )
        held["forward"] = results[:6]
        return results[6]

    down_own = sum_slots(forward_work).astype(BF16)
    attn_raw, attn_scale, hidden_b, gate_proj, up_proj, mixed_act = held["forward"]
    mlp_parts = [None] * cols

    def backward_work(slot, down_rows):
        results = backward_chunk(
            slot_index[slot], down_rows, attn_raw, attn_scale, block_input, grad_output, attn_row, mlp_row,
            gate_proj, up_proj, full_gate, full_up, down_halves, chunk, held["backward"],
        )
        held["backward"] = results[:4]
        mlp_parts[slot] = results[4]
        gain_sums["mlp"] = gain_sums["mlp"] + results[5]
        return results[4]

    gather_slots(down_own, backward_work)
    block_output, grad_down_in, grad_gate_in, grad_up_in = held["backward"]

    blocks = {}
    got = {}

    def mlp_window(step, gate):
        down_left, down_right, hidden_left, gate_right, up_right = after(
            (grad_down_in, mixed_act, hidden_b, grad_gate_in, grad_up_in), gate
        )
        if step == 1:
            got["down"] = sum_sent(down_left, other_half(down_right, 1))
            got["gate"] = sum_sent(hidden_left, other_half(gate_right, 1))
            return got["down"], got["gate"]
        if step == 2:
            blocks["down"] = sum_kept(down_left, own_half(down_right, 1), got["down"])
            got["up"] = sum_sent(hidden_left, other_half(up_right, 1))
            return blocks["down"][0], got["up"]
        blocks["gate"] = sum_kept(hidden_left, own_half(gate_right, 1), got["gate"])
        blocks["up"] = sum_kept(hidden_left, own_half(up_right, 1), got["up"])
        return blocks["gate"][0], blocks["up"][0]

    mlp_own = sum_slots(lambda slot, gate: mlp_parts[slot], mlp_window).astype(BF16)

    def attention_work(slot, mlp_rows):
        results = attention_chunk(
            slot_index[slot], mlp_rows, grad_output, attn_raw, attn_scale, attn_row, out_halves, half_width,
            chunk, held["attention"],
        )
        held["attention"] = results[:2]
        gain_sums["attn"] = gain_sums["attn"] + results[2]
        return results[1]

    gather_halves(mlp_own, attention_work)
    grad_attn_in, grad_att = held["attention"]
    own_grad_hidden = slot_rows(grad_output, 3).astype(F32) + mlp_own.astype(F32)

    query_dz, key_dz, grad_value_in, query_dot, key_dot, grad_query_gain, grad_key_gain = attend_backward(
        qkv, scales, gains, tables, seg_col, seg_row,
        (query_rot, key_rot, value_heads, attended, log_total), grad_att, heads,
    )
    query_dot, key_dot = lax.psum((query_dot[:, 0], key_dot[:, 0]), "col")
    grad_query_in = (
        query_scale * (query_dz - query_raw * query_scale * (query_dot / width)[:, None])
    ).astype(BF16)
    grad_key_in = (
        key_scale * (key_dz - key_raw * key_scale * (key_dot / width)[:, None])
    ).astype(BF16)
    grad_qkv = jnp.concatenate([grad_query_in, grad_key_in, grad_value_in], axis=1)
    gain_pack = jnp.concatenate([grad_query_gain, grad_key_gain, gain_sums["attn"], gain_sums["mlp"]], axis=1)

    def interleaved(picker, pieces_in):
        return jnp.concatenate([picker(one, 1) for one in pieces_in], axis=1)

    def input_window(step, gate):
        nonlocal gain_pack
        pack, *pieces_in, tokens_in, left_out, right_out = after(
            (gain_pack, grad_query_in, grad_key_in, grad_value_in, block_input, grad_attn_in, attended), gate
        )
        if step == 1:
            got["qkv"] = sum_sent(tokens_in, interleaved(other_half, pieces_in))
            got["out"] = sum_sent(left_out, other_half(right_out, 1))
            gain_pack = pack + lax.ppermute(pack, "dp", swap)
            return got["qkv"], got["out"], gain_pack
        if step == 2:
            blocks["qkv"] = sum_kept(tokens_in, interleaved(own_half, pieces_in), got["qkv"])
            if rows == 4:
                gain_pack = pack + lax.ppermute(pack, "row", by_x)
            return blocks["qkv"][0], gain_pack
        blocks["out"] = sum_kept(left_out, own_half(right_out, 1), got["out"])
        gain_pack = pack + lax.ppermute(pack, "row", by_y) if rows == 4 else lax.psum(pack, "row")
        return blocks["out"][0], gain_pack

    input_own = sum_slots(
        lambda slot, gate: times_transposed(after(slot_rows(grad_qkv, slot), gate), full_qkv).astype(BF16), input_window
    )

    results = {}
    quarter = local_width // 2

    def projection(index):
        pair = both_cores(blocks["qkv"][1][None, :, index * quarter : (index + 1) * quarter], 0)
        return jnp.concatenate([pair[0], pair[1]], axis=1)

    def output_work(slot, rows_in):
        held["output"] = (place_rows(slot_index[slot], rows_in, tokens_here, F32, held["output"]),)
        if slot == 3:
            results["down"] = jnp.transpose(both_cores(blocks["down"][1], 1))
            results["gate"] = both_cores(blocks["gate"][1], 1)
            return held["output"], results["down"], results["gate"]
        if slot == 2:
            results["up"] = both_cores(blocks["up"][1], 1)
            return held["output"], results["up"]
        if slot == 1:
            results["out"] = jnp.transpose(both_cores(blocks["out"][1], 1))
            results["qkv"] = [projection(index) for index in range(3)]
            return held["output"], results["out"], results["qkv"]
        return held["output"]

    gather_halves((own_grad_hidden + input_own).astype(BF16), output_work)
    ends = (local_width, 2 * local_width, 2 * local_width + width)
    gain_grads = jnp.split(gain_pack[0], ends)
    return (
        block_output,
        held["output"][0],
        *results["qkv"],
        results["out"],
        results["gate"],
        results["up"],
        results["down"],
        *gain_grads,
    )


def layer(sizes, *arrays):
    return shards(sizes, *arrays)


def solution(mesh):
    in_specs = (
        P(("dp", "row"), None),
        P(("dp", "row")),
        P(("dp", "row")),
        P("row", "col"),
        P("row", "col"),
        P("row", "col"),
        P("col", "row"),
        P("row", "col"),
        P("row", "col"),
        P("col", "row"),
        P("col"),
        P("col"),
        P(),
        P(),
        P(("dp", "row"), None),
    )
    out_specs = (
        P(("dp", "row"), None),
        P(("dp", "row"), None),
        P("row", "col"),
        P("row", "col"),
        P("row", "col"),
        P("col", "row"),
        P("row", "col"),
        P("row", "col"),
        P("col", "row"),
        P("col"),
        P("col"),
        P(),
        P(),
    )
    sizes = (mesh.shape["dp"], mesh.shape["row"], mesh.shape["col"])
    return jax.shard_map(
        functools.partial(layer, sizes), mesh=mesh, in_specs=in_specs, out_specs=out_specs, check_vma=False
    )
```

```python
import functools

import jax
import jax.numpy as jnp
from jax import lax
from jax.experimental import pallas as pl
from jax.experimental.pallas import tpu as pltpu
from jax.sharding import PartitionSpec as P


HD = 128
LEN = 1024
BQ = 256
VMEM = 60 << 20

EPS = 1e-06
THETA = 500000.0
NEG_FILL = -1e30
SCORE_SCALE = HD ** (-0.5)
F32 = jnp.float32
BF16 = jnp.bfloat16


def plain_dot(left_mat, right_mat):
    return jnp.dot(left_mat, right_mat, preferred_element_type=F32)


def times_transposed(left_mat, right_mat):
    return lax.dot_general(
        left_mat, right_mat, (((1,), (1,)), ((), ())), preferred_element_type=F32
    )


def left_transposed(left_mat, right_mat):
    return lax.dot_general(
        left_mat, right_mat, (((0,), (0,)), ((), ())), preferred_element_type=F32
    )


def rope_tables(positions):
    half_dim = HD // 2
    inv_freq = THETA ** (-(jnp.arange(half_dim, dtype=F32) * 2.0) / HD)
    angles = positions.astype(F32)[:, None] * inv_freq[None, :]
    cos_half, sin_half = jnp.cos(angles), jnp.sin(angles)
    cosine = jnp.concatenate([cos_half, cos_half], axis=-1)
    sine_signed = jnp.concatenate([-sin_half, sin_half], axis=-1)
    return cosine, sine_signed


def fill_mask(bias_ref, seg_col_ref, seg_row_ref):
    @pl.when(pl.program_id(0) == 0)
    def _():
        for first in range(0, LEN, BQ):
            keys = first + BQ
            rows = seg_col_ref[first:keys, :]
            cols = seg_row_ref[:, :keys]
            query_index = first + lax.broadcasted_iota(jnp.int32, (BQ, keys), 0)
            key_index = lax.broadcasted_iota(jnp.int32, (BQ, keys), 1)
            allowed = (rows == cols) & (key_index <= query_index)
            bias_ref[first:keys, :keys] = jnp.where(allowed, 0.0, NEG_FILL)


def attend_forward_kernel(
    q_ref, k_ref, v_ref, qs_ref, ks_ref, qg_ref, kg_ref, cos_ref, sin_ref, segc_ref, segr_ref,
    qrot_ref, krot_ref, vb_ref, att_ref, log_ref, bias_ref,
):
    fill_mask(bias_ref, segc_ref, segr_ref)
    cosine, sine = cos_ref[...], sin_ref[...]

    def turned(raw, scale, gain):
        norm = raw * scale * gain
        return (norm * cosine + pltpu.roll(norm, HD // 2, 1) * sine).astype(BF16)

    qrot_ref[...] = turned(q_ref[...], qs_ref[...], qg_ref[...])
    krot_ref[...] = turned(k_ref[...], ks_ref[...], kg_ref[...])
    vb_ref[...] = v_ref[...].astype(BF16)
    for first in range(0, LEN, BQ):
        keys = first + BQ
        scores = times_transposed(qrot_ref[first:keys, :], krot_ref[:keys, :]) * SCORE_SCALE
        masked = scores + bias_ref[first:keys, :keys]
        peak = jnp.max(masked, axis=1, keepdims=True)
        weight = jnp.exp(masked - peak)
        total = jnp.sum(weight, axis=1, keepdims=True)
        probs = (weight * (1.0 / total)).astype(BF16)
        att_ref[first:keys, :] = plain_dot(probs, vb_ref[:keys, :]).astype(BF16)
        log_ref[0, first:keys, :] = peak + jnp.log(total)


def attend_backward_kernel(
    q_ref, k_ref, qs_ref, ks_ref, qg_ref, kg_ref, cos_ref, sin_ref, segc_ref, segr_ref,
    qrot_ref, krot_ref, vb_ref, att_ref, log_ref, grad_ref,
    dzq_ref, dzk_ref, gv_ref, dotq_ref, dotk_ref, gainq_ref, gaink_ref,
    dq_acc, dk_acc, dv_acc, bias_ref,
):
    fill_mask(bias_ref, segc_ref, segr_ref)
    dk_acc[...] = jnp.zeros_like(dk_acc)
    dv_acc[...] = jnp.zeros_like(dv_acc)
    for first in range(0, LEN, BQ):
        keys = first + BQ
        queries = qrot_ref[first:keys, :]
        grads = grad_ref[first:keys, :]
        scores = times_transposed(queries, krot_ref[:keys, :]) * SCORE_SCALE
        probs = jnp.exp(scores + bias_ref[first:keys, :keys] - log_ref[0, first:keys, :])
        delta = jnp.sum(
            grads.astype(F32) * att_ref[first:keys, :].astype(F32), axis=1, keepdims=True
        )
        grad_probs = times_transposed(grads, vb_ref[:keys, :])
        grad_scores = (probs * (grad_probs - delta) * SCORE_SCALE).astype(BF16)
        dq_acc[first:keys, :] = plain_dot(grad_scores, krot_ref[:keys, :])
        dk_acc[:keys, :] += left_transposed(grad_scores, queries)
        dv_acc[:keys, :] += left_transposed(probs.astype(BF16), grads)
    gv_ref[...] = dv_acc[...].astype(BF16)
    cosine, sine = cos_ref[...], sin_ref[...]

    def finish(acc, raw_ref, scale_ref, gain_ref, dz_ref, dot_ref, gain_grad_ref):
        grad_rot = acc[...]
        grad_norm = grad_rot * cosine - pltpu.roll(grad_rot, HD // 2, 1) * sine
        unit = raw_ref[...] * scale_ref[...]
        gain_grad_ref[...] = jnp.sum(grad_norm * unit, axis=0, keepdims=True)
        grad_unit = grad_norm * gain_ref[...]
        dz_ref[...] = grad_unit
        part = jnp.sum(grad_unit * unit, axis=1, keepdims=True)

        @pl.when(pl.program_id(0) == 0)
        def _():
            dot_ref[...] = part

        @pl.when(pl.program_id(0) > 0)
        def _():
            dot_ref[...] += part

    finish(dq_acc, q_ref, qs_ref, qg_ref, dzq_ref, dotq_ref, gainq_ref)
    finish(dk_acc, k_ref, ks_ref, kg_ref, dzk_ref, dotk_ref, gaink_ref)


def head_spec(offset):
    return pl.BlockSpec((LEN, HD), lambda h: (0, offset + h))


def whole_spec(shape):
    return pl.BlockSpec(shape, lambda h: (0,) * len(shape))


def gain_spec():
    return pl.BlockSpec((1, HD), lambda h: (0, h))


LOG_SPEC = pl.BlockSpec((1, LEN, 1), lambda h: (h, 0, 0))
COLUMN = (LEN, 1)
TABLE = (LEN, HD)


def attend_forward(qkv, scales, gains, tables, seg_col, seg_row, heads):
    width = heads * HD
    piece = jax.ShapeDtypeStruct((LEN, width), BF16)
    return pl.pallas_call(
        attend_forward_kernel,
        grid=(heads,),
        in_specs=[
            head_spec(0), head_spec(heads), head_spec(2 * heads),
            whole_spec(COLUMN), whole_spec(COLUMN), gain_spec(), gain_spec(),
            whole_spec(TABLE), whole_spec(TABLE), whole_spec(COLUMN), whole_spec((1, LEN)),
        ],
        out_specs=[head_spec(0)] * 4 + [LOG_SPEC],
        out_shape=[piece] * 4 + [jax.ShapeDtypeStruct((heads, LEN, 1), F32)],
        scratch_shapes=[pltpu.VMEM((LEN, LEN), F32)],
        compiler_params=pltpu.CompilerParams(vmem_limit_bytes=VMEM),
        cost_estimate=pl.CostEstimate(
            flops=heads * 4 * LEN * LEN * HD, bytes_accessed=LEN * width * 20, transcendentals=0
        ),
        name="attend_forward",
    )(qkv, qkv, qkv, *scales, *gains, *tables, seg_col, seg_row)


def attend_backward(qkv, scales, gains, tables, seg_col, seg_row, saved, grad_att, heads):
    width = heads * HD
    full = jax.ShapeDtypeStruct((LEN, width), F32)
    column = jax.ShapeDtypeStruct(COLUMN, F32)
    gain_row = jax.ShapeDtypeStruct((1, width), F32)
    return pl.pallas_call(
        attend_backward_kernel,
        grid=(heads,),
        in_specs=[
            head_spec(0), head_spec(heads),
            whole_spec(COLUMN), whole_spec(COLUMN), gain_spec(), gain_spec(),
            whole_spec(TABLE), whole_spec(TABLE), whole_spec(COLUMN), whole_spec((1, LEN)),
            head_spec(0), head_spec(0), head_spec(0), head_spec(0), LOG_SPEC, head_spec(0),
        ],
        out_specs=[
            head_spec(0), head_spec(0), head_spec(0),
            whole_spec(COLUMN), whole_spec(COLUMN), gain_spec(), gain_spec(),
        ],
        out_shape=[
            full, full, jax.ShapeDtypeStruct((LEN, width), BF16), column, column, gain_row, gain_row,
        ],
        scratch_shapes=[pltpu.VMEM((LEN, HD), F32)] * 3 + [pltpu.VMEM((LEN, LEN), F32)],
        compiler_params=pltpu.CompilerParams(vmem_limit_bytes=VMEM),
        cost_estimate=pl.CostEstimate(
            flops=heads * 10 * LEN * LEN * HD, bytes_accessed=LEN * width * 40, transcendentals=0
        ),
        name="attend_backward",
    )(qkv, qkv, *scales, *gains, *tables, seg_col, seg_row, *saved, grad_att)


def half_tile(step, core, tiles):
    per_half = tiles // 2
    return ((core + step // per_half) % 2) * per_half + step % per_half


def forward_chunk_kernel(
    idx_ref, *refs, blocks, tiles,
):
    own_ref, left1, left2, left3, right1, right2, right3 = refs[:7]
    wo_own_ref, wo_oth_ref, x_ref, gain_ref, wg_ref, wu_ref, wd_own_ref, wd_oth_ref = refs[7:15]
    raw_ref, scale_ref, hb_ref, gate_ref, up_ref, mixed_ref, part_ref, acc_ref, att_ref = refs[-9:]
    block = wo_own_ref.shape[2]
    depth = wo_own_ref.shape[1]
    step = pl.program_id(0)
    core = idx_ref[1]

    @pl.when(step == 0)
    def _():
        quarter = own_ref.shape[1] // 2
        pieces = (
            own_ref[...], right1[...] + left3[...], right2[...] + left2[...], right3[...] + left1[...],
        )
        for half in range(2):
            for number, piece in enumerate(pieces):
                start = half * depth + number * quarter
                att_ref[:, start : start + quarter] = piece[:, half * quarter : (half + 1) * quarter]

    @pl.when(step < blocks)
    def _():
        own = att_ref[:, pl.ds(pl.multiple_of(core * depth, depth), depth)]
        other = att_ref[:, pl.ds(pl.multiple_of((1 - core) * depth, depth), depth)]
        raw_ref[:, pl.ds(pl.multiple_of(step * block, block), block)] = plain_dot(
            own, wo_own_ref[0]
        ) + plain_dot(other, wo_oth_ref[0])

    @pl.when(step == blocks - 1)
    def _():
        raw = raw_ref[...]
        scale = lax.rsqrt(jnp.mean(raw * raw, axis=1, keepdims=True) + EPS)
        scale_ref[...] = scale
        hb_ref[...] = (x_ref[...].astype(F32) + raw * scale * gain_ref[...]).astype(BF16)
        acc_ref[...] = jnp.zeros_like(acc_ref)

    def tile_work(wd_ref):
        hidden_b = hb_ref[...]
        gate = plain_dot(hidden_b, wg_ref[...])
        up = plain_dot(hidden_b, wu_ref[...])
        mixed = (gate * jax.nn.sigmoid(gate) * up).astype(BF16)
        gate_ref[...] = gate.astype(BF16)
        up_ref[...] = up.astype(BF16)
        mixed_ref[...] = mixed
        for j in range(blocks):
            acc_ref[:, j * block : (j + 1) * block] += plain_dot(mixed, wd_ref[j])

    @pl.when((step >= blocks) & (step < blocks + tiles // 2))
    def _():
        tile_work(wd_own_ref)

    @pl.when(step >= blocks + tiles // 2)
    def _():
        tile_work(wd_oth_ref)

    @pl.when(step == blocks + tiles - 1)
    def _():
        part_ref[...] = acc_ref[...].astype(BF16)


TILE = 512


def forward_chunk(index, attended, out_halves, block_input, gain, w_gate, w_up, down_halves, chunk, before):
    tokens, width = block_input.shape
    hidden = w_gate.shape[1]
    blocks, depth, block = out_halves[0].shape
    tiles = hidden // TILE

    def tile_of(j, idx):
        return half_tile(jnp.maximum(j - blocks, 0), idx[1], tiles)

    rows = pl.BlockSpec((chunk, width), lambda j, idx: (idx[0], 0))
    out_half = pl.BlockSpec((1, depth, block), lambda j, idx: (jnp.minimum(j, blocks - 1), 0, 0))
    up_tile = pl.BlockSpec((width, TILE), lambda j, idx: (0, tile_of(j, idx)))
    down_own = pl.BlockSpec(
        (blocks, TILE, block), lambda j, idx: (0, jnp.clip(j - blocks, 0, tiles // 2 - 1), 0)
    )
    down_oth = pl.BlockSpec(
        (blocks, TILE, block), lambda j, idx: (0, jnp.maximum(j - blocks - tiles // 2, 0), 0)
    )
    act_tile = pl.BlockSpec((chunk, TILE), lambda j, idx: (idx[0], tile_of(j, idx)))
    before = tuple(before)
    return pl.pallas_call(
        functools.partial(forward_chunk_kernel, blocks=blocks, tiles=tiles),
        grid_spec=pltpu.PrefetchScalarGridSpec(
            num_scalar_prefetch=1,
            grid=(blocks + tiles,),
            in_specs=[
                *[pl.BlockSpec((chunk, attended[0].shape[1]), lambda j, idx: (idx[0], 0))] * 7,
                out_half, out_half, rows, pl.BlockSpec((1, width), lambda j, idx: (0, 0)),
                up_tile, up_tile, down_own, down_oth,
            ] + [pl.BlockSpec(memory_space=pl.ANY)] * len(before),
            out_specs=[
                rows, pl.BlockSpec((chunk, 1), lambda j, idx: (idx[0], 0)), rows, act_tile, act_tile, act_tile,
                pl.BlockSpec((chunk, width), lambda j, idx: (0, 0)),
            ],
            scratch_shapes=[pltpu.VMEM((chunk, width), F32), pltpu.VMEM((chunk, 2 * depth), BF16)],
        ),
        out_shape=[
            jax.ShapeDtypeStruct((tokens, width), F32),
            jax.ShapeDtypeStruct((tokens, 1), F32),
            jax.ShapeDtypeStruct((tokens, width), BF16),
            jax.ShapeDtypeStruct((tokens, hidden), BF16),
            jax.ShapeDtypeStruct((tokens, hidden), BF16),
            jax.ShapeDtypeStruct((tokens, hidden), BF16),
            jax.ShapeDtypeStruct((chunk, width), BF16),
        ],
        input_output_aliases={16 + i: i for i in range(len(before))},
        compiler_params=pltpu.CompilerParams(vmem_limit_bytes=VMEM),
        cost_estimate=pl.CostEstimate(
            flops=2 * chunk * width * (width + 3 * hidden),
            bytes_accessed=2 * width * (width + 3 * hidden),
            transcendentals=0,
        ),
        name="forward_chunk",
    )(index, *attended, *out_halves, block_input, gain, w_gate, w_up, *down_halves, *before)


def backward_chunk_kernel(
    idx_ref, down_ref, raw_ref, scale_ref, x_ref, grad_ref, attn_gain_ref, mlp_gain_ref,
    gate_ref, up_ref, wg_ref, wu_ref, wd_own_ref, wd_oth_ref, *refs, blocks, tiles,
):
    out_ref, gdi_ref, gg_ref, gu_ref, part_ref, gain_grad_ref, acc_ref = refs[-7:]
    block = wd_own_ref.shape[2]
    step = pl.program_id(0)

    @pl.when(step == 0)
    def _():
        down_raw = down_ref[...].astype(F32)
        down_scale = lax.rsqrt(jnp.mean(down_raw * down_raw, axis=1, keepdims=True) + EPS)
        unit = down_raw * down_scale
        mlp_gain = mlp_gain_ref[...]
        hidden = x_ref[...].astype(F32) + raw_ref[...] * scale_ref[...] * attn_gain_ref[...]
        out_ref[...] = (hidden + unit * mlp_gain).astype(BF16)
        grad_y = grad_ref[...].astype(F32)
        gain_grad_ref[...] = jnp.sum(grad_y * unit, axis=0, keepdims=True)
        grad_unit = grad_y * mlp_gain
        mean = jnp.mean(grad_unit * unit, axis=1, keepdims=True)
        gdi_ref[...] = (down_scale * (grad_unit - unit * mean)).astype(BF16)
        acc_ref[...] = jnp.zeros_like(acc_ref)

    def tile_work(wd_ref):
        grad_mixed = times_transposed(gdi_ref[:, :block], wd_ref[0])
        for j in range(1, blocks):
            grad_mixed += times_transposed(gdi_ref[:, j * block : (j + 1) * block], wd_ref[j])
        gate = gate_ref[...].astype(F32)
        sig = jax.nn.sigmoid(gate)
        grad_gate = (grad_mixed * up_ref[...].astype(F32) * sig * (1.0 + gate * (1.0 - sig))).astype(BF16)
        grad_up = (grad_mixed * (gate * sig)).astype(BF16)
        gg_ref[...] = grad_gate
        gu_ref[...] = grad_up
        acc_ref[...] += times_transposed(grad_gate, wg_ref[...]) + times_transposed(grad_up, wu_ref[...])

    @pl.when(step < tiles // 2)
    def _():
        tile_work(wd_own_ref)

    @pl.when(step >= tiles // 2)
    def _():
        tile_work(wd_oth_ref)

    @pl.when(step == tiles - 1)
    def _():
        part_ref[...] = acc_ref[...].astype(BF16)


def backward_chunk(
    index, down_rows, raw, scale, block_input, grad_output, attn_gain, mlp_gain, gate, up, w_gate, w_up,
    down_halves, chunk, before,
):
    tokens, width = block_input.shape
    hidden = w_gate.shape[1]
    blocks, _, block = down_halves[0].shape
    tiles = hidden // TILE

    def tile_of(j, idx):
        return half_tile(j, idx[1], tiles)

    rows = pl.BlockSpec((chunk, width), lambda j, idx: (idx[0], 0))
    fixed = pl.BlockSpec((chunk, width), lambda j, idx: (0, 0))
    gain_row = pl.BlockSpec((1, width), lambda j, idx: (0, 0))
    up_tile = pl.BlockSpec((width, TILE), lambda j, idx: (0, tile_of(j, idx)))
    act_tile = pl.BlockSpec((chunk, TILE), lambda j, idx: (idx[0], tile_of(j, idx)))
    before = tuple(before)
    return pl.pallas_call(
        functools.partial(backward_chunk_kernel, blocks=blocks, tiles=tiles),
        grid_spec=pltpu.PrefetchScalarGridSpec(
            num_scalar_prefetch=1,
            grid=(tiles,),
            in_specs=[
                fixed, rows, pl.BlockSpec((chunk, 1), lambda j, idx: (idx[0], 0)), rows, rows, gain_row, gain_row,
                act_tile, act_tile, up_tile, up_tile,
                pl.BlockSpec((blocks, TILE, block), lambda j, idx: (0, jnp.minimum(j, tiles // 2 - 1), 0)),
                pl.BlockSpec((blocks, TILE, block), lambda j, idx: (0, jnp.maximum(j - tiles // 2, 0), 0)),
            ] + [pl.BlockSpec(memory_space=pl.ANY)] * len(before),
            out_specs=[rows, rows, act_tile, act_tile, fixed, gain_row],
            scratch_shapes=[pltpu.VMEM((chunk, width), F32)],
        ),
        out_shape=[
            jax.ShapeDtypeStruct((tokens, width), BF16),
            jax.ShapeDtypeStruct((tokens, width), BF16),
            jax.ShapeDtypeStruct((tokens, hidden), BF16),
            jax.ShapeDtypeStruct((tokens, hidden), BF16),
            jax.ShapeDtypeStruct((chunk, width), BF16),
            jax.ShapeDtypeStruct((1, width), F32),
        ],
        input_output_aliases={14 + i: i for i in range(len(before))},
        compiler_params=pltpu.CompilerParams(vmem_limit_bytes=VMEM),
        cost_estimate=pl.CostEstimate(
            flops=6 * chunk * width * hidden, bytes_accessed=6 * width * hidden, transcendentals=0
        ),
        name="backward_chunk",
    )(
        index, down_rows, raw, scale, block_input, grad_output, attn_gain, mlp_gain, gate, up, w_gate, w_up,
        *down_halves, *before,
    )


def attention_chunk_kernel(
    idx_ref, mlp_ref, grad_ref, raw_ref, scale_ref, gain_ref, wo_own_ref, wo_oth_ref, *refs, blocks,
):
    gai_ref, gatt_ref, gain_grad_ref = refs[-3:]
    half, block = wo_own_ref.shape[1:]
    core = idx_ref[1]
    scale = scale_ref[...]
    unit = raw_ref[...] * scale
    grad_hidden = grad_ref[...].astype(F32) + mlp_ref[...].astype(F32)
    gain_grad_ref[...] = jnp.sum(grad_hidden * unit, axis=0, keepdims=True)
    grad_unit = grad_hidden * gain_ref[...]
    mean = jnp.mean(grad_unit * unit, axis=1, keepdims=True)
    gai_ref[...] = (scale * (grad_unit - unit * mean)).astype(BF16)
    for place, w_ref in ((core, wo_own_ref), (1 - core, wo_oth_ref)):
        total = times_transposed(gai_ref[:, :block], w_ref[0])
        for j in range(1, blocks):
            total += times_transposed(gai_ref[:, j * block : (j + 1) * block], w_ref[j])
        gatt_ref[:, pl.ds(pl.multiple_of(place * half, half), half)] = total.astype(BF16)


def attention_chunk(index, mlp_rows, grad_output, raw, scale, gain, out_halves, half, chunk, before):
    tokens, width = grad_output.shape
    blocks, _, block = out_halves[0].shape
    rows = pl.BlockSpec((chunk, width), lambda j, idx: (idx[0], 0))
    fixed = pl.BlockSpec((chunk, width), lambda j, idx: (0, 0))
    gain_row = pl.BlockSpec((1, width), lambda j, idx: (0, 0))
    own_heads = pl.BlockSpec((blocks, half, block), lambda j, idx: (0, 0, 0))
    before = tuple(before)
    return pl.pallas_call(
        functools.partial(attention_chunk_kernel, blocks=blocks),
        grid_spec=pltpu.PrefetchScalarGridSpec(
            num_scalar_prefetch=1,
            grid=(1,),
            in_specs=[
                fixed, rows, rows, pl.BlockSpec((chunk, 1), lambda j, idx: (idx[0], 0)), gain_row,
                own_heads, own_heads,
            ] + [pl.BlockSpec(memory_space=pl.ANY)] * len(before),
            out_specs=[rows, pl.BlockSpec((chunk, 2 * half), lambda j, idx: (idx[0], 0)), gain_row],
        ),
        out_shape=[
            jax.ShapeDtypeStruct((tokens, width), BF16),
            jax.ShapeDtypeStruct((tokens, 2 * half), BF16),
            jax.ShapeDtypeStruct((1, width), F32),
        ],
        input_output_aliases={8 + i: i for i in range(len(before))},
        compiler_params=pltpu.CompilerParams(vmem_limit_bytes=VMEM),
        cost_estimate=pl.CostEstimate(
            flops=4 * chunk * width * half, bytes_accessed=16 * chunk * width, transcendentals=0
        ),
        name="attention_chunk",
    )(index, mlp_rows, grad_output, raw, scale, gain, *out_halves, *before)


def place_rows_kernel(idx_ref, rows_ref, *refs):
    refs[-1][...] = rows_ref[...].astype(refs[-1].dtype)


def place_rows(index, rows_in, tokens, dtype, before):
    chunk, width = rows_in.shape
    before = tuple(before)
    return pl.pallas_call(
        place_rows_kernel,
        grid_spec=pltpu.PrefetchScalarGridSpec(
            num_scalar_prefetch=1,
            grid=(2,),
            in_specs=[pl.BlockSpec((chunk // 2, width), lambda j, idx: (j, 0))]
            + [pl.BlockSpec(memory_space=pl.ANY)] * len(before),
            out_specs=pl.BlockSpec((chunk // 2, width), lambda j, idx: (2 * idx[0] + j, 0)),
        ),
        out_shape=jax.ShapeDtypeStruct((tokens, width), dtype),
        input_output_aliases={2: 0} if before else {},
        compiler_params=pltpu.CompilerParams(vmem_limit_bytes=VMEM),
        cost_estimate=pl.CostEstimate(flops=0, bytes_accessed=6 * chunk * width, transcendentals=0),
        name="place_rows",
    )(index, rows_in, *before)


def after(value, *tokens):
    return lax.optimization_barrier((value, tokens))[0]


def unset_kernel(out_ref):
    pass


def unset(shape, dtype):
    return pl.pallas_call(
        unset_kernel,
        out_specs=pl.BlockSpec(memory_space=pl.ANY),
        out_shape=jax.ShapeDtypeStruct(shape, dtype),
        name="unset",
    )()


def shards(
    sizes,
    block_input,
    segment_ids,
    positions,
    w_query,
    w_key,
    w_value,
    w_out,
    w_gate,
    w_up,
    w_down,
    query_gain,
    key_gain,
    attn_gain,
    mlp_gain,
    grad_output,
):
    cores, rows, cols = sizes
    tokens_here, width = block_input.shape
    assert tokens_here == LEN and cores == 2 and cols == 4
    local_width = w_query.shape[1]
    half_width = local_width // 2
    heads = local_width // HD
    chunk = tokens_here // cols
    core = lax.axis_index("dp")
    row = lax.axis_index("row")
    col = lax.axis_index("col")
    swap = [(0, 1), (1, 0)]
    attn_row, mlp_row = attn_gain[None, :], mlp_gain[None, :]

    def own_half(array, axis):
        half = array.shape[axis] // 2
        return lax.dynamic_slice_in_dim(array, core * half, half, axis)

    def other_half(array, axis):
        half = array.shape[axis] // 2
        return lax.dynamic_slice_in_dim(array, (1 - core) * half, half, axis)

    def gather(weight, axis):
        return lax.all_gather(own_half(weight, axis), ("row", "dp"), axis=axis, tiled=True)

    def line_step(from_left, from_right, step):
        from_left = lax.ppermute(from_left, "col", [(i, i + 1) for i in range(step - 1, cols - 1)])
        from_right = lax.ppermute(from_right, "col", [(i + 1, i) for i in range(cols - step)])
        return from_left, from_right

    def sum_step(up, down, step):
        up = lax.ppermute(up, "col", [(i, i + 1) for i in range(step)])
        down = lax.ppermute(down, "col", [(cols - 1 - i, cols - 2 - i) for i in range(step)])
        return up, down

    def pick(at_zero, at_one, at_two, at_three):
        low = jnp.where(col == 0, at_zero, at_one)
        high = jnp.where(col == 2, at_two, at_three)
        return jnp.where(col < 2, low, high)

    slot_chunk = [pick(3, 3, 0, 0), pick(2, 2, 1, 1), pick(1, 0, 3, 2), col]
    slot_index = [jnp.stack([one, core]).astype(jnp.int32) for one in slot_chunk]

    def slot_rows(array, slot):
        return lax.dynamic_slice_in_dim(array, slot_chunk[slot] * chunk, chunk, 0)

    def gather_slots(own, work):
        left, right, token = [own], [own], ()
        arrived = (
            lambda lefts, rights: lefts[0],
            lambda lefts, rights: jnp.where(col % 2 == 0, rights[1], lefts[1]),
            lambda lefts, rights: pick(rights[2], rights[1], lefts[1], lefts[2]),
            lambda lefts, rights: pick(rights[3], rights[2], lefts[2], lefts[3]),
        )
        for step in range(1, cols + 1):
            seen = tuple(left), tuple(right)
            if step < cols:
                from_left, from_right = line_step(left[-1], right[-1], step)
                left.append(from_left)
                right.append(from_right)
            token = work(cols - step, arrived[step - 1](*after(seen, token)))

    def sum_slots(make, window=lambda step, gate: ()):
        def at(step, gate):
            window(step, gate)
            return make(step, gate)

        first = make(0, ())
        up, down = sum_step(first, first, 1)
        second = at(1, first)
        up = jnp.where(col == 0, second, first) + up
        down = jnp.where(col == 3, second, first) + down
        gate = (up, down)
        up, down = sum_step(up, down, 2)
        third = at(2, gate)
        up = jnp.where(col == 1, second, third) + up
        down = jnp.where(col == 2, second, third) + down
        gate = (up, down)
        up, down = sum_step(up, down, 3)
        fourth = at(3, gate)
        return fourth.astype(F32) + up.astype(F32) + down.astype(F32)

    def both_cores(half, axis):
        other = lax.ppermute(half, "dp", swap)
        first = jnp.where(core == 0, half, other)
        second = jnp.where(core == 0, other, half)
        return jnp.concatenate([first, second], axis=axis).astype(F32)

    def sum_sent(left_mat, right_other):
        return lax.ppermute(left_transposed(left_mat, right_other).astype(BF16), "dp", swap)

    def sum_kept(left_mat, right_own, got):
        total = (left_transposed(left_mat, right_own) + got.astype(F32)).astype(BF16)
        return total, lax.psum_scatter(total, "row", scatter_dimension=0, tiled=True)

    by_x = [(0, 1), (1, 0), (2, 3), (3, 2)]
    by_y = [(0, 2), (2, 0), (1, 3), (3, 1)]

    def row_first(half):
        if rows != 4:
            return (half,)
        return half, lax.ppermute(half, "row", by_x), lax.ppermute(half, "row", by_y)

    def row_second(pieces):
        if rows != 4:
            return pieces
        middle = pieces[0].shape[0] // 2
        return (
            *pieces,
            lax.ppermute(pieces[1][:middle], "row", by_y),
            lax.ppermute(pieces[2][middle:], "row", by_x),
        )

    def row_blocks(pieces):
        if rows != 4:
            whole = lax.all_gather(pieces[0], ("row", "dp"), axis=0, tiled=False)
            whole = whole.reshape(rows, cores, *pieces[0].shape)
            return tuple(lax.dynamic_index_in_dim(whole, one, 1, keepdims=False) for one in (core, 1 - core))
        own, by_one, by_two, corner_top, corner_low = pieces
        middle = own.shape[0] // 2
        held = unset((rows, *own.shape), own.dtype)
        for piece, block, start in (
            (own, row, 0), (by_one, row ^ 1, 0), (by_two, row ^ 2, 0),
            (corner_top, row ^ 3, 0), (corner_low, row ^ 3, middle),
        ):
            held = lax.dynamic_update_slice(held, piece[None], (block, start, 0))
        return held, lax.ppermute(held, "dp", swap)

    full_qkv = gather(jnp.concatenate([w_query, w_key, w_value], axis=1), 0)
    full_gate = gather(w_gate, 0)
    full_up = gather(w_up, 0)
    out_half = own_half(w_out, 0)
    out_stack = jnp.concatenate(
        [out_half]
        + [
            lax.ppermute(out_half, "col", [(i, (i - step) % cols) for i in range(cols)])
            for step in range(1, cols)
        ],
        axis=0,
    )
    down_start, out_start = after((own_half(w_down, 0), out_stack), full_qkv)
    down_pieces = row_first(down_start)
    out_pieces = row_first(out_start)

    qkv = plain_dot(block_input, full_qkv)
    query_raw, key_raw = qkv[:, :local_width], qkv[:, local_width : 2 * local_width]
    query_sq, key_sq = lax.psum(
        (jnp.sum(query_raw * query_raw, axis=1), jnp.sum(key_raw * key_raw, axis=1)), "col"
    )
    query_scale = lax.rsqrt(query_sq / width + EPS)[:, None]
    key_scale = lax.rsqrt(key_sq / width + EPS)[:, None]
    scales = (query_scale, key_scale)
    gains = (query_gain[None, :], key_gain[None, :])
    tables = rope_tables(positions)
    seg_col, seg_row = segment_ids[:, None], segment_ids[None, :]
    query_rot, key_rot, value_heads, attended, log_total = attend_forward(
        qkv, scales, gains, tables, seg_col, seg_row, heads
    )

    lefts, rights = [attended], [attended]
    for step in range(1, cols):
        from_left, from_right = line_step(lefts[-1], rights[-1], step)
        lefts.append(from_left)
        rights.append(from_right)
        if step == 1:
            down_pieces = row_second(after(down_pieces, attended))
            out_pieces = row_second(after(out_pieces, attended))
            out_halves = row_blocks(out_pieces)
        if step == 2:
            down_halves = row_blocks(down_pieces)
    attended_all = (attended, *lefts[1:], *rights[1:])

    held = dict(forward=(), backward=(), attention=(), output=())
    gain_sums = dict(mlp=0.0, attn=0.0)

    def forward_work(slot, gate):
        results = forward_chunk(
            slot_index[slot], after(attended_all, gate), out_halves, block_input, attn_row, full_gate, full_up,
            down_halves, chunk, held["forward"],
        )
        held["forward"] = results[:6]
        return results[6]

    down_own = sum_slots(forward_work).astype(BF16)
    attn_raw, attn_scale, hidden_b, gate_proj, up_proj, mixed_act = held["forward"]
    mlp_parts = [None] * cols

    def backward_work(slot, down_rows):
        results = backward_chunk(
            slot_index[slot], down_rows, attn_raw, attn_scale, block_input, grad_output, attn_row, mlp_row,
            gate_proj, up_proj, full_gate, full_up, down_halves, chunk, held["backward"],
        )
        held["backward"] = results[:4]
        mlp_parts[slot] = results[4]
        gain_sums["mlp"] = gain_sums["mlp"] + results[5]
        return results[4]

    gather_slots(down_own, backward_work)
    block_output, grad_down_in, grad_gate_in, grad_up_in = held["backward"]

    blocks = {}
    got = {}

    def mlp_window(step, gate):
        down_left, down_right, hidden_left, gate_right, up_right = after(
            (grad_down_in, mixed_act, hidden_b, grad_gate_in, grad_up_in), gate
        )
        if step == 1:
            got["down"] = sum_sent(down_left, other_half(down_right, 1))
            got["gate"] = sum_sent(hidden_left, other_half(gate_right, 1))
            return got["down"], got["gate"]
        if step == 2:
            blocks["down"] = sum_kept(down_left, own_half(down_right, 1), got["down"])
            got["up"] = sum_sent(hidden_left, other_half(up_right, 1))
            return blocks["down"][0], got["up"]
        blocks["gate"] = sum_kept(hidden_left, own_half(gate_right, 1), got["gate"])
        return blocks["gate"][0]

    mlp_own = sum_slots(lambda slot, gate: mlp_parts[slot], mlp_window).astype(BF16)

    def attention_work(slot, mlp_rows):
        results = attention_chunk(
            slot_index[slot], mlp_rows, grad_output, attn_raw, attn_scale, attn_row, out_halves, half_width,
            chunk, held["attention"],
        )
        held["attention"] = results[:2]
        gain_sums["attn"] = gain_sums["attn"] + results[2]
        if slot == 3:
            hidden_left, up_right = after((hidden_b, grad_up_in), mlp_rows)
            blocks["up"] = sum_kept(hidden_left, own_half(up_right, 1), got["up"])
        return results[1]

    gather_slots(mlp_own, attention_work)
    grad_attn_in, grad_att = held["attention"]
    own_grad_hidden = slot_rows(grad_output, 3).astype(F32) + mlp_own.astype(F32)

    query_dz, key_dz, grad_value_in, query_dot, key_dot, grad_query_gain, grad_key_gain = attend_backward(
        qkv, scales, gains, tables, seg_col, seg_row,
        (query_rot, key_rot, value_heads, attended, log_total), grad_att, heads,
    )
    query_dot, key_dot = lax.psum((query_dot[:, 0], key_dot[:, 0]), "col")
    grad_query_in = (
        query_scale * (query_dz - query_raw * query_scale * (query_dot / width)[:, None])
    ).astype(BF16)
    grad_key_in = (
        key_scale * (key_dz - key_raw * key_scale * (key_dot / width)[:, None])
    ).astype(BF16)
    grad_qkv = jnp.concatenate([grad_query_in, grad_key_in, grad_value_in], axis=1)
    gain_pack = jnp.concatenate([grad_query_gain, grad_key_gain, gain_sums["attn"], gain_sums["mlp"]], axis=1)

    def interleaved(picker, pieces_in):
        return jnp.concatenate([picker(one, 1) for one in pieces_in], axis=1)

    def input_window(step, gate):
        nonlocal gain_pack
        pack, *pieces_in, tokens_in, left_out, right_out = after(
            (gain_pack, grad_query_in, grad_key_in, grad_value_in, block_input, grad_attn_in, attended), gate
        )
        if step == 1:
            got["qkv"] = sum_sent(tokens_in, interleaved(other_half, pieces_in))
            got["out"] = sum_sent(left_out, other_half(right_out, 1))
            gain_pack = pack + lax.ppermute(pack, "dp", swap)
            return got["qkv"], got["out"], gain_pack
        if step == 2:
            blocks["qkv"] = sum_kept(tokens_in, interleaved(own_half, pieces_in), got["qkv"])
            if rows == 4:
                gain_pack = pack + lax.ppermute(pack, "row", by_x)
            return blocks["qkv"][0], gain_pack
        blocks["out"] = sum_kept(left_out, own_half(right_out, 1), got["out"])
        gain_pack = pack + lax.ppermute(pack, "row", by_y) if rows == 4 else lax.psum(pack, "row")
        return blocks["out"][0], gain_pack

    input_own = sum_slots(
        lambda slot, gate: times_transposed(after(slot_rows(grad_qkv, slot), gate), full_qkv).astype(BF16), input_window
    )

    results = {}
    quarter = local_width // 2

    def projection(index):
        pair = both_cores(blocks["qkv"][1][None, :, index * quarter : (index + 1) * quarter], 0)
        return jnp.concatenate([pair[0], pair[1]], axis=1)

    def output_work(slot, rows_in):
        held["output"] = (place_rows(slot_index[slot], rows_in, tokens_here, F32, held["output"]),)
        if slot == 3:
            results["down"] = jnp.transpose(both_cores(blocks["down"][1], 1))
            results["gate"] = both_cores(blocks["gate"][1], 1)
            return held["output"], results["down"], results["gate"]
        if slot == 2:
            results["up"] = both_cores(blocks["up"][1], 1)
            return held["output"], results["up"]
        if slot == 1:
            results["out"] = jnp.transpose(both_cores(blocks["out"][1], 1))
            results["qkv"] = [projection(index) for index in range(3)]
            return held["output"], results["out"], results["qkv"]
        return held["output"]

    gather_slots((own_grad_hidden + input_own).astype(BF16), output_work)
    ends = (local_width, 2 * local_width, 2 * local_width + width)
    gain_grads = jnp.split(gain_pack[0], ends)
    return (
        block_output,
        held["output"][0],
        *results["qkv"],
        results["out"],
        results["gate"],
        results["up"],
        results["down"],
        *gain_grads,
    )


def layer(sizes, *arrays):
    return shards(sizes, *arrays)


def solution(mesh):
    in_specs = (
        P(("dp", "row"), None),
        P(("dp", "row")),
        P(("dp", "row")),
        P("row", "col"),
        P("row", "col"),
        P("row", "col"),
        P("col", "row"),
        P("row", "col"),
        P("row", "col"),
        P("col", "row"),
        P("col"),
        P("col"),
        P(),
        P(),
        P(("dp", "row"), None),
    )
    out_specs = (
        P(("dp", "row"), None),
        P(("dp", "row"), None),
        P("row", "col"),
        P("row", "col"),
        P("row", "col"),
        P("col", "row"),
        P("row", "col"),
        P("row", "col"),
        P("col", "row"),
        P("col"),
        P("col"),
        P(),
        P(),
    )
    sizes = (mesh.shape["dp"], mesh.shape["row"], mesh.shape["col"])
    return jax.shard_map(
        functools.partial(layer, sizes), mesh=mesh, in_specs=in_specs, out_specs=out_specs, check_vma=False
    )
```

```python
import functools

import jax
import jax.numpy as jnp
from jax import lax
from jax.experimental import pallas as pl
from jax.experimental.pallas import tpu as pltpu
from jax.sharding import PartitionSpec as P


HD = 128
LEN = 1024
BQ = 256
VMEM = 60 << 20

EPS = 1e-06
THETA = 500000.0
NEG_FILL = -1e30
SCORE_SCALE = HD ** (-0.5)
F32 = jnp.float32
BF16 = jnp.bfloat16


def plain_dot(left_mat, right_mat):
    return jnp.dot(left_mat, right_mat, preferred_element_type=F32)


def times_transposed(left_mat, right_mat):
    return lax.dot_general(
        left_mat, right_mat, (((1,), (1,)), ((), ())), preferred_element_type=F32
    )


def left_transposed(left_mat, right_mat):
    return lax.dot_general(
        left_mat, right_mat, (((0,), (0,)), ((), ())), preferred_element_type=F32
    )


def rope_tables(positions):
    half_dim = HD // 2
    inv_freq = THETA ** (-(jnp.arange(half_dim, dtype=F32) * 2.0) / HD)
    angles = positions.astype(F32)[:, None] * inv_freq[None, :]
    cos_half, sin_half = jnp.cos(angles), jnp.sin(angles)
    cosine = jnp.concatenate([cos_half, cos_half], axis=-1)
    sine_signed = jnp.concatenate([-sin_half, sin_half], axis=-1)
    return cosine, sine_signed


def fill_mask(bias_ref, seg_col_ref, seg_row_ref):
    @pl.when(pl.program_id(0) == 0)
    def _():
        for first in range(0, LEN, BQ):
            keys = first + BQ
            rows = seg_col_ref[first:keys, :]
            cols = seg_row_ref[:, :keys]
            query_index = first + lax.broadcasted_iota(jnp.int32, (BQ, keys), 0)
            key_index = lax.broadcasted_iota(jnp.int32, (BQ, keys), 1)
            allowed = (rows == cols) & (key_index <= query_index)
            bias_ref[first:keys, :keys] = jnp.where(allowed, 0.0, NEG_FILL)


def attend_forward_kernel(
    q_ref, k_ref, v_ref, qs_ref, ks_ref, qg_ref, kg_ref, cos_ref, sin_ref, segc_ref, segr_ref,
    qrot_ref, krot_ref, vb_ref, att_ref, log_ref, bias_ref,
):
    fill_mask(bias_ref, segc_ref, segr_ref)
    cosine, sine = cos_ref[...], sin_ref[...]

    def turned(raw, scale, gain):
        norm = raw * scale * gain
        return (norm * cosine + pltpu.roll(norm, HD // 2, 1) * sine).astype(BF16)

    qrot_ref[...] = turned(q_ref[...], qs_ref[...], qg_ref[...])
    krot_ref[...] = turned(k_ref[...], ks_ref[...], kg_ref[...])
    vb_ref[...] = v_ref[...].astype(BF16)
    for first in range(0, LEN, BQ):
        keys = first + BQ
        scores = times_transposed(qrot_ref[first:keys, :], krot_ref[:keys, :]) * SCORE_SCALE
        masked = scores + bias_ref[first:keys, :keys]
        peak = jnp.max(masked, axis=1, keepdims=True)
        weight = jnp.exp(masked - peak)
        total = jnp.sum(weight, axis=1, keepdims=True)
        probs = (weight * (1.0 / total)).astype(BF16)
        att_ref[first:keys, :] = plain_dot(probs, vb_ref[:keys, :]).astype(BF16)
        log_ref[0, first:keys, :] = peak + jnp.log(total)


def attend_backward_kernel(
    q_ref, k_ref, qs_ref, ks_ref, qg_ref, kg_ref, cos_ref, sin_ref, segc_ref, segr_ref,
    qrot_ref, krot_ref, vb_ref, att_ref, log_ref, grad_ref,
    dzq_ref, dzk_ref, gv_ref, dotq_ref, dotk_ref, gainq_ref, gaink_ref,
    dq_acc, dk_acc, dv_acc, bias_ref,
):
    fill_mask(bias_ref, segc_ref, segr_ref)
    dk_acc[...] = jnp.zeros_like(dk_acc)
    dv_acc[...] = jnp.zeros_like(dv_acc)
    for first in range(0, LEN, BQ):
        keys = first + BQ
        queries = qrot_ref[first:keys, :]
        grads = grad_ref[first:keys, :]
        scores = times_transposed(queries, krot_ref[:keys, :]) * SCORE_SCALE
        probs = jnp.exp(scores + bias_ref[first:keys, :keys] - log_ref[0, first:keys, :])
        delta = jnp.sum(
            grads.astype(F32) * att_ref[first:keys, :].astype(F32), axis=1, keepdims=True
        )
        grad_probs = times_transposed(grads, vb_ref[:keys, :])
        grad_scores = (probs * (grad_probs - delta) * SCORE_SCALE).astype(BF16)
        dq_acc[first:keys, :] = plain_dot(grad_scores, krot_ref[:keys, :])
        dk_acc[:keys, :] += left_transposed(grad_scores, queries)
        dv_acc[:keys, :] += left_transposed(probs.astype(BF16), grads)
    gv_ref[...] = dv_acc[...].astype(BF16)
    cosine, sine = cos_ref[...], sin_ref[...]

    def finish(acc, raw_ref, scale_ref, gain_ref, dz_ref, dot_ref, gain_grad_ref):
        grad_rot = acc[...]
        grad_norm = grad_rot * cosine - pltpu.roll(grad_rot, HD // 2, 1) * sine
        unit = raw_ref[...] * scale_ref[...]
        gain_grad_ref[...] = jnp.sum(grad_norm * unit, axis=0, keepdims=True)
        grad_unit = grad_norm * gain_ref[...]
        dz_ref[...] = grad_unit
        part = jnp.sum(grad_unit * unit, axis=1, keepdims=True)

        @pl.when(pl.program_id(0) == 0)
        def _():
            dot_ref[...] = part

        @pl.when(pl.program_id(0) > 0)
        def _():
            dot_ref[...] += part

    finish(dq_acc, q_ref, qs_ref, qg_ref, dzq_ref, dotq_ref, gainq_ref)
    finish(dk_acc, k_ref, ks_ref, kg_ref, dzk_ref, dotk_ref, gaink_ref)


def head_spec(offset):
    return pl.BlockSpec((LEN, HD), lambda h: (0, offset + h))


def whole_spec(shape):
    return pl.BlockSpec(shape, lambda h: (0,) * len(shape))


def gain_spec():
    return pl.BlockSpec((1, HD), lambda h: (0, h))


LOG_SPEC = pl.BlockSpec((1, LEN, 1), lambda h: (h, 0, 0))
COLUMN = (LEN, 1)
TABLE = (LEN, HD)


def attend_forward(qkv, scales, gains, tables, seg_col, seg_row, heads):
    width = heads * HD
    piece = jax.ShapeDtypeStruct((LEN, width), BF16)
    return pl.pallas_call(
        attend_forward_kernel,
        grid=(heads,),
        in_specs=[
            head_spec(0), head_spec(heads), head_spec(2 * heads),
            whole_spec(COLUMN), whole_spec(COLUMN), gain_spec(), gain_spec(),
            whole_spec(TABLE), whole_spec(TABLE), whole_spec(COLUMN), whole_spec((1, LEN)),
        ],
        out_specs=[head_spec(0)] * 4 + [LOG_SPEC],
        out_shape=[piece] * 4 + [jax.ShapeDtypeStruct((heads, LEN, 1), F32)],
        scratch_shapes=[pltpu.VMEM((LEN, LEN), F32)],
        compiler_params=pltpu.CompilerParams(vmem_limit_bytes=VMEM),
        cost_estimate=pl.CostEstimate(
            flops=heads * 4 * LEN * LEN * HD, bytes_accessed=LEN * width * 20, transcendentals=0
        ),
        name="attend_forward",
    )(qkv, qkv, qkv, *scales, *gains, *tables, seg_col, seg_row)


def attend_backward(qkv, scales, gains, tables, seg_col, seg_row, saved, grad_att, heads):
    width = heads * HD
    full = jax.ShapeDtypeStruct((LEN, width), F32)
    column = jax.ShapeDtypeStruct(COLUMN, F32)
    gain_row = jax.ShapeDtypeStruct((1, width), F32)
    return pl.pallas_call(
        attend_backward_kernel,
        grid=(heads,),
        in_specs=[
            head_spec(0), head_spec(heads),
            whole_spec(COLUMN), whole_spec(COLUMN), gain_spec(), gain_spec(),
            whole_spec(TABLE), whole_spec(TABLE), whole_spec(COLUMN), whole_spec((1, LEN)),
            head_spec(0), head_spec(0), head_spec(0), head_spec(0), LOG_SPEC, head_spec(0),
        ],
        out_specs=[
            head_spec(0), head_spec(0), head_spec(0),
            whole_spec(COLUMN), whole_spec(COLUMN), gain_spec(), gain_spec(),
        ],
        out_shape=[
            full, full, jax.ShapeDtypeStruct((LEN, width), BF16), column, column, gain_row, gain_row,
        ],
        scratch_shapes=[pltpu.VMEM((LEN, HD), F32)] * 3 + [pltpu.VMEM((LEN, LEN), F32)],
        compiler_params=pltpu.CompilerParams(vmem_limit_bytes=VMEM),
        cost_estimate=pl.CostEstimate(
            flops=heads * 10 * LEN * LEN * HD, bytes_accessed=LEN * width * 40, transcendentals=0
        ),
        name="attend_backward",
    )(qkv, qkv, *scales, *gains, *tables, seg_col, seg_row, *saved, grad_att)


def fetch_choice(idx_ref, refs, held_ref, sem):
    for number, ref in enumerate(refs):

        @pl.when(idx_ref[2] == number)
        def _():
            copy = pltpu.make_async_copy(ref, held_ref, sem)
            copy.start()
            copy.wait()


def half_tile(step, core, tiles):
    per_half = tiles // 2
    return ((core + step // per_half) % 2) * per_half + step % per_half


def forward_chunk_kernel(
    idx_ref, *refs, blocks, tiles,
):
    own_ref, left1, left2, left3, right1, right2, right3 = refs[:7]
    wo_own_ref, wo_oth_ref, x_ref, gain_ref, wg_ref, wu_ref, wd_own_ref, wd_oth_ref = refs[7:15]
    raw_ref, scale_ref, hb_ref, gate_ref, up_ref, mixed_ref, part_ref, acc_ref, att_ref = refs[-9:]
    block = wo_own_ref.shape[2]
    depth = wo_own_ref.shape[1]
    step = pl.program_id(0)
    core = idx_ref[1]

    @pl.when(step == 0)
    def _():
        quarter = own_ref.shape[1] // 2
        pieces = (
            own_ref[...], right1[...] + left3[...], right2[...] + left2[...], right3[...] + left1[...],
        )
        for half in range(2):
            for number, piece in enumerate(pieces):
                start = half * depth + number * quarter
                att_ref[:, start : start + quarter] = piece[:, half * quarter : (half + 1) * quarter]

    @pl.when(step < blocks)
    def _():
        own = att_ref[:, pl.ds(pl.multiple_of(core * depth, depth), depth)]
        other = att_ref[:, pl.ds(pl.multiple_of((1 - core) * depth, depth), depth)]
        raw_ref[:, pl.ds(pl.multiple_of(step * block, block), block)] = plain_dot(
            own, wo_own_ref[0]
        ) + plain_dot(other, wo_oth_ref[0])

    @pl.when(step == blocks - 1)
    def _():
        raw = raw_ref[...]
        scale = lax.rsqrt(jnp.mean(raw * raw, axis=1, keepdims=True) + EPS)
        scale_ref[...] = scale
        hb_ref[...] = (x_ref[...].astype(F32) + raw * scale * gain_ref[...]).astype(BF16)
        acc_ref[...] = jnp.zeros_like(acc_ref)

    def tile_work(wd_ref):
        hidden_b = hb_ref[...]
        gate = plain_dot(hidden_b, wg_ref[...])
        up = plain_dot(hidden_b, wu_ref[...])
        mixed = (gate * jax.nn.sigmoid(gate) * up).astype(BF16)
        gate_ref[...] = gate.astype(BF16)
        up_ref[...] = up.astype(BF16)
        mixed_ref[...] = mixed
        for j in range(blocks):
            acc_ref[:, j * block : (j + 1) * block] += plain_dot(mixed, wd_ref[j])

    @pl.when((step >= blocks) & (step < blocks + tiles // 2))
    def _():
        tile_work(wd_own_ref)

    @pl.when(step >= blocks + tiles // 2)
    def _():
        tile_work(wd_oth_ref)

    @pl.when(step == blocks + tiles - 1)
    def _():
        part_ref[...] = acc_ref[...].astype(BF16)


TILE = 512


def forward_chunk(index, attended, out_halves, block_input, gain, w_gate, w_up, down_halves, chunk, before):
    tokens, width = block_input.shape
    hidden = w_gate.shape[1]
    blocks, depth, block = out_halves[0].shape
    tiles = hidden // TILE

    def tile_of(j, idx):
        return half_tile(jnp.maximum(j - blocks, 0), idx[1], tiles)

    rows = pl.BlockSpec((chunk, width), lambda j, idx: (idx[0], 0))
    out_half = pl.BlockSpec((1, depth, block), lambda j, idx: (jnp.minimum(j, blocks - 1), 0, 0))
    up_tile = pl.BlockSpec((width, TILE), lambda j, idx: (0, tile_of(j, idx)))
    down_own = pl.BlockSpec(
        (blocks, TILE, block), lambda j, idx: (0, jnp.clip(j - blocks, 0, tiles // 2 - 1), 0)
    )
    down_oth = pl.BlockSpec(
        (blocks, TILE, block), lambda j, idx: (0, jnp.maximum(j - blocks - tiles // 2, 0), 0)
    )
    act_tile = pl.BlockSpec((chunk, TILE), lambda j, idx: (idx[0], tile_of(j, idx)))
    before = tuple(before)
    return pl.pallas_call(
        functools.partial(forward_chunk_kernel, blocks=blocks, tiles=tiles),
        grid_spec=pltpu.PrefetchScalarGridSpec(
            num_scalar_prefetch=1,
            grid=(blocks + tiles,),
            in_specs=[
                *[pl.BlockSpec((chunk, attended[0].shape[1]), lambda j, idx: (idx[0], 0))] * 7,
                out_half, out_half, rows, pl.BlockSpec((1, width), lambda j, idx: (0, 0)),
                up_tile, up_tile, down_own, down_oth,
            ] + [pl.BlockSpec(memory_space=pl.ANY)] * len(before),
            out_specs=[
                rows, pl.BlockSpec((chunk, 1), lambda j, idx: (idx[0], 0)), rows, act_tile, act_tile, act_tile,
                pl.BlockSpec((chunk, width), lambda j, idx: (0, 0)),
            ],
            scratch_shapes=[pltpu.VMEM((chunk, width), F32), pltpu.VMEM((chunk, 2 * depth), BF16)],
        ),
        out_shape=[
            jax.ShapeDtypeStruct((tokens, width), F32),
            jax.ShapeDtypeStruct((tokens, 1), F32),
            jax.ShapeDtypeStruct((tokens, width), BF16),
            jax.ShapeDtypeStruct((tokens, hidden), BF16),
            jax.ShapeDtypeStruct((tokens, hidden), BF16),
            jax.ShapeDtypeStruct((tokens, hidden), BF16),
            jax.ShapeDtypeStruct((chunk, width), BF16),
        ],
        input_output_aliases={16 + i: i for i in range(len(before))},
        compiler_params=pltpu.CompilerParams(vmem_limit_bytes=VMEM),
        cost_estimate=pl.CostEstimate(
            flops=2 * chunk * width * (width + 3 * hidden),
            bytes_accessed=2 * width * (width + 3 * hidden),
            transcendentals=0,
        ),
        name="forward_chunk",
    )(index, *attended, *out_halves, block_input, gain, w_gate, w_up, *down_halves, *before)


def backward_chunk_kernel(
    idx_ref, raw_ref, scale_ref, x_ref, grad_ref, attn_gain_ref, mlp_gain_ref,
    gate_ref, up_ref, wg_ref, wu_ref, wd_own_ref, wd_oth_ref, *refs, blocks, tiles, choices,
):
    out_ref, gdi_ref, gg_ref, gu_ref, part_ref, gain_grad_ref, acc_ref, down_ref, sem = refs[-9:]
    block = wd_own_ref.shape[2]
    step = pl.program_id(0)

    @pl.when(step == 0)
    def _():
        fetch_choice(idx_ref, refs[:choices], down_ref, sem)
        down_raw = down_ref[...].astype(F32)
        down_scale = lax.rsqrt(jnp.mean(down_raw * down_raw, axis=1, keepdims=True) + EPS)
        unit = down_raw * down_scale
        mlp_gain = mlp_gain_ref[...]
        hidden = x_ref[...].astype(F32) + raw_ref[...] * scale_ref[...] * attn_gain_ref[...]
        out_ref[...] = (hidden + unit * mlp_gain).astype(BF16)
        grad_y = grad_ref[...].astype(F32)
        gain_grad_ref[...] = jnp.sum(grad_y * unit, axis=0, keepdims=True)
        grad_unit = grad_y * mlp_gain
        mean = jnp.mean(grad_unit * unit, axis=1, keepdims=True)
        gdi_ref[...] = (down_scale * (grad_unit - unit * mean)).astype(BF16)
        acc_ref[...] = jnp.zeros_like(acc_ref)

    def tile_work(wd_ref):
        grad_mixed = times_transposed(gdi_ref[:, :block], wd_ref[0])
        for j in range(1, blocks):
            grad_mixed += times_transposed(gdi_ref[:, j * block : (j + 1) * block], wd_ref[j])
        gate = gate_ref[...].astype(F32)
        sig = jax.nn.sigmoid(gate)
        grad_gate = (grad_mixed * up_ref[...].astype(F32) * sig * (1.0 + gate * (1.0 - sig))).astype(BF16)
        grad_up = (grad_mixed * (gate * sig)).astype(BF16)
        gg_ref[...] = grad_gate
        gu_ref[...] = grad_up
        acc_ref[...] += times_transposed(grad_gate, wg_ref[...]) + times_transposed(grad_up, wu_ref[...])

    @pl.when(step < tiles // 2)
    def _():
        tile_work(wd_own_ref)

    @pl.when(step >= tiles // 2)
    def _():
        tile_work(wd_oth_ref)

    @pl.when(step == tiles - 1)
    def _():
        part_ref[...] = acc_ref[...].astype(BF16)


def backward_chunk(
    index, down_rows, raw, scale, block_input, grad_output, attn_gain, mlp_gain, gate, up, w_gate, w_up,
    down_halves, chunk, before,
):
    tokens, width = block_input.shape
    hidden = w_gate.shape[1]
    blocks, _, block = down_halves[0].shape
    tiles = hidden // TILE

    def tile_of(j, idx):
        return half_tile(j, idx[1], tiles)

    rows = pl.BlockSpec((chunk, width), lambda j, idx: (idx[0], 0))
    fixed = pl.BlockSpec((chunk, width), lambda j, idx: (0, 0))
    gain_row = pl.BlockSpec((1, width), lambda j, idx: (0, 0))
    up_tile = pl.BlockSpec((width, TILE), lambda j, idx: (0, tile_of(j, idx)))
    act_tile = pl.BlockSpec((chunk, TILE), lambda j, idx: (idx[0], tile_of(j, idx)))
    before = tuple(before)
    return pl.pallas_call(
        functools.partial(backward_chunk_kernel, blocks=blocks, tiles=tiles, choices=len(down_rows)),
        grid_spec=pltpu.PrefetchScalarGridSpec(
            num_scalar_prefetch=1,
            grid=(tiles,),
            in_specs=[
                rows, pl.BlockSpec((chunk, 1), lambda j, idx: (idx[0], 0)), rows, rows, gain_row, gain_row,
                act_tile, act_tile, up_tile, up_tile,
                pl.BlockSpec((blocks, TILE, block), lambda j, idx: (0, jnp.minimum(j, tiles // 2 - 1), 0)),
                pl.BlockSpec((blocks, TILE, block), lambda j, idx: (0, jnp.maximum(j - tiles // 2, 0), 0)),
            ] + [pl.BlockSpec(memory_space=pl.ANY)] * (len(down_rows) + len(before)),
            out_specs=[rows, rows, act_tile, act_tile, fixed, gain_row],
            scratch_shapes=[
                pltpu.VMEM((chunk, width), F32), pltpu.VMEM((chunk, width), BF16), pltpu.SemaphoreType.DMA(()),
            ],
        ),
        out_shape=[
            jax.ShapeDtypeStruct((tokens, width), BF16),
            jax.ShapeDtypeStruct((tokens, width), BF16),
            jax.ShapeDtypeStruct((tokens, hidden), BF16),
            jax.ShapeDtypeStruct((tokens, hidden), BF16),
            jax.ShapeDtypeStruct((chunk, width), BF16),
            jax.ShapeDtypeStruct((1, width), F32),
        ],
        input_output_aliases={13 + len(down_rows) + i: i for i in range(len(before))},
        compiler_params=pltpu.CompilerParams(vmem_limit_bytes=VMEM),
        cost_estimate=pl.CostEstimate(
            flops=6 * chunk * width * hidden, bytes_accessed=6 * width * hidden, transcendentals=0
        ),
        name="backward_chunk",
    )(
        index, raw, scale, block_input, grad_output, attn_gain, mlp_gain, gate, up, w_gate, w_up,
        *down_halves, *down_rows, *before,
    )


def attention_chunk_kernel(
    idx_ref, grad_ref, raw_ref, scale_ref, gain_ref, wo_own_ref, wo_oth_ref, *refs, blocks, choices,
):
    gai_ref, gatt_ref, gain_grad_ref, mlp_ref, sem = refs[-5:]
    fetch_choice(idx_ref, refs[:choices], mlp_ref, sem)
    half, block = wo_own_ref.shape[1:]
    core = idx_ref[1]
    scale = scale_ref[...]
    unit = raw_ref[...] * scale
    grad_hidden = grad_ref[...].astype(F32) + mlp_ref[...].astype(F32)
    gain_grad_ref[...] = jnp.sum(grad_hidden * unit, axis=0, keepdims=True)
    grad_unit = grad_hidden * gain_ref[...]
    mean = jnp.mean(grad_unit * unit, axis=1, keepdims=True)
    gai_ref[...] = (scale * (grad_unit - unit * mean)).astype(BF16)
    for place, w_ref in ((core, wo_own_ref), (1 - core, wo_oth_ref)):
        total = times_transposed(gai_ref[:, :block], w_ref[0])
        for j in range(1, blocks):
            total += times_transposed(gai_ref[:, j * block : (j + 1) * block], w_ref[j])
        gatt_ref[:, pl.ds(pl.multiple_of(place * half, half), half)] = total.astype(BF16)


def attention_chunk(index, mlp_rows, grad_output, raw, scale, gain, out_halves, half, chunk, before):
    tokens, width = grad_output.shape
    blocks, _, block = out_halves[0].shape
    rows = pl.BlockSpec((chunk, width), lambda j, idx: (idx[0], 0))
    gain_row = pl.BlockSpec((1, width), lambda j, idx: (0, 0))
    own_heads = pl.BlockSpec((blocks, half, block), lambda j, idx: (0, 0, 0))
    before = tuple(before)
    return pl.pallas_call(
        functools.partial(attention_chunk_kernel, blocks=blocks, choices=len(mlp_rows)),
        grid_spec=pltpu.PrefetchScalarGridSpec(
            num_scalar_prefetch=1,
            grid=(1,),
            in_specs=[
                rows, rows, pl.BlockSpec((chunk, 1), lambda j, idx: (idx[0], 0)), gain_row,
                own_heads, own_heads,
            ] + [pl.BlockSpec(memory_space=pl.ANY)] * (len(mlp_rows) + len(before)),
            out_specs=[rows, pl.BlockSpec((chunk, 2 * half), lambda j, idx: (idx[0], 0)), gain_row],
            scratch_shapes=[pltpu.VMEM((chunk, width), BF16), pltpu.SemaphoreType.DMA(())],
        ),
        out_shape=[
            jax.ShapeDtypeStruct((tokens, width), BF16),
            jax.ShapeDtypeStruct((tokens, 2 * half), BF16),
            jax.ShapeDtypeStruct((1, width), F32),
        ],
        input_output_aliases={7 + len(mlp_rows) + i: i for i in range(len(before))},
        compiler_params=pltpu.CompilerParams(vmem_limit_bytes=VMEM),
        cost_estimate=pl.CostEstimate(
            flops=4 * chunk * width * half, bytes_accessed=16 * chunk * width, transcendentals=0
        ),
        name="attention_chunk",
    )(index, grad_output, raw, scale, gain, *out_halves, *mlp_rows, *before)


def place_rows_kernel(idx_ref, *refs, choices):
    out_ref, held_ref, sem = refs[-3:]
    step = pl.program_id(0)

    @pl.when(step == 0)
    def _():
        fetch_choice(idx_ref, refs[:choices], held_ref, sem)

    size = out_ref.shape[0]
    out_ref[...] = held_ref[pl.ds(pl.multiple_of(step * size, size), size), :].astype(out_ref.dtype)


def place_rows(index, rows_in, tokens, dtype, before):
    chunk, width = rows_in[0].shape
    before = tuple(before)
    return pl.pallas_call(
        functools.partial(place_rows_kernel, choices=len(rows_in)),
        grid_spec=pltpu.PrefetchScalarGridSpec(
            num_scalar_prefetch=1,
            grid=(4,),
            in_specs=[pl.BlockSpec(memory_space=pl.ANY)] * (len(rows_in) + len(before)),
            out_specs=pl.BlockSpec((chunk // 4, width), lambda j, idx: (4 * idx[0] + j, 0)),
            scratch_shapes=[pltpu.VMEM((chunk, width), BF16), pltpu.SemaphoreType.DMA(())],
        ),
        out_shape=jax.ShapeDtypeStruct((tokens, width), dtype),
        input_output_aliases={1 + len(rows_in): 0} if before else {},
        compiler_params=pltpu.CompilerParams(vmem_limit_bytes=VMEM),
        cost_estimate=pl.CostEstimate(flops=0, bytes_accessed=6 * chunk * width, transcendentals=0),
        name="place_rows",
    )(index, *rows_in, *before)


def after(value, *tokens):
    return lax.optimization_barrier((value, tokens))[0]


def unset_kernel(out_ref):
    pass


def unset(shape, dtype):
    return pl.pallas_call(
        unset_kernel,
        out_specs=pl.BlockSpec(memory_space=pl.ANY),
        out_shape=jax.ShapeDtypeStruct(shape, dtype),
        name="unset",
    )()


def shards(
    sizes,
    block_input,
    segment_ids,
    positions,
    w_query,
    w_key,
    w_value,
    w_out,
    w_gate,
    w_up,
    w_down,
    query_gain,
    key_gain,
    attn_gain,
    mlp_gain,
    grad_output,
):
    cores, rows, cols = sizes
    tokens_here, width = block_input.shape
    assert tokens_here == LEN and cores == 2 and cols == 4
    local_width = w_query.shape[1]
    half_width = local_width // 2
    heads = local_width // HD
    chunk = tokens_here // cols
    core = lax.axis_index("dp")
    row = lax.axis_index("row")
    col = lax.axis_index("col")
    swap = [(0, 1), (1, 0)]
    attn_row, mlp_row = attn_gain[None, :], mlp_gain[None, :]

    def own_half(array, axis):
        half = array.shape[axis] // 2
        return lax.dynamic_slice_in_dim(array, core * half, half, axis)

    def other_half(array, axis):
        half = array.shape[axis] // 2
        return lax.dynamic_slice_in_dim(array, (1 - core) * half, half, axis)

    def gather(weight, axis):
        return lax.all_gather(own_half(weight, axis), ("row", "dp"), axis=axis, tiled=True)

    def line_step(from_left, from_right, step):
        from_left = lax.ppermute(from_left, "col", [(i, i + 1) for i in range(step - 1, cols - 1)])
        from_right = lax.ppermute(from_right, "col", [(i + 1, i) for i in range(cols - step)])
        return from_left, from_right

    def sum_step(up, down, step):
        up = lax.ppermute(up, "col", [(i, i + 1) for i in range(step)])
        down = lax.ppermute(down, "col", [(cols - 1 - i, cols - 2 - i) for i in range(step)])
        return up, down

    def pick(at_zero, at_one, at_two, at_three):
        low = jnp.where(col == 0, at_zero, at_one)
        high = jnp.where(col == 2, at_two, at_three)
        return jnp.where(col < 2, low, high)

    slot_chunk = [pick(3, 3, 0, 0), pick(2, 2, 1, 1), pick(1, 0, 3, 2), col]
    slot_index = [
        jnp.stack([one, core, choice]).astype(jnp.int32)
        for one, choice in zip(slot_chunk, (col, col, col % 2, 0 * col))
    ]

    def slot_rows(array, slot):
        return lax.dynamic_slice_in_dim(array, slot_chunk[slot] * chunk, chunk, 0)

    def gather_slots(own, work):
        left, right, token = [own], [own], ()
        arrived = (
            lambda lefts, rights: (lefts[0],),
            lambda lefts, rights: (rights[1], lefts[1]),
            lambda lefts, rights: (rights[2], rights[1], lefts[1], lefts[2]),
            lambda lefts, rights: (rights[3], rights[2], lefts[2], lefts[3]),
        )
        for step in range(1, cols + 1):
            seen = tuple(left), tuple(right)
            if step < cols:
                from_left, from_right = line_step(left[-1], right[-1], step)
                left.append(from_left)
                right.append(from_right)
            token = work(cols - step, arrived[step - 1](*after(seen, token)))

    def sum_slots(make, window=lambda step, gate: ()):
        def at(step, gate):
            window(step, gate)
            return make(step, gate)

        first = make(0, ())
        up, down = sum_step(first, first, 1)
        second = at(1, first)
        up = jnp.where(col == 0, second, first) + up
        down = jnp.where(col == 3, second, first) + down
        gate = (up, down)
        up, down = sum_step(up, down, 2)
        third = at(2, gate)
        up = jnp.where(col == 1, second, third) + up
        down = jnp.where(col == 2, second, third) + down
        gate = (up, down)
        up, down = sum_step(up, down, 3)
        fourth = lax.optimization_barrier(at(3, gate))
        return fourth.astype(F32) + up.astype(F32) + down.astype(F32)

    def both_cores(half, axis):
        other = lax.ppermute(half, "dp", swap)
        first = jnp.where(core == 0, half, other)
        second = jnp.where(core == 0, other, half)
        return jnp.concatenate([first, second], axis=axis).astype(F32)

    def sum_sent(left_mat, right_other):
        return lax.ppermute(left_transposed(left_mat, right_other).astype(BF16), "dp", swap)

    def sum_kept(left_mat, right_own, got):
        total = (left_transposed(left_mat, right_own) + got.astype(F32)).astype(BF16)
        return total, lax.psum_scatter(total, "row", scatter_dimension=0, tiled=True)

    by_x = [(0, 1), (1, 0), (2, 3), (3, 2)]
    by_y = [(0, 2), (2, 0), (1, 3), (3, 1)]

    def row_first(half):
        if rows != 4:
            return (half,)
        return half, lax.ppermute(half, "row", by_x), lax.ppermute(half, "row", by_y)

    def row_second(pieces):
        if rows != 4:
            return pieces
        middle = pieces[0].shape[0] // 2
        return (
            *pieces,
            lax.ppermute(pieces[1][:middle], "row", by_y),
            lax.ppermute(pieces[2][middle:], "row", by_x),
        )

    def row_blocks(pieces):
        if rows != 4:
            whole = lax.all_gather(pieces[0], ("row", "dp"), axis=0, tiled=False)
            whole = whole.reshape(rows, cores, *pieces[0].shape)
            return tuple(lax.dynamic_index_in_dim(whole, one, 1, keepdims=False) for one in (core, 1 - core))
        own, by_one, by_two, corner_top, corner_low = pieces
        middle = own.shape[0] // 2
        held = unset((rows, *own.shape), own.dtype)
        for piece, block, start in (
            (own, row, 0), (by_one, row ^ 1, 0), (by_two, row ^ 2, 0),
            (corner_top, row ^ 3, 0), (corner_low, row ^ 3, middle),
        ):
            held = lax.dynamic_update_slice(held, piece[None], (block, start, 0))
        return held, lax.ppermute(held, "dp", swap)

    full_qkv = gather(jnp.concatenate([w_query, w_key, w_value], axis=1), 0)
    full_gate = gather(w_gate, 0)
    full_up = gather(w_up, 0)
    out_half = own_half(w_out, 0)
    out_stack = jnp.concatenate(
        [out_half]
        + [
            lax.ppermute(out_half, "col", [(i, (i - step) % cols) for i in range(cols)])
            for step in range(1, cols)
        ],
        axis=0,
    )
    down_start, out_start = after((own_half(w_down, 0), out_stack), full_qkv)
    down_pieces = row_first(down_start)
    out_pieces = row_first(out_start)

    qkv = plain_dot(block_input, full_qkv)
    query_raw, key_raw = qkv[:, :local_width], qkv[:, local_width : 2 * local_width]
    query_sq, key_sq = lax.psum(
        (jnp.sum(query_raw * query_raw, axis=1), jnp.sum(key_raw * key_raw, axis=1)), "col"
    )
    query_scale = lax.rsqrt(query_sq / width + EPS)[:, None]
    key_scale = lax.rsqrt(key_sq / width + EPS)[:, None]
    scales = (query_scale, key_scale)
    gains = (query_gain[None, :], key_gain[None, :])
    tables = rope_tables(positions)
    seg_col, seg_row = segment_ids[:, None], segment_ids[None, :]
    query_rot, key_rot, value_heads, attended, log_total = attend_forward(
        qkv, scales, gains, tables, seg_col, seg_row, heads
    )

    lefts, rights = [attended], [attended]
    for step in range(1, cols):
        from_left, from_right = line_step(lefts[-1], rights[-1], step)
        lefts.append(from_left)
        rights.append(from_right)
        if step == 2:
            down_pieces = row_second(after(down_pieces, lefts[1], rights[1]))
            out_pieces = row_second(after(out_pieces, lefts[1], rights[1]))
        if step == 3:
            out_halves = row_blocks(out_pieces)
            down_halves = row_blocks(down_pieces)
    attended_all = (attended, *lefts[1:], *rights[1:])

    held = dict(forward=(), backward=(), attention=(), output=())
    gain_sums = dict(mlp=0.0, attn=0.0)

    def forward_work(slot, gate):
        results = forward_chunk(
            slot_index[slot], after(attended_all, gate), out_halves, block_input, attn_row, full_gate, full_up,
            down_halves, chunk, held["forward"],
        )
        held["forward"] = results[:6]
        return results[6]

    down_own = sum_slots(forward_work).astype(BF16)
    attn_raw, attn_scale, hidden_b, gate_proj, up_proj, mixed_act = held["forward"]
    mlp_parts = [None] * cols

    def backward_work(slot, down_rows):
        results = backward_chunk(
            slot_index[slot], down_rows, attn_raw, attn_scale, block_input, grad_output, attn_row, mlp_row,
            gate_proj, up_proj, full_gate, full_up, down_halves, chunk, held["backward"],
        )
        held["backward"] = results[:4]
        mlp_parts[slot] = results[4]
        gain_sums["mlp"] = gain_sums["mlp"] + results[5]
        return results[4]

    gather_slots(down_own, backward_work)
    block_output, grad_down_in, grad_gate_in, grad_up_in = held["backward"]

    blocks = {}
    got = {}

    def mlp_window(step, gate):
        down_left, down_right, hidden_left, gate_right, up_right = after(
            (grad_down_in, mixed_act, hidden_b, grad_gate_in, grad_up_in), gate
        )
        if step == 1:
            got["down"] = sum_sent(down_left, other_half(down_right, 1))
            got["gate"] = sum_sent(hidden_left, other_half(gate_right, 1))
            return got["down"], got["gate"]
        if step == 2:
            blocks["down"] = sum_kept(down_left, own_half(down_right, 1), got["down"])
            got["up"] = sum_sent(hidden_left, other_half(up_right, 1))
            return blocks["down"][0], got["up"]
        blocks["gate"] = sum_kept(hidden_left, own_half(gate_right, 1), got["gate"])
        return blocks["gate"][0]

    mlp_own = sum_slots(lambda slot, gate: mlp_parts[slot], mlp_window).astype(BF16)

    def attention_work(slot, mlp_rows):
        results = attention_chunk(
            slot_index[slot], mlp_rows, grad_output, attn_raw, attn_scale, attn_row, out_halves, half_width,
            chunk, held["attention"],
        )
        held["attention"] = results[:2]
        gain_sums["attn"] = gain_sums["attn"] + results[2]
        if slot == 3:
            hidden_left, up_right = after((hidden_b, grad_up_in), mlp_rows[0])
            blocks["up"] = sum_kept(hidden_left, own_half(up_right, 1), got["up"])
        return results[1]

    gather_slots(mlp_own, attention_work)
    grad_attn_in, grad_att = held["attention"]
    own_grad_hidden = slot_rows(grad_output, 3).astype(F32) + mlp_own.astype(F32)

    query_dz, key_dz, grad_value_in, query_dot, key_dot, grad_query_gain, grad_key_gain = attend_backward(
        qkv, scales, gains, tables, seg_col, seg_row,
        (query_rot, key_rot, value_heads, attended, log_total), grad_att, heads,
    )
    query_dot, key_dot = lax.psum((query_dot[:, 0], key_dot[:, 0]), "col")
    grad_query_in = (
        query_scale * (query_dz - query_raw * query_scale * (query_dot / width)[:, None])
    ).astype(BF16)
    grad_key_in = (
        key_scale * (key_dz - key_raw * key_scale * (key_dot / width)[:, None])
    ).astype(BF16)
    grad_qkv = jnp.concatenate([grad_query_in, grad_key_in, grad_value_in], axis=1)
    gain_pack = jnp.concatenate([grad_query_gain, grad_key_gain, gain_sums["attn"], gain_sums["mlp"]], axis=1)

    def interleaved(picker, pieces_in):
        return jnp.concatenate([picker(one, 1) for one in pieces_in], axis=1)

    def input_window(step, gate):
        nonlocal gain_pack
        pack, *pieces_in, tokens_in, left_out, right_out = after(
            (gain_pack, grad_query_in, grad_key_in, grad_value_in, block_input, grad_attn_in, attended), gate
        )
        if step == 1:
            got["qkv"] = sum_sent(tokens_in, interleaved(other_half, pieces_in))
            got["out"] = sum_sent(left_out, other_half(right_out, 1))
            gain_pack = pack + lax.ppermute(pack, "dp", swap)
            return got["qkv"], got["out"], gain_pack
        if step == 2:
            blocks["qkv"] = sum_kept(tokens_in, interleaved(own_half, pieces_in), got["qkv"])
            if rows == 4:
                gain_pack = pack + lax.ppermute(pack, "row", by_x)
            return blocks["qkv"][0], gain_pack
        blocks["out"] = sum_kept(left_out, own_half(right_out, 1), got["out"])
        gain_pack = pack + lax.ppermute(pack, "row", by_y) if rows == 4 else lax.psum(pack, "row")
        return blocks["out"][0], gain_pack

    input_own = sum_slots(
        lambda slot, gate: times_transposed(after(slot_rows(grad_qkv, slot), gate), full_qkv).astype(BF16), input_window
    )

    results = {}
    quarter = local_width // 2

    def projection(index):
        pair = both_cores(blocks["qkv"][1][None, :, index * quarter : (index + 1) * quarter], 0)
        return jnp.concatenate([pair[0], pair[1]], axis=1)

    def output_work(slot, rows_in):
        held["output"] = (place_rows(slot_index[slot], rows_in, tokens_here, F32, held["output"]),)
        if slot == 3:
            results["down"] = jnp.transpose(both_cores(blocks["down"][1], 1))
            results["gate"] = both_cores(blocks["gate"][1], 1)
            return held["output"], results["down"], results["gate"]
        if slot == 2:
            results["up"] = both_cores(blocks["up"][1], 1)
            return held["output"], results["up"]
        if slot == 1:
            results["out"] = jnp.transpose(both_cores(blocks["out"][1], 1))
            results["qkv"] = [projection(index) for index in range(3)]
            return held["output"], results["out"], results["qkv"]
        return held["output"]

    gather_slots((own_grad_hidden + input_own).astype(BF16), output_work)
    ends = (local_width, 2 * local_width, 2 * local_width + width)
    gain_grads = jnp.split(gain_pack[0], ends)
    return (
        block_output,
        held["output"][0],
        *results["qkv"],
        results["out"],
        results["gate"],
        results["up"],
        results["down"],
        *gain_grads,
    )


def layer(sizes, *arrays):
    return shards(sizes, *arrays)


def solution(mesh):
    in_specs = (
        P(("dp", "row"), None),
        P(("dp", "row")),
        P(("dp", "row")),
        P("row", "col"),
        P("row", "col"),
        P("row", "col"),
        P("col", "row"),
        P("row", "col"),
        P("row", "col"),
        P("col", "row"),
        P("col"),
        P("col"),
        P(),
        P(),
        P(("dp", "row"), None),
    )
    out_specs = (
        P(("dp", "row"), None),
        P(("dp", "row"), None),
        P("row", "col"),
        P("row", "col"),
        P("row", "col"),
        P("col", "row"),
        P("row", "col"),
        P("row", "col"),
        P("col", "row"),
        P("col"),
        P("col"),
        P(),
        P(),
    )
    sizes = (mesh.shape["dp"], mesh.shape["row"], mesh.shape["col"])
    return jax.shard_map(
        functools.partial(layer, sizes), mesh=mesh, in_specs=in_specs, out_specs=out_specs, check_vma=False
    )
```

```python
import functools

import jax
import jax.numpy as jnp
from jax import lax
from jax.experimental import pallas as pl
from jax.experimental.pallas import tpu as pltpu
from jax.sharding import PartitionSpec as P


HD = 128
LEN = 1024
BQ = 256
VMEM = 60 << 20

EPS = 1e-06
THETA = 500000.0
NEG_FILL = -1e30
SCORE_SCALE = HD ** (-0.5)
F32 = jnp.float32
BF16 = jnp.bfloat16


def plain_dot(left_mat, right_mat):
    return jnp.dot(left_mat, right_mat, preferred_element_type=F32)


def times_transposed(left_mat, right_mat):
    return lax.dot_general(
        left_mat, right_mat, (((1,), (1,)), ((), ())), preferred_element_type=F32
    )


def left_transposed(left_mat, right_mat):
    return lax.dot_general(
        left_mat, right_mat, (((0,), (0,)), ((), ())), preferred_element_type=F32
    )


def rope_tables(positions):
    half_dim = HD // 2
    inv_freq = THETA ** (-(jnp.arange(half_dim, dtype=F32) * 2.0) / HD)
    angles = positions.astype(F32)[:, None] * inv_freq[None, :]
    cos_half, sin_half = jnp.cos(angles), jnp.sin(angles)
    cosine = jnp.concatenate([cos_half, cos_half], axis=-1)
    sine_signed = jnp.concatenate([-sin_half, sin_half], axis=-1)
    return cosine, sine_signed


def fill_mask(bias_ref, seg_col_ref, seg_row_ref):
    @pl.when(pl.program_id(0) == 0)
    def _():
        for first in range(0, LEN, BQ):
            keys = first + BQ
            rows = seg_col_ref[first:keys, :]
            cols = seg_row_ref[:, :keys]
            query_index = first + lax.broadcasted_iota(jnp.int32, (BQ, keys), 0)
            key_index = lax.broadcasted_iota(jnp.int32, (BQ, keys), 1)
            allowed = (rows == cols) & (key_index <= query_index)
            bias_ref[first:keys, :keys] = jnp.where(allowed, 0.0, NEG_FILL)


def attend_forward_kernel(
    q_ref, k_ref, v_ref, qs_ref, ks_ref, qg_ref, kg_ref, cos_ref, sin_ref, segc_ref, segr_ref,
    qrot_ref, krot_ref, vb_ref, att_ref, log_ref, bias_ref,
):
    fill_mask(bias_ref, segc_ref, segr_ref)
    cosine, sine = cos_ref[...], sin_ref[...]

    def turned(raw, scale, gain):
        norm = raw * scale * gain
        return (norm * cosine + pltpu.roll(norm, HD // 2, 1) * sine).astype(BF16)

    qrot_ref[...] = turned(q_ref[...], qs_ref[...], qg_ref[...])
    krot_ref[...] = turned(k_ref[...], ks_ref[...], kg_ref[...])
    vb_ref[...] = v_ref[...].astype(BF16)
    for first in range(0, LEN, BQ):
        keys = first + BQ
        scores = times_transposed(qrot_ref[first:keys, :], krot_ref[:keys, :]) * SCORE_SCALE
        masked = scores + bias_ref[first:keys, :keys]
        peak = jnp.max(masked, axis=1, keepdims=True)
        weight = jnp.exp(masked - peak)
        total = jnp.sum(weight, axis=1, keepdims=True)
        probs = (weight * (1.0 / total)).astype(BF16)
        att_ref[first:keys, :] = plain_dot(probs, vb_ref[:keys, :]).astype(BF16)
        log_ref[0, first:keys, :] = peak + jnp.log(total)


def attend_backward_kernel(
    q_ref, k_ref, qs_ref, ks_ref, qg_ref, kg_ref, cos_ref, sin_ref, segc_ref, segr_ref,
    qrot_ref, krot_ref, vb_ref, att_ref, log_ref, grad_ref,
    dzq_ref, dzk_ref, gv_ref, dotq_ref, dotk_ref, gainq_ref, gaink_ref,
    dq_acc, dk_acc, dv_acc, bias_ref,
):
    fill_mask(bias_ref, segc_ref, segr_ref)
    dk_acc[...] = jnp.zeros_like(dk_acc)
    dv_acc[...] = jnp.zeros_like(dv_acc)
    for first in range(0, LEN, BQ):
        keys = first + BQ
        queries = qrot_ref[first:keys, :]
        grads = grad_ref[first:keys, :]
        scores = times_transposed(queries, krot_ref[:keys, :]) * SCORE_SCALE
        probs = jnp.exp(scores + bias_ref[first:keys, :keys] - log_ref[0, first:keys, :])
        delta = jnp.sum(
            grads.astype(F32) * att_ref[first:keys, :].astype(F32), axis=1, keepdims=True
        )
        grad_probs = times_transposed(grads, vb_ref[:keys, :])
        grad_scores = (probs * (grad_probs - delta) * SCORE_SCALE).astype(BF16)
        dq_acc[first:keys, :] = plain_dot(grad_scores, krot_ref[:keys, :])
        dk_acc[:keys, :] += left_transposed(grad_scores, queries)
        dv_acc[:keys, :] += left_transposed(probs.astype(BF16), grads)
    gv_ref[...] = dv_acc[...].astype(BF16)
    cosine, sine = cos_ref[...], sin_ref[...]

    def finish(acc, raw_ref, scale_ref, gain_ref, dz_ref, dot_ref, gain_grad_ref):
        grad_rot = acc[...]
        grad_norm = grad_rot * cosine - pltpu.roll(grad_rot, HD // 2, 1) * sine
        unit = raw_ref[...] * scale_ref[...]
        gain_grad_ref[...] = jnp.sum(grad_norm * unit, axis=0, keepdims=True)
        grad_unit = grad_norm * gain_ref[...]
        dz_ref[...] = grad_unit
        part = jnp.sum(grad_unit * unit, axis=1, keepdims=True)

        @pl.when(pl.program_id(0) == 0)
        def _():
            dot_ref[...] = part

        @pl.when(pl.program_id(0) > 0)
        def _():
            dot_ref[...] += part

    finish(dq_acc, q_ref, qs_ref, qg_ref, dzq_ref, dotq_ref, gainq_ref)
    finish(dk_acc, k_ref, ks_ref, kg_ref, dzk_ref, dotk_ref, gaink_ref)


def head_spec(offset):
    return pl.BlockSpec((LEN, HD), lambda h: (0, offset + h))


def whole_spec(shape):
    return pl.BlockSpec(shape, lambda h: (0,) * len(shape))


def gain_spec():
    return pl.BlockSpec((1, HD), lambda h: (0, h))


LOG_SPEC = pl.BlockSpec((1, LEN, 1), lambda h: (h, 0, 0))
COLUMN = (LEN, 1)
TABLE = (LEN, HD)


def attend_forward(qkv, scales, gains, tables, seg_col, seg_row, heads):
    width = heads * HD
    piece = jax.ShapeDtypeStruct((LEN, width), BF16)
    return pl.pallas_call(
        attend_forward_kernel,
        grid=(heads,),
        in_specs=[
            head_spec(0), head_spec(heads), head_spec(2 * heads),
            whole_spec(COLUMN), whole_spec(COLUMN), gain_spec(), gain_spec(),
            whole_spec(TABLE), whole_spec(TABLE), whole_spec(COLUMN), whole_spec((1, LEN)),
        ],
        out_specs=[head_spec(0)] * 4 + [LOG_SPEC],
        out_shape=[piece] * 4 + [jax.ShapeDtypeStruct((heads, LEN, 1), F32)],
        scratch_shapes=[pltpu.VMEM((LEN, LEN), F32)],
        compiler_params=pltpu.CompilerParams(vmem_limit_bytes=VMEM),
        cost_estimate=pl.CostEstimate(
            flops=heads * 4 * LEN * LEN * HD, bytes_accessed=LEN * width * 20, transcendentals=0
        ),
        name="attend_forward",
    )(qkv, qkv, qkv, *scales, *gains, *tables, seg_col, seg_row)


def attend_backward(qkv, scales, gains, tables, seg_col, seg_row, saved, grad_att, heads):
    width = heads * HD
    full = jax.ShapeDtypeStruct((LEN, width), F32)
    column = jax.ShapeDtypeStruct(COLUMN, F32)
    gain_row = jax.ShapeDtypeStruct((1, width), F32)
    return pl.pallas_call(
        attend_backward_kernel,
        grid=(heads,),
        in_specs=[
            head_spec(0), head_spec(heads),
            whole_spec(COLUMN), whole_spec(COLUMN), gain_spec(), gain_spec(),
            whole_spec(TABLE), whole_spec(TABLE), whole_spec(COLUMN), whole_spec((1, LEN)),
            head_spec(0), head_spec(0), head_spec(0), head_spec(0), LOG_SPEC, head_spec(0),
        ],
        out_specs=[
            head_spec(0), head_spec(0), head_spec(0),
            whole_spec(COLUMN), whole_spec(COLUMN), gain_spec(), gain_spec(),
        ],
        out_shape=[
            full, full, jax.ShapeDtypeStruct((LEN, width), BF16), column, column, gain_row, gain_row,
        ],
        scratch_shapes=[pltpu.VMEM((LEN, HD), F32)] * 3 + [pltpu.VMEM((LEN, LEN), F32)],
        compiler_params=pltpu.CompilerParams(vmem_limit_bytes=VMEM),
        cost_estimate=pl.CostEstimate(
            flops=heads * 10 * LEN * LEN * HD, bytes_accessed=LEN * width * 40, transcendentals=0
        ),
        name="attend_backward",
    )(qkv, qkv, *scales, *gains, *tables, seg_col, seg_row, *saved, grad_att)


def fetch_choice(idx_ref, refs, held_ref, sem):
    for number, ref in enumerate(refs):

        @pl.when(idx_ref[2] == number)
        def _():
            copy = pltpu.make_async_copy(ref, held_ref, sem)
            copy.start()
            copy.wait()


def half_tile(step, core, tiles):
    per_half = tiles // 2
    return ((core + step // per_half) % 2) * per_half + step % per_half


def forward_chunk_kernel(
    idx_ref, *refs, out_steps, tiles,
):
    own_ref, left1, left2, left3, right1, right2, right3 = refs[:7]
    wo_own_ref, wo_oth_ref, x_ref, gain_ref, wg_ref, wu_ref, wd_own_ref, wd_oth_ref = refs[7:15]
    raw_ref, scale_ref, hb_ref, gate_ref, up_ref, mixed_ref, part_ref, acc_ref, att_ref = refs[-9:]
    depth, out_tile = wo_own_ref.shape
    blocks, _, block = wd_own_ref.shape
    step = pl.program_id(0)
    core = idx_ref[1]

    @pl.when(step == 0)
    def _():
        quarter = own_ref.shape[1] // 2
        pieces = (
            own_ref[...], right1[...] + left3[...], right2[...] + left2[...], right3[...] + left1[...],
        )
        for half in range(2):
            for number, piece in enumerate(pieces):
                start = half * depth + number * quarter
                att_ref[:, start : start + quarter] = piece[:, half * quarter : (half + 1) * quarter]

    @pl.when(step < out_steps)
    def _():
        own = att_ref[:, pl.ds(pl.multiple_of(core * depth, depth), depth)]
        other = att_ref[:, pl.ds(pl.multiple_of((1 - core) * depth, depth), depth)]
        acc_ref[:, pl.ds(pl.multiple_of(step * out_tile, out_tile), out_tile)] = plain_dot(
            own, wo_own_ref[...]
        ) + plain_dot(other, wo_oth_ref[...])

    @pl.when(step == out_steps - 1)
    def _():
        raw = acc_ref[...]
        scale = lax.rsqrt(jnp.mean(raw * raw, axis=1, keepdims=True) + EPS)
        raw_ref[...] = raw.astype(BF16)
        scale_ref[...] = scale
        hb_ref[...] = (x_ref[...].astype(F32) + raw * scale * gain_ref[...]).astype(BF16)
        acc_ref[...] = jnp.zeros_like(acc_ref)

    def tile_work(wd_ref):
        hidden_b = hb_ref[...]
        gate = plain_dot(hidden_b, wg_ref[...])
        up = plain_dot(hidden_b, wu_ref[...])
        mixed = (gate * jax.nn.sigmoid(gate) * up).astype(BF16)
        gate_ref[...] = gate.astype(BF16)
        up_ref[...] = up.astype(BF16)
        mixed_ref[...] = mixed
        for j in range(blocks):
            acc_ref[:, j * block : (j + 1) * block] += plain_dot(mixed, wd_ref[j])

    @pl.when((step >= out_steps) & (step < out_steps + tiles // 2))
    def _():
        tile_work(wd_own_ref)

    @pl.when(step >= out_steps + tiles // 2)
    def _():
        tile_work(wd_oth_ref)

    @pl.when(step == out_steps + tiles - 1)
    def _():
        part_ref[...] = acc_ref[...].astype(BF16)


TILE = 512


def forward_chunk(index, attended, out_halves, block_input, gain, w_gate, w_up, down_halves, chunk, before):
    tokens, width = block_input.shape
    hidden = w_gate.shape[1]
    depth = out_halves[0].shape[0]
    blocks, _, block = down_halves[0].shape
    tiles = hidden // TILE
    out_steps = width // TILE

    def tile_of(j, idx):
        return half_tile(jnp.maximum(j - out_steps, 0), idx[1], tiles)

    rows = pl.BlockSpec((chunk, width), lambda j, idx: (idx[0], 0))
    out_half = pl.BlockSpec((depth, TILE), lambda j, idx: (0, jnp.minimum(j, out_steps - 1)))
    up_tile = pl.BlockSpec((width, TILE), lambda j, idx: (0, tile_of(j, idx)))
    down_own = pl.BlockSpec(
        (blocks, TILE, block), lambda j, idx: (0, jnp.clip(j - out_steps, 0, tiles // 2 - 1), 0)
    )
    down_oth = pl.BlockSpec(
        (blocks, TILE, block), lambda j, idx: (0, jnp.maximum(j - out_steps - tiles // 2, 0), 0)
    )
    act_tile = pl.BlockSpec((chunk, TILE), lambda j, idx: (idx[0], tile_of(j, idx)))
    before = tuple(before)
    return pl.pallas_call(
        functools.partial(forward_chunk_kernel, out_steps=out_steps, tiles=tiles),
        grid_spec=pltpu.PrefetchScalarGridSpec(
            num_scalar_prefetch=1,
            grid=(out_steps + tiles,),
            in_specs=[
                *[pl.BlockSpec((chunk, attended[0].shape[1]), lambda j, idx: (idx[0], 0))] * 7,
                out_half, out_half, rows, pl.BlockSpec((1, width), lambda j, idx: (0, 0)),
                up_tile, up_tile, down_own, down_oth,
            ] + [pl.BlockSpec(memory_space=pl.ANY)] * len(before),
            out_specs=[
                rows, pl.BlockSpec((chunk, 1), lambda j, idx: (idx[0], 0)), rows, act_tile, act_tile, act_tile,
                pl.BlockSpec((chunk, width), lambda j, idx: (0, 0)),
            ],
            scratch_shapes=[pltpu.VMEM((chunk, width), F32), pltpu.VMEM((chunk, 2 * depth), BF16)],
        ),
        out_shape=[
            jax.ShapeDtypeStruct((tokens, width), BF16),
            jax.ShapeDtypeStruct((tokens, 1), F32),
            jax.ShapeDtypeStruct((tokens, width), BF16),
            jax.ShapeDtypeStruct((tokens, hidden), BF16),
            jax.ShapeDtypeStruct((tokens, hidden), BF16),
            jax.ShapeDtypeStruct((tokens, hidden), BF16),
            jax.ShapeDtypeStruct((chunk, width), BF16),
        ],
        input_output_aliases={16 + i: i for i in range(len(before))},
        compiler_params=pltpu.CompilerParams(vmem_limit_bytes=VMEM),
        cost_estimate=pl.CostEstimate(
            flops=2 * chunk * width * (width + 3 * hidden),
            bytes_accessed=2 * width * (width + 3 * hidden),
            transcendentals=0,
        ),
        name="forward_chunk",
    )(index, *attended, *out_halves, block_input, gain, w_gate, w_up, *down_halves, *before)


def backward_chunk_kernel(
    idx_ref, grad_ref, mlp_gain_ref, gate_ref, up_ref, wg_ref, wu_ref, wd_own_ref, wd_oth_ref, *refs, tiles, choices,
):
    gdi_ref, gg_ref, gu_ref, part_ref, gain_grad_ref, acc_ref, down_ref, sem = refs[-8:]
    blocks, _, block = wd_own_ref.shape
    step = pl.program_id(0)

    @pl.when(step == 0)
    def _():
        fetch_choice(idx_ref, refs[:choices], down_ref, sem)
        down_raw = down_ref[...].astype(F32)
        down_scale = lax.rsqrt(jnp.mean(down_raw * down_raw, axis=1, keepdims=True) + EPS)
        unit = down_raw * down_scale
        grad_y = grad_ref[...].astype(F32)
        gain_grad_ref[...] = jnp.sum(grad_y * unit, axis=0, keepdims=True)
        grad_unit = grad_y * mlp_gain_ref[...]
        mean = jnp.mean(grad_unit * unit, axis=1, keepdims=True)
        gdi_ref[...] = (down_scale * (grad_unit - unit * mean)).astype(BF16)
        acc_ref[...] = jnp.zeros_like(acc_ref)

    def tile_work(wd_ref):
        grad_mixed = times_transposed(gdi_ref[:, :block], wd_ref[0])
        for j in range(1, blocks):
            grad_mixed += times_transposed(gdi_ref[:, j * block : (j + 1) * block], wd_ref[j])
        gate = gate_ref[...].astype(F32)
        sig = jax.nn.sigmoid(gate)
        grad_gate = (grad_mixed * up_ref[...].astype(F32) * sig * (1.0 + gate * (1.0 - sig))).astype(BF16)
        grad_up = (grad_mixed * (gate * sig)).astype(BF16)
        gg_ref[...] = grad_gate
        gu_ref[...] = grad_up
        acc_ref[...] += times_transposed(grad_gate, wg_ref[...]) + times_transposed(grad_up, wu_ref[...])

    @pl.when(step < tiles // 2)
    def _():
        tile_work(wd_own_ref)

    @pl.when(step >= tiles // 2)
    def _():
        tile_work(wd_oth_ref)

    @pl.when(step == tiles - 1)
    def _():
        part_ref[...] = acc_ref[...].astype(BF16)


def backward_chunk(
    index, down_rows, grad_output, mlp_gain, gate, up, w_gate, w_up, down_halves, chunk, before,
):
    tokens, width = grad_output.shape
    hidden = w_gate.shape[1]
    blocks, _, block = down_halves[0].shape
    tiles = hidden // TILE

    def tile_of(j, idx):
        return half_tile(j, idx[1], tiles)

    rows = pl.BlockSpec((chunk, width), lambda j, idx: (idx[0], 0))
    gain_row = pl.BlockSpec((1, width), lambda j, idx: (0, 0))
    up_tile = pl.BlockSpec((width, TILE), lambda j, idx: (0, tile_of(j, idx)))
    act_tile = pl.BlockSpec((chunk, TILE), lambda j, idx: (idx[0], tile_of(j, idx)))
    before = tuple(before)
    return pl.pallas_call(
        functools.partial(backward_chunk_kernel, tiles=tiles, choices=len(down_rows)),
        grid_spec=pltpu.PrefetchScalarGridSpec(
            num_scalar_prefetch=1,
            grid=(tiles,),
            in_specs=[
                rows, gain_row, act_tile, act_tile, up_tile, up_tile,
                pl.BlockSpec((blocks, TILE, block), lambda j, idx: (0, jnp.minimum(j, tiles // 2 - 1), 0)),
                pl.BlockSpec((blocks, TILE, block), lambda j, idx: (0, jnp.maximum(j - tiles // 2, 0), 0)),
            ] + [pl.BlockSpec(memory_space=pl.ANY)] * (len(down_rows) + len(before)),
            out_specs=[rows, act_tile, act_tile, pl.BlockSpec((chunk, width), lambda j, idx: (0, 0)), gain_row],
            scratch_shapes=[
                pltpu.VMEM((chunk, width), F32), pltpu.VMEM((chunk, width), BF16), pltpu.SemaphoreType.DMA(()),
            ],
        ),
        out_shape=[
            jax.ShapeDtypeStruct((tokens, width), BF16),
            jax.ShapeDtypeStruct((tokens, hidden), BF16),
            jax.ShapeDtypeStruct((tokens, hidden), BF16),
            jax.ShapeDtypeStruct((chunk, width), BF16),
            jax.ShapeDtypeStruct((1, width), F32),
        ],
        input_output_aliases={9 + len(down_rows) + i: i for i in range(len(before))},
        compiler_params=pltpu.CompilerParams(vmem_limit_bytes=VMEM),
        cost_estimate=pl.CostEstimate(
            flops=6 * chunk * width * hidden, bytes_accessed=6 * width * hidden, transcendentals=0
        ),
        name="backward_chunk",
    )(index, grad_output, mlp_gain, gate, up, w_gate, w_up, *down_halves, *down_rows, *before)


PARTS = 4


def attention_chunk_kernel(
    idx_ref, grad_ref, raw_ref, scale_ref, x_ref, attn_gain_ref, mlp_gain_ref, wo_own_ref, wo_oth_ref, *refs, choices,
):
    gai_ref, gatt_ref, out_ref, gain_grad_ref, mlp_held_ref, down_held_ref, sem = refs[-7:]
    half = wo_own_ref.shape[0]
    core = idx_ref[1]
    step = pl.program_id(0)

    @pl.when(step == 0)
    def _():
        fetch_choice(idx_ref, refs[:choices], mlp_held_ref, sem)
        fetch_choice(idx_ref, refs[choices : 2 * choices], down_held_ref, sem)
        gain_grad_ref[...] = jnp.zeros_like(gain_grad_ref)

    size = grad_ref.shape[0]
    here = pl.ds(pl.multiple_of(step * size, size), size)
    scale = scale_ref[...]
    unit = raw_ref[...].astype(F32) * scale
    grad_hidden = grad_ref[...].astype(F32) + mlp_held_ref[here, :].astype(F32)
    gain_grad_ref[...] += jnp.sum(grad_hidden * unit, axis=0, keepdims=True)
    grad_unit = grad_hidden * attn_gain_ref[...]
    mean = jnp.mean(grad_unit * unit, axis=1, keepdims=True)
    grad_attn_in = (scale * (grad_unit - unit * mean)).astype(BF16)
    gai_ref[...] = grad_attn_in
    for place, w_ref in ((core, wo_own_ref), (1 - core, wo_oth_ref)):
        gatt_ref[:, pl.ds(pl.multiple_of(place * half, half), half)] = times_transposed(
            grad_attn_in, w_ref[...]
        ).astype(BF16)
    down_raw = down_held_ref[here, :].astype(F32)
    down_scale = lax.rsqrt(jnp.mean(down_raw * down_raw, axis=1, keepdims=True) + EPS)
    hidden = x_ref[...].astype(F32) + unit * attn_gain_ref[...]
    out_ref[...] = (hidden + down_raw * down_scale * mlp_gain_ref[...]).astype(BF16)


def attention_chunk(
    index, mlp_rows, down_rows, grad_output, raw, scale, block_input, attn_gain, mlp_gain, out_halves, half, chunk,
    before,
):
    tokens, width = grad_output.shape
    size = chunk // PARTS
    rows = pl.BlockSpec((size, width), lambda j, idx: (PARTS * idx[0] + j, 0))
    gain_row = pl.BlockSpec((1, width), lambda j, idx: (0, 0))
    own_heads = pl.BlockSpec((half, width), lambda j, idx: (0, 0))
    before = tuple(before)
    chosen = (*mlp_rows, *down_rows)
    return pl.pallas_call(
        functools.partial(attention_chunk_kernel, choices=len(mlp_rows)),
        grid_spec=pltpu.PrefetchScalarGridSpec(
            num_scalar_prefetch=1,
            grid=(PARTS,),
            in_specs=[
                rows, rows, pl.BlockSpec((size, 1), lambda j, idx: (PARTS * idx[0] + j, 0)), rows, gain_row, gain_row,
                own_heads, own_heads,
            ] + [pl.BlockSpec(memory_space=pl.ANY)] * (len(chosen) + len(before)),
            out_specs=[
                rows, pl.BlockSpec((size, 2 * half), lambda j, idx: (PARTS * idx[0] + j, 0)), rows, gain_row,
            ],
            scratch_shapes=[
                pltpu.VMEM((chunk, width), BF16), pltpu.VMEM((chunk, width), BF16), pltpu.SemaphoreType.DMA(()),
            ],
        ),
        out_shape=[
            jax.ShapeDtypeStruct((tokens, width), BF16),
            jax.ShapeDtypeStruct((tokens, 2 * half), BF16),
            jax.ShapeDtypeStruct((tokens, width), BF16),
            jax.ShapeDtypeStruct((1, width), F32),
        ],
        input_output_aliases={9 + len(chosen) + i: i for i in range(len(before))},
        compiler_params=pltpu.CompilerParams(vmem_limit_bytes=VMEM),
        cost_estimate=pl.CostEstimate(
            flops=4 * chunk * width * half, bytes_accessed=16 * chunk * width, transcendentals=0
        ),
        name="attention_chunk",
    )(index, grad_output, raw, scale, block_input, attn_gain, mlp_gain, *out_halves, *chosen, *before)


def place_rows_kernel(idx_ref, *refs, choices):
    out_ref, held_ref, sem = refs[-3:]
    step = pl.program_id(0)

    @pl.when(step == 0)
    def _():
        fetch_choice(idx_ref, refs[:choices], held_ref, sem)

    size = out_ref.shape[0]
    out_ref[...] = held_ref[pl.ds(pl.multiple_of(step * size, size), size), :].astype(out_ref.dtype)


def place_rows(index, rows_in, tokens, dtype, before):
    chunk, width = rows_in[0].shape
    before = tuple(before)
    return pl.pallas_call(
        functools.partial(place_rows_kernel, choices=len(rows_in)),
        grid_spec=pltpu.PrefetchScalarGridSpec(
            num_scalar_prefetch=1,
            grid=(4,),
            in_specs=[pl.BlockSpec(memory_space=pl.ANY)] * (len(rows_in) + len(before)),
            out_specs=pl.BlockSpec((chunk // 4, width), lambda j, idx: (4 * idx[0] + j, 0)),
            scratch_shapes=[pltpu.VMEM((chunk, width), BF16), pltpu.SemaphoreType.DMA(())],
        ),
        out_shape=jax.ShapeDtypeStruct((tokens, width), dtype),
        input_output_aliases={1 + len(rows_in): 0} if before else {},
        compiler_params=pltpu.CompilerParams(vmem_limit_bytes=VMEM),
        cost_estimate=pl.CostEstimate(flops=0, bytes_accessed=6 * chunk * width, transcendentals=0),
        name="place_rows",
    )(index, *rows_in, *before)


def after(value, *tokens):
    return lax.optimization_barrier((value, tokens))[0]


def unset_kernel(out_ref):
    pass


def unset(shape, dtype):
    return pl.pallas_call(
        unset_kernel,
        out_specs=pl.BlockSpec(memory_space=pl.ANY),
        out_shape=jax.ShapeDtypeStruct(shape, dtype),
        name="unset",
    )()


def shards(
    sizes,
    block_input,
    segment_ids,
    positions,
    w_query,
    w_key,
    w_value,
    w_out,
    w_gate,
    w_up,
    w_down,
    query_gain,
    key_gain,
    attn_gain,
    mlp_gain,
    grad_output,
):
    cores, rows, cols = sizes
    tokens_here, width = block_input.shape
    assert tokens_here == LEN and cores == 2 and cols == 4
    local_width = w_query.shape[1]
    half_width = local_width // 2
    heads = local_width // HD
    chunk = tokens_here // cols
    core = lax.axis_index("dp")
    row = lax.axis_index("row")
    col = lax.axis_index("col")
    swap = [(0, 1), (1, 0)]
    attn_row, mlp_row = attn_gain[None, :], mlp_gain[None, :]

    def own_half(array, axis):
        half = array.shape[axis] // 2
        return lax.dynamic_slice_in_dim(array, core * half, half, axis)

    def other_half(array, axis):
        half = array.shape[axis] // 2
        return lax.dynamic_slice_in_dim(array, (1 - core) * half, half, axis)

    def gather(weight, axis):
        return lax.all_gather(own_half(weight, axis), ("row", "dp"), axis=axis, tiled=True)

    def line_step(from_left, from_right, step):
        from_left = lax.ppermute(from_left, "col", [(i, i + 1) for i in range(step - 1, cols - 1)])
        from_right = lax.ppermute(from_right, "col", [(i + 1, i) for i in range(cols - step)])
        return from_left, from_right

    def sum_step(up, down, step):
        up = lax.ppermute(up, "col", [(i, i + 1) for i in range(step)])
        down = lax.ppermute(down, "col", [(cols - 1 - i, cols - 2 - i) for i in range(step)])
        return up, down

    def pick(at_zero, at_one, at_two, at_three):
        low = jnp.where(col == 0, at_zero, at_one)
        high = jnp.where(col == 2, at_two, at_three)
        return jnp.where(col < 2, low, high)

    slot_chunk = [pick(3, 3, 0, 0), pick(2, 2, 1, 1), pick(1, 0, 3, 2), col]
    slot_index = [
        jnp.stack([one, core, choice]).astype(jnp.int32)
        for one, choice in zip(slot_chunk, (col, col, col % 2, 0 * col))
    ]

    def slot_rows(array, slot):
        return lax.dynamic_slice_in_dim(array, slot_chunk[slot] * chunk, chunk, 0)

    def gather_slots(own, work):
        left, right, token = [own], [own], ()
        arrived = (
            lambda lefts, rights: (lefts[0],),
            lambda lefts, rights: (rights[1], lefts[1]),
            lambda lefts, rights: (rights[2], rights[1], lefts[1], lefts[2]),
            lambda lefts, rights: (rights[3], rights[2], lefts[2], lefts[3]),
        )
        for step in range(1, cols + 1):
            seen = tuple(left), tuple(right)
            if step < cols:
                from_left, from_right = line_step(left[-1], right[-1], step)
                left.append(from_left)
                right.append(from_right)
            token = work(cols - step, arrived[step - 1](*after(seen, token)))

    def sum_slots(make, window=lambda step, gate: ()):
        def at(step, gate):
            window(step, gate)
            return make(step, gate)

        first = make(0, ())
        up, down = sum_step(first, first, 1)
        second = at(1, first)
        up = jnp.where(col == 0, second, first) + up
        down = jnp.where(col == 3, second, first) + down
        gate = (up, down)
        up, down = sum_step(up, down, 2)
        third = at(2, gate)
        up = jnp.where(col == 1, second, third) + up
        down = jnp.where(col == 2, second, third) + down
        gate = (up, down)
        up, down = sum_step(up, down, 3)
        fourth = lax.optimization_barrier(at(3, gate))
        return fourth.astype(F32) + up.astype(F32) + down.astype(F32)

    def both_cores(half, axis):
        other = lax.ppermute(half, "dp", swap)
        first = jnp.where(core == 0, half, other)
        second = jnp.where(core == 0, other, half)
        return jnp.concatenate([first, second], axis=axis).astype(F32)

    def sum_sent(left_mat, right_other):
        return lax.ppermute(left_transposed(left_mat, right_other).astype(BF16), "dp", swap)

    def sum_kept(left_mat, right_own, got):
        total = (left_transposed(left_mat, right_own) + got.astype(F32)).astype(BF16)
        return total, lax.psum_scatter(total, "row", scatter_dimension=0, tiled=True)

    by_x = [(0, 1), (1, 0), (2, 3), (3, 2)]
    by_y = [(0, 2), (2, 0), (1, 3), (3, 1)]

    def row_first(half):
        if rows != 4:
            return (half,)
        return half, lax.ppermute(half, "row", by_x), lax.ppermute(half, "row", by_y)

    def row_second(pieces):
        if rows != 4:
            return pieces
        middle = pieces[0].shape[0] // 2
        return (
            *pieces,
            lax.ppermute(pieces[1][:middle], "row", by_y),
            lax.ppermute(pieces[2][middle:], "row", by_x),
        )

    def row_blocks(pieces):
        if rows != 4:
            whole = lax.all_gather(pieces[0], ("row", "dp"), axis=0, tiled=False)
            whole = whole.reshape(rows, cores, *pieces[0].shape)
            return tuple(lax.dynamic_index_in_dim(whole, one, 1, keepdims=False) for one in (core, 1 - core))
        own, by_one, by_two, corner_top, corner_low = pieces
        middle = own.shape[0] // 2
        held = unset((rows, *own.shape), own.dtype)
        for piece, block, start in (
            (own, row, 0), (by_one, row ^ 1, 0), (by_two, row ^ 2, 0),
            (corner_top, row ^ 3, 0), (corner_low, row ^ 3, middle),
        ):
            held = lax.dynamic_update_slice(held, piece[None], (block, start, 0))
        return held, lax.ppermute(held, "dp", swap)

    def row_columns(pieces):
        if rows != 4:
            return lax.all_gather(pieces[0], "row", axis=1, tiled=True)
        own, by_one, by_two, corner_top, corner_low = pieces
        height, block = own.shape
        held = unset((height, rows * block), own.dtype)
        for piece, number, start in (
            (own, row, 0), (by_one, row ^ 1, 0), (by_two, row ^ 2, 0),
            (corner_top, row ^ 3, 0), (corner_low, row ^ 3, height // 2),
        ):
            held = lax.dynamic_update_slice(held, piece, (start, number * block))
        return held

    full_qkv = gather(jnp.concatenate([w_query, w_key, w_value], axis=1), 0)
    full_gate = gather(w_gate, 0)
    full_up = gather(w_up, 0)
    out_pieces = row_first(own_half(w_out, 0))
    out_pieces = row_second(out_pieces)
    out_own = row_columns(out_pieces)
    out_left, out_right = [out_own], [out_own]
    for step in range(1, cols):
        one, two = line_step(out_left[-1], out_right[-1], step)
        out_left.append(one)
        out_right.append(two)
    down_pieces = row_first(after(own_half(w_down, 0), full_qkv))

    qkv = plain_dot(block_input, full_qkv)
    query_raw, key_raw = qkv[:, :local_width], qkv[:, local_width : 2 * local_width]
    query_sq, key_sq = lax.psum(
        (jnp.sum(query_raw * query_raw, axis=1), jnp.sum(key_raw * key_raw, axis=1)), "col"
    )
    query_scale = lax.rsqrt(query_sq / width + EPS)[:, None]
    key_scale = lax.rsqrt(key_sq / width + EPS)[:, None]
    scales = (query_scale, key_scale)
    gains = (query_gain[None, :], key_gain[None, :])
    tables = rope_tables(positions)
    seg_col, seg_row = segment_ids[:, None], segment_ids[None, :]
    query_rot, key_rot, value_heads, attended, log_total = attend_forward(
        qkv, scales, gains, tables, seg_col, seg_row, heads
    )

    lefts, rights = [attended], [attended]
    for step in range(1, cols):
        from_left, from_right = line_step(lefts[-1], rights[-1], step)
        lefts.append(from_left)
        rights.append(from_right)
        if step == 1:
            out_halves = jnp.concatenate(
                [out_own] + [out_right[k] + out_left[cols - k] for k in range(1, cols)], axis=0
            )
            out_halves = (out_halves, lax.ppermute(out_halves, "dp", swap))
        if step == 2:
            down_pieces = row_second(after(down_pieces, lefts[1], rights[1]))
        if step == 3:
            down_halves = row_blocks(down_pieces)
    attended_all = (attended, *lefts[1:], *rights[1:])

    held = dict(forward=(), backward=(), attention=(), output=())
    gain_sums = dict(mlp=0.0, attn=0.0)

    def forward_work(slot, gate):
        results = forward_chunk(
            slot_index[slot], after(attended_all, gate), out_halves, block_input, attn_row, full_gate, full_up,
            down_halves, chunk, held["forward"],
        )
        held["forward"] = results[:6]
        return results[6]

    down_own = sum_slots(forward_work).astype(BF16)
    attn_raw, attn_scale, hidden_b, gate_proj, up_proj, mixed_act = held["forward"]
    mlp_parts = [None] * cols
    down_slots = [None] * cols

    def backward_work(slot, down_rows):
        down_slots[slot] = down_rows
        results = backward_chunk(
            slot_index[slot], down_rows, grad_output, mlp_row, gate_proj, up_proj, full_gate, full_up,
            down_halves, chunk, held["backward"],
        )
        held["backward"] = results[:3]
        mlp_parts[slot] = results[3]
        gain_sums["mlp"] = gain_sums["mlp"] + results[4]
        return results[3]

    gather_slots(down_own, backward_work)
    grad_down_in, grad_gate_in, grad_up_in = held["backward"]

    blocks = {}
    got = {}

    def mlp_window(step, gate):
        down_left, down_right, hidden_left, gate_right, up_right = after(
            (grad_down_in, mixed_act, hidden_b, grad_gate_in, grad_up_in), gate
        )
        if step == 1:
            got["down"] = sum_sent(down_left, other_half(down_right, 1))
            got["gate"] = sum_sent(hidden_left, other_half(gate_right, 1))
            return got["down"], got["gate"]
        if step == 2:
            blocks["down"] = sum_kept(down_left, own_half(down_right, 1), got["down"])
            got["up"] = sum_sent(hidden_left, other_half(up_right, 1))
            return blocks["down"][0], got["up"]
        blocks["gate"] = sum_kept(hidden_left, own_half(gate_right, 1), got["gate"])
        return blocks["gate"][0]

    mlp_own = sum_slots(lambda slot, gate: mlp_parts[slot], mlp_window).astype(BF16)

    def attention_work(slot, mlp_rows):
        results = attention_chunk(
            slot_index[slot], mlp_rows, down_slots[slot], grad_output, attn_raw, attn_scale, block_input, attn_row,
            mlp_row, out_halves, half_width, chunk, held["attention"],
        )
        held["attention"] = results[:3]
        gain_sums["attn"] = gain_sums["attn"] + results[3]
        if slot == 3:
            hidden_left, up_right = after((hidden_b, grad_up_in), mlp_rows[0])
            blocks["up"] = sum_kept(hidden_left, own_half(up_right, 1), got["up"])
        return results[1]

    gather_slots(mlp_own, attention_work)
    grad_attn_in, grad_att, block_output = held["attention"]
    own_grad_hidden = slot_rows(grad_output, 3).astype(F32) + mlp_own.astype(F32)

    query_dz, key_dz, grad_value_in, query_dot, key_dot, grad_query_gain, grad_key_gain = attend_backward(
        qkv, scales, gains, tables, seg_col, seg_row,
        (query_rot, key_rot, value_heads, attended, log_total), grad_att, heads,
    )
    query_dot, key_dot = lax.psum((query_dot[:, 0], key_dot[:, 0]), "col")
    grad_query_in = (
        query_scale * (query_dz - query_raw * query_scale * (query_dot / width)[:, None])
    ).astype(BF16)
    grad_key_in = (
        key_scale * (key_dz - key_raw * key_scale * (key_dot / width)[:, None])
    ).astype(BF16)
    grad_qkv = jnp.concatenate([grad_query_in, grad_key_in, grad_value_in], axis=1)
    gain_pack = jnp.concatenate([grad_query_gain, grad_key_gain, gain_sums["attn"], gain_sums["mlp"]], axis=1)

    def interleaved(picker, pieces_in):
        return jnp.concatenate([picker(one, 1) for one in pieces_in], axis=1)

    def input_window(step, gate):
        nonlocal gain_pack
        pack, *pieces_in, tokens_in, left_out, right_out = after(
            (gain_pack, grad_query_in, grad_key_in, grad_value_in, block_input, grad_attn_in, attended), gate
        )
        if step == 1:
            got["qkv"] = sum_sent(tokens_in, interleaved(other_half, pieces_in))
            got["out"] = sum_sent(left_out, other_half(right_out, 1))
            gain_pack = pack + lax.ppermute(pack, "dp", swap)
            return got["qkv"], got["out"], gain_pack
        if step == 2:
            blocks["qkv"] = sum_kept(tokens_in, interleaved(own_half, pieces_in), got["qkv"])
            if rows == 4:
                gain_pack = pack + lax.ppermute(pack, "row", by_x)
            return blocks["qkv"][0], gain_pack
        blocks["out"] = sum_kept(left_out, own_half(right_out, 1), got["out"])
        gain_pack = pack + lax.ppermute(pack, "row", by_y) if rows == 4 else lax.psum(pack, "row")
        return blocks["out"][0], gain_pack

    input_own = sum_slots(
        lambda slot, gate: times_transposed(after(slot_rows(grad_qkv, slot), gate), full_qkv).astype(BF16), input_window
    )

    results = {}
    quarter = local_width // 2

    def projection(index):
        pair = both_cores(blocks["qkv"][1][None, :, index * quarter : (index + 1) * quarter], 0)
        return jnp.concatenate([pair[0], pair[1]], axis=1)

    def output_work(slot, rows_in):
        held["output"] = (place_rows(slot_index[slot], rows_in, tokens_here, F32, held["output"]),)
        if slot == 3:
            results["down"] = jnp.transpose(both_cores(blocks["down"][1], 1))
            results["gate"] = both_cores(blocks["gate"][1], 1)
            return held["output"], results["down"], results["gate"]
        if slot == 2:
            results["up"] = both_cores(blocks["up"][1], 1)
            return held["output"], results["up"]
        if slot == 1:
            results["out"] = jnp.transpose(both_cores(blocks["out"][1], 1))
            results["qkv"] = [projection(index) for index in range(3)]
            return held["output"], results["out"], results["qkv"]
        return held["output"]

    gather_slots((own_grad_hidden + input_own).astype(BF16), output_work)
    ends = (local_width, 2 * local_width, 2 * local_width + width)
    gain_grads = jnp.split(gain_pack[0], ends)
    return (
        block_output,
        held["output"][0],
        *results["qkv"],
        results["out"],
        results["gate"],
        results["up"],
        results["down"],
        *gain_grads,
    )


def layer(sizes, *arrays):
    return shards(sizes, *arrays)


def solution(mesh):
    in_specs = (
        P(("dp", "row"), None),
        P(("dp", "row")),
        P(("dp", "row")),
        P("row", "col"),
        P("row", "col"),
        P("row", "col"),
        P("col", "row"),
        P("row", "col"),
        P("row", "col"),
        P("col", "row"),
        P("col"),
        P("col"),
        P(),
        P(),
        P(("dp", "row"), None),
    )
    out_specs = (
        P(("dp", "row"), None),
        P(("dp", "row"), None),
        P("row", "col"),
        P("row", "col"),
        P("row", "col"),
        P("col", "row"),
        P("row", "col"),
        P("row", "col"),
        P("col", "row"),
        P("col"),
        P("col"),
        P(),
        P(),
    )
    sizes = (mesh.shape["dp"], mesh.shape["row"], mesh.shape["col"])
    return jax.shard_map(
        functools.partial(layer, sizes), mesh=mesh, in_specs=in_specs, out_specs=out_specs, check_vma=False
    )
```

```python
import functools

import jax
import jax.numpy as jnp
from jax import lax
from jax.experimental import pallas as pl
from jax.experimental.pallas import tpu as pltpu
from jax.sharding import PartitionSpec as P


HD = 128
LEN = 1024
BQ = 256
VMEM = 60 << 20

EPS = 1e-06
THETA = 500000.0
NEG_FILL = -1e30
SCORE_SCALE = HD ** (-0.5)
F32 = jnp.float32
BF16 = jnp.bfloat16


def plain_dot(left_mat, right_mat):
    return jnp.dot(left_mat, right_mat, preferred_element_type=F32)


def times_transposed(left_mat, right_mat):
    return lax.dot_general(
        left_mat, right_mat, (((1,), (1,)), ((), ())), preferred_element_type=F32
    )


def left_transposed(left_mat, right_mat):
    return lax.dot_general(
        left_mat, right_mat, (((0,), (0,)), ((), ())), preferred_element_type=F32
    )


def rope_tables(positions):
    half_dim = HD // 2
    inv_freq = THETA ** (-(jnp.arange(half_dim, dtype=F32) * 2.0) / HD)
    angles = positions.astype(F32)[:, None] * inv_freq[None, :]
    cos_half, sin_half = jnp.cos(angles), jnp.sin(angles)
    cosine = jnp.concatenate([cos_half, cos_half], axis=-1)
    sine_signed = jnp.concatenate([-sin_half, sin_half], axis=-1)
    return cosine, sine_signed


def fill_mask(bias_ref, seg_col_ref, seg_row_ref):
    @pl.when(pl.program_id(0) == 0)
    def _():
        for first in range(0, LEN, BQ):
            keys = first + BQ
            rows = seg_col_ref[first:keys, :]
            cols = seg_row_ref[:, :keys]
            query_index = first + lax.broadcasted_iota(jnp.int32, (BQ, keys), 0)
            key_index = lax.broadcasted_iota(jnp.int32, (BQ, keys), 1)
            allowed = (rows == cols) & (key_index <= query_index)
            bias_ref[first:keys, :keys] = jnp.where(allowed, 0.0, NEG_FILL)


def attend_forward_kernel(
    q_ref, k_ref, v_ref, qs_ref, ks_ref, qg_ref, kg_ref, cos_ref, sin_ref, segc_ref, segr_ref,
    qrot_ref, krot_ref, vb_ref, att_ref, log_ref, bias_ref,
):
    fill_mask(bias_ref, segc_ref, segr_ref)
    cosine, sine = cos_ref[...], sin_ref[...]

    def turned(raw, scale, gain):
        norm = raw * scale * gain
        return (norm * cosine + pltpu.roll(norm, HD // 2, 1) * sine).astype(BF16)

    qrot_ref[...] = turned(q_ref[...], qs_ref[...], qg_ref[...])
    krot_ref[...] = turned(k_ref[...], ks_ref[...], kg_ref[...])
    vb_ref[...] = v_ref[...].astype(BF16)
    for first in range(0, LEN, BQ):
        keys = first + BQ
        scores = times_transposed(qrot_ref[first:keys, :], krot_ref[:keys, :]) * SCORE_SCALE
        masked = scores + bias_ref[first:keys, :keys]
        peak = jnp.max(masked, axis=1, keepdims=True)
        weight = jnp.exp(masked - peak)
        total = jnp.sum(weight, axis=1, keepdims=True)
        probs = (weight * (1.0 / total)).astype(BF16)
        att_ref[first:keys, :] = plain_dot(probs, vb_ref[:keys, :]).astype(BF16)
        log_ref[0, first:keys, :] = peak + jnp.log(total)


def attend_backward_kernel(
    q_ref, k_ref, qs_ref, ks_ref, qg_ref, kg_ref, cos_ref, sin_ref, segc_ref, segr_ref,
    qrot_ref, krot_ref, vb_ref, att_ref, log_ref, grad_ref,
    dzq_ref, dzk_ref, gv_ref, dotq_ref, dotk_ref, gainq_ref, gaink_ref,
    dq_acc, dk_acc, dv_acc, bias_ref,
):
    fill_mask(bias_ref, segc_ref, segr_ref)
    dk_acc[...] = jnp.zeros_like(dk_acc)
    dv_acc[...] = jnp.zeros_like(dv_acc)
    for first in range(0, LEN, BQ):
        keys = first + BQ
        queries = qrot_ref[first:keys, :]
        grads = grad_ref[first:keys, :]
        scores = times_transposed(queries, krot_ref[:keys, :]) * SCORE_SCALE
        probs = jnp.exp(scores + bias_ref[first:keys, :keys] - log_ref[0, first:keys, :])
        delta = jnp.sum(
            grads.astype(F32) * att_ref[first:keys, :].astype(F32), axis=1, keepdims=True
        )
        grad_probs = times_transposed(grads, vb_ref[:keys, :])
        grad_scores = (probs * (grad_probs - delta) * SCORE_SCALE).astype(BF16)
        dq_acc[first:keys, :] = plain_dot(grad_scores, krot_ref[:keys, :])
        dk_acc[:keys, :] += left_transposed(grad_scores, queries)
        dv_acc[:keys, :] += left_transposed(probs.astype(BF16), grads)
    gv_ref[...] = dv_acc[...].astype(BF16)
    cosine, sine = cos_ref[...], sin_ref[...]

    def finish(acc, raw_ref, scale_ref, gain_ref, dz_ref, dot_ref, gain_grad_ref):
        grad_rot = acc[...]
        grad_norm = grad_rot * cosine - pltpu.roll(grad_rot, HD // 2, 1) * sine
        unit = raw_ref[...] * scale_ref[...]
        gain_grad_ref[...] = jnp.sum(grad_norm * unit, axis=0, keepdims=True)
        grad_unit = grad_norm * gain_ref[...]
        dz_ref[...] = grad_unit
        part = jnp.sum(grad_unit * unit, axis=1, keepdims=True)

        @pl.when(pl.program_id(0) == 0)
        def _():
            dot_ref[...] = part

        @pl.when(pl.program_id(0) > 0)
        def _():
            dot_ref[...] += part

    finish(dq_acc, q_ref, qs_ref, qg_ref, dzq_ref, dotq_ref, gainq_ref)
    finish(dk_acc, k_ref, ks_ref, kg_ref, dzk_ref, dotk_ref, gaink_ref)


def head_spec(offset):
    return pl.BlockSpec((LEN, HD), lambda h: (0, offset + h))


def whole_spec(shape):
    return pl.BlockSpec(shape, lambda h: (0,) * len(shape))


def gain_spec():
    return pl.BlockSpec((1, HD), lambda h: (0, h))


LOG_SPEC = pl.BlockSpec((1, LEN, 1), lambda h: (h, 0, 0))
COLUMN = (LEN, 1)
TABLE = (LEN, HD)


def attend_forward(qkv, scales, gains, tables, seg_col, seg_row, heads):
    width = heads * HD
    piece = jax.ShapeDtypeStruct((LEN, width), BF16)
    return pl.pallas_call(
        attend_forward_kernel,
        grid=(heads,),
        in_specs=[
            head_spec(0), head_spec(heads), head_spec(2 * heads),
            whole_spec(COLUMN), whole_spec(COLUMN), gain_spec(), gain_spec(),
            whole_spec(TABLE), whole_spec(TABLE), whole_spec(COLUMN), whole_spec((1, LEN)),
        ],
        out_specs=[head_spec(0)] * 4 + [LOG_SPEC],
        out_shape=[piece] * 4 + [jax.ShapeDtypeStruct((heads, LEN, 1), F32)],
        scratch_shapes=[pltpu.VMEM((LEN, LEN), F32)],
        compiler_params=pltpu.CompilerParams(vmem_limit_bytes=VMEM),
        cost_estimate=pl.CostEstimate(
            flops=heads * 4 * LEN * LEN * HD, bytes_accessed=LEN * width * 20, transcendentals=0
        ),
        name="attend_forward",
    )(qkv, qkv, qkv, *scales, *gains, *tables, seg_col, seg_row)


def attend_backward(qkv, scales, gains, tables, seg_col, seg_row, saved, grad_att, heads):
    width = heads * HD
    full = jax.ShapeDtypeStruct((LEN, width), F32)
    column = jax.ShapeDtypeStruct(COLUMN, F32)
    gain_row = jax.ShapeDtypeStruct((1, width), F32)
    return pl.pallas_call(
        attend_backward_kernel,
        grid=(heads,),
        in_specs=[
            head_spec(0), head_spec(heads),
            whole_spec(COLUMN), whole_spec(COLUMN), gain_spec(), gain_spec(),
            whole_spec(TABLE), whole_spec(TABLE), whole_spec(COLUMN), whole_spec((1, LEN)),
            head_spec(0), head_spec(0), head_spec(0), head_spec(0), LOG_SPEC, head_spec(0),
        ],
        out_specs=[
            head_spec(0), head_spec(0), head_spec(0),
            whole_spec(COLUMN), whole_spec(COLUMN), gain_spec(), gain_spec(),
        ],
        out_shape=[
            full, full, jax.ShapeDtypeStruct((LEN, width), BF16), column, column, gain_row, gain_row,
        ],
        scratch_shapes=[pltpu.VMEM((LEN, HD), F32)] * 3 + [pltpu.VMEM((LEN, LEN), F32)],
        compiler_params=pltpu.CompilerParams(vmem_limit_bytes=VMEM),
        cost_estimate=pl.CostEstimate(
            flops=heads * 10 * LEN * LEN * HD, bytes_accessed=LEN * width * 40, transcendentals=0
        ),
        name="attend_backward",
    )(qkv, qkv, *scales, *gains, *tables, seg_col, seg_row, *saved, grad_att)


def fetch_choice(idx_ref, refs, held_ref, sem):
    for number, ref in enumerate(refs):

        @pl.when(idx_ref[2] == number)
        def _():
            copy = pltpu.make_async_copy(ref, held_ref, sem)
            copy.start()
            copy.wait()


def half_tile(step, core, tiles):
    per_half = tiles // 2
    return ((core + step // per_half) % 2) * per_half + step % per_half


def forward_chunk_kernel(
    idx_ref, *refs, out_steps, tiles,
):
    own_ref, left1, left2, left3, right1, right2, right3 = refs[:7]
    wo_own_ref, wo_oth_ref, x_ref, gain_ref, wg_ref, wu_ref, wd_own_ref, wd_oth_ref = refs[7:15]
    raw_ref, scale_ref, hb_ref, gate_ref, up_ref, mixed_ref, part_ref, acc_ref, att_ref = refs[-9:]
    depth, out_tile = wo_own_ref.shape
    blocks, _, block = wd_own_ref.shape
    step = pl.program_id(0)
    core = idx_ref[1]

    @pl.when(step == 0)
    def _():
        quarter = own_ref.shape[1] // 2
        pieces = (
            own_ref[...], right1[...] + left3[...], right2[...] + left2[...], right3[...] + left1[...],
        )
        for half in range(2):
            for number, piece in enumerate(pieces):
                start = half * depth + number * quarter
                att_ref[:, start : start + quarter] = piece[:, half * quarter : (half + 1) * quarter]

    @pl.when(step < out_steps)
    def _():
        own = att_ref[:, pl.ds(pl.multiple_of(core * depth, depth), depth)]
        other = att_ref[:, pl.ds(pl.multiple_of((1 - core) * depth, depth), depth)]
        acc_ref[:, pl.ds(pl.multiple_of(step * out_tile, out_tile), out_tile)] = plain_dot(
            own, wo_own_ref[...]
        ) + plain_dot(other, wo_oth_ref[...])

    @pl.when(step == out_steps - 1)
    def _():
        raw = acc_ref[...]
        scale = lax.rsqrt(jnp.mean(raw * raw, axis=1, keepdims=True) + EPS)
        raw_ref[...] = raw.astype(BF16)
        scale_ref[...] = scale
        hb_ref[...] = (x_ref[...].astype(F32) + raw * scale * gain_ref[...]).astype(BF16)
        acc_ref[...] = jnp.zeros_like(acc_ref)

    def tile_work(wd_ref):
        hidden_b = hb_ref[...]
        gate = plain_dot(hidden_b, wg_ref[...])
        up = plain_dot(hidden_b, wu_ref[...])
        mixed = (gate * jax.nn.sigmoid(gate) * up).astype(BF16)
        gate_ref[...] = gate.astype(BF16)
        up_ref[...] = up.astype(BF16)
        mixed_ref[...] = mixed
        for j in range(blocks):
            acc_ref[:, j * block : (j + 1) * block] += plain_dot(mixed, wd_ref[j])

    @pl.when((step >= out_steps) & (step < out_steps + tiles // 2))
    def _():
        tile_work(wd_own_ref)

    @pl.when(step >= out_steps + tiles // 2)
    def _():
        tile_work(wd_oth_ref)

    @pl.when(step == out_steps + tiles - 1)
    def _():
        part_ref[...] = acc_ref[...].astype(BF16)


TILE = 512


def forward_chunk(index, attended, out_halves, block_input, gain, w_gate_up, down_halves, chunk, before):
    tokens, width = block_input.shape
    hidden = w_gate_up.shape[1] // 2
    depth = out_halves[0].shape[0]
    blocks, _, block = down_halves[0].shape
    tiles = hidden // TILE
    out_steps = width // TILE

    def tile_of(j, idx):
        return half_tile(jnp.maximum(j - out_steps, 0), idx[1], tiles)

    rows = pl.BlockSpec((chunk, width), lambda j, idx: (idx[0], 0))
    out_half = pl.BlockSpec((depth, TILE), lambda j, idx: (0, jnp.minimum(j, out_steps - 1)))
    gate_tile = pl.BlockSpec((width, TILE), lambda j, idx: (0, tile_of(j, idx)))
    up_tile = pl.BlockSpec((width, TILE), lambda j, idx: (0, tiles + tile_of(j, idx)))
    down_own = pl.BlockSpec(
        (blocks, TILE, block), lambda j, idx: (0, jnp.clip(j - out_steps, 0, tiles // 2 - 1), 0)
    )
    down_oth = pl.BlockSpec(
        (blocks, TILE, block), lambda j, idx: (0, jnp.maximum(j - out_steps - tiles // 2, 0), 0)
    )
    act_tile = pl.BlockSpec((chunk, TILE), lambda j, idx: (idx[0], tile_of(j, idx)))
    before = tuple(before)
    return pl.pallas_call(
        functools.partial(forward_chunk_kernel, out_steps=out_steps, tiles=tiles),
        grid_spec=pltpu.PrefetchScalarGridSpec(
            num_scalar_prefetch=1,
            grid=(out_steps + tiles,),
            in_specs=[
                *[pl.BlockSpec((chunk, attended[0].shape[1]), lambda j, idx: (idx[0], 0))] * 7,
                out_half, out_half, rows, pl.BlockSpec((1, width), lambda j, idx: (0, 0)),
                gate_tile, up_tile, down_own, down_oth,
            ] + [pl.BlockSpec(memory_space=pl.ANY)] * len(before),
            out_specs=[
                rows, pl.BlockSpec((chunk, 1), lambda j, idx: (idx[0], 0)), rows, act_tile, act_tile, act_tile,
                pl.BlockSpec((chunk, width), lambda j, idx: (0, 0)),
            ],
            scratch_shapes=[pltpu.VMEM((chunk, width), F32), pltpu.VMEM((chunk, 2 * depth), BF16)],
        ),
        out_shape=[
            jax.ShapeDtypeStruct((tokens, width), BF16),
            jax.ShapeDtypeStruct((tokens, 1), F32),
            jax.ShapeDtypeStruct((tokens, width), BF16),
            jax.ShapeDtypeStruct((tokens, hidden), BF16),
            jax.ShapeDtypeStruct((tokens, hidden), BF16),
            jax.ShapeDtypeStruct((tokens, hidden), BF16),
            jax.ShapeDtypeStruct((chunk, width), BF16),
        ],
        input_output_aliases={16 + i: i for i in range(len(before))},
        compiler_params=pltpu.CompilerParams(vmem_limit_bytes=VMEM),
        cost_estimate=pl.CostEstimate(
            flops=2 * chunk * width * (width + 3 * hidden),
            bytes_accessed=2 * width * (width + 3 * hidden),
            transcendentals=0,
        ),
        name="forward_chunk",
    )(index, *attended, *out_halves, block_input, gain, w_gate_up, w_gate_up, *down_halves, *before)


def backward_chunk_kernel(
    idx_ref, grad_ref, mlp_gain_ref, gate_ref, up_ref, wg_ref, wu_ref, wd_own_ref, wd_oth_ref, *refs, tiles, choices,
):
    gdi_ref, gg_ref, gu_ref, part_ref, gain_grad_ref, acc_ref, down_ref, sem = refs[-8:]
    blocks, _, block = wd_own_ref.shape
    step = pl.program_id(0)

    @pl.when(step == 0)
    def _():
        fetch_choice(idx_ref, refs[:choices], down_ref, sem)
        down_raw = down_ref[...].astype(F32)
        down_scale = lax.rsqrt(jnp.mean(down_raw * down_raw, axis=1, keepdims=True) + EPS)
        unit = down_raw * down_scale
        grad_y = grad_ref[...].astype(F32)
        gain_grad_ref[...] = jnp.sum(grad_y * unit, axis=0, keepdims=True)
        grad_unit = grad_y * mlp_gain_ref[...]
        mean = jnp.mean(grad_unit * unit, axis=1, keepdims=True)
        gdi_ref[...] = (down_scale * (grad_unit - unit * mean)).astype(BF16)
        acc_ref[...] = jnp.zeros_like(acc_ref)

    def tile_work(wd_ref):
        grad_mixed = times_transposed(gdi_ref[:, :block], wd_ref[0])
        for j in range(1, blocks):
            grad_mixed += times_transposed(gdi_ref[:, j * block : (j + 1) * block], wd_ref[j])
        gate = gate_ref[...].astype(F32)
        sig = jax.nn.sigmoid(gate)
        grad_gate = (grad_mixed * up_ref[...].astype(F32) * sig * (1.0 + gate * (1.0 - sig))).astype(BF16)
        grad_up = (grad_mixed * (gate * sig)).astype(BF16)
        gg_ref[...] = grad_gate
        gu_ref[...] = grad_up
        acc_ref[...] += times_transposed(grad_gate, wg_ref[...]) + times_transposed(grad_up, wu_ref[...])

    @pl.when(step < tiles // 2)
    def _():
        tile_work(wd_own_ref)

    @pl.when(step >= tiles // 2)
    def _():
        tile_work(wd_oth_ref)

    @pl.when(step == tiles - 1)
    def _():
        part_ref[...] = acc_ref[...].astype(BF16)


def backward_chunk(
    index, down_rows, grad_output, mlp_gain, gate, up, w_gate_up, down_halves, chunk, before,
):
    tokens, width = grad_output.shape
    hidden = w_gate_up.shape[1] // 2
    blocks, _, block = down_halves[0].shape
    tiles = hidden // TILE

    def tile_of(j, idx):
        return half_tile(j, idx[1], tiles)

    rows = pl.BlockSpec((chunk, width), lambda j, idx: (idx[0], 0))
    gain_row = pl.BlockSpec((1, width), lambda j, idx: (0, 0))
    gate_tile = pl.BlockSpec((width, TILE), lambda j, idx: (0, tile_of(j, idx)))
    up_tile = pl.BlockSpec((width, TILE), lambda j, idx: (0, tiles + tile_of(j, idx)))
    act_tile = pl.BlockSpec((chunk, TILE), lambda j, idx: (idx[0], tile_of(j, idx)))
    before = tuple(before)
    return pl.pallas_call(
        functools.partial(backward_chunk_kernel, tiles=tiles, choices=len(down_rows)),
        grid_spec=pltpu.PrefetchScalarGridSpec(
            num_scalar_prefetch=1,
            grid=(tiles,),
            in_specs=[
                rows, gain_row, act_tile, act_tile, gate_tile, up_tile,
                pl.BlockSpec((blocks, TILE, block), lambda j, idx: (0, jnp.minimum(j, tiles // 2 - 1), 0)),
                pl.BlockSpec((blocks, TILE, block), lambda j, idx: (0, jnp.maximum(j - tiles // 2, 0), 0)),
            ] + [pl.BlockSpec(memory_space=pl.ANY)] * (len(down_rows) + len(before)),
            out_specs=[rows, act_tile, act_tile, pl.BlockSpec((chunk, width), lambda j, idx: (0, 0)), gain_row],
            scratch_shapes=[
                pltpu.VMEM((chunk, width), F32), pltpu.VMEM((chunk, width), BF16), pltpu.SemaphoreType.DMA(()),
            ],
        ),
        out_shape=[
            jax.ShapeDtypeStruct((tokens, width), BF16),
            jax.ShapeDtypeStruct((tokens, hidden), BF16),
            jax.ShapeDtypeStruct((tokens, hidden), BF16),
            jax.ShapeDtypeStruct((chunk, width), BF16),
            jax.ShapeDtypeStruct((1, width), F32),
        ],
        input_output_aliases={9 + len(down_rows) + i: i for i in range(len(before))},
        compiler_params=pltpu.CompilerParams(vmem_limit_bytes=VMEM),
        cost_estimate=pl.CostEstimate(
            flops=6 * chunk * width * hidden, bytes_accessed=6 * width * hidden, transcendentals=0
        ),
        name="backward_chunk",
    )(index, grad_output, mlp_gain, gate, up, w_gate_up, w_gate_up, *down_halves, *down_rows, *before)


PARTS = 4


def attention_chunk_kernel(
    idx_ref, grad_ref, raw_ref, scale_ref, gain_ref, wo_own_ref, wo_oth_ref, *refs, choices,
):
    gai_ref, gatt_ref, gain_grad_ref, held_ref, sem = refs[-5:]
    half = wo_own_ref.shape[0]
    core = idx_ref[1]
    step = pl.program_id(0)

    @pl.when(step == 0)
    def _():
        fetch_choice(idx_ref, refs[:choices], held_ref, sem)
        gain_grad_ref[...] = jnp.zeros_like(gain_grad_ref)

    size = grad_ref.shape[0]
    scale = scale_ref[...]
    unit = raw_ref[...].astype(F32) * scale
    mlp = held_ref[pl.ds(pl.multiple_of(step * size, size), size), :]
    grad_hidden = grad_ref[...].astype(F32) + mlp.astype(F32)
    gain_grad_ref[...] += jnp.sum(grad_hidden * unit, axis=0, keepdims=True)
    grad_unit = grad_hidden * gain_ref[...]
    mean = jnp.mean(grad_unit * unit, axis=1, keepdims=True)
    grad_attn_in = (scale * (grad_unit - unit * mean)).astype(BF16)
    gai_ref[...] = grad_attn_in
    for place, w_ref in ((core, wo_own_ref), (1 - core, wo_oth_ref)):
        gatt_ref[:, pl.ds(pl.multiple_of(place * half, half), half)] = times_transposed(
            grad_attn_in, w_ref[...]
        ).astype(BF16)


def attention_chunk(index, mlp_rows, grad_output, raw, scale, gain, out_halves, half, chunk, before):
    tokens, width = grad_output.shape
    size = chunk // PARTS
    rows = pl.BlockSpec((size, width), lambda j, idx: (PARTS * idx[0] + j, 0))
    gain_row = pl.BlockSpec((1, width), lambda j, idx: (0, 0))
    own_heads = pl.BlockSpec((half, width), lambda j, idx: (0, 0))
    before = tuple(before)
    return pl.pallas_call(
        functools.partial(attention_chunk_kernel, choices=len(mlp_rows)),
        grid_spec=pltpu.PrefetchScalarGridSpec(
            num_scalar_prefetch=1,
            grid=(PARTS,),
            in_specs=[
                rows, rows, pl.BlockSpec((size, 1), lambda j, idx: (PARTS * idx[0] + j, 0)), gain_row,
                own_heads, own_heads,
            ] + [pl.BlockSpec(memory_space=pl.ANY)] * (len(mlp_rows) + len(before)),
            out_specs=[rows, pl.BlockSpec((size, 2 * half), lambda j, idx: (PARTS * idx[0] + j, 0)), gain_row],
            scratch_shapes=[pltpu.VMEM((chunk, width), BF16), pltpu.SemaphoreType.DMA(())],
        ),
        out_shape=[
            jax.ShapeDtypeStruct((tokens, width), BF16),
            jax.ShapeDtypeStruct((tokens, 2 * half), BF16),
            jax.ShapeDtypeStruct((1, width), F32),
        ],
        input_output_aliases={7 + len(mlp_rows) + i: i for i in range(len(before))},
        compiler_params=pltpu.CompilerParams(vmem_limit_bytes=VMEM),
        cost_estimate=pl.CostEstimate(
            flops=4 * chunk * width * half, bytes_accessed=16 * chunk * width, transcendentals=0
        ),
        name="attention_chunk",
    )(index, grad_output, raw, scale, gain, *out_halves, *mlp_rows, *before)


def output_chunk_kernel(idx_ref, raw_ref, scale_ref, x_ref, attn_gain_ref, mlp_gain_ref, *refs, choices):
    out_ref, held_ref, sem = refs[-3:]
    step = pl.program_id(0)

    @pl.when(step == 0)
    def _():
        fetch_choice(idx_ref, refs[:choices], held_ref, sem)

    size = out_ref.shape[0]
    down_raw = held_ref[pl.ds(pl.multiple_of(step * size, size), size), :].astype(F32)
    down_scale = lax.rsqrt(jnp.mean(down_raw * down_raw, axis=1, keepdims=True) + EPS)
    hidden = x_ref[...].astype(F32) + raw_ref[...].astype(F32) * scale_ref[...] * attn_gain_ref[...]
    out_ref[...] = (hidden + down_raw * down_scale * mlp_gain_ref[...]).astype(BF16)


def output_chunk(index, down_rows, raw, scale, block_input, attn_gain, mlp_gain, chunk, before):
    tokens, width = block_input.shape
    size = chunk // PARTS
    rows = pl.BlockSpec((size, width), lambda j, idx: (PARTS * idx[0] + j, 0))
    gain_row = pl.BlockSpec((1, width), lambda j, idx: (0, 0))
    before = tuple(before)
    return pl.pallas_call(
        functools.partial(output_chunk_kernel, choices=len(down_rows)),
        grid_spec=pltpu.PrefetchScalarGridSpec(
            num_scalar_prefetch=1,
            grid=(PARTS,),
            in_specs=[
                rows, pl.BlockSpec((size, 1), lambda j, idx: (PARTS * idx[0] + j, 0)), rows, gain_row, gain_row,
            ] + [pl.BlockSpec(memory_space=pl.ANY)] * (len(down_rows) + len(before)),
            out_specs=rows,
            scratch_shapes=[pltpu.VMEM((chunk, width), BF16), pltpu.SemaphoreType.DMA(())],
        ),
        out_shape=jax.ShapeDtypeStruct((tokens, width), BF16),
        input_output_aliases={6 + len(down_rows): 0} if before else {},
        compiler_params=pltpu.CompilerParams(vmem_limit_bytes=VMEM),
        cost_estimate=pl.CostEstimate(flops=0, bytes_accessed=8 * chunk * width, transcendentals=0),
        name="output_chunk",
    )(index, raw, scale, block_input, attn_gain, mlp_gain, *down_rows, *before)


def place_rows_kernel(idx_ref, *refs, choices):
    out_ref, held_ref, sem = refs[-3:]
    step = pl.program_id(0)

    @pl.when(step == 0)
    def _():
        fetch_choice(idx_ref, refs[:choices], held_ref, sem)

    size = out_ref.shape[0]
    out_ref[...] = held_ref[pl.ds(pl.multiple_of(step * size, size), size), :].astype(out_ref.dtype)


def place_rows(index, rows_in, tokens, dtype, before):
    chunk, width = rows_in[0].shape
    before = tuple(before)
    return pl.pallas_call(
        functools.partial(place_rows_kernel, choices=len(rows_in)),
        grid_spec=pltpu.PrefetchScalarGridSpec(
            num_scalar_prefetch=1,
            grid=(4,),
            in_specs=[pl.BlockSpec(memory_space=pl.ANY)] * (len(rows_in) + len(before)),
            out_specs=pl.BlockSpec((chunk // 4, width), lambda j, idx: (4 * idx[0] + j, 0)),
            scratch_shapes=[pltpu.VMEM((chunk, width), BF16), pltpu.SemaphoreType.DMA(())],
        ),
        out_shape=jax.ShapeDtypeStruct((tokens, width), dtype),
        input_output_aliases={1 + len(rows_in): 0} if before else {},
        compiler_params=pltpu.CompilerParams(vmem_limit_bytes=VMEM),
        cost_estimate=pl.CostEstimate(flops=0, bytes_accessed=6 * chunk * width, transcendentals=0),
        name="place_rows",
    )(index, *rows_in, *before)


def after(value, *tokens):
    return lax.optimization_barrier((value, tokens))[0]


def unset_kernel(out_ref):
    pass


def unset(shape, dtype):
    return pl.pallas_call(
        unset_kernel,
        out_specs=pl.BlockSpec(memory_space=pl.ANY),
        out_shape=jax.ShapeDtypeStruct(shape, dtype),
        name="unset",
    )()


def shards(
    sizes,
    block_input,
    segment_ids,
    positions,
    w_query,
    w_key,
    w_value,
    w_out,
    w_gate,
    w_up,
    w_down,
    query_gain,
    key_gain,
    attn_gain,
    mlp_gain,
    grad_output,
):
    cores, rows, cols = sizes
    tokens_here, width = block_input.shape
    assert tokens_here == LEN and cores == 2 and cols == 4
    local_width = w_query.shape[1]
    half_width = local_width // 2
    heads = local_width // HD
    chunk = tokens_here // cols
    core = lax.axis_index("dp")
    row = lax.axis_index("row")
    col = lax.axis_index("col")
    swap = [(0, 1), (1, 0)]
    attn_row, mlp_row = attn_gain[None, :], mlp_gain[None, :]

    def own_half(array, axis):
        half = array.shape[axis] // 2
        return lax.dynamic_slice_in_dim(array, core * half, half, axis)

    def other_half(array, axis):
        half = array.shape[axis] // 2
        return lax.dynamic_slice_in_dim(array, (1 - core) * half, half, axis)

    def gather(weight, axis):
        return lax.all_gather(own_half(weight, axis), ("row", "dp"), axis=axis, tiled=True)

    def line_step(from_left, from_right, step):
        from_left = lax.ppermute(from_left, "col", [(i, i + 1) for i in range(step - 1, cols - 1)])
        from_right = lax.ppermute(from_right, "col", [(i + 1, i) for i in range(cols - step)])
        return from_left, from_right

    def sum_step(up, down, step):
        up = lax.ppermute(up, "col", [(i, i + 1) for i in range(step)])
        down = lax.ppermute(down, "col", [(cols - 1 - i, cols - 2 - i) for i in range(step)])
        return up, down

    def pick(at_zero, at_one, at_two, at_three):
        low = jnp.where(col == 0, at_zero, at_one)
        high = jnp.where(col == 2, at_two, at_three)
        return jnp.where(col < 2, low, high)

    slot_chunk = [pick(3, 3, 0, 0), pick(2, 2, 1, 1), pick(1, 0, 3, 2), col]
    slot_index = [
        jnp.stack([one, core, choice]).astype(jnp.int32)
        for one, choice in zip(slot_chunk, (col, col, col % 2, 0 * col))
    ]

    def slot_rows(array, slot):
        return lax.dynamic_slice_in_dim(array, slot_chunk[slot] * chunk, chunk, 0)

    def gather_slots(own, work):
        left, right, token = [own], [own], ()
        arrived = (
            lambda lefts, rights: (lefts[0],),
            lambda lefts, rights: (rights[1], lefts[1]),
            lambda lefts, rights: (rights[2], rights[1], lefts[1], lefts[2]),
            lambda lefts, rights: (rights[3], rights[2], lefts[2], lefts[3]),
        )
        for step in range(1, cols + 1):
            seen = tuple(left), tuple(right)
            if step < cols:
                from_left, from_right = line_step(left[-1], right[-1], step)
                left.append(from_left)
                right.append(from_right)
            token = work(cols - step, arrived[step - 1](*after(seen, token)))

    def sum_slots(make, window=lambda step, gate: ()):
        def at(step, gate):
            window(step, gate)
            return make(step, gate)

        first = make(0, ())
        up, down = sum_step(first, first, 1)
        second = at(1, first)
        up = jnp.where(col == 0, second, first) + up
        down = jnp.where(col == 3, second, first) + down
        gate = (up, down)
        up, down = sum_step(up, down, 2)
        third = at(2, gate)
        up = jnp.where(col == 1, second, third) + up
        down = jnp.where(col == 2, second, third) + down
        gate = (up, down)
        up, down = sum_step(up, down, 3)
        fourth = lax.optimization_barrier(at(3, gate))
        return fourth.astype(F32) + up.astype(F32) + down.astype(F32)

    def both_cores(half, axis):
        other = lax.ppermute(half, "dp", swap)
        first = jnp.where(core == 0, half, other)
        second = jnp.where(core == 0, other, half)
        return jnp.concatenate([first, second], axis=axis).astype(F32)

    def sum_sent(left_mat, right_other):
        return lax.ppermute(left_transposed(left_mat, right_other).astype(BF16), "dp", swap)

    def sum_kept(left_mat, right_own, sent):
        total = (left_transposed(left_mat, right_own) + sent.astype(F32)).astype(BF16)
        return total, lax.psum_scatter(total, "row", scatter_dimension=0, tiled=True)

    by_x = [(0, 1), (1, 0), (2, 3), (3, 2)]
    by_y = [(0, 2), (2, 0), (1, 3), (3, 1)]

    def row_first(half):
        if rows != 4:
            return (half,)
        return half, lax.ppermute(half, "row", by_x), lax.ppermute(half, "row", by_y)

    def row_second(pieces):
        if rows != 4:
            return pieces
        middle = pieces[0].shape[0] // 2
        return (
            *pieces,
            lax.ppermute(pieces[1][:middle], "row", by_y),
            lax.ppermute(pieces[2][middle:], "row", by_x),
        )

    def row_blocks(pieces):
        if rows != 4:
            whole = lax.all_gather(pieces[0], ("row", "dp"), axis=0, tiled=False)
            whole = whole.reshape(rows, cores, *pieces[0].shape)
            return tuple(lax.dynamic_index_in_dim(whole, one, 1, keepdims=False) for one in (core, 1 - core))
        own, by_one, by_two, corner_top, corner_low = pieces
        middle = own.shape[0] // 2
        held = unset((rows, *own.shape), own.dtype)
        for piece, block, start in (
            (own, row, 0), (by_one, row ^ 1, 0), (by_two, row ^ 2, 0),
            (corner_top, row ^ 3, 0), (corner_low, row ^ 3, middle),
        ):
            held = lax.dynamic_update_slice(held, piece[None], (block, start, 0))
        return held, lax.ppermute(held, "dp", swap)

    def row_columns(pieces):
        if rows != 4:
            return lax.all_gather(pieces[0], "row", axis=1, tiled=True)
        own, by_one, by_two, corner_top, corner_low = pieces
        height, block = own.shape
        held = unset((height, rows * block), own.dtype)
        for piece, number, start in (
            (own, row, 0), (by_one, row ^ 1, 0), (by_two, row ^ 2, 0),
            (corner_top, row ^ 3, 0), (corner_low, row ^ 3, height // 2),
        ):
            held = lax.dynamic_update_slice(held, piece, (start, number * block))
        return held

    full_qkv = gather(jnp.concatenate([w_query, w_key, w_value], axis=1), 0)
    full_gate_up = gather(jnp.concatenate([w_gate, w_up], axis=1), 0)
    out_pieces = row_first(own_half(w_out, 0))
    out_pieces = row_second(out_pieces)
    out_own = row_columns(out_pieces)
    out_left, out_right = [out_own], [out_own]
    for step in range(1, cols):
        one, two = line_step(out_left[-1], out_right[-1], step)
        out_left.append(one)
        out_right.append(two)
    down_pieces = row_first(after(own_half(w_down, 0), full_qkv))

    qkv = plain_dot(block_input, full_qkv)
    query_raw, key_raw = qkv[:, :local_width], qkv[:, local_width : 2 * local_width]
    query_sq, key_sq = lax.psum(
        (jnp.sum(query_raw * query_raw, axis=1), jnp.sum(key_raw * key_raw, axis=1)), "col"
    )
    query_scale = lax.rsqrt(query_sq / width + EPS)[:, None]
    key_scale = lax.rsqrt(key_sq / width + EPS)[:, None]
    scales = (query_scale, key_scale)
    gains = (query_gain[None, :], key_gain[None, :])
    tables = rope_tables(positions)
    seg_col, seg_row = segment_ids[:, None], segment_ids[None, :]
    query_rot, key_rot, value_heads, attended, log_total = attend_forward(
        qkv, scales, gains, tables, seg_col, seg_row, heads
    )

    lefts, rights = [attended], [attended]
    for step in range(1, cols):
        from_left, from_right = line_step(lefts[-1], rights[-1], step)
        lefts.append(from_left)
        rights.append(from_right)
        if step == 1:
            out_halves = jnp.concatenate(
                [out_own] + [out_right[k] + out_left[cols - k] for k in range(1, cols)], axis=0
            )
            out_halves = (out_halves, lax.ppermute(out_halves, "dp", swap))
        if step == 2:
            down_pieces = row_second(after(down_pieces, lefts[1], rights[1]))
        if step == 3:
            down_halves = row_blocks(down_pieces)
    attended_all = (attended, *lefts[1:], *rights[1:])

    held = dict(forward=(), backward=(), attention=(), output=(), block_output=())
    gain_sums = dict(mlp=0.0, attn=0.0)

    def forward_work(slot, gate):
        results = forward_chunk(
            slot_index[slot], after(attended_all, gate), out_halves, block_input, attn_row, full_gate_up,
            down_halves, chunk, held["forward"],
        )
        held["forward"] = results[:6]
        return results[6]

    down_own = sum_slots(forward_work).astype(BF16)
    attn_raw, attn_scale, hidden_b, gate_proj, up_proj, mixed_act = held["forward"]
    mlp_parts = [None] * cols
    down_slots = [None] * cols

    def backward_work(slot, down_rows):
        down_slots[slot] = down_rows
        results = backward_chunk(
            slot_index[slot], down_rows, grad_output, mlp_row, gate_proj, up_proj, full_gate_up,
            down_halves, chunk, held["backward"],
        )
        held["backward"] = results[:3]
        mlp_parts[slot] = results[3]
        gain_sums["mlp"] = gain_sums["mlp"] + results[4]
        return results[3]

    gather_slots(down_own, backward_work)
    grad_down_in, grad_gate_in, grad_up_in = held["backward"]

    blocks = {}
    got = {}

    def mlp_window(step, gate):
        down_left, down_right, hidden_left, gate_right, up_right = after(
            (grad_down_in, mixed_act, hidden_b, grad_gate_in, grad_up_in), gate
        )
        if step == 1:
            got["down"] = sum_sent(down_left, other_half(down_right, 1))
            got["gate"] = sum_sent(hidden_left, other_half(gate_right, 1))
            return got["down"], got["gate"]
        if step == 2:
            blocks["down"] = sum_kept(down_left, own_half(down_right, 1), got["down"])
            got["up"] = sum_sent(hidden_left, other_half(up_right, 1))
            return blocks["down"][0], got["up"]
        blocks["gate"] = sum_kept(hidden_left, own_half(gate_right, 1), got["gate"])
        return blocks["gate"][0]

    mlp_own = sum_slots(lambda slot, gate: mlp_parts[slot], mlp_window).astype(BF16)

    def attention_work(slot, mlp_rows):
        results = attention_chunk(
            slot_index[slot], mlp_rows, grad_output, attn_raw, attn_scale, attn_row, out_halves, half_width,
            chunk, held["attention"],
        )
        held["attention"] = results[:2]
        gain_sums["attn"] = gain_sums["attn"] + results[2]
        if slot == 3:
            hidden_left, up_right = after((hidden_b, grad_up_in), mlp_rows[0])
            blocks["up"] = sum_kept(hidden_left, own_half(up_right, 1), got["up"])
        for other in {2: (3, 2), 1: (1, 0)}.get(slot, ()):
            output = output_chunk(
                slot_index[other], down_slots[other], after(attn_raw, mlp_rows), attn_scale, block_input, attn_row,
                mlp_row, chunk, held["block_output"],
            )
            held["block_output"] = (output,)
        return results[1]

    gather_slots(mlp_own, attention_work)
    grad_attn_in, grad_att = held["attention"]
    (block_output,) = held["block_output"]
    own_grad_hidden = slot_rows(grad_output, 3).astype(F32) + mlp_own.astype(F32)

    query_dz, key_dz, grad_value_in, query_dot, key_dot, grad_query_gain, grad_key_gain = attend_backward(
        qkv, scales, gains, tables, seg_col, seg_row,
        (query_rot, key_rot, value_heads, attended, log_total), grad_att, heads,
    )
    query_dot, key_dot = lax.psum((query_dot[:, 0], key_dot[:, 0]), "col")
    grad_query_in = (
        query_scale * (query_dz - query_raw * query_scale * (query_dot / width)[:, None])
    ).astype(BF16)
    grad_key_in = (
        key_scale * (key_dz - key_raw * key_scale * (key_dot / width)[:, None])
    ).astype(BF16)
    grad_qkv = jnp.concatenate([grad_query_in, grad_key_in, grad_value_in], axis=1)
    gain_pack = jnp.concatenate([grad_query_gain, grad_key_gain, gain_sums["attn"], gain_sums["mlp"]], axis=1)

    def interleaved(picker, pieces_in):
        return jnp.concatenate([picker(one, 1) for one in pieces_in], axis=1)

    def input_window(step, gate):
        nonlocal gain_pack
        pack, *pieces_in, tokens_in, left_out, right_out = after(
            (gain_pack, grad_query_in, grad_key_in, grad_value_in, block_input, grad_attn_in, attended), gate
        )
        if step == 1:
            got["qkv"] = sum_sent(tokens_in, interleaved(other_half, pieces_in))
            got["out"] = sum_sent(left_out, other_half(right_out, 1))
            gain_pack = pack + lax.ppermute(pack, "dp", swap)
            return got["qkv"], got["out"], gain_pack
        if step == 2:
            blocks["out"] = sum_kept(left_out, own_half(right_out, 1), got["out"])
            blocks["qkv"] = sum_kept(after(tokens_in, blocks["out"][0]), interleaved(own_half, pieces_in), got["qkv"]
            )
            if rows == 4:
                gain_pack = pack + lax.ppermute(pack, "row", by_x)
            return
        gain_pack = pack + lax.ppermute(pack, "row", by_y) if rows == 4 else lax.psum(pack, "row")

    input_own = sum_slots(
        lambda slot, gate: times_transposed(after(slot_rows(grad_qkv, slot), gate), full_qkv).astype(BF16), input_window
    )

    results = {}
    quarter = local_width // 2

    def projection(index):
        pair = both_cores(blocks["qkv"][1][None, :, index * quarter : (index + 1) * quarter], 0)
        return jnp.concatenate([pair[0], pair[1]], axis=1)

    def output_work(slot, rows_in):
        held["output"] = (place_rows(slot_index[slot], rows_in, tokens_here, F32, held["output"]),)
        if slot == 3:
            results["down"] = jnp.transpose(both_cores(blocks["down"][1], 1))
            results["gate"] = both_cores(blocks["gate"][1], 1)
            return held["output"], results["down"], results["gate"]
        if slot == 2:
            results["up"] = both_cores(blocks["up"][1], 1)
            return held["output"], results["up"]
        if slot == 1:
            results["out"] = jnp.transpose(both_cores(blocks["out"][1], 1))
            results["qkv"] = [projection(index) for index in range(3)]
            return held["output"], results["out"], results["qkv"]
        return held["output"]

    gather_slots((own_grad_hidden + input_own).astype(BF16), output_work)
    ends = (local_width, 2 * local_width, 2 * local_width + width)
    gain_grads = jnp.split(gain_pack[0], ends)
    return (
        block_output,
        held["output"][0],
        *results["qkv"],
        results["out"],
        results["gate"],
        results["up"],
        results["down"],
        *gain_grads,
    )


def layer(sizes, *arrays):
    return shards(sizes, *arrays)


def solution(mesh):
    in_specs = (
        P(("dp", "row"), None),
        P(("dp", "row")),
        P(("dp", "row")),
        P("row", "col"),
        P("row", "col"),
        P("row", "col"),
        P("col", "row"),
        P("row", "col"),
        P("row", "col"),
        P("col", "row"),
        P("col"),
        P("col"),
        P(),
        P(),
        P(("dp", "row"), None),
    )
    out_specs = (
        P(("dp", "row"), None),
        P(("dp", "row"), None),
        P("row", "col"),
        P("row", "col"),
        P("row", "col"),
        P("col", "row"),
        P("row", "col"),
        P("row", "col"),
        P("col", "row"),
        P("col"),
        P("col"),
        P(),
        P(),
    )
    sizes = (mesh.shape["dp"], mesh.shape["row"], mesh.shape["col"])
    return jax.shard_map(
        functools.partial(layer, sizes), mesh=mesh, in_specs=in_specs, out_specs=out_specs, check_vma=False
    )
```

```python
import functools

import jax
import jax.numpy as jnp
from jax import lax
from jax.experimental import pallas as pl
from jax.experimental.pallas import tpu as pltpu
from jax.sharding import PartitionSpec as P


HD = 128
LEN = 1024
BQ = 256
VMEM = 60 << 20

EPS = 1e-06
THETA = 500000.0
NEG_FILL = -1e30
SCORE_SCALE = HD ** (-0.5)
F32 = jnp.float32
BF16 = jnp.bfloat16


def plain_dot(left_mat, right_mat):
    return jnp.dot(left_mat, right_mat, preferred_element_type=F32)


def times_transposed(left_mat, right_mat):
    return lax.dot_general(
        left_mat, right_mat, (((1,), (1,)), ((), ())), preferred_element_type=F32
    )


def left_transposed(left_mat, right_mat):
    return lax.dot_general(
        left_mat, right_mat, (((0,), (0,)), ((), ())), preferred_element_type=F32
    )


def rope_tables(positions):
    half_dim = HD // 2
    inv_freq = THETA ** (-(jnp.arange(half_dim, dtype=F32) * 2.0) / HD)
    angles = positions.astype(F32)[:, None] * inv_freq[None, :]
    cos_half, sin_half = jnp.cos(angles), jnp.sin(angles)
    cosine = jnp.concatenate([cos_half, cos_half], axis=-1)
    sine_signed = jnp.concatenate([-sin_half, sin_half], axis=-1)
    return cosine, sine_signed


def fill_mask(bias_ref, seg_col_ref, seg_row_ref):
    @pl.when(pl.program_id(0) == 0)
    def _():
        for first in range(0, LEN, BQ):
            keys = first + BQ
            rows = seg_col_ref[first:keys, :]
            cols = seg_row_ref[:, :keys]
            query_index = first + lax.broadcasted_iota(jnp.int32, (BQ, keys), 0)
            key_index = lax.broadcasted_iota(jnp.int32, (BQ, keys), 1)
            allowed = (rows == cols) & (key_index <= query_index)
            bias_ref[first:keys, :keys] = jnp.where(allowed, 0.0, NEG_FILL)


def attend_forward_kernel(
    q_ref, k_ref, v_ref, qs_ref, ks_ref, qg_ref, kg_ref, cos_ref, sin_ref, segc_ref, segr_ref,
    qrot_ref, krot_ref, vb_ref, att_ref, log_ref, bias_ref,
):
    fill_mask(bias_ref, segc_ref, segr_ref)
    cosine, sine = cos_ref[...], sin_ref[...]

    def turned(raw, scale, gain):
        norm = raw * scale * gain
        return (norm * cosine + pltpu.roll(norm, HD // 2, 1) * sine).astype(BF16)

    qrot_ref[...] = turned(q_ref[...], qs_ref[...], qg_ref[...])
    krot_ref[...] = turned(k_ref[...], ks_ref[...], kg_ref[...])
    vb_ref[...] = v_ref[...].astype(BF16)
    for first in range(0, LEN, BQ):
        keys = first + BQ
        scores = times_transposed(qrot_ref[first:keys, :], krot_ref[:keys, :]) * SCORE_SCALE
        masked = scores + bias_ref[first:keys, :keys]
        peak = jnp.max(masked, axis=1, keepdims=True)
        weight = jnp.exp(masked - peak)
        total = jnp.sum(weight, axis=1, keepdims=True)
        probs = (weight * (1.0 / total)).astype(BF16)
        att_ref[first:keys, :] = plain_dot(probs, vb_ref[:keys, :]).astype(BF16)
        log_ref[0, first:keys, :] = peak + jnp.log(total)


def attend_backward_kernel(
    q_ref, k_ref, qs_ref, ks_ref, qg_ref, kg_ref, cos_ref, sin_ref, segc_ref, segr_ref,
    qrot_ref, krot_ref, vb_ref, att_ref, log_ref, grad_ref,
    dzq_ref, dzk_ref, gv_ref, dotq_ref, dotk_ref, gainq_ref, gaink_ref,
    dq_acc, dk_acc, dv_acc, bias_ref,
):
    fill_mask(bias_ref, segc_ref, segr_ref)
    dk_acc[...] = jnp.zeros_like(dk_acc)
    dv_acc[...] = jnp.zeros_like(dv_acc)
    for first in range(0, LEN, BQ):
        keys = first + BQ
        queries = qrot_ref[first:keys, :]
        grads = grad_ref[first:keys, :]
        scores = times_transposed(queries, krot_ref[:keys, :]) * SCORE_SCALE
        probs = jnp.exp(scores + bias_ref[first:keys, :keys] - log_ref[0, first:keys, :])
        delta = jnp.sum(
            grads.astype(F32) * att_ref[first:keys, :].astype(F32), axis=1, keepdims=True
        )
        grad_probs = times_transposed(grads, vb_ref[:keys, :])
        grad_scores = (probs * (grad_probs - delta) * SCORE_SCALE).astype(BF16)
        dq_acc[first:keys, :] = plain_dot(grad_scores, krot_ref[:keys, :])
        dk_acc[:keys, :] += left_transposed(grad_scores, queries)
        dv_acc[:keys, :] += left_transposed(probs.astype(BF16), grads)
    gv_ref[...] = dv_acc[...].astype(BF16)
    cosine, sine = cos_ref[...], sin_ref[...]

    def finish(acc, raw_ref, scale_ref, gain_ref, dz_ref, dot_ref, gain_grad_ref):
        grad_rot = acc[...]
        grad_norm = grad_rot * cosine - pltpu.roll(grad_rot, HD // 2, 1) * sine
        unit = raw_ref[...] * scale_ref[...]
        gain_grad_ref[...] = jnp.sum(grad_norm * unit, axis=0, keepdims=True)
        grad_unit = grad_norm * gain_ref[...]
        dz_ref[...] = grad_unit
        part = jnp.sum(grad_unit * unit, axis=1, keepdims=True)

        @pl.when(pl.program_id(0) == 0)
        def _():
            dot_ref[...] = part

        @pl.when(pl.program_id(0) > 0)
        def _():
            dot_ref[...] += part

    finish(dq_acc, q_ref, qs_ref, qg_ref, dzq_ref, dotq_ref, gainq_ref)
    finish(dk_acc, k_ref, ks_ref, kg_ref, dzk_ref, dotk_ref, gaink_ref)


def head_spec(offset):
    return pl.BlockSpec((LEN, HD), lambda h: (0, offset + h))


def whole_spec(shape):
    return pl.BlockSpec(shape, lambda h: (0,) * len(shape))


def gain_spec():
    return pl.BlockSpec((1, HD), lambda h: (0, h))


LOG_SPEC = pl.BlockSpec((1, LEN, 1), lambda h: (h, 0, 0))
COLUMN = (LEN, 1)
TABLE = (LEN, HD)


def attend_forward(qkv, scales, gains, tables, seg_col, seg_row, heads):
    width = heads * HD
    piece = jax.ShapeDtypeStruct((LEN, width), BF16)
    return pl.pallas_call(
        attend_forward_kernel,
        grid=(heads,),
        in_specs=[
            head_spec(0), head_spec(heads), head_spec(2 * heads),
            whole_spec(COLUMN), whole_spec(COLUMN), gain_spec(), gain_spec(),
            whole_spec(TABLE), whole_spec(TABLE), whole_spec(COLUMN), whole_spec((1, LEN)),
        ],
        out_specs=[head_spec(0)] * 4 + [LOG_SPEC],
        out_shape=[piece] * 4 + [jax.ShapeDtypeStruct((heads, LEN, 1), F32)],
        scratch_shapes=[pltpu.VMEM((LEN, LEN), F32)],
        compiler_params=pltpu.CompilerParams(vmem_limit_bytes=VMEM),
        cost_estimate=pl.CostEstimate(
            flops=heads * 4 * LEN * LEN * HD, bytes_accessed=LEN * width * 20, transcendentals=0
        ),
        name="attend_forward",
    )(qkv, qkv, qkv, *scales, *gains, *tables, seg_col, seg_row)


def attend_backward(qkv, scales, gains, tables, seg_col, seg_row, saved, grad_att, heads):
    width = heads * HD
    full = jax.ShapeDtypeStruct((LEN, width), F32)
    column = jax.ShapeDtypeStruct(COLUMN, F32)
    gain_row = jax.ShapeDtypeStruct((1, width), F32)
    return pl.pallas_call(
        attend_backward_kernel,
        grid=(heads,),
        in_specs=[
            head_spec(0), head_spec(heads),
            whole_spec(COLUMN), whole_spec(COLUMN), gain_spec(), gain_spec(),
            whole_spec(TABLE), whole_spec(TABLE), whole_spec(COLUMN), whole_spec((1, LEN)),
            head_spec(0), head_spec(0), head_spec(0), head_spec(0), LOG_SPEC, head_spec(0),
        ],
        out_specs=[
            head_spec(0), head_spec(0), head_spec(0),
            whole_spec(COLUMN), whole_spec(COLUMN), gain_spec(), gain_spec(),
        ],
        out_shape=[
            full, full, jax.ShapeDtypeStruct((LEN, width), BF16), column, column, gain_row, gain_row,
        ],
        scratch_shapes=[pltpu.VMEM((LEN, HD), F32)] * 3 + [pltpu.VMEM((LEN, LEN), F32)],
        compiler_params=pltpu.CompilerParams(vmem_limit_bytes=VMEM),
        cost_estimate=pl.CostEstimate(
            flops=heads * 10 * LEN * LEN * HD, bytes_accessed=LEN * width * 40, transcendentals=0
        ),
        name="attend_backward",
    )(qkv, qkv, *scales, *gains, *tables, seg_col, seg_row, *saved, grad_att)


def fetch_choice(idx_ref, refs, held_ref, sem):
    for number, ref in enumerate(refs):

        @pl.when(idx_ref[2] == number)
        def _():
            copy = pltpu.make_async_copy(ref, held_ref, sem)
            copy.start()
            copy.wait()


def qkv_kernel(idx_ref, x_ref, own_ref, oth_ref, out_ref):
    step = pl.program_id(0)

    @pl.when(step < 3)
    def _():
        out_ref[...] = plain_dot(x_ref[...], own_ref[...])

    @pl.when(step >= 3)
    def _():
        out_ref[...] = plain_dot(x_ref[...], oth_ref[...])


def qkv_product(index, block_input, halves):
    tokens, width = block_input.shape
    part = halves[0].shape[1] // 3
    return pl.pallas_call(
        qkv_kernel,
        grid_spec=pltpu.PrefetchScalarGridSpec(
            num_scalar_prefetch=1,
            grid=(6,),
            in_specs=[
                pl.BlockSpec((tokens, width), lambda j, idx: (0, 0)),
                pl.BlockSpec((width, part), lambda j, idx: (0, jnp.minimum(j, 2))),
                pl.BlockSpec((width, part), lambda j, idx: (0, jnp.maximum(j - 3, 0))),
            ],
            out_specs=pl.BlockSpec((tokens, part), lambda j, idx: (0, 2 * (j % 3) + (idx[1] + j // 3) % 2)),
        ),
        out_shape=jax.ShapeDtypeStruct((tokens, 6 * part), F32),
        compiler_params=pltpu.CompilerParams(vmem_limit_bytes=VMEM),
        cost_estimate=pl.CostEstimate(
            flops=12 * tokens * width * part, bytes_accessed=20 * tokens * width, transcendentals=0
        ),
        name="qkv",
    )(index, block_input, *halves)


def half_tile(step, core, tiles):
    per_half = tiles // 2
    return ((core + step // per_half) % 2) * per_half + step % per_half


def forward_chunk_kernel(
    idx_ref, *refs, out_steps, tiles,
):
    own_ref, left1, left2, left3, right1, right2, right3 = refs[:7]
    wo_own_ref, wo_oth_ref, x_ref, gain_ref, wg_ref, wu_ref, wd_own_ref, wd_oth_ref = refs[7:15]
    raw_ref, scale_ref, hb_ref, gate_ref, up_ref, mixed_ref, part_ref, acc_ref, att_ref = refs[-9:]
    depth, out_tile = wo_own_ref.shape
    blocks, _, block = wd_own_ref.shape
    step = pl.program_id(0)
    core = idx_ref[1]

    @pl.when(step == 0)
    def _():
        quarter = own_ref.shape[1] // 2
        pieces = (
            own_ref[...], right1[...] + left3[...], right2[...] + left2[...], right3[...] + left1[...],
        )
        for half in range(2):
            for number, piece in enumerate(pieces):
                start = half * depth + number * quarter
                att_ref[:, start : start + quarter] = piece[:, half * quarter : (half + 1) * quarter]

    @pl.when(step < out_steps)
    def _():
        own = att_ref[:, pl.ds(pl.multiple_of(core * depth, depth), depth)]
        other = att_ref[:, pl.ds(pl.multiple_of((1 - core) * depth, depth), depth)]
        acc_ref[:, pl.ds(pl.multiple_of(step * out_tile, out_tile), out_tile)] = plain_dot(
            own, wo_own_ref[...]
        ) + plain_dot(other, wo_oth_ref[...])

    @pl.when(step == out_steps - 1)
    def _():
        raw = acc_ref[...]
        scale = lax.rsqrt(jnp.mean(raw * raw, axis=1, keepdims=True) + EPS)
        raw_ref[...] = raw.astype(BF16)
        scale_ref[...] = scale
        hb_ref[...] = (x_ref[...].astype(F32) + raw * scale * gain_ref[...]).astype(BF16)
        acc_ref[...] = jnp.zeros_like(acc_ref)

    def tile_work(wd_ref):
        hidden_b = hb_ref[...]
        gate = plain_dot(hidden_b, wg_ref[...])
        up = plain_dot(hidden_b, wu_ref[...])
        mixed = (gate * jax.nn.sigmoid(gate) * up).astype(BF16)
        gate_ref[...] = gate.astype(BF16)
        up_ref[...] = up.astype(BF16)
        mixed_ref[...] = mixed
        for j in range(blocks):
            acc_ref[:, j * block : (j + 1) * block] += plain_dot(mixed, wd_ref[j])

    @pl.when((step >= out_steps) & (step < out_steps + tiles // 2))
    def _():
        tile_work(wd_own_ref)

    @pl.when(step >= out_steps + tiles // 2)
    def _():
        tile_work(wd_oth_ref)

    @pl.when(step == out_steps + tiles - 1)
    def _():
        part_ref[...] = acc_ref[...].astype(BF16)


TILE = 512


def forward_chunk(index, attended, out_halves, block_input, gain, w_gate_up, down_halves, chunk, before):
    tokens, width = block_input.shape
    hidden = w_gate_up.shape[1] // 2
    depth = out_halves[0].shape[0]
    blocks, _, block = down_halves[0].shape
    tiles = hidden // TILE
    out_steps = width // TILE

    def tile_of(j, idx):
        return half_tile(jnp.maximum(j - out_steps, 0), idx[1], tiles)

    rows = pl.BlockSpec((chunk, width), lambda j, idx: (idx[0], 0))
    out_half = pl.BlockSpec((depth, TILE), lambda j, idx: (0, jnp.minimum(j, out_steps - 1)))
    gate_tile = pl.BlockSpec((width, TILE), lambda j, idx: (0, tile_of(j, idx)))
    up_tile = pl.BlockSpec((width, TILE), lambda j, idx: (0, tiles + tile_of(j, idx)))
    down_own = pl.BlockSpec(
        (blocks, TILE, block), lambda j, idx: (0, jnp.clip(j - out_steps, 0, tiles // 2 - 1), 0)
    )
    down_oth = pl.BlockSpec(
        (blocks, TILE, block), lambda j, idx: (0, jnp.maximum(j - out_steps - tiles // 2, 0), 0)
    )
    act_tile = pl.BlockSpec((chunk, TILE), lambda j, idx: (idx[0], tile_of(j, idx)))
    before = tuple(before)
    return pl.pallas_call(
        functools.partial(forward_chunk_kernel, out_steps=out_steps, tiles=tiles),
        grid_spec=pltpu.PrefetchScalarGridSpec(
            num_scalar_prefetch=1,
            grid=(out_steps + tiles,),
            in_specs=[
                *[pl.BlockSpec((chunk, attended[0].shape[1]), lambda j, idx: (idx[0], 0))] * 7,
                out_half, out_half, rows, pl.BlockSpec((1, width), lambda j, idx: (0, 0)),
                gate_tile, up_tile, down_own, down_oth,
            ] + [pl.BlockSpec(memory_space=pl.ANY)] * len(before),
            out_specs=[
                rows, pl.BlockSpec((chunk, 1), lambda j, idx: (idx[0], 0)), rows, act_tile, act_tile, act_tile,
                pl.BlockSpec((chunk, width), lambda j, idx: (0, 0)),
            ],
            scratch_shapes=[pltpu.VMEM((chunk, width), F32), pltpu.VMEM((chunk, 2 * depth), BF16)],
        ),
        out_shape=[
            jax.ShapeDtypeStruct((tokens, width), BF16),
            jax.ShapeDtypeStruct((tokens, 1), F32),
            jax.ShapeDtypeStruct((tokens, width), BF16),
            jax.ShapeDtypeStruct((tokens, hidden), BF16),
            jax.ShapeDtypeStruct((tokens, hidden), BF16),
            jax.ShapeDtypeStruct((tokens, hidden), BF16),
            jax.ShapeDtypeStruct((chunk, width), BF16),
        ],
        input_output_aliases={16 + i: i for i in range(len(before))},
        compiler_params=pltpu.CompilerParams(vmem_limit_bytes=VMEM),
        cost_estimate=pl.CostEstimate(
            flops=2 * chunk * width * (width + 3 * hidden),
            bytes_accessed=2 * width * (width + 3 * hidden),
            transcendentals=0,
        ),
        name="forward_chunk",
    )(index, *attended, *out_halves, block_input, gain, w_gate_up, w_gate_up, *down_halves, *before)


def backward_chunk_kernel(
    idx_ref, grad_ref, mlp_gain_ref, gate_ref, up_ref, wg_ref, wu_ref, wd_own_ref, wd_oth_ref, *refs, tiles, choices,
):
    gdi_ref, gg_ref, gu_ref, part_ref, gain_grad_ref, acc_ref, down_ref, sem = refs[-8:]
    blocks, _, block = wd_own_ref.shape
    step = pl.program_id(0)

    @pl.when(step == 0)
    def _():
        fetch_choice(idx_ref, refs[:choices], down_ref, sem)
        down_raw = down_ref[...].astype(F32)
        down_scale = lax.rsqrt(jnp.mean(down_raw * down_raw, axis=1, keepdims=True) + EPS)
        unit = down_raw * down_scale
        grad_y = grad_ref[...].astype(F32)
        gain_grad_ref[...] = jnp.sum(grad_y * unit, axis=0, keepdims=True)
        grad_unit = grad_y * mlp_gain_ref[...]
        mean = jnp.mean(grad_unit * unit, axis=1, keepdims=True)
        gdi_ref[...] = (down_scale * (grad_unit - unit * mean)).astype(BF16)
        acc_ref[...] = jnp.zeros_like(acc_ref)

    def tile_work(wd_ref):
        grad_mixed = times_transposed(gdi_ref[:, :block], wd_ref[0])
        for j in range(1, blocks):
            grad_mixed += times_transposed(gdi_ref[:, j * block : (j + 1) * block], wd_ref[j])
        gate = gate_ref[...].astype(F32)
        sig = jax.nn.sigmoid(gate)
        grad_gate = (grad_mixed * up_ref[...].astype(F32) * sig * (1.0 + gate * (1.0 - sig))).astype(BF16)
        grad_up = (grad_mixed * (gate * sig)).astype(BF16)
        gg_ref[...] = grad_gate
        gu_ref[...] = grad_up
        acc_ref[...] += times_transposed(grad_gate, wg_ref[...]) + times_transposed(grad_up, wu_ref[...])

    @pl.when(step < tiles // 2)
    def _():
        tile_work(wd_own_ref)

    @pl.when(step >= tiles // 2)
    def _():
        tile_work(wd_oth_ref)

    @pl.when(step == tiles - 1)
    def _():
        part_ref[...] = acc_ref[...].astype(BF16)


def backward_chunk(
    index, down_rows, grad_output, mlp_gain, gate, up, w_gate_up, down_halves, chunk, before,
):
    tokens, width = grad_output.shape
    hidden = w_gate_up.shape[1] // 2
    blocks, _, block = down_halves[0].shape
    tiles = hidden // TILE

    def tile_of(j, idx):
        return half_tile(j, idx[1], tiles)

    rows = pl.BlockSpec((chunk, width), lambda j, idx: (idx[0], 0))
    gain_row = pl.BlockSpec((1, width), lambda j, idx: (0, 0))
    gate_tile = pl.BlockSpec((width, TILE), lambda j, idx: (0, tile_of(j, idx)))
    up_tile = pl.BlockSpec((width, TILE), lambda j, idx: (0, tiles + tile_of(j, idx)))
    act_tile = pl.BlockSpec((chunk, TILE), lambda j, idx: (idx[0], tile_of(j, idx)))
    before = tuple(before)
    return pl.pallas_call(
        functools.partial(backward_chunk_kernel, tiles=tiles, choices=len(down_rows)),
        grid_spec=pltpu.PrefetchScalarGridSpec(
            num_scalar_prefetch=1,
            grid=(tiles,),
            in_specs=[
                rows, gain_row, act_tile, act_tile, gate_tile, up_tile,
                pl.BlockSpec((blocks, TILE, block), lambda j, idx: (0, jnp.minimum(j, tiles // 2 - 1), 0)),
                pl.BlockSpec((blocks, TILE, block), lambda j, idx: (0, jnp.maximum(j - tiles // 2, 0), 0)),
            ] + [pl.BlockSpec(memory_space=pl.ANY)] * (len(down_rows) + len(before)),
            out_specs=[rows, act_tile, act_tile, pl.BlockSpec((chunk, width), lambda j, idx: (0, 0)), gain_row],
            scratch_shapes=[
                pltpu.VMEM((chunk, width), F32), pltpu.VMEM((chunk, width), BF16), pltpu.SemaphoreType.DMA(()),
            ],
        ),
        out_shape=[
            jax.ShapeDtypeStruct((tokens, width), BF16),
            jax.ShapeDtypeStruct((tokens, hidden), BF16),
            jax.ShapeDtypeStruct((tokens, hidden), BF16),
            jax.ShapeDtypeStruct((chunk, width), BF16),
            jax.ShapeDtypeStruct((1, width), F32),
        ],
        input_output_aliases={9 + len(down_rows) + i: i for i in range(len(before))},
        compiler_params=pltpu.CompilerParams(vmem_limit_bytes=VMEM),
        cost_estimate=pl.CostEstimate(
            flops=6 * chunk * width * hidden, bytes_accessed=6 * width * hidden, transcendentals=0
        ),
        name="backward_chunk",
    )(index, grad_output, mlp_gain, gate, up, w_gate_up, w_gate_up, *down_halves, *down_rows, *before)


PARTS = 4


def attention_chunk_kernel(
    idx_ref, grad_ref, raw_ref, scale_ref, gain_ref, wo_own_ref, wo_oth_ref, *refs, choices,
):
    gai_ref, gatt_ref, gain_grad_ref, held_ref, sem = refs[-5:]
    half = wo_own_ref.shape[0]
    core = idx_ref[1]
    step = pl.program_id(0)

    @pl.when(step == 0)
    def _():
        fetch_choice(idx_ref, refs[:choices], held_ref, sem)
        gain_grad_ref[...] = jnp.zeros_like(gain_grad_ref)

    size = grad_ref.shape[0]
    scale = scale_ref[...]
    unit = raw_ref[...].astype(F32) * scale
    mlp = held_ref[pl.ds(pl.multiple_of(step * size, size), size), :]
    grad_hidden = grad_ref[...].astype(F32) + mlp.astype(F32)
    gain_grad_ref[...] += jnp.sum(grad_hidden * unit, axis=0, keepdims=True)
    grad_unit = grad_hidden * gain_ref[...]
    mean = jnp.mean(grad_unit * unit, axis=1, keepdims=True)
    grad_attn_in = (scale * (grad_unit - unit * mean)).astype(BF16)
    gai_ref[...] = grad_attn_in
    for place, w_ref in ((core, wo_own_ref), (1 - core, wo_oth_ref)):
        gatt_ref[:, pl.ds(pl.multiple_of(place * half, half), half)] = times_transposed(
            grad_attn_in, w_ref[...]
        ).astype(BF16)


def attention_chunk(index, mlp_rows, grad_output, raw, scale, gain, out_halves, half, chunk, before):
    tokens, width = grad_output.shape
    size = chunk
    rows = pl.BlockSpec((size, width), lambda j, idx: (idx[0], 0))
    gain_row = pl.BlockSpec((1, width), lambda j, idx: (0, 0))
    own_heads = pl.BlockSpec((half, width), lambda j, idx: (0, 0))
    before = tuple(before)
    return pl.pallas_call(
        functools.partial(attention_chunk_kernel, choices=len(mlp_rows)),
        grid_spec=pltpu.PrefetchScalarGridSpec(
            num_scalar_prefetch=1,
            grid=(1,),
            in_specs=[
                rows, rows, pl.BlockSpec((size, 1), lambda j, idx: (idx[0], 0)), gain_row,
                own_heads, own_heads,
            ] + [pl.BlockSpec(memory_space=pl.ANY)] * (len(mlp_rows) + len(before)),
            out_specs=[rows, pl.BlockSpec((size, 2 * half), lambda j, idx: (idx[0], 0)), gain_row],
            scratch_shapes=[pltpu.VMEM((chunk, width), BF16), pltpu.SemaphoreType.DMA(())],
        ),
        out_shape=[
            jax.ShapeDtypeStruct((tokens, width), BF16),
            jax.ShapeDtypeStruct((tokens, 2 * half), BF16),
            jax.ShapeDtypeStruct((1, width), F32),
        ],
        input_output_aliases={7 + len(mlp_rows) + i: i for i in range(len(before))},
        compiler_params=pltpu.CompilerParams(vmem_limit_bytes=VMEM),
        cost_estimate=pl.CostEstimate(
            flops=4 * chunk * width * half, bytes_accessed=16 * chunk * width, transcendentals=0
        ),
        name="attention_chunk",
    )(index, grad_output, raw, scale, gain, *out_halves, *mlp_rows, *before)


def output_chunk_kernel(idx_ref, raw_ref, scale_ref, x_ref, attn_gain_ref, mlp_gain_ref, *refs, choices):
    out_ref, held_ref, sem = refs[-3:]
    step = pl.program_id(0)

    @pl.when(step == 0)
    def _():
        fetch_choice(idx_ref, refs[:choices], held_ref, sem)

    size = out_ref.shape[0]
    down_raw = held_ref[pl.ds(pl.multiple_of(step * size, size), size), :].astype(F32)
    down_scale = lax.rsqrt(jnp.mean(down_raw * down_raw, axis=1, keepdims=True) + EPS)
    hidden = x_ref[...].astype(F32) + raw_ref[...].astype(F32) * scale_ref[...] * attn_gain_ref[...]
    out_ref[...] = (hidden + down_raw * down_scale * mlp_gain_ref[...]).astype(BF16)


def output_chunk(index, down_rows, raw, scale, block_input, attn_gain, mlp_gain, chunk, before):
    tokens, width = block_input.shape
    size = chunk // PARTS
    rows = pl.BlockSpec((size, width), lambda j, idx: (PARTS * idx[0] + j, 0))
    gain_row = pl.BlockSpec((1, width), lambda j, idx: (0, 0))
    before = tuple(before)
    return pl.pallas_call(
        functools.partial(output_chunk_kernel, choices=len(down_rows)),
        grid_spec=pltpu.PrefetchScalarGridSpec(
            num_scalar_prefetch=1,
            grid=(PARTS,),
            in_specs=[
                rows, pl.BlockSpec((size, 1), lambda j, idx: (PARTS * idx[0] + j, 0)), rows, gain_row, gain_row,
            ] + [pl.BlockSpec(memory_space=pl.ANY)] * (len(down_rows) + len(before)),
            out_specs=rows,
            scratch_shapes=[pltpu.VMEM((chunk, width), BF16), pltpu.SemaphoreType.DMA(())],
        ),
        out_shape=jax.ShapeDtypeStruct((tokens, width), BF16),
        input_output_aliases={6 + len(down_rows): 0} if before else {},
        compiler_params=pltpu.CompilerParams(vmem_limit_bytes=VMEM),
        cost_estimate=pl.CostEstimate(flops=0, bytes_accessed=8 * chunk * width, transcendentals=0),
        name="output_chunk",
    )(index, raw, scale, block_input, attn_gain, mlp_gain, *down_rows, *before)


def place_rows_kernel(idx_ref, *refs, choices):
    out_ref, held_ref, sem = refs[-3:]
    step = pl.program_id(0)

    @pl.when(step == 0)
    def _():
        fetch_choice(idx_ref, refs[:choices], held_ref, sem)

    size = out_ref.shape[0]
    out_ref[...] = held_ref[pl.ds(pl.multiple_of(step * size, size), size), :].astype(out_ref.dtype)


def place_rows(index, rows_in, tokens, dtype, before):
    chunk, width = rows_in[0].shape
    before = tuple(before)
    return pl.pallas_call(
        functools.partial(place_rows_kernel, choices=len(rows_in)),
        grid_spec=pltpu.PrefetchScalarGridSpec(
            num_scalar_prefetch=1,
            grid=(4,),
            in_specs=[pl.BlockSpec(memory_space=pl.ANY)] * (len(rows_in) + len(before)),
            out_specs=pl.BlockSpec((chunk // 4, width), lambda j, idx: (4 * idx[0] + j, 0)),
            scratch_shapes=[pltpu.VMEM((chunk, width), BF16), pltpu.SemaphoreType.DMA(())],
        ),
        out_shape=jax.ShapeDtypeStruct((tokens, width), dtype),
        input_output_aliases={1 + len(rows_in): 0} if before else {},
        compiler_params=pltpu.CompilerParams(vmem_limit_bytes=VMEM),
        cost_estimate=pl.CostEstimate(flops=0, bytes_accessed=6 * chunk * width, transcendentals=0),
        name="place_rows",
    )(index, *rows_in, *before)


def after(value, *tokens):
    return lax.optimization_barrier((value, tokens))[0]


def unset_kernel(out_ref):
    pass


def unset(shape, dtype):
    return pl.pallas_call(
        unset_kernel,
        out_specs=pl.BlockSpec(memory_space=pl.ANY),
        out_shape=jax.ShapeDtypeStruct(shape, dtype),
        name="unset",
    )()


def shards(
    sizes,
    block_input,
    segment_ids,
    positions,
    w_query,
    w_key,
    w_value,
    w_out,
    w_gate,
    w_up,
    w_down,
    query_gain,
    key_gain,
    attn_gain,
    mlp_gain,
    grad_output,
):
    cores, rows, cols = sizes
    tokens_here, width = block_input.shape
    assert tokens_here == LEN and cores == 2 and cols == 4
    local_width = w_query.shape[1]
    half_width = local_width // 2
    heads = local_width // HD
    chunk = tokens_here // cols
    core = lax.axis_index("dp")
    row = lax.axis_index("row")
    col = lax.axis_index("col")
    swap = [(0, 1), (1, 0)]
    attn_row, mlp_row = attn_gain[None, :], mlp_gain[None, :]

    def own_half(array, axis):
        half = array.shape[axis] // 2
        return lax.dynamic_slice_in_dim(array, core * half, half, axis)

    def other_half(array, axis):
        half = array.shape[axis] // 2
        return lax.dynamic_slice_in_dim(array, (1 - core) * half, half, axis)

    def line_step(from_left, from_right, step):
        from_left = lax.ppermute(from_left, "col", [(i, i + 1) for i in range(step - 1, cols - 1)])
        from_right = lax.ppermute(from_right, "col", [(i + 1, i) for i in range(cols - step)])
        return from_left, from_right

    def sum_step(up, down, step):
        up = lax.ppermute(up, "col", [(i, i + 1) for i in range(step)])
        down = lax.ppermute(down, "col", [(cols - 1 - i, cols - 2 - i) for i in range(step)])
        return up, down

    def pick(at_zero, at_one, at_two, at_three):
        low = jnp.where(col == 0, at_zero, at_one)
        high = jnp.where(col == 2, at_two, at_three)
        return jnp.where(col < 2, low, high)

    slot_chunk = [pick(3, 3, 0, 0), pick(2, 2, 1, 1), pick(1, 0, 3, 2), col]
    slot_index = [
        jnp.stack([one, core, choice]).astype(jnp.int32)
        for one, choice in zip(slot_chunk, (col, col, col % 2, 0 * col))
    ]

    def slot_rows(array, slot):
        return lax.dynamic_slice_in_dim(array, slot_chunk[slot] * chunk, chunk, 0)

    def gather_slots(own, work):
        left, right, token = [own], [own], ()
        arrived = (
            lambda lefts, rights: (lefts[0],),
            lambda lefts, rights: (rights[1], lefts[1]),
            lambda lefts, rights: (rights[2], rights[1], lefts[1], lefts[2]),
            lambda lefts, rights: (rights[3], rights[2], lefts[2], lefts[3]),
        )
        for step in range(1, cols + 1):
            seen = tuple(left), tuple(right)
            if step < cols:
                from_left, from_right = line_step(left[-1], right[-1], step)
                left.append(from_left)
                right.append(from_right)
            token = work(cols - step, arrived[step - 1](*after(seen, token)))

    def sum_slots(make, window=lambda step, gate: ()):
        def at(step, gate):
            window(step, gate)
            return make(step, gate)

        first = make(0, ())
        up, down = sum_step(first, first, 1)
        second = at(1, first)
        up = jnp.where(col == 0, second, first) + up
        down = jnp.where(col == 3, second, first) + down
        gate = (up, down)
        up, down = sum_step(up, down, 2)
        third = at(2, gate)
        up = jnp.where(col == 1, second, third) + up
        down = jnp.where(col == 2, second, third) + down
        gate = (up, down)
        up, down = sum_step(up, down, 3)
        fourth = lax.optimization_barrier(at(3, gate))
        return fourth.astype(F32) + up.astype(F32) + down.astype(F32)

    def both_cores(half, axis):
        other = lax.ppermute(half, "dp", swap)
        first = jnp.where(core == 0, half, other)
        second = jnp.where(core == 0, other, half)
        return jnp.concatenate([first, second], axis=axis).astype(F32)

    def sum_sent(left_mat, right_other):
        return lax.ppermute(left_transposed(left_mat, right_other).astype(BF16), "dp", swap)

    def sum_kept(left_mat, right_own, sent):
        total = (left_transposed(left_mat, right_own) + sent.astype(F32)).astype(BF16)
        return total, lax.psum_scatter(total, "row", scatter_dimension=0, tiled=True)

    by_x = [(0, 1), (1, 0), (2, 3), (3, 2)]
    by_y = [(0, 2), (2, 0), (1, 3), (3, 1)]

    def row_first(half):
        if rows != 4:
            return (half,)
        return half, lax.ppermute(half, "row", by_x), lax.ppermute(half, "row", by_y)

    def row_second(pieces):
        if rows != 4:
            return pieces
        middle = pieces[0].shape[0] // 2
        return (
            *pieces,
            lax.ppermute(pieces[1][:middle], "row", by_y),
            lax.ppermute(pieces[2][middle:], "row", by_x),
        )

    def row_blocks(pieces):
        if rows != 4:
            whole = lax.all_gather(pieces[0], ("row", "dp"), axis=0, tiled=False)
            whole = whole.reshape(rows, cores, *pieces[0].shape)
            return tuple(lax.dynamic_index_in_dim(whole, one, 1, keepdims=False) for one in (core, 1 - core))
        own, by_one, by_two, corner_top, corner_low = pieces
        middle = own.shape[0] // 2
        held = unset((rows, *own.shape), own.dtype)
        for piece, block, start in (
            (own, row, 0), (by_one, row ^ 1, 0), (by_two, row ^ 2, 0),
            (corner_top, row ^ 3, 0), (corner_low, row ^ 3, middle),
        ):
            held = lax.dynamic_update_slice(held, piece[None], (block, start, 0))
        return held, lax.ppermute(held, "dp", swap)

    def row_columns(pieces):
        if rows != 4:
            return lax.all_gather(pieces[0], "row", axis=1, tiled=True)
        own, by_one, by_two, corner_top, corner_low = pieces
        height, block = own.shape
        held = unset((height, rows * block), own.dtype)
        for piece, number, start in (
            (own, row, 0), (by_one, row ^ 1, 0), (by_two, row ^ 2, 0),
            (corner_top, row ^ 3, 0), (corner_low, row ^ 3, height // 2),
        ):
            held = lax.dynamic_update_slice(held, piece, (start, number * block))
        return held

    qkv_start = jnp.concatenate([own_half(one, 1) for one in (w_query, w_key, w_value)], axis=1)
    qkv_pieces = row_first(qkv_start)
    tables = rope_tables(positions)
    seg_col, seg_row = segment_ids[:, None], segment_ids[None, :]
    qkv_pieces = row_second(after(qkv_pieces, tables, seg_col))
    out_pieces = row_first(own_half(w_out, 0))
    out_pieces = row_second(out_pieces)
    out_own = row_columns(out_pieces)
    out_left, out_right = [out_own], [out_own]
    for step in range(1, cols):
        one, two = line_step(out_left[-1], out_right[-1], step)
        out_left.append(one)
        out_right.append(two)
    gate_up_half, down_half = after(
        (own_half(jnp.concatenate([w_gate, w_up], axis=1), 0), own_half(w_down, 0)), qkv_pieces
    )
    full_gate_up = lax.all_gather(gate_up_half, ("row", "dp"), axis=0, tiled=True)
    down_pieces = row_first(down_half)
    qkv_halves = [one.reshape(width, 3 * half_width) for one in row_blocks(qkv_pieces)]

    qkv = qkv_product(slot_index[3], block_input, qkv_halves)
    query_raw, key_raw = qkv[:, :local_width], qkv[:, local_width : 2 * local_width]
    query_sq, key_sq = lax.psum(
        (jnp.sum(query_raw * query_raw, axis=1), jnp.sum(key_raw * key_raw, axis=1)), "col"
    )
    query_scale = lax.rsqrt(query_sq / width + EPS)[:, None]
    key_scale = lax.rsqrt(key_sq / width + EPS)[:, None]
    scales = (query_scale, key_scale)
    gains = (query_gain[None, :], key_gain[None, :])
    query_rot, key_rot, value_heads, attended, log_total = attend_forward(
        qkv, scales, gains, tables, seg_col, seg_row, heads
    )

    lefts, rights = [attended], [attended]
    for step in range(1, cols):
        from_left, from_right = line_step(lefts[-1], rights[-1], step)
        lefts.append(from_left)
        rights.append(from_right)
        if step == 1:
            out_halves = jnp.concatenate(
                [out_own] + [out_right[k] + out_left[cols - k] for k in range(1, cols)], axis=0
            )
            out_halves = (out_halves, lax.ppermute(out_halves, "dp", swap))
        if step == 2:
            down_pieces = row_second(after(down_pieces, lefts[1], rights[1]))
        if step == 3:
            down_halves = row_blocks(down_pieces)
    attended_all = (attended, *lefts[1:], *rights[1:])

    held = dict(f=(), b=(), a=(), o=(), m=())
    gain_sums = dict(mlp=0.0, attn=0.0)

    def forward_work(slot, gate):
        results = forward_chunk(
            slot_index[slot], after(attended_all, gate), out_halves, block_input, attn_row, full_gate_up,
            down_halves, chunk, held["f"],
        )
        held["f"] = results[:6]
        return results[6]

    down_own = sum_slots(forward_work).astype(BF16)
    attn_raw, attn_scale, hidden_b, gate_proj, up_proj, mixed_act = held["f"]
    mlp_parts = [None] * cols
    down_slots = [None] * cols

    def backward_work(slot, down_rows):
        down_slots[slot] = down_rows
        results = backward_chunk(
            slot_index[slot], down_rows, grad_output, mlp_row, gate_proj, up_proj, full_gate_up,
            down_halves, chunk, held["b"],
        )
        held["b"] = results[:3]
        mlp_parts[slot] = results[3]
        gain_sums["mlp"] = gain_sums["mlp"] + results[4]
        return results[3]

    gather_slots(down_own, backward_work)
    grad_down_in, grad_gate_in, grad_up_in = held["b"]

    blocks = {}
    got = {}

    def mlp_window(step, gate):
        down_left, down_right, hidden_left, gate_right, up_right = after(
            (grad_down_in, mixed_act, hidden_b, grad_gate_in, grad_up_in), gate
        )
        if step == 1:
            got["down"] = sum_sent(down_left, other_half(down_right, 1))
            got["gate"] = sum_sent(hidden_left, other_half(gate_right, 1))
            return got["down"], got["gate"]
        if step == 2:
            blocks["down"] = sum_kept(down_left, own_half(down_right, 1), got["down"])
            got["up"] = sum_sent(hidden_left, other_half(up_right, 1))
            return blocks["down"][0], got["up"]
        blocks["gate"] = sum_kept(hidden_left, own_half(gate_right, 1), got["gate"])
        return blocks["gate"][0]

    mlp_own = sum_slots(lambda slot, gate: mlp_parts[slot], mlp_window).astype(BF16)

    def attention_work(slot, mlp_rows):
        results = attention_chunk(
            slot_index[slot], mlp_rows, grad_output, attn_raw, attn_scale, attn_row, out_halves, half_width,
            chunk, held["a"],
        )
        held["a"] = results[:2]
        gain_sums["attn"] = gain_sums["attn"] + results[2]
        if slot == 3:
            hidden_left, up_right = after((hidden_b, grad_up_in), mlp_rows[0])
            blocks["up"] = sum_kept(hidden_left, own_half(up_right, 1), got["up"])
        for other in {2: (3, 2), 1: (1, 0)}.get(slot, ()):
            output = output_chunk(
                slot_index[other], down_slots[other], after(attn_raw, mlp_rows), attn_scale, block_input, attn_row,
                mlp_row, chunk, held["m"],
            )
            held["m"] = (output,)
        return results[1]

    gather_slots(mlp_own, attention_work)
    grad_attn_in, grad_att = held["a"]
    (block_output,) = held["m"]
    own_grad_hidden = slot_rows(grad_output, 3).astype(F32) + mlp_own.astype(F32)

    query_dz, key_dz, grad_value_in, query_dot, key_dot, grad_query_gain, grad_key_gain = attend_backward(
        qkv, scales, gains, tables, seg_col, seg_row,
        (query_rot, key_rot, value_heads, attended, log_total), grad_att, heads,
    )
    query_dot, key_dot = lax.psum((query_dot[:, 0], key_dot[:, 0]), "col")
    grad_query_in = (
        query_scale * (query_dz - query_raw * query_scale * (query_dot / width)[:, None])
    ).astype(BF16)
    grad_key_in = (
        key_scale * (key_dz - key_raw * key_scale * (key_dot / width)[:, None])
    ).astype(BF16)
    gain_pack = jnp.concatenate([grad_query_gain, grad_key_gain, gain_sums["attn"], gain_sums["mlp"]], axis=1)

    grad_halves = [
        jnp.concatenate([picker(one, 1) for one in (grad_query_in, grad_key_in, grad_value_in)], axis=1)
        for picker in (own_half, other_half)
    ]

    def input_work(slot, gate):
        own, other = after([slot_rows(one, slot) for one in grad_halves], gate)
        return (times_transposed(own, qkv_halves[0]) + times_transposed(other, qkv_halves[1])).astype(BF16)

    def input_window(step, gate):
        nonlocal gain_pack
        pack, own, other, tokens_in, left_out, right_out = after(
            (gain_pack, *grad_halves, block_input, grad_attn_in, attended), gate
        )
        if step == 1:
            got["qkv"] = sum_sent(tokens_in, other)
            got["out"] = sum_sent(left_out, other_half(right_out, 1))
            gain_pack = pack + lax.ppermute(pack, "dp", swap)
            return got["qkv"], got["out"], gain_pack
        if step == 2:
            blocks["out"] = sum_kept(left_out, own_half(right_out, 1), got["out"])
            blocks["qkv"] = sum_kept(after(tokens_in, blocks["out"][0]), own, got["qkv"])
            if rows == 4:
                gain_pack = pack + lax.ppermute(pack, "row", by_x)
            return
        gain_pack = pack + lax.ppermute(pack, "row", by_y) if rows == 4 else lax.psum(pack, "row")

    input_own = sum_slots(input_work, input_window)

    results = {}
    quarter = local_width // 2

    def projection(index):
        pair = both_cores(blocks["qkv"][1][None, :, index * quarter : (index + 1) * quarter], 0)
        return jnp.concatenate([pair[0], pair[1]], axis=1)

    def output_work(slot, rows_in):
        held["o"] = (place_rows(slot_index[slot], rows_in, tokens_here, F32, held["o"]),)
        if slot == 3:
            results["down"] = jnp.transpose(both_cores(blocks["down"][1], 1))
            results["gate"] = both_cores(blocks["gate"][1], 1)
            return held["o"], results["down"], results["gate"]
        if slot == 2:
            results["up"] = both_cores(blocks["up"][1], 1)
            return held["o"], results["up"]
        if slot == 1:
            results["out"] = jnp.transpose(both_cores(blocks["out"][1], 1))
            results["qkv"] = [projection(index) for index in range(3)]
            return held["o"], results["out"], results["qkv"]
        return held["o"]

    gather_slots((own_grad_hidden + input_own).astype(BF16), output_work)
    ends = (local_width, 2 * local_width, 2 * local_width + width)
    gain_grads = jnp.split(gain_pack[0], ends)
    return (
        block_output,
        held["o"][0],
        *results["qkv"],
        results["out"],
        results["gate"],
        results["up"],
        results["down"],
        *gain_grads,
    )


def layer(sizes, *arrays):
    return shards(sizes, *arrays)


def solution(mesh):
    in_specs = (
        P(("dp", "row"), None),
        P(("dp", "row")),
        P(("dp", "row")),
        P("row", "col"),
        P("row", "col"),
        P("row", "col"),
        P("col", "row"),
        P("row", "col"),
        P("row", "col"),
        P("col", "row"),
        P("col"),
        P("col"),
        P(),
        P(),
        P(("dp", "row"), None),
    )
    out_specs = (
        P(("dp", "row"), None),
        P(("dp", "row"), None),
        P("row", "col"),
        P("row", "col"),
        P("row", "col"),
        P("col", "row"),
        P("row", "col"),
        P("row", "col"),
        P("col", "row"),
        P("col"),
        P("col"),
        P(),
        P(),
    )
    sizes = (mesh.shape["dp"], mesh.shape["row"], mesh.shape["col"])
    return jax.shard_map(
        functools.partial(layer, sizes), mesh=mesh, in_specs=in_specs, out_specs=out_specs, check_vma=False
    )
```

```python
import functools

import jax
import jax.numpy as jnp
from jax import lax
from jax.experimental import pallas as pl
from jax.experimental.pallas import tpu as pltpu
from jax.sharding import PartitionSpec as P


HD = 128
LEN = 1024
BQ = 256
VMEM = 60 << 20

EPS = 1e-06
THETA = 500000.0
NEG_FILL = -1e30
SCORE_SCALE = HD ** (-0.5)
F32 = jnp.float32
BF16 = jnp.bfloat16


def plain_dot(left_mat, right_mat):
    return jnp.dot(left_mat, right_mat, preferred_element_type=F32)


def times_transposed(left_mat, right_mat):
    return lax.dot_general(
        left_mat, right_mat, (((1,), (1,)), ((), ())), preferred_element_type=F32
    )


def left_transposed(left_mat, right_mat):
    return lax.dot_general(
        left_mat, right_mat, (((0,), (0,)), ((), ())), preferred_element_type=F32
    )


def rope_tables(positions):
    half_dim = HD // 2
    inv_freq = THETA ** (-(jnp.arange(half_dim, dtype=F32) * 2.0) / HD)
    angles = positions.astype(F32)[:, None] * inv_freq[None, :]
    cos_half, sin_half = jnp.cos(angles), jnp.sin(angles)
    cosine = jnp.concatenate([cos_half, cos_half], axis=-1)
    sine_signed = jnp.concatenate([-sin_half, sin_half], axis=-1)
    return cosine, sine_signed


def fill_mask(bias_ref, seg_col_ref, seg_row_ref):
    @pl.when(pl.program_id(0) == 0)
    def _():
        for first in range(0, LEN, BQ):
            keys = first + BQ
            rows = seg_col_ref[first:keys, :]
            cols = seg_row_ref[:, :keys]
            query_index = first + lax.broadcasted_iota(jnp.int32, (BQ, keys), 0)
            key_index = lax.broadcasted_iota(jnp.int32, (BQ, keys), 1)
            allowed = (rows == cols) & (key_index <= query_index)
            bias_ref[first:keys, :keys] = jnp.where(allowed, 0.0, NEG_FILL)


def attend_forward_kernel(
    q_ref, k_ref, v_ref, qs_ref, ks_ref, qg_ref, kg_ref, cos_ref, sin_ref, segc_ref, segr_ref,
    qrot_ref, krot_ref, vb_ref, att_ref, log_ref, bias_ref,
):
    fill_mask(bias_ref, segc_ref, segr_ref)
    cosine, sine = cos_ref[...], sin_ref[...]

    def turned(raw, scale, gain):
        norm = raw * scale * gain
        return (norm * cosine + pltpu.roll(norm, HD // 2, 1) * sine).astype(BF16)

    qrot_ref[...] = turned(q_ref[...], qs_ref[...], qg_ref[...])
    krot_ref[...] = turned(k_ref[...], ks_ref[...], kg_ref[...])
    vb_ref[...] = v_ref[...].astype(BF16)
    for first in range(0, LEN, BQ):
        keys = first + BQ
        scores = times_transposed(qrot_ref[first:keys, :], krot_ref[:keys, :]) * SCORE_SCALE
        masked = scores + bias_ref[first:keys, :keys]
        peak = jnp.max(masked, axis=1, keepdims=True)
        weight = jnp.exp(masked - peak)
        total = jnp.sum(weight, axis=1, keepdims=True)
        probs = (weight * (1.0 / total)).astype(BF16)
        att_ref[first:keys, :] = plain_dot(probs, vb_ref[:keys, :]).astype(BF16)
        log_ref[0, first:keys, :] = peak + jnp.log(total)


def attend_backward_kernel(
    q_ref, k_ref, qs_ref, ks_ref, qg_ref, kg_ref, cos_ref, sin_ref, segc_ref, segr_ref,
    qrot_ref, krot_ref, vb_ref, att_ref, log_ref, grad_ref,
    dzq_ref, dzk_ref, gv_ref, dotq_ref, dotk_ref, gainq_ref, gaink_ref,
    dq_acc, dk_acc, dv_acc, bias_ref,
):
    fill_mask(bias_ref, segc_ref, segr_ref)
    dk_acc[...] = jnp.zeros_like(dk_acc)
    dv_acc[...] = jnp.zeros_like(dv_acc)
    for first in range(0, LEN, BQ):
        keys = first + BQ
        queries = qrot_ref[first:keys, :]
        grads = grad_ref[first:keys, :]
        scores = times_transposed(queries, krot_ref[:keys, :]) * SCORE_SCALE
        probs = jnp.exp(scores + bias_ref[first:keys, :keys] - log_ref[0, first:keys, :])
        delta = jnp.sum(
            grads.astype(F32) * att_ref[first:keys, :].astype(F32), axis=1, keepdims=True
        )
        grad_probs = times_transposed(grads, vb_ref[:keys, :])
        grad_scores = (probs * (grad_probs - delta) * SCORE_SCALE).astype(BF16)
        dq_acc[first:keys, :] = plain_dot(grad_scores, krot_ref[:keys, :])
        dk_acc[:keys, :] += left_transposed(grad_scores, queries)
        dv_acc[:keys, :] += left_transposed(probs.astype(BF16), grads)
    gv_ref[...] = dv_acc[...].astype(BF16)
    cosine, sine = cos_ref[...], sin_ref[...]

    def finish(acc, raw_ref, scale_ref, gain_ref, dz_ref, dot_ref, gain_grad_ref):
        grad_rot = acc[...]
        grad_norm = grad_rot * cosine - pltpu.roll(grad_rot, HD // 2, 1) * sine
        unit = raw_ref[...] * scale_ref[...]
        gain_grad_ref[...] = jnp.sum(grad_norm * unit, axis=0, keepdims=True)
        grad_unit = grad_norm * gain_ref[...]
        dz_ref[...] = grad_unit
        part = jnp.sum(grad_unit * unit, axis=1, keepdims=True)

        @pl.when(pl.program_id(0) == 0)
        def _():
            dot_ref[...] = part

        @pl.when(pl.program_id(0) > 0)
        def _():
            dot_ref[...] += part

    finish(dq_acc, q_ref, qs_ref, qg_ref, dzq_ref, dotq_ref, gainq_ref)
    finish(dk_acc, k_ref, ks_ref, kg_ref, dzk_ref, dotk_ref, gaink_ref)


def head_spec(offset):
    return pl.BlockSpec((LEN, HD), lambda h: (0, offset + h))


def whole_spec(shape):
    return pl.BlockSpec(shape, lambda h: (0,) * len(shape))


def gain_spec():
    return pl.BlockSpec((1, HD), lambda h: (0, h))


LOG_SPEC = pl.BlockSpec((1, LEN, 1), lambda h: (h, 0, 0))
COLUMN = (LEN, 1)
TABLE = (LEN, HD)


def attend_forward(qkv, scales, gains, tables, seg_col, seg_row, heads):
    width = heads * HD
    piece = jax.ShapeDtypeStruct((LEN, width), BF16)
    return pl.pallas_call(
        attend_forward_kernel,
        grid=(heads,),
        in_specs=[
            head_spec(0), head_spec(heads), head_spec(2 * heads),
            whole_spec(COLUMN), whole_spec(COLUMN), gain_spec(), gain_spec(),
            whole_spec(TABLE), whole_spec(TABLE), whole_spec(COLUMN), whole_spec((1, LEN)),
        ],
        out_specs=[head_spec(0)] * 4 + [LOG_SPEC],
        out_shape=[piece] * 4 + [jax.ShapeDtypeStruct((heads, LEN, 1), F32)],
        scratch_shapes=[pltpu.VMEM((LEN, LEN), F32)],
        compiler_params=pltpu.CompilerParams(vmem_limit_bytes=VMEM),
        cost_estimate=pl.CostEstimate(
            flops=heads * 4 * LEN * LEN * HD, bytes_accessed=LEN * width * 20, transcendentals=0
        ),
        name="attend_forward",
    )(qkv, qkv, qkv, *scales, *gains, *tables, seg_col, seg_row)


def attend_backward(qkv, scales, gains, tables, seg_col, seg_row, saved, grad_att, heads):
    width = heads * HD
    full = jax.ShapeDtypeStruct((LEN, width), F32)
    column = jax.ShapeDtypeStruct(COLUMN, F32)
    gain_row = jax.ShapeDtypeStruct((1, width), F32)
    return pl.pallas_call(
        attend_backward_kernel,
        grid=(heads,),
        in_specs=[
            head_spec(0), head_spec(heads),
            whole_spec(COLUMN), whole_spec(COLUMN), gain_spec(), gain_spec(),
            whole_spec(TABLE), whole_spec(TABLE), whole_spec(COLUMN), whole_spec((1, LEN)),
            head_spec(0), head_spec(0), head_spec(0), head_spec(0), LOG_SPEC, head_spec(0),
        ],
        out_specs=[
            head_spec(0), head_spec(0), head_spec(0),
            whole_spec(COLUMN), whole_spec(COLUMN), gain_spec(), gain_spec(),
        ],
        out_shape=[
            full, full, jax.ShapeDtypeStruct((LEN, width), BF16), column, column, gain_row, gain_row,
        ],
        scratch_shapes=[pltpu.VMEM((LEN, HD), F32)] * 3 + [pltpu.VMEM((LEN, LEN), F32)],
        compiler_params=pltpu.CompilerParams(vmem_limit_bytes=VMEM),
        cost_estimate=pl.CostEstimate(
            flops=heads * 10 * LEN * LEN * HD, bytes_accessed=LEN * width * 40, transcendentals=0
        ),
        name="attend_backward",
    )(qkv, qkv, *scales, *gains, *tables, seg_col, seg_row, *saved, grad_att)


def fetch_choice(idx_ref, refs, held_ref, sem):
    for number, ref in enumerate(refs):

        @pl.when(idx_ref[2] == number)
        def _():
            copy = pltpu.make_async_copy(ref, held_ref, sem)
            copy.start()
            copy.wait()


def half_tile(step, core, tiles):
    per_half = tiles // 2
    return ((core + step // per_half) % 2) * per_half + step % per_half


def forward_chunk_kernel(
    idx_ref, *refs, out_steps, tiles,
):
    own_ref, left1, left2, left3, right1, right2, right3 = refs[:7]
    wo_own_ref, wo_oth_ref, x_ref, gain_ref, wg_ref, wu_ref, wd_own_ref, wd_oth_ref = refs[7:15]
    raw_ref, scale_ref, hb_ref, gate_ref, up_ref, mixed_ref, part_ref, acc_ref, att_ref = refs[-9:]
    depth, out_tile = wo_own_ref.shape
    blocks, _, block = wd_own_ref.shape
    step = pl.program_id(0)
    core = idx_ref[1]

    @pl.when(step == 0)
    def _():
        quarter = own_ref.shape[1] // 2
        pieces = (
            own_ref[...], right1[...] + left3[...], right2[...] + left2[...], right3[...] + left1[...],
        )
        for half in range(2):
            for number, piece in enumerate(pieces):
                start = half * depth + number * quarter
                att_ref[:, start : start + quarter] = piece[:, half * quarter : (half + 1) * quarter]

    @pl.when(step < out_steps)
    def _():
        own = att_ref[:, pl.ds(pl.multiple_of(core * depth, depth), depth)]
        other = att_ref[:, pl.ds(pl.multiple_of((1 - core) * depth, depth), depth)]
        acc_ref[:, pl.ds(pl.multiple_of(step * out_tile, out_tile), out_tile)] = plain_dot(
            own, wo_own_ref[...]
        ) + plain_dot(other, wo_oth_ref[...])

    @pl.when(step == out_steps - 1)
    def _():
        raw = acc_ref[...]
        scale = lax.rsqrt(jnp.mean(raw * raw, axis=1, keepdims=True) + EPS)
        raw_ref[...] = raw.astype(BF16)
        scale_ref[...] = scale
        hb_ref[...] = (x_ref[...].astype(F32) + raw * scale * gain_ref[...]).astype(BF16)
        acc_ref[...] = jnp.zeros_like(acc_ref)

    def tile_work(wd_ref):
        hidden_b = hb_ref[...]
        gate = plain_dot(hidden_b, wg_ref[...])
        up = plain_dot(hidden_b, wu_ref[...])
        mixed = (gate * jax.nn.sigmoid(gate) * up).astype(BF16)
        gate_ref[...] = gate.astype(BF16)
        up_ref[...] = up.astype(BF16)
        mixed_ref[...] = mixed
        for j in range(blocks):
            acc_ref[:, j * block : (j + 1) * block] += plain_dot(mixed, wd_ref[j])

    @pl.when((step >= out_steps) & (step < out_steps + tiles // 2))
    def _():
        tile_work(wd_own_ref)

    @pl.when(step >= out_steps + tiles // 2)
    def _():
        tile_work(wd_oth_ref)

    @pl.when(step == out_steps + tiles - 1)
    def _():
        part_ref[...] = acc_ref[...].astype(BF16)


TILE = 512


def forward_chunk(index, attended, out_halves, block_input, gain, w_gate_up, down_halves, chunk, before):
    tokens, width = block_input.shape
    hidden = w_gate_up.shape[1] // 2
    depth = out_halves[0].shape[0]
    blocks, _, block = down_halves[0].shape
    tiles = hidden // TILE
    out_steps = width // TILE

    def tile_of(j, idx):
        return half_tile(jnp.maximum(j - out_steps, 0), idx[1], tiles)

    rows = pl.BlockSpec((chunk, width), lambda j, idx: (idx[0], 0))
    out_half = pl.BlockSpec((depth, TILE), lambda j, idx: (0, jnp.minimum(j, out_steps - 1)))
    gate_tile = pl.BlockSpec((width, TILE), lambda j, idx: (0, tile_of(j, idx)))
    up_tile = pl.BlockSpec((width, TILE), lambda j, idx: (0, tiles + tile_of(j, idx)))
    down_own = pl.BlockSpec(
        (blocks, TILE, block), lambda j, idx: (0, jnp.clip(j - out_steps, 0, tiles // 2 - 1), 0)
    )
    down_oth = pl.BlockSpec(
        (blocks, TILE, block), lambda j, idx: (0, jnp.maximum(j - out_steps - tiles // 2, 0), 0)
    )
    act_tile = pl.BlockSpec((chunk, TILE), lambda j, idx: (idx[0], tile_of(j, idx)))
    before = tuple(before)
    return pl.pallas_call(
        functools.partial(forward_chunk_kernel, out_steps=out_steps, tiles=tiles),
        grid_spec=pltpu.PrefetchScalarGridSpec(
            num_scalar_prefetch=1,
            grid=(out_steps + tiles,),
            in_specs=[
                *[pl.BlockSpec((chunk, attended[0].shape[1]), lambda j, idx: (idx[0], 0))] * 7,
                out_half, out_half, rows, pl.BlockSpec((1, width), lambda j, idx: (0, 0)),
                gate_tile, up_tile, down_own, down_oth,
            ] + [pl.BlockSpec(memory_space=pl.ANY)] * len(before),
            out_specs=[
                rows, pl.BlockSpec((chunk, 1), lambda j, idx: (idx[0], 0)), rows, act_tile, act_tile, act_tile,
                pl.BlockSpec((chunk, width), lambda j, idx: (0, 0)),
            ],
            scratch_shapes=[pltpu.VMEM((chunk, width), F32), pltpu.VMEM((chunk, 2 * depth), BF16)],
        ),
        out_shape=[
            jax.ShapeDtypeStruct((tokens, width), BF16),
            jax.ShapeDtypeStruct((tokens, 1), F32),
            jax.ShapeDtypeStruct((tokens, width), BF16),
            jax.ShapeDtypeStruct((tokens, hidden), BF16),
            jax.ShapeDtypeStruct((tokens, hidden), BF16),
            jax.ShapeDtypeStruct((tokens, hidden), BF16),
            jax.ShapeDtypeStruct((chunk, width), BF16),
        ],
        input_output_aliases={16 + i: i for i in range(len(before))},
        compiler_params=pltpu.CompilerParams(vmem_limit_bytes=VMEM),
        cost_estimate=pl.CostEstimate(
            flops=2 * chunk * width * (width + 3 * hidden),
            bytes_accessed=2 * width * (width + 3 * hidden),
            transcendentals=0,
        ),
        name="forward_chunk",
    )(index, *attended, *out_halves, block_input, gain, w_gate_up, w_gate_up, *down_halves, *before)


def backward_chunk_kernel(
    idx_ref, grad_ref, mlp_gain_ref, gate_ref, up_ref, wg_ref, wu_ref, wd_own_ref, wd_oth_ref, *refs, tiles, choices,
):
    gdi_ref, gg_ref, gu_ref, part_ref, gain_grad_ref, acc_ref, down_ref, sem = refs[-8:]
    blocks, _, block = wd_own_ref.shape
    step = pl.program_id(0)

    @pl.when(step == 0)
    def _():
        fetch_choice(idx_ref, refs[:choices], down_ref, sem)
        down_raw = down_ref[...].astype(F32)
        down_scale = lax.rsqrt(jnp.mean(down_raw * down_raw, axis=1, keepdims=True) + EPS)
        unit = down_raw * down_scale
        grad_y = grad_ref[...].astype(F32)
        gain_grad_ref[...] = jnp.sum(grad_y * unit, axis=0, keepdims=True)
        grad_unit = grad_y * mlp_gain_ref[...]
        mean = jnp.mean(grad_unit * unit, axis=1, keepdims=True)
        gdi_ref[...] = (down_scale * (grad_unit - unit * mean)).astype(BF16)
        acc_ref[...] = jnp.zeros_like(acc_ref)

    def tile_work(wd_ref):
        grad_mixed = times_transposed(gdi_ref[:, :block], wd_ref[0])
        for j in range(1, blocks):
            grad_mixed += times_transposed(gdi_ref[:, j * block : (j + 1) * block], wd_ref[j])
        gate = gate_ref[...].astype(F32)
        sig = jax.nn.sigmoid(gate)
        grad_gate = (grad_mixed * up_ref[...].astype(F32) * sig * (1.0 + gate * (1.0 - sig))).astype(BF16)
        grad_up = (grad_mixed * (gate * sig)).astype(BF16)
        gg_ref[...] = grad_gate
        gu_ref[...] = grad_up
        acc_ref[...] += times_transposed(grad_gate, wg_ref[...]) + times_transposed(grad_up, wu_ref[...])

    @pl.when(step < tiles // 2)
    def _():
        tile_work(wd_own_ref)

    @pl.when(step >= tiles // 2)
    def _():
        tile_work(wd_oth_ref)

    @pl.when(step == tiles - 1)
    def _():
        part_ref[...] = acc_ref[...].astype(BF16)


def backward_chunk(
    index, down_rows, grad_output, mlp_gain, gate, up, w_gate_up, down_halves, chunk, before,
):
    tokens, width = grad_output.shape
    hidden = w_gate_up.shape[1] // 2
    blocks, _, block = down_halves[0].shape
    tiles = hidden // TILE

    def tile_of(j, idx):
        return half_tile(j, idx[1], tiles)

    rows = pl.BlockSpec((chunk, width), lambda j, idx: (idx[0], 0))
    gain_row = pl.BlockSpec((1, width), lambda j, idx: (0, 0))
    gate_tile = pl.BlockSpec((width, TILE), lambda j, idx: (0, tile_of(j, idx)))
    up_tile = pl.BlockSpec((width, TILE), lambda j, idx: (0, tiles + tile_of(j, idx)))
    act_tile = pl.BlockSpec((chunk, TILE), lambda j, idx: (idx[0], tile_of(j, idx)))
    before = tuple(before)
    return pl.pallas_call(
        functools.partial(backward_chunk_kernel, tiles=tiles, choices=len(down_rows)),
        grid_spec=pltpu.PrefetchScalarGridSpec(
            num_scalar_prefetch=1,
            grid=(tiles,),
            in_specs=[
                rows, gain_row, act_tile, act_tile, gate_tile, up_tile,
                pl.BlockSpec((blocks, TILE, block), lambda j, idx: (0, jnp.minimum(j, tiles // 2 - 1), 0)),
                pl.BlockSpec((blocks, TILE, block), lambda j, idx: (0, jnp.maximum(j - tiles // 2, 0), 0)),
            ] + [pl.BlockSpec(memory_space=pl.ANY)] * (len(down_rows) + len(before)),
            out_specs=[rows, act_tile, act_tile, pl.BlockSpec((chunk, width), lambda j, idx: (0, 0)), gain_row],
            scratch_shapes=[
                pltpu.VMEM((chunk, width), F32), pltpu.VMEM((chunk, width), BF16), pltpu.SemaphoreType.DMA(()),
            ],
        ),
        out_shape=[
            jax.ShapeDtypeStruct((tokens, width), BF16),
            jax.ShapeDtypeStruct((tokens, hidden), BF16),
            jax.ShapeDtypeStruct((tokens, hidden), BF16),
            jax.ShapeDtypeStruct((chunk, width), BF16),
            jax.ShapeDtypeStruct((1, width), F32),
        ],
        input_output_aliases={9 + len(down_rows) + i: i for i in range(len(before))},
        compiler_params=pltpu.CompilerParams(vmem_limit_bytes=VMEM),
        cost_estimate=pl.CostEstimate(
            flops=6 * chunk * width * hidden, bytes_accessed=6 * width * hidden, transcendentals=0
        ),
        name="backward_chunk",
    )(index, grad_output, mlp_gain, gate, up, w_gate_up, w_gate_up, *down_halves, *down_rows, *before)


PARTS = 4


def attention_chunk_kernel(
    idx_ref, grad_ref, raw_ref, scale_ref, gain_ref, wo_own_ref, wo_oth_ref, *refs, choices,
):
    gai_ref, gatt_ref, gain_grad_ref, held_ref, sem = refs[-5:]
    half = wo_own_ref.shape[0]
    core = idx_ref[1]
    step = pl.program_id(0)

    @pl.when(step == 0)
    def _():
        fetch_choice(idx_ref, refs[:choices], held_ref, sem)
        gain_grad_ref[...] = jnp.zeros_like(gain_grad_ref)

    size = grad_ref.shape[0]
    scale = scale_ref[...]
    unit = raw_ref[...].astype(F32) * scale
    mlp = held_ref[pl.ds(pl.multiple_of(step * size, size), size), :]
    grad_hidden = grad_ref[...].astype(F32) + mlp.astype(F32)
    gain_grad_ref[...] += jnp.sum(grad_hidden * unit, axis=0, keepdims=True)
    grad_unit = grad_hidden * gain_ref[...]
    mean = jnp.mean(grad_unit * unit, axis=1, keepdims=True)
    grad_attn_in = (scale * (grad_unit - unit * mean)).astype(BF16)
    gai_ref[...] = grad_attn_in
    for place, w_ref in ((core, wo_own_ref), (1 - core, wo_oth_ref)):
        gatt_ref[:, pl.ds(pl.multiple_of(place * half, half), half)] = times_transposed(
            grad_attn_in, w_ref[...]
        ).astype(BF16)


def attention_chunk(index, mlp_rows, grad_output, raw, scale, gain, out_halves, half, chunk, before):
    tokens, width = grad_output.shape
    size = chunk
    rows = pl.BlockSpec((size, width), lambda j, idx: (idx[0], 0))
    gain_row = pl.BlockSpec((1, width), lambda j, idx: (0, 0))
    own_heads = pl.BlockSpec((half, width), lambda j, idx: (0, 0))
    before = tuple(before)
    return pl.pallas_call(
        functools.partial(attention_chunk_kernel, choices=len(mlp_rows)),
        grid_spec=pltpu.PrefetchScalarGridSpec(
            num_scalar_prefetch=1,
            grid=(1,),
            in_specs=[
                rows, rows, pl.BlockSpec((size, 1), lambda j, idx: (idx[0], 0)), gain_row,
                own_heads, own_heads,
            ] + [pl.BlockSpec(memory_space=pl.ANY)] * (len(mlp_rows) + len(before)),
            out_specs=[rows, pl.BlockSpec((size, 2 * half), lambda j, idx: (idx[0], 0)), gain_row],
            scratch_shapes=[pltpu.VMEM((chunk, width), BF16), pltpu.SemaphoreType.DMA(())],
        ),
        out_shape=[
            jax.ShapeDtypeStruct((tokens, width), BF16),
            jax.ShapeDtypeStruct((tokens, 2 * half), BF16),
            jax.ShapeDtypeStruct((1, width), F32),
        ],
        input_output_aliases={7 + len(mlp_rows) + i: i for i in range(len(before))},
        compiler_params=pltpu.CompilerParams(vmem_limit_bytes=VMEM),
        cost_estimate=pl.CostEstimate(
            flops=4 * chunk * width * half, bytes_accessed=16 * chunk * width, transcendentals=0
        ),
        name="attention_chunk",
    )(index, grad_output, raw, scale, gain, *out_halves, *mlp_rows, *before)


def output_chunk_kernel(idx_ref, raw_ref, scale_ref, x_ref, attn_gain_ref, mlp_gain_ref, *refs, choices):
    out_ref, held_ref, sem = refs[-3:]
    step = pl.program_id(0)

    @pl.when(step == 0)
    def _():
        fetch_choice(idx_ref, refs[:choices], held_ref, sem)

    size = out_ref.shape[0]
    down_raw = held_ref[pl.ds(pl.multiple_of(step * size, size), size), :].astype(F32)
    down_scale = lax.rsqrt(jnp.mean(down_raw * down_raw, axis=1, keepdims=True) + EPS)
    hidden = x_ref[...].astype(F32) + raw_ref[...].astype(F32) * scale_ref[...] * attn_gain_ref[...]
    out_ref[...] = (hidden + down_raw * down_scale * mlp_gain_ref[...]).astype(BF16)


def output_chunk(index, down_rows, raw, scale, block_input, attn_gain, mlp_gain, chunk, before):
    tokens, width = block_input.shape
    size = chunk // PARTS
    rows = pl.BlockSpec((size, width), lambda j, idx: (PARTS * idx[0] + j, 0))
    gain_row = pl.BlockSpec((1, width), lambda j, idx: (0, 0))
    before = tuple(before)
    return pl.pallas_call(
        functools.partial(output_chunk_kernel, choices=len(down_rows)),
        grid_spec=pltpu.PrefetchScalarGridSpec(
            num_scalar_prefetch=1,
            grid=(PARTS,),
            in_specs=[
                rows, pl.BlockSpec((size, 1), lambda j, idx: (PARTS * idx[0] + j, 0)), rows, gain_row, gain_row,
            ] + [pl.BlockSpec(memory_space=pl.ANY)] * (len(down_rows) + len(before)),
            out_specs=rows,
            scratch_shapes=[pltpu.VMEM((chunk, width), BF16), pltpu.SemaphoreType.DMA(())],
        ),
        out_shape=jax.ShapeDtypeStruct((tokens, width), BF16),
        input_output_aliases={6 + len(down_rows): 0} if before else {},
        compiler_params=pltpu.CompilerParams(vmem_limit_bytes=VMEM),
        cost_estimate=pl.CostEstimate(flops=0, bytes_accessed=8 * chunk * width, transcendentals=0),
        name="output_chunk",
    )(index, raw, scale, block_input, attn_gain, mlp_gain, *down_rows, *before)


def place_rows_kernel(idx_ref, *refs, choices):
    out_ref, held_ref, sem = refs[-3:]
    step = pl.program_id(0)

    @pl.when(step == 0)
    def _():
        fetch_choice(idx_ref, refs[:choices], held_ref, sem)

    size = out_ref.shape[0]
    out_ref[...] = held_ref[pl.ds(pl.multiple_of(step * size, size), size), :].astype(out_ref.dtype)


def place_rows(index, rows_in, tokens, dtype, before):
    chunk, width = rows_in[0].shape
    before = tuple(before)
    return pl.pallas_call(
        functools.partial(place_rows_kernel, choices=len(rows_in)),
        grid_spec=pltpu.PrefetchScalarGridSpec(
            num_scalar_prefetch=1,
            grid=(4,),
            in_specs=[pl.BlockSpec(memory_space=pl.ANY)] * (len(rows_in) + len(before)),
            out_specs=pl.BlockSpec((chunk // 4, width), lambda j, idx: (4 * idx[0] + j, 0)),
            scratch_shapes=[pltpu.VMEM((chunk, width), BF16), pltpu.SemaphoreType.DMA(())],
        ),
        out_shape=jax.ShapeDtypeStruct((tokens, width), dtype),
        input_output_aliases={1 + len(rows_in): 0} if before else {},
        compiler_params=pltpu.CompilerParams(vmem_limit_bytes=VMEM),
        cost_estimate=pl.CostEstimate(flops=0, bytes_accessed=6 * chunk * width, transcendentals=0),
        name="place_rows",
    )(index, *rows_in, *before)


def after(value, *tokens):
    return lax.optimization_barrier((value, tokens))[0]


def unset_kernel(out_ref):
    pass


def unset(shape, dtype):
    return pl.pallas_call(
        unset_kernel,
        out_specs=pl.BlockSpec(memory_space=pl.ANY),
        out_shape=jax.ShapeDtypeStruct(shape, dtype),
        name="unset",
    )()


def shards(
    sizes,
    block_input,
    segment_ids,
    positions,
    w_query,
    w_key,
    w_value,
    w_out,
    w_gate,
    w_up,
    w_down,
    query_gain,
    key_gain,
    attn_gain,
    mlp_gain,
    grad_output,
):
    cores, rows, cols = sizes
    tokens_here, width = block_input.shape
    assert tokens_here == LEN and cores == 2 and cols == 4
    local_width = w_query.shape[1]
    half_width = local_width // 2
    heads = local_width // HD
    chunk = tokens_here // cols
    core = lax.axis_index("dp")
    row = lax.axis_index("row")
    col = lax.axis_index("col")
    swap = [(0, 1), (1, 0)]
    attn_row, mlp_row = attn_gain[None, :], mlp_gain[None, :]

    def own_half(array, axis):
        half = array.shape[axis] // 2
        return lax.dynamic_slice_in_dim(array, core * half, half, axis)

    def other_half(array, axis):
        half = array.shape[axis] // 2
        return lax.dynamic_slice_in_dim(array, (1 - core) * half, half, axis)

    def gather(weight, axis):
        return lax.all_gather(own_half(weight, axis), ("row", "dp"), axis=axis, tiled=True)

    def line_step(from_left, from_right, step):
        from_left = lax.ppermute(from_left, "col", [(i, i + 1) for i in range(step - 1, cols - 1)])
        from_right = lax.ppermute(from_right, "col", [(i + 1, i) for i in range(cols - step)])
        return from_left, from_right

    def sum_step(up, down, step):
        up = lax.ppermute(up, "col", [(i, i + 1) for i in range(step)])
        down = lax.ppermute(down, "col", [(cols - 1 - i, cols - 2 - i) for i in range(step)])
        return up, down

    def pick(at_zero, at_one, at_two, at_three):
        low = jnp.where(col == 0, at_zero, at_one)
        high = jnp.where(col == 2, at_two, at_three)
        return jnp.where(col < 2, low, high)

    slot_chunk = [pick(3, 3, 0, 0), pick(2, 2, 1, 1), pick(1, 0, 3, 2), col]
    slot_index = [
        jnp.stack([one, core, choice]).astype(jnp.int32)
        for one, choice in zip(slot_chunk, (col, col, col % 2, 0 * col))
    ]

    def slot_rows(array, slot):
        return lax.dynamic_slice_in_dim(array, slot_chunk[slot] * chunk, chunk, 0)

    def gather_slots(own, work):
        left, right, token = [own], [own], ()
        arrived = (
            lambda lefts, rights: (lefts[0],),
            lambda lefts, rights: (rights[1], lefts[1]),
            lambda lefts, rights: (rights[2], rights[1], lefts[1], lefts[2]),
            lambda lefts, rights: (rights[3], rights[2], lefts[2], lefts[3]),
        )
        for step in range(1, cols + 1):
            seen = tuple(left), tuple(right)
            if step < cols:
                from_left, from_right = line_step(left[-1], right[-1], step)
                left.append(from_left)
                right.append(from_right)
            token = work(cols - step, arrived[step - 1](*after(seen, token)))

    def sum_slots(make, window=lambda step, gate: ()):
        def at(step, gate):
            window(step, gate)
            return make(step, gate)

        first = make(0, ())
        up, down = sum_step(first, first, 1)
        second = at(1, first)
        up = jnp.where(col == 0, second, first) + up
        down = jnp.where(col == 3, second, first) + down
        gate = (up, down)
        up, down = sum_step(up, down, 2)
        third = at(2, gate)
        up = jnp.where(col == 1, second, third) + up
        down = jnp.where(col == 2, second, third) + down
        gate = (up, down)
        up, down = sum_step(up, down, 3)
        fourth = lax.optimization_barrier(at(3, gate))
        return fourth.astype(F32) + up.astype(F32) + down.astype(F32)

    def both_cores(half, axis):
        other = lax.ppermute(half, "dp", swap)
        first = jnp.where(core == 0, half, other)
        second = jnp.where(core == 0, other, half)
        return jnp.concatenate([first, second], axis=axis).astype(F32)

    def sum_sent(left_mat, right_other):
        return lax.ppermute(left_transposed(left_mat, right_other).astype(BF16), "dp", swap)

    def sum_kept(left_mat, right_own, sent):
        total = (left_transposed(left_mat, right_own) + sent.astype(F32)).astype(BF16)
        return total, lax.psum_scatter(total, "row", scatter_dimension=0, tiled=True)

    by_x = [(0, 1), (1, 0), (2, 3), (3, 2)]
    by_y = [(0, 2), (2, 0), (1, 3), (3, 1)]

    def row_first(half):
        if rows != 4:
            return (half,)
        return half, lax.ppermute(half, "row", by_x), lax.ppermute(half, "row", by_y)

    def row_second(pieces):
        if rows != 4:
            return pieces
        middle = pieces[0].shape[0] // 2
        return (
            *pieces,
            lax.ppermute(pieces[1][:middle], "row", by_y),
            lax.ppermute(pieces[2][middle:], "row", by_x),
        )

    def row_blocks(pieces):
        if rows != 4:
            whole = lax.all_gather(pieces[0], ("row", "dp"), axis=0, tiled=False)
            whole = whole.reshape(rows, cores, *pieces[0].shape)
            return tuple(lax.dynamic_index_in_dim(whole, one, 1, keepdims=False) for one in (core, 1 - core))
        own, by_one, by_two, corner_top, corner_low = pieces
        middle = own.shape[0] // 2
        held = unset((rows, *own.shape), own.dtype)
        for piece, block, start in (
            (own, row, 0), (by_one, row ^ 1, 0), (by_two, row ^ 2, 0),
            (corner_top, row ^ 3, 0), (corner_low, row ^ 3, middle),
        ):
            held = lax.dynamic_update_slice(held, piece[None], (block, start, 0))
        return held, lax.ppermute(held, "dp", swap)

    def row_columns(pieces):
        if rows != 4:
            return lax.all_gather(pieces[0], "row", axis=1, tiled=True)
        own, by_one, by_two, corner_top, corner_low = pieces
        height, block = own.shape
        held = unset((height, rows * block), own.dtype)
        for piece, number, start in (
            (own, row, 0), (by_one, row ^ 1, 0), (by_two, row ^ 2, 0),
            (corner_top, row ^ 3, 0), (corner_low, row ^ 3, height // 2),
        ):
            held = lax.dynamic_update_slice(held, piece, (start, number * block))
        return held

    full_qkv = gather(jnp.concatenate([w_query, w_key, w_value], axis=1), 0)
    full_gate_up = gather(jnp.concatenate([w_gate, w_up], axis=1), 0)
    out_pieces = row_first(own_half(w_out, 0))
    out_pieces = row_second(out_pieces)
    out_own = row_columns(out_pieces)
    out_left, out_right = [out_own], [out_own]
    for step in range(1, cols):
        one, two = line_step(out_left[-1], out_right[-1], step)
        out_left.append(one)
        out_right.append(two)
    down_pieces = row_first(after(own_half(w_down, 0), full_qkv))

    qkv = plain_dot(block_input, full_qkv)
    query_raw, key_raw = qkv[:, :local_width], qkv[:, local_width : 2 * local_width]
    query_sq, key_sq = lax.psum(
        (jnp.sum(query_raw * query_raw, axis=1), jnp.sum(key_raw * key_raw, axis=1)), "col"
    )
    query_scale = lax.rsqrt(query_sq / width + EPS)[:, None]
    key_scale = lax.rsqrt(key_sq / width + EPS)[:, None]
    scales = (query_scale, key_scale)
    gains = (query_gain[None, :], key_gain[None, :])
    tables = rope_tables(positions)
    seg_col, seg_row = segment_ids[:, None], segment_ids[None, :]
    query_rot, key_rot, value_heads, attended, log_total = attend_forward(
        qkv, scales, gains, tables, seg_col, seg_row, heads
    )

    lefts, rights = [attended], [attended]
    for step in range(1, cols):
        from_left, from_right = line_step(lefts[-1], rights[-1], step)
        lefts.append(from_left)
        rights.append(from_right)
        if step == 1:
            out_halves = jnp.concatenate(
                [out_own] + [out_right[k] + out_left[cols - k] for k in range(1, cols)], axis=0
            )
            out_halves = (out_halves, lax.ppermute(out_halves, "dp", swap))
        if step == 2:
            down_pieces = row_second(after(down_pieces, lefts[1], rights[1]))
        if step == 3:
            down_halves = row_blocks(down_pieces)
    attended_all = (attended, *lefts[1:], *rights[1:])

    held = dict(f=(), b=(), a=(), o=(), m=())
    gain_sums = dict(mlp=0.0, attn=0.0)

    def forward_work(slot, gate):
        results = forward_chunk(
            slot_index[slot], after(attended_all, gate), out_halves, block_input, attn_row, full_gate_up,
            down_halves, chunk, held["f"],
        )
        held["f"] = results[:6]
        return results[6]

    down_own = sum_slots(forward_work).astype(BF16)
    attn_raw, attn_scale, hidden_b, gate_proj, up_proj, mixed_act = held["f"]
    mlp_parts = [None] * cols
    down_slots = [None] * cols

    def backward_work(slot, down_rows):
        down_slots[slot] = down_rows
        results = backward_chunk(
            slot_index[slot], down_rows, grad_output, mlp_row, gate_proj, up_proj, full_gate_up,
            down_halves, chunk, held["b"],
        )
        held["b"] = results[:3]
        mlp_parts[slot] = results[3]
        gain_sums["mlp"] = gain_sums["mlp"] + results[4]
        return results[3]

    gather_slots(down_own, backward_work)
    grad_down_in, grad_gate_in, grad_up_in = held["b"]

    blocks = {}
    got = {}

    def mlp_window(step, gate):
        down_left, down_right, hidden_left, gate_right, up_right = after(
            (grad_down_in, mixed_act, hidden_b, grad_gate_in, grad_up_in), gate
        )
        if step == 1:
            got["down"] = sum_sent(down_left, other_half(down_right, 1))
            got["gate"] = sum_sent(hidden_left, other_half(gate_right, 1))
            return got["down"], got["gate"]
        if step == 2:
            blocks["down"] = sum_kept(down_left, own_half(down_right, 1), got["down"])
            got["up"] = sum_sent(hidden_left, other_half(up_right, 1))
            return blocks["down"][0], got["up"]
        blocks["gate"] = sum_kept(hidden_left, own_half(gate_right, 1), got["gate"])
        return blocks["gate"][0]

    mlp_own = sum_slots(lambda slot, gate: mlp_parts[slot], mlp_window).astype(BF16)

    def attention_work(slot, mlp_rows):
        results = attention_chunk(
            slot_index[slot], mlp_rows, grad_output, attn_raw, attn_scale, attn_row, out_halves, half_width,
            chunk, held["a"],
        )
        held["a"] = results[:2]
        gain_sums["attn"] = gain_sums["attn"] + results[2]
        if slot == 3:
            hidden_left, up_right = after((hidden_b, grad_up_in), mlp_rows[0])
            blocks["up"] = sum_kept(hidden_left, own_half(up_right, 1), got["up"])
        for other in {2: (3, 2), 1: (1, 0)}.get(slot, ()):
            output = output_chunk(
                slot_index[other], down_slots[other], after(attn_raw, mlp_rows), attn_scale, block_input, attn_row,
                mlp_row, chunk, held["m"],
            )
            held["m"] = (output,)
        return results[1]

    gather_slots(mlp_own, attention_work)
    grad_attn_in, grad_att = held["a"]
    (block_output,) = held["m"]
    own_grad_hidden = slot_rows(grad_output, 3).astype(F32) + mlp_own.astype(F32)

    query_dz, key_dz, grad_value_in, query_dot, key_dot, grad_query_gain, grad_key_gain = attend_backward(
        qkv, scales, gains, tables, seg_col, seg_row,
        (query_rot, key_rot, value_heads, attended, log_total), grad_att, heads,
    )
    query_dot, key_dot = lax.psum((query_dot[:, 0], key_dot[:, 0]), "col")

    def qkv_grads(pick_rows):
        pieces = []
        for grad, raw, scale, dot in (
            (query_dz, query_raw, query_scale, query_dot), (key_dz, key_raw, key_scale, key_dot),
        ):
            grad, raw, scale, dot = (pick_rows(one) for one in (grad, raw, scale, (dot / width)[:, None]))
            pieces.append((scale * (grad - raw * scale * dot)).astype(BF16))
        return (*pieces, pick_rows(grad_value_in))

    first_rows = jnp.concatenate(qkv_grads(lambda one: slot_rows(one, 0)), axis=1)
    first_part = times_transposed(first_rows, full_qkv).astype(BF16)
    query_dz, key_dz = after((query_dz, key_dz), first_part)
    grad_query_in, grad_key_in, grad_value_in = qkv_grads(lambda one: one)
    grad_qkv = jnp.concatenate([grad_query_in, grad_key_in, grad_value_in], axis=1)
    gain_pack = jnp.concatenate([grad_query_gain, grad_key_gain, gain_sums["attn"], gain_sums["mlp"]], axis=1)

    def interleaved(picker, pieces_in):
        return jnp.concatenate([picker(one, 1) for one in pieces_in], axis=1)

    def input_window(step, gate):
        nonlocal gain_pack
        pack, *pieces_in, tokens_in, left_out, right_out = after(
            (gain_pack, grad_query_in, grad_key_in, grad_value_in, block_input, grad_attn_in, attended), gate
        )
        if step == 1:
            got["qkv"] = sum_sent(tokens_in, interleaved(other_half, pieces_in))
            got["out"] = sum_sent(left_out, other_half(right_out, 1))
            gain_pack = pack + lax.ppermute(pack, "dp", swap)
            return got["qkv"], got["out"], gain_pack
        if step == 2:
            blocks["out"] = sum_kept(left_out, own_half(right_out, 1), got["out"])
            blocks["qkv"] = sum_kept(after(tokens_in, blocks["out"][0]), interleaved(own_half, pieces_in), got["qkv"]
            )
            if rows == 4:
                gain_pack = pack + lax.ppermute(pack, "row", by_x)
            return
        gain_pack = pack + lax.ppermute(pack, "row", by_y) if rows == 4 else lax.psum(pack, "row")

    def input_work(slot, gate):
        if slot == 0:
            return first_part
        return times_transposed(after(slot_rows(grad_qkv, slot), gate), full_qkv).astype(BF16)

    input_own = sum_slots(input_work, input_window)

    results = {}
    quarter = local_width // 2

    def projection(index):
        pair = both_cores(blocks["qkv"][1][None, :, index * quarter : (index + 1) * quarter], 0)
        return jnp.concatenate([pair[0], pair[1]], axis=1)

    def output_work(slot, rows_in):
        held["o"] = (place_rows(slot_index[slot], rows_in, tokens_here, F32, held["o"]),)
        if slot == 3:
            results["down"] = jnp.transpose(both_cores(blocks["down"][1], 1))
            results["gate"] = both_cores(blocks["gate"][1], 1)
            return held["o"], results["down"], results["gate"]
        if slot == 2:
            results["up"] = both_cores(blocks["up"][1], 1)
            return held["o"], results["up"]
        if slot == 1:
            results["out"] = jnp.transpose(both_cores(blocks["out"][1], 1))
            results["qkv"] = [projection(index) for index in range(3)]
            return held["o"], results["out"], results["qkv"]
        return held["o"]

    gather_slots((own_grad_hidden + input_own).astype(BF16), output_work)
    ends = (local_width, 2 * local_width, 2 * local_width + width)
    gain_grads = jnp.split(gain_pack[0], ends)
    return (
        block_output,
        held["o"][0],
        *results["qkv"],
        results["out"],
        results["gate"],
        results["up"],
        results["down"],
        *gain_grads,
    )


def layer(sizes, *arrays):
    return shards(sizes, *arrays)


def solution(mesh):
    in_specs = (
        P(("dp", "row"), None),
        P(("dp", "row")),
        P(("dp", "row")),
        P("row", "col"),
        P("row", "col"),
        P("row", "col"),
        P("col", "row"),
        P("row", "col"),
        P("row", "col"),
        P("col", "row"),
        P("col"),
        P("col"),
        P(),
        P(),
        P(("dp", "row"), None),
    )
    out_specs = (
        P(("dp", "row"), None),
        P(("dp", "row"), None),
        P("row", "col"),
        P("row", "col"),
        P("row", "col"),
        P("col", "row"),
        P("row", "col"),
        P("row", "col"),
        P("col", "row"),
        P("col"),
        P("col"),
        P(),
        P(),
    )
    sizes = (mesh.shape["dp"], mesh.shape["row"], mesh.shape["col"])
    return jax.shard_map(
        functools.partial(layer, sizes), mesh=mesh, in_specs=in_specs, out_specs=out_specs, check_vma=False
    )
```

```python
import functools

import jax
import jax.numpy as jnp
from jax import lax
from jax.experimental import pallas as pl
from jax.experimental.pallas import tpu as pltpu
from jax.sharding import PartitionSpec as P


HD = 128
LEN = 1024
BQ = 256
VMEM = 60 << 20

EPS = 1e-06
THETA = 500000.0
NEG_FILL = -1e30
SCORE_SCALE = HD ** (-0.5)
F32 = jnp.float32
BF16 = jnp.bfloat16


def plain_dot(left_mat, right_mat):
    return jnp.dot(left_mat, right_mat, preferred_element_type=F32)


def times_transposed(left_mat, right_mat):
    return lax.dot_general(
        left_mat, right_mat, (((1,), (1,)), ((), ())), preferred_element_type=F32
    )


def left_transposed(left_mat, right_mat):
    return lax.dot_general(
        left_mat, right_mat, (((0,), (0,)), ((), ())), preferred_element_type=F32
    )


def rope_tables(positions):
    half_dim = HD // 2
    inv_freq = THETA ** (-(jnp.arange(half_dim, dtype=F32) * 2.0) / HD)
    angles = positions.astype(F32)[:, None] * inv_freq[None, :]
    cos_half, sin_half = jnp.cos(angles), jnp.sin(angles)
    cosine = jnp.concatenate([cos_half, cos_half], axis=-1)
    sine_signed = jnp.concatenate([-sin_half, sin_half], axis=-1)
    return cosine, sine_signed


def fill_mask(bias_ref, seg_col_ref, seg_row_ref):
    @pl.when(pl.program_id(0) == 0)
    def _():
        for first in range(0, LEN, BQ):
            keys = first + BQ
            rows = seg_col_ref[first:keys, :]
            cols = seg_row_ref[:, :keys]
            query_index = first + lax.broadcasted_iota(jnp.int32, (BQ, keys), 0)
            key_index = lax.broadcasted_iota(jnp.int32, (BQ, keys), 1)
            allowed = (rows == cols) & (key_index <= query_index)
            bias_ref[first:keys, :keys] = jnp.where(allowed, 0.0, NEG_FILL)


def attend_forward_kernel(
    q_ref, k_ref, v_ref, qs_ref, ks_ref, qg_ref, kg_ref, cos_ref, sin_ref, segc_ref, segr_ref,
    qrot_ref, krot_ref, vb_ref, att_ref, log_ref, bias_ref,
):
    fill_mask(bias_ref, segc_ref, segr_ref)
    cosine, sine = cos_ref[...], sin_ref[...]

    def turned(raw, scale, gain):
        norm = raw * scale * gain
        return (norm * cosine + pltpu.roll(norm, HD // 2, 1) * sine).astype(BF16)

    qrot_ref[...] = turned(q_ref[...], qs_ref[...], qg_ref[...])
    krot_ref[...] = turned(k_ref[...], ks_ref[...], kg_ref[...])
    vb_ref[...] = v_ref[...].astype(BF16)
    for first in range(0, LEN, BQ):
        keys = first + BQ
        scores = times_transposed(qrot_ref[first:keys, :], krot_ref[:keys, :]) * SCORE_SCALE
        masked = scores + bias_ref[first:keys, :keys]
        peak = jnp.max(masked, axis=1, keepdims=True)
        weight = jnp.exp(masked - peak)
        total = jnp.sum(weight, axis=1, keepdims=True)
        probs = (weight * (1.0 / total)).astype(BF16)
        att_ref[first:keys, :] = plain_dot(probs, vb_ref[:keys, :]).astype(BF16)
        log_ref[0, first:keys, :] = peak + jnp.log(total)


def attend_backward_kernel(
    q_ref, k_ref, qs_ref, ks_ref, qg_ref, kg_ref, cos_ref, sin_ref, segc_ref, segr_ref,
    qrot_ref, krot_ref, vb_ref, att_ref, log_ref, grad_ref,
    dzq_ref, dzk_ref, gv_ref, dotq_ref, dotk_ref, gainq_ref, gaink_ref,
    dq_acc, dk_acc, dv_acc, bias_ref,
):
    fill_mask(bias_ref, segc_ref, segr_ref)
    dk_acc[...] = jnp.zeros_like(dk_acc)
    dv_acc[...] = jnp.zeros_like(dv_acc)
    for first in range(0, LEN, BQ):
        keys = first + BQ
        queries = qrot_ref[first:keys, :]
        grads = grad_ref[first:keys, :]
        scores = times_transposed(queries, krot_ref[:keys, :]) * SCORE_SCALE
        probs = jnp.exp(scores + bias_ref[first:keys, :keys] - log_ref[0, first:keys, :])
        delta = jnp.sum(
            grads.astype(F32) * att_ref[first:keys, :].astype(F32), axis=1, keepdims=True
        )
        grad_probs = times_transposed(grads, vb_ref[:keys, :])
        grad_scores = (probs * (grad_probs - delta) * SCORE_SCALE).astype(BF16)
        dq_acc[first:keys, :] = plain_dot(grad_scores, krot_ref[:keys, :])
        dk_acc[:keys, :] += left_transposed(grad_scores, queries)
        dv_acc[:keys, :] += left_transposed(probs.astype(BF16), grads)
    gv_ref[...] = dv_acc[...].astype(BF16)
    cosine, sine = cos_ref[...], sin_ref[...]

    def finish(acc, raw_ref, scale_ref, gain_ref, dz_ref, dot_ref, gain_grad_ref):
        grad_rot = acc[...]
        grad_norm = grad_rot * cosine - pltpu.roll(grad_rot, HD // 2, 1) * sine
        unit = raw_ref[...] * scale_ref[...]
        gain_grad_ref[...] = jnp.sum(grad_norm * unit, axis=0, keepdims=True)
        grad_unit = grad_norm * gain_ref[...]
        dz_ref[...] = grad_unit
        part = jnp.sum(grad_unit * unit, axis=1, keepdims=True)

        @pl.when(pl.program_id(0) == 0)
        def _():
            dot_ref[...] = part

        @pl.when(pl.program_id(0) > 0)
        def _():
            dot_ref[...] += part

    finish(dq_acc, q_ref, qs_ref, qg_ref, dzq_ref, dotq_ref, gainq_ref)
    finish(dk_acc, k_ref, ks_ref, kg_ref, dzk_ref, dotk_ref, gaink_ref)


def head_spec(offset):
    return pl.BlockSpec((LEN, HD), lambda h: (0, offset + h))


def whole_spec(shape):
    return pl.BlockSpec(shape, lambda h: (0,) * len(shape))


def gain_spec():
    return pl.BlockSpec((1, HD), lambda h: (0, h))


LOG_SPEC = pl.BlockSpec((1, LEN, 1), lambda h: (h, 0, 0))
COLUMN = (LEN, 1)
TABLE = (LEN, HD)


def attend_forward(qkv, scales, gains, tables, seg_col, seg_row, heads):
    width = heads * HD
    piece = jax.ShapeDtypeStruct((LEN, width), BF16)
    return pl.pallas_call(
        attend_forward_kernel,
        grid=(heads,),
        in_specs=[
            head_spec(0), head_spec(heads), head_spec(2 * heads),
            whole_spec(COLUMN), whole_spec(COLUMN), gain_spec(), gain_spec(),
            whole_spec(TABLE), whole_spec(TABLE), whole_spec(COLUMN), whole_spec((1, LEN)),
        ],
        out_specs=[head_spec(0)] * 4 + [LOG_SPEC],
        out_shape=[piece] * 4 + [jax.ShapeDtypeStruct((heads, LEN, 1), F32)],
        scratch_shapes=[pltpu.VMEM((LEN, LEN), F32)],
        compiler_params=pltpu.CompilerParams(vmem_limit_bytes=VMEM),
        cost_estimate=pl.CostEstimate(
            flops=heads * 4 * LEN * LEN * HD, bytes_accessed=LEN * width * 20, transcendentals=0
        ),
        name="attend_forward",
    )(qkv, qkv, qkv, *scales, *gains, *tables, seg_col, seg_row)


def attend_backward(qkv, scales, gains, tables, seg_col, seg_row, saved, grad_att, heads):
    width = heads * HD
    full = jax.ShapeDtypeStruct((LEN, width), F32)
    column = jax.ShapeDtypeStruct(COLUMN, F32)
    gain_row = jax.ShapeDtypeStruct((1, width), F32)
    return pl.pallas_call(
        attend_backward_kernel,
        grid=(heads,),
        in_specs=[
            head_spec(0), head_spec(heads),
            whole_spec(COLUMN), whole_spec(COLUMN), gain_spec(), gain_spec(),
            whole_spec(TABLE), whole_spec(TABLE), whole_spec(COLUMN), whole_spec((1, LEN)),
            head_spec(0), head_spec(0), head_spec(0), head_spec(0), LOG_SPEC, head_spec(0),
        ],
        out_specs=[
            head_spec(0), head_spec(0), head_spec(0),
            whole_spec(COLUMN), whole_spec(COLUMN), gain_spec(), gain_spec(),
        ],
        out_shape=[
            full, full, jax.ShapeDtypeStruct((LEN, width), BF16), column, column, gain_row, gain_row,
        ],
        scratch_shapes=[pltpu.VMEM((LEN, HD), F32)] * 3 + [pltpu.VMEM((LEN, LEN), F32)],
        compiler_params=pltpu.CompilerParams(vmem_limit_bytes=VMEM),
        cost_estimate=pl.CostEstimate(
            flops=heads * 10 * LEN * LEN * HD, bytes_accessed=LEN * width * 40, transcendentals=0
        ),
        name="attend_backward",
    )(qkv, qkv, *scales, *gains, *tables, seg_col, seg_row, *saved, grad_att)


def fetch_choice(idx_ref, refs, held_ref, sem):
    for number, ref in enumerate(refs):

        @pl.when(idx_ref[2] == number)
        def _():
            copy = pltpu.make_async_copy(ref, held_ref, sem)
            copy.start()
            copy.wait()


def half_tile(step, core, tiles):
    per_half = tiles // 2
    return ((core + step // per_half) % 2) * per_half + step % per_half


def forward_chunk_kernel(
    idx_ref, *refs, out_steps, tiles,
):
    own_ref, left1, left2, left3, right1, right2, right3 = refs[:7]
    wo_own_ref, wo_oth_ref, x_ref, gain_ref, wg_ref, wu_ref, wd_own_ref, wd_oth_ref = refs[7:15]
    raw_ref, scale_ref, hb_ref, gate_ref, up_ref, mixed_ref, part_ref, acc_ref, att_ref = refs[-9:]
    depth, out_tile = wo_own_ref.shape
    blocks, _, block = wd_own_ref.shape
    step = pl.program_id(0)
    core = idx_ref[1]

    @pl.when(step == 0)
    def _():
        quarter = own_ref.shape[1] // 2
        pieces = (
            own_ref[...], right1[...] + left3[...], right2[...] + left2[...], right3[...] + left1[...],
        )
        for half in range(2):
            for number, piece in enumerate(pieces):
                start = half * depth + number * quarter
                att_ref[:, start : start + quarter] = piece[:, half * quarter : (half + 1) * quarter]

    @pl.when(step < out_steps)
    def _():
        own = att_ref[:, pl.ds(pl.multiple_of(core * depth, depth), depth)]
        other = att_ref[:, pl.ds(pl.multiple_of((1 - core) * depth, depth), depth)]
        acc_ref[:, pl.ds(pl.multiple_of(step * out_tile, out_tile), out_tile)] = plain_dot(
            own, wo_own_ref[...]
        ) + plain_dot(other, wo_oth_ref[...])

    @pl.when(step == out_steps - 1)
    def _():
        raw = acc_ref[...]
        scale = lax.rsqrt(jnp.mean(raw * raw, axis=1, keepdims=True) + EPS)
        raw_ref[...] = raw.astype(BF16)
        scale_ref[...] = scale
        hb_ref[...] = (x_ref[...].astype(F32) + raw * scale * gain_ref[...]).astype(BF16)
        acc_ref[...] = jnp.zeros_like(acc_ref)

    def tile_work(wd_ref):
        hidden_b = hb_ref[...]
        gate = plain_dot(hidden_b, wg_ref[...])
        up = plain_dot(hidden_b, wu_ref[...])
        mixed = (gate * jax.nn.sigmoid(gate) * up).astype(BF16)
        gate_ref[...] = gate.astype(BF16)
        up_ref[...] = up.astype(BF16)
        mixed_ref[...] = mixed
        for j in range(blocks):
            acc_ref[:, j * block : (j + 1) * block] += plain_dot(mixed, wd_ref[j])

    @pl.when((step >= out_steps) & (step < out_steps + tiles // 2))
    def _():
        tile_work(wd_own_ref)

    @pl.when(step >= out_steps + tiles // 2)
    def _():
        tile_work(wd_oth_ref)

    @pl.when(step == out_steps + tiles - 1)
    def _():
        part_ref[...] = acc_ref[...].astype(BF16)


TILE = 512


def forward_chunk(index, attended, out_halves, block_input, gain, w_gate_up, down_halves, chunk, before):
    tokens, width = block_input.shape
    hidden = w_gate_up.shape[1] // 2
    depth = out_halves[0].shape[0]
    blocks, _, block = down_halves[0].shape
    tiles = hidden // TILE
    out_steps = width // TILE

    def tile_of(j, idx):
        return half_tile(jnp.maximum(j - out_steps, 0), idx[1], tiles)

    rows = pl.BlockSpec((chunk, width), lambda j, idx: (idx[0], 0))
    out_half = pl.BlockSpec((depth, TILE), lambda j, idx: (0, jnp.minimum(j, out_steps - 1)))
    gate_tile = pl.BlockSpec((width, TILE), lambda j, idx: (0, tile_of(j, idx)))
    up_tile = pl.BlockSpec((width, TILE), lambda j, idx: (0, tiles + tile_of(j, idx)))
    down_own = pl.BlockSpec(
        (blocks, TILE, block), lambda j, idx: (0, jnp.clip(j - out_steps, 0, tiles // 2 - 1), 0)
    )
    down_oth = pl.BlockSpec(
        (blocks, TILE, block), lambda j, idx: (0, jnp.maximum(j - out_steps - tiles // 2, 0), 0)
    )
    act_tile = pl.BlockSpec((chunk, TILE), lambda j, idx: (idx[0], tile_of(j, idx)))
    before = tuple(before)
    return pl.pallas_call(
        functools.partial(forward_chunk_kernel, out_steps=out_steps, tiles=tiles),
        grid_spec=pltpu.PrefetchScalarGridSpec(
            num_scalar_prefetch=1,
            grid=(out_steps + tiles,),
            in_specs=[
                *[pl.BlockSpec((chunk, attended[0].shape[1]), lambda j, idx: (idx[0], 0))] * 7,
                out_half, out_half, rows, pl.BlockSpec((1, width), lambda j, idx: (0, 0)),
                gate_tile, up_tile, down_own, down_oth,
            ] + [pl.BlockSpec(memory_space=pl.ANY)] * len(before),
            out_specs=[
                rows, pl.BlockSpec((chunk, 1), lambda j, idx: (idx[0], 0)), rows, act_tile, act_tile, act_tile,
                pl.BlockSpec((chunk, width), lambda j, idx: (0, 0)),
            ],
            scratch_shapes=[pltpu.VMEM((chunk, width), F32), pltpu.VMEM((chunk, 2 * depth), BF16)],
        ),
        out_shape=[
            jax.ShapeDtypeStruct((tokens, width), BF16),
            jax.ShapeDtypeStruct((tokens, 1), F32),
            jax.ShapeDtypeStruct((tokens, width), BF16),
            jax.ShapeDtypeStruct((tokens, hidden), BF16),
            jax.ShapeDtypeStruct((tokens, hidden), BF16),
            jax.ShapeDtypeStruct((tokens, hidden), BF16),
            jax.ShapeDtypeStruct((chunk, width), BF16),
        ],
        input_output_aliases={16 + i: i for i in range(len(before))},
        compiler_params=pltpu.CompilerParams(vmem_limit_bytes=VMEM),
        cost_estimate=pl.CostEstimate(
            flops=2 * chunk * width * (width + 3 * hidden),
            bytes_accessed=2 * width * (width + 3 * hidden),
            transcendentals=0,
        ),
        name="forward_chunk",
    )(index, *attended, *out_halves, block_input, gain, w_gate_up, w_gate_up, *down_halves, *before)


def backward_chunk_kernel(
    idx_ref, grad_ref, mlp_gain_ref, gate_ref, up_ref, wg_ref, wu_ref, wd_own_ref, wd_oth_ref, *refs, tiles, choices,
):
    gdi_ref, gg_ref, gu_ref, part_ref, gain_grad_ref, acc_ref, down_ref, sem = refs[-8:]
    blocks, _, block = wd_own_ref.shape
    step = pl.program_id(0)

    @pl.when(step == 0)
    def _():
        fetch_choice(idx_ref, refs[:choices], down_ref, sem)
        down_raw = down_ref[...].astype(F32)
        down_scale = lax.rsqrt(jnp.mean(down_raw * down_raw, axis=1, keepdims=True) + EPS)
        unit = down_raw * down_scale
        grad_y = grad_ref[...].astype(F32)
        gain_grad_ref[...] = jnp.sum(grad_y * unit, axis=0, keepdims=True)
        grad_unit = grad_y * mlp_gain_ref[...]
        mean = jnp.mean(grad_unit * unit, axis=1, keepdims=True)
        gdi_ref[...] = (down_scale * (grad_unit - unit * mean)).astype(BF16)
        acc_ref[...] = jnp.zeros_like(acc_ref)

    def tile_work(wd_ref):
        grad_mixed = times_transposed(gdi_ref[:, :block], wd_ref[0])
        for j in range(1, blocks):
            grad_mixed += times_transposed(gdi_ref[:, j * block : (j + 1) * block], wd_ref[j])
        gate = gate_ref[...].astype(F32)
        sig = jax.nn.sigmoid(gate)
        grad_gate = (grad_mixed * up_ref[...].astype(F32) * sig * (1.0 + gate * (1.0 - sig))).astype(BF16)
        grad_up = (grad_mixed * (gate * sig)).astype(BF16)
        gg_ref[...] = grad_gate
        gu_ref[...] = grad_up
        acc_ref[...] += times_transposed(grad_gate, wg_ref[...]) + times_transposed(grad_up, wu_ref[...])

    @pl.when(step < tiles // 2)
    def _():
        tile_work(wd_own_ref)

    @pl.when(step >= tiles // 2)
    def _():
        tile_work(wd_oth_ref)

    @pl.when(step == tiles - 1)
    def _():
        part_ref[...] = acc_ref[...].astype(BF16)


def backward_chunk(
    index, down_rows, grad_output, mlp_gain, gate, up, w_gate_up, down_halves, chunk, before,
):
    tokens, width = grad_output.shape
    hidden = w_gate_up.shape[1] // 2
    blocks, _, block = down_halves[0].shape
    tiles = hidden // TILE

    def tile_of(j, idx):
        return half_tile(j, idx[1], tiles)

    rows = pl.BlockSpec((chunk, width), lambda j, idx: (idx[0], 0))
    gain_row = pl.BlockSpec((1, width), lambda j, idx: (0, 0))
    gate_tile = pl.BlockSpec((width, TILE), lambda j, idx: (0, tile_of(j, idx)))
    up_tile = pl.BlockSpec((width, TILE), lambda j, idx: (0, tiles + tile_of(j, idx)))
    act_tile = pl.BlockSpec((chunk, TILE), lambda j, idx: (idx[0], tile_of(j, idx)))
    before = tuple(before)
    return pl.pallas_call(
        functools.partial(backward_chunk_kernel, tiles=tiles, choices=len(down_rows)),
        grid_spec=pltpu.PrefetchScalarGridSpec(
            num_scalar_prefetch=1,
            grid=(tiles,),
            in_specs=[
                rows, gain_row, act_tile, act_tile, gate_tile, up_tile,
                pl.BlockSpec((blocks, TILE, block), lambda j, idx: (0, jnp.minimum(j, tiles // 2 - 1), 0)),
                pl.BlockSpec((blocks, TILE, block), lambda j, idx: (0, jnp.maximum(j - tiles // 2, 0), 0)),
            ] + [pl.BlockSpec(memory_space=pl.ANY)] * (len(down_rows) + len(before)),
            out_specs=[rows, act_tile, act_tile, pl.BlockSpec((chunk, width), lambda j, idx: (0, 0)), gain_row],
            scratch_shapes=[
                pltpu.VMEM((chunk, width), F32), pltpu.VMEM((chunk, width), BF16), pltpu.SemaphoreType.DMA(()),
            ],
        ),
        out_shape=[
            jax.ShapeDtypeStruct((tokens, width), BF16),
            jax.ShapeDtypeStruct((tokens, hidden), BF16),
            jax.ShapeDtypeStruct((tokens, hidden), BF16),
            jax.ShapeDtypeStruct((chunk, width), BF16),
            jax.ShapeDtypeStruct((1, width), F32),
        ],
        input_output_aliases={9 + len(down_rows) + i: i for i in range(len(before))},
        compiler_params=pltpu.CompilerParams(vmem_limit_bytes=VMEM),
        cost_estimate=pl.CostEstimate(
            flops=6 * chunk * width * hidden, bytes_accessed=6 * width * hidden, transcendentals=0
        ),
        name="backward_chunk",
    )(index, grad_output, mlp_gain, gate, up, w_gate_up, w_gate_up, *down_halves, *down_rows, *before)


PARTS = 4


def attention_chunk_kernel(
    idx_ref, grad_ref, raw_ref, scale_ref, gain_ref, wo_own_ref, wo_oth_ref, *refs, choices,
):
    gai_ref, gatt_ref, gain_grad_ref, held_ref, sem = refs[-5:]
    half = wo_own_ref.shape[0]
    core = idx_ref[1]
    step = pl.program_id(0)

    @pl.when(step == 0)
    def _():
        fetch_choice(idx_ref, refs[:choices], held_ref, sem)
        gain_grad_ref[...] = jnp.zeros_like(gain_grad_ref)

    size = grad_ref.shape[0]
    scale = scale_ref[...]
    unit = raw_ref[...].astype(F32) * scale
    mlp = held_ref[pl.ds(pl.multiple_of(step * size, size), size), :]
    grad_hidden = grad_ref[...].astype(F32) + mlp.astype(F32)
    gain_grad_ref[...] += jnp.sum(grad_hidden * unit, axis=0, keepdims=True)
    grad_unit = grad_hidden * gain_ref[...]
    mean = jnp.mean(grad_unit * unit, axis=1, keepdims=True)
    grad_attn_in = (scale * (grad_unit - unit * mean)).astype(BF16)
    gai_ref[...] = grad_attn_in
    for place, w_ref in ((core, wo_own_ref), (1 - core, wo_oth_ref)):
        gatt_ref[:, pl.ds(pl.multiple_of(place * half, half), half)] = times_transposed(
            grad_attn_in, w_ref[...]
        ).astype(BF16)


def attention_chunk(index, mlp_rows, grad_output, raw, scale, gain, out_halves, half, chunk, before):
    tokens, width = grad_output.shape
    size = chunk
    rows = pl.BlockSpec((size, width), lambda j, idx: (idx[0], 0))
    gain_row = pl.BlockSpec((1, width), lambda j, idx: (0, 0))
    own_heads = pl.BlockSpec((half, width), lambda j, idx: (0, 0))
    before = tuple(before)
    return pl.pallas_call(
        functools.partial(attention_chunk_kernel, choices=len(mlp_rows)),
        grid_spec=pltpu.PrefetchScalarGridSpec(
            num_scalar_prefetch=1,
            grid=(1,),
            in_specs=[
                rows, rows, pl.BlockSpec((size, 1), lambda j, idx: (idx[0], 0)), gain_row,
                own_heads, own_heads,
            ] + [pl.BlockSpec(memory_space=pl.ANY)] * (len(mlp_rows) + len(before)),
            out_specs=[rows, pl.BlockSpec((size, 2 * half), lambda j, idx: (idx[0], 0)), gain_row],
            scratch_shapes=[pltpu.VMEM((chunk, width), BF16), pltpu.SemaphoreType.DMA(())],
        ),
        out_shape=[
            jax.ShapeDtypeStruct((tokens, width), BF16),
            jax.ShapeDtypeStruct((tokens, 2 * half), BF16),
            jax.ShapeDtypeStruct((1, width), F32),
        ],
        input_output_aliases={7 + len(mlp_rows) + i: i for i in range(len(before))},
        compiler_params=pltpu.CompilerParams(vmem_limit_bytes=VMEM),
        cost_estimate=pl.CostEstimate(
            flops=4 * chunk * width * half, bytes_accessed=16 * chunk * width, transcendentals=0
        ),
        name="attention_chunk",
    )(index, grad_output, raw, scale, gain, *out_halves, *mlp_rows, *before)


def output_chunk_kernel(idx_ref, raw_ref, scale_ref, x_ref, attn_gain_ref, mlp_gain_ref, *refs, choices):
    out_ref, held_ref, sem = refs[-3:]
    step = pl.program_id(0)

    @pl.when(step == 0)
    def _():
        fetch_choice(idx_ref, refs[:choices], held_ref, sem)

    size = out_ref.shape[0]
    down_raw = held_ref[pl.ds(pl.multiple_of(step * size, size), size), :].astype(F32)
    down_scale = lax.rsqrt(jnp.mean(down_raw * down_raw, axis=1, keepdims=True) + EPS)
    hidden = x_ref[...].astype(F32) + raw_ref[...].astype(F32) * scale_ref[...] * attn_gain_ref[...]
    out_ref[...] = (hidden + down_raw * down_scale * mlp_gain_ref[...]).astype(BF16)


def output_chunk(index, down_rows, raw, scale, block_input, attn_gain, mlp_gain, chunk, before):
    tokens, width = block_input.shape
    size = chunk // PARTS
    rows = pl.BlockSpec((size, width), lambda j, idx: (PARTS * idx[0] + j, 0))
    gain_row = pl.BlockSpec((1, width), lambda j, idx: (0, 0))
    before = tuple(before)
    return pl.pallas_call(
        functools.partial(output_chunk_kernel, choices=len(down_rows)),
        grid_spec=pltpu.PrefetchScalarGridSpec(
            num_scalar_prefetch=1,
            grid=(PARTS,),
            in_specs=[
                rows, pl.BlockSpec((size, 1), lambda j, idx: (PARTS * idx[0] + j, 0)), rows, gain_row, gain_row,
            ] + [pl.BlockSpec(memory_space=pl.ANY)] * (len(down_rows) + len(before)),
            out_specs=rows,
            scratch_shapes=[pltpu.VMEM((chunk, width), BF16), pltpu.SemaphoreType.DMA(())],
        ),
        out_shape=jax.ShapeDtypeStruct((tokens, width), BF16),
        input_output_aliases={6 + len(down_rows): 0} if before else {},
        compiler_params=pltpu.CompilerParams(vmem_limit_bytes=VMEM),
        cost_estimate=pl.CostEstimate(flops=0, bytes_accessed=8 * chunk * width, transcendentals=0),
        name="output_chunk",
    )(index, raw, scale, block_input, attn_gain, mlp_gain, *down_rows, *before)


def place_rows_kernel(idx_ref, *refs, choices):
    out_ref, held_ref, sem = refs[-3:]
    step = pl.program_id(0)

    @pl.when(step == 0)
    def _():
        fetch_choice(idx_ref, refs[:choices], held_ref, sem)

    size = out_ref.shape[0]
    out_ref[...] = held_ref[pl.ds(pl.multiple_of(step * size, size), size), :].astype(out_ref.dtype)


def place_rows(index, rows_in, tokens, dtype, before):
    chunk, width = rows_in[0].shape
    before = tuple(before)
    return pl.pallas_call(
        functools.partial(place_rows_kernel, choices=len(rows_in)),
        grid_spec=pltpu.PrefetchScalarGridSpec(
            num_scalar_prefetch=1,
            grid=(4,),
            in_specs=[pl.BlockSpec(memory_space=pl.ANY)] * (len(rows_in) + len(before)),
            out_specs=pl.BlockSpec((chunk // 4, width), lambda j, idx: (4 * idx[0] + j, 0)),
            scratch_shapes=[pltpu.VMEM((chunk, width), BF16), pltpu.SemaphoreType.DMA(())],
        ),
        out_shape=jax.ShapeDtypeStruct((tokens, width), dtype),
        input_output_aliases={1 + len(rows_in): 0} if before else {},
        compiler_params=pltpu.CompilerParams(vmem_limit_bytes=VMEM),
        cost_estimate=pl.CostEstimate(flops=0, bytes_accessed=6 * chunk * width, transcendentals=0),
        name="place_rows",
    )(index, *rows_in, *before)


def after(value, *tokens):
    return lax.optimization_barrier((value, tokens))[0]


def unset_kernel(out_ref):
    pass


def unset(shape, dtype):
    return pl.pallas_call(
        unset_kernel,
        out_specs=pl.BlockSpec(memory_space=pl.ANY),
        out_shape=jax.ShapeDtypeStruct(shape, dtype),
        name="unset",
    )()


def shards(
    sizes,
    block_input,
    segment_ids,
    positions,
    w_query,
    w_key,
    w_value,
    w_out,
    w_gate,
    w_up,
    w_down,
    query_gain,
    key_gain,
    attn_gain,
    mlp_gain,
    grad_output,
):
    cores, rows, cols = sizes
    tokens_here, width = block_input.shape
    assert tokens_here == LEN and cores == 2 and cols == 4
    local_width = w_query.shape[1]
    half_width = local_width // 2
    heads = local_width // HD
    chunk = tokens_here // cols
    core = lax.axis_index("dp")
    row = lax.axis_index("row")
    col = lax.axis_index("col")
    swap = [(0, 1), (1, 0)]
    attn_row, mlp_row = attn_gain[None, :], mlp_gain[None, :]

    def own_half(array, axis):
        half = array.shape[axis] // 2
        return lax.dynamic_slice_in_dim(array, core * half, half, axis)

    def other_half(array, axis):
        half = array.shape[axis] // 2
        return lax.dynamic_slice_in_dim(array, (1 - core) * half, half, axis)

    def gather(weight, axis):
        return lax.all_gather(own_half(weight, axis), ("row", "dp"), axis=axis, tiled=True)

    def line_step(from_left, from_right, step):
        from_left = lax.ppermute(from_left, "col", [(i, i + 1) for i in range(step - 1, cols - 1)])
        from_right = lax.ppermute(from_right, "col", [(i + 1, i) for i in range(cols - step)])
        return from_left, from_right

    def sum_step(up, down, step):
        up = lax.ppermute(up, "col", [(i, i + 1) for i in range(step)])
        down = lax.ppermute(down, "col", [(cols - 1 - i, cols - 2 - i) for i in range(step)])
        return up, down

    def pick(at_zero, at_one, at_two, at_three):
        low = jnp.where(col == 0, at_zero, at_one)
        high = jnp.where(col == 2, at_two, at_three)
        return jnp.where(col < 2, low, high)

    slot_chunk = [pick(3, 3, 0, 0), pick(2, 2, 1, 1), pick(1, 0, 3, 2), col]
    slot_index = [
        jnp.stack([one, core, choice]).astype(jnp.int32)
        for one, choice in zip(slot_chunk, (col, col, col % 2, 0 * col))
    ]

    def slot_rows(array, slot):
        return lax.dynamic_slice_in_dim(array, slot_chunk[slot] * chunk, chunk, 0)

    def gather_slots(own, work):
        left, right, token = [own], [own], ()
        arrived = (
            lambda lefts, rights: (lefts[0],),
            lambda lefts, rights: (rights[1], lefts[1]),
            lambda lefts, rights: (rights[2], rights[1], lefts[1], lefts[2]),
            lambda lefts, rights: (rights[3], rights[2], lefts[2], lefts[3]),
        )
        for step in range(1, cols + 1):
            seen = tuple(left), tuple(right)
            if step < cols:
                from_left, from_right = line_step(left[-1], right[-1], step)
                left.append(from_left)
                right.append(from_right)
            token = work(cols - step, arrived[step - 1](*after(seen, token)))

    def sum_slots(make, window=lambda step, gate: ()):
        def at(step, gate):
            window(step, gate)
            return make(step, gate)

        first = make(0, ())
        up, down = sum_step(first, first, 1)
        second = at(1, first)
        up = jnp.where(col == 0, second, first) + up
        down = jnp.where(col == 3, second, first) + down
        gate = (up, down)
        up, down = sum_step(up, down, 2)
        third = at(2, gate)
        up = jnp.where(col == 1, second, third) + up
        down = jnp.where(col == 2, second, third) + down
        gate = (up, down)
        up, down = sum_step(up, down, 3)
        fourth = lax.optimization_barrier(at(3, gate))
        return fourth.astype(F32) + up.astype(F32) + down.astype(F32)

    def both_cores(half, axis):
        other = lax.ppermute(half, "dp", swap)
        first = jnp.where(core == 0, half, other)
        second = jnp.where(core == 0, other, half)
        return jnp.concatenate([first, second], axis=axis).astype(F32)

    def sum_sent(left_mat, right_other):
        return lax.ppermute(left_transposed(left_mat, right_other).astype(BF16), "dp", swap)

    def sum_kept(left_mat, right_own, sent):
        total = (left_transposed(left_mat, right_own) + sent.astype(F32)).astype(BF16)
        return total, lax.psum_scatter(total, "row", scatter_dimension=0, tiled=True)

    by_x = [(0, 1), (1, 0), (2, 3), (3, 2)]
    by_y = [(0, 2), (2, 0), (1, 3), (3, 1)]

    def row_first(half):
        if rows != 4:
            return (half,)
        return half, lax.ppermute(half, "row", by_x), lax.ppermute(half, "row", by_y)

    def row_second(pieces):
        if rows != 4:
            return pieces
        middle = pieces[0].shape[0] // 2
        return (
            *pieces,
            lax.ppermute(pieces[1][:middle], "row", by_y),
            lax.ppermute(pieces[2][middle:], "row", by_x),
        )

    def row_blocks(pieces):
        if rows != 4:
            whole = lax.all_gather(pieces[0], ("row", "dp"), axis=0, tiled=False)
            whole = whole.reshape(rows, cores, *pieces[0].shape)
            return tuple(lax.dynamic_index_in_dim(whole, one, 1, keepdims=False) for one in (core, 1 - core))
        own, by_one, by_two, corner_top, corner_low = pieces
        middle = own.shape[0] // 2
        held = unset((rows, *own.shape), own.dtype)
        for piece, block, start in (
            (own, row, 0), (by_one, row ^ 1, 0), (by_two, row ^ 2, 0),
            (corner_top, row ^ 3, 0), (corner_low, row ^ 3, middle),
        ):
            held = lax.dynamic_update_slice(held, piece[None], (block, start, 0))
        return held, lax.ppermute(held, "dp", swap)

    def row_columns(pieces):
        if rows != 4:
            return lax.all_gather(pieces[0], "row", axis=1, tiled=True)
        own, by_one, by_two, corner_top, corner_low = pieces
        height, block = own.shape
        held = unset((height, rows * block), own.dtype)
        for piece, number, start in (
            (own, row, 0), (by_one, row ^ 1, 0), (by_two, row ^ 2, 0),
            (corner_top, row ^ 3, 0), (corner_low, row ^ 3, height // 2),
        ):
            held = lax.dynamic_update_slice(held, piece, (start, number * block))
        return held

    full_qkv = gather(jnp.concatenate([w_query, w_key, w_value], axis=1), 0)
    full_gate_up = gather(jnp.concatenate([w_gate, w_up], axis=1), 0)
    out_pieces = row_first(own_half(w_out, 0))
    out_pieces = row_second(out_pieces)
    out_own = row_columns(out_pieces)
    out_left, out_right = [out_own], [out_own]
    for step in range(1, cols):
        one, two = line_step(out_left[-1], out_right[-1], step)
        out_left.append(one)
        out_right.append(two)
    down_pieces = row_first(after(own_half(w_down, 0), full_qkv))

    qkv = plain_dot(block_input, full_qkv)
    query_raw, key_raw = qkv[:, :local_width], qkv[:, local_width : 2 * local_width]
    query_sq, key_sq = lax.psum(
        (jnp.sum(query_raw * query_raw, axis=1), jnp.sum(key_raw * key_raw, axis=1)), "col"
    )
    query_scale = lax.rsqrt(query_sq / width + EPS)[:, None]
    key_scale = lax.rsqrt(key_sq / width + EPS)[:, None]
    scales = (query_scale, key_scale)
    gains = (query_gain[None, :], key_gain[None, :])
    tables = rope_tables(positions)
    seg_col, seg_row = segment_ids[:, None], segment_ids[None, :]
    query_rot, key_rot, value_heads, attended, log_total = attend_forward(
        qkv, scales, gains, tables, seg_col, seg_row, heads
    )

    lefts, rights = [attended], [attended]
    for step in range(1, cols):
        from_left, from_right = line_step(lefts[-1], rights[-1], step)
        lefts.append(from_left)
        rights.append(from_right)
        if step == 1:
            out_halves = jnp.concatenate(
                [out_own] + [out_right[k] + out_left[cols - k] for k in range(1, cols)], axis=0
            )
            out_halves = (out_halves, lax.ppermute(out_halves, "dp", swap))
        if step == 2:
            down_pieces = row_second(after(down_pieces, lefts[1], rights[1]))
        if step == 3:
            down_halves = row_blocks(down_pieces)
    attended_all = (attended, *lefts[1:], *rights[1:])

    held = dict(f=(), b=(), a=(), o=(), m=())
    gain_sums = dict(mlp=0.0, attn=0.0)

    def forward_work(slot, gate):
        results = forward_chunk(
            slot_index[slot], after(attended_all, gate), out_halves, block_input, attn_row, full_gate_up,
            down_halves, chunk, held["f"],
        )
        held["f"] = results[:6]
        return results[6]

    down_own = sum_slots(forward_work).astype(BF16)
    attn_raw, attn_scale, hidden_b, gate_proj, up_proj, mixed_act = held["f"]
    mlp_parts = [None] * cols
    down_slots = [None] * cols

    def backward_work(slot, down_rows):
        down_slots[slot] = down_rows
        results = backward_chunk(
            slot_index[slot], down_rows, grad_output, mlp_row, gate_proj, up_proj, full_gate_up,
            down_halves, chunk, held["b"],
        )
        held["b"] = results[:3]
        mlp_parts[slot] = results[3]
        gain_sums["mlp"] = gain_sums["mlp"] + results[4]
        return results[3]

    gather_slots(down_own, backward_work)
    grad_down_in, grad_gate_in, grad_up_in = held["b"]

    blocks = {}
    got = {}

    def mlp_window(step, gate):
        down_left, down_right, hidden_left, gate_right, up_right = after(
            (grad_down_in, mixed_act, hidden_b, grad_gate_in, grad_up_in), gate
        )
        if step == 1:
            got["down"] = sum_sent(down_left, other_half(down_right, 1))
            got["gate"] = sum_sent(hidden_left, other_half(gate_right, 1))
            return got["down"], got["gate"]
        if step == 2:
            blocks["down"] = sum_kept(down_left, own_half(down_right, 1), got["down"])
            got["up"] = sum_sent(hidden_left, other_half(up_right, 1))
            return blocks["down"][0], got["up"]
        blocks["gate"] = sum_kept(hidden_left, own_half(gate_right, 1), got["gate"])
        return blocks["gate"][0]

    mlp_own = sum_slots(lambda slot, gate: mlp_parts[slot], mlp_window).astype(BF16)

    def attention_work(slot, mlp_rows):
        results = attention_chunk(
            slot_index[slot], mlp_rows, grad_output, attn_raw, attn_scale, attn_row, out_halves, half_width,
            chunk, held["a"],
        )
        held["a"] = results[:2]
        gain_sums["attn"] = gain_sums["attn"] + results[2]
        if slot == 3:
            hidden_left, up_right = after((hidden_b, grad_up_in), mlp_rows[0])
            blocks["up"] = sum_kept(hidden_left, own_half(up_right, 1), got["up"])
        for other in {2: (3, 2), 1: (1, 0)}.get(slot, ()):
            output = output_chunk(
                slot_index[other], down_slots[other], after(attn_raw, mlp_rows), attn_scale, block_input, attn_row,
                mlp_row, chunk, held["m"],
            )
            held["m"] = (output,)
        return results[1]

    gather_slots(mlp_own, attention_work)
    grad_attn_in, grad_att = held["a"]
    (block_output,) = held["m"]
    own_grad_hidden = slot_rows(grad_output, 3).astype(F32) + mlp_own.astype(F32)

    query_dz, key_dz, grad_value_in, query_dot, key_dot, grad_query_gain, grad_key_gain = attend_backward(
        qkv, scales, gains, tables, seg_col, seg_row,
        (query_rot, key_rot, value_heads, attended, log_total), grad_att, heads,
    )
    query_dot, key_dot = lax.psum((query_dot[:, 0], key_dot[:, 0]), "col")
    grad_query_in = (
        query_scale * (query_dz - query_raw * query_scale * (query_dot / width)[:, None])
    ).astype(BF16)
    grad_key_in = (
        key_scale * (key_dz - key_raw * key_scale * (key_dot / width)[:, None])
    ).astype(BF16)
    grad_qkv = jnp.concatenate([grad_query_in, grad_key_in, grad_value_in], axis=1)
    gain_pack = jnp.concatenate([grad_query_gain, grad_key_gain, gain_sums["attn"], gain_sums["mlp"]], axis=1)

    def interleaved(picker, pieces_in):
        return jnp.concatenate([picker(one, 1) for one in pieces_in], axis=1)

    def input_window(step, gate):
        nonlocal gain_pack
        pack, *pieces_in, tokens_in, left_out, right_out = after(
            (gain_pack, grad_query_in, grad_key_in, grad_value_in, block_input, grad_attn_in, attended), gate
        )
        if step == 1:
            got["qkv"] = sum_sent(tokens_in, interleaved(other_half, pieces_in))
            got["out"] = sum_sent(left_out, other_half(right_out, 1))
            gain_pack = pack + lax.ppermute(pack, "dp", swap)
            return got["qkv"], got["out"], gain_pack
        if step == 2:
            blocks["out"] = sum_kept(left_out, own_half(right_out, 1), got["out"])
            blocks["qkv"] = sum_kept(after(tokens_in, blocks["out"][0]), interleaved(own_half, pieces_in), got["qkv"]
            )
            if rows == 4:
                gain_pack = pack + lax.ppermute(pack, "row", by_x)
            return
        gain_pack = pack + lax.ppermute(pack, "row", by_y) if rows == 4 else lax.psum(pack, "row")

    rest = {}

    def input_work(slot, gate):
        if slot == 0:
            return times_transposed(slot_rows(grad_qkv, 0), full_qkv).astype(BF16)
        if slot == 1:
            others = jnp.concatenate([slot_rows(grad_qkv, one) for one in (1, 2, 3)], axis=0)
            rest[0] = times_transposed(after(others, gate), full_qkv).astype(BF16)
        return rest[0][(slot - 1) * chunk : slot * chunk]

    input_own = sum_slots(input_work, input_window)

    results = {}
    quarter = local_width // 2

    def projection(index):
        pair = both_cores(blocks["qkv"][1][None, :, index * quarter : (index + 1) * quarter], 0)
        return jnp.concatenate([pair[0], pair[1]], axis=1)

    def output_work(slot, rows_in):
        held["o"] = (place_rows(slot_index[slot], rows_in, tokens_here, F32, held["o"]),)
        if slot == 3:
            results["down"] = jnp.transpose(both_cores(blocks["down"][1], 1))
            results["gate"] = both_cores(blocks["gate"][1], 1)
            return held["o"], results["down"], results["gate"]
        if slot == 2:
            results["up"] = both_cores(blocks["up"][1], 1)
            return held["o"], results["up"]
        if slot == 1:
            results["out"] = jnp.transpose(both_cores(blocks["out"][1], 1))
            results["qkv"] = [projection(index) for index in range(3)]
            return held["o"], results["out"], results["qkv"]
        return held["o"]

    gather_slots((own_grad_hidden + input_own).astype(BF16), output_work)
    ends = (local_width, 2 * local_width, 2 * local_width + width)
    gain_grads = jnp.split(gain_pack[0], ends)
    return (
        block_output,
        held["o"][0],
        *results["qkv"],
        results["out"],
        results["gate"],
        results["up"],
        results["down"],
        *gain_grads,
    )


def layer(sizes, *arrays):
    return shards(sizes, *arrays)


def solution(mesh):
    in_specs = (
        P(("dp", "row"), None),
        P(("dp", "row")),
        P(("dp", "row")),
        P("row", "col"),
        P("row", "col"),
        P("row", "col"),
        P("col", "row"),
        P("row", "col"),
        P("row", "col"),
        P("col", "row"),
        P("col"),
        P("col"),
        P(),
        P(),
        P(("dp", "row"), None),
    )
    out_specs = (
        P(("dp", "row"), None),
        P(("dp", "row"), None),
        P("row", "col"),
        P("row", "col"),
        P("row", "col"),
        P("col", "row"),
        P("row", "col"),
        P("row", "col"),
        P("col", "row"),
        P("col"),
        P("col"),
        P(),
        P(),
    )
    sizes = (mesh.shape["dp"], mesh.shape["row"], mesh.shape["col"])
    return jax.shard_map(
        functools.partial(layer, sizes), mesh=mesh, in_specs=in_specs, out_specs=out_specs, check_vma=False
    )
```

```python
import functools

import jax
import jax.numpy as jnp
from jax import lax
from jax.experimental import pallas as pl
from jax.experimental.pallas import tpu as pltpu
from jax.sharding import PartitionSpec as P


HD = 128
LEN = 1024
BQ = 256
VMEM = 60 << 20

EPS = 1e-06
THETA = 500000.0
NEG_FILL = -1e30
SCORE_SCALE = HD ** (-0.5)
F32 = jnp.float32
BF16 = jnp.bfloat16


def plain_dot(left_mat, right_mat):
    return jnp.dot(left_mat, right_mat, preferred_element_type=F32)


def times_transposed(left_mat, right_mat):
    return lax.dot_general(
        left_mat, right_mat, (((1,), (1,)), ((), ())), preferred_element_type=F32
    )


def left_transposed(left_mat, right_mat):
    return lax.dot_general(
        left_mat, right_mat, (((0,), (0,)), ((), ())), preferred_element_type=F32
    )


def rope_tables(positions):
    half_dim = HD // 2
    inv_freq = THETA ** (-(jnp.arange(half_dim, dtype=F32) * 2.0) / HD)
    angles = positions.astype(F32)[:, None] * inv_freq[None, :]
    cos_half, sin_half = jnp.cos(angles), jnp.sin(angles)
    cosine = jnp.concatenate([cos_half, cos_half], axis=-1)
    sine_signed = jnp.concatenate([-sin_half, sin_half], axis=-1)
    return cosine, sine_signed


def fill_mask(bias_ref, seg_col_ref, seg_row_ref):
    @pl.when(pl.program_id(0) == 0)
    def _():
        for first in range(0, LEN, BQ):
            keys = first + BQ
            rows = seg_col_ref[first:keys, :]
            cols = seg_row_ref[:, :keys]
            query_index = first + lax.broadcasted_iota(jnp.int32, (BQ, keys), 0)
            key_index = lax.broadcasted_iota(jnp.int32, (BQ, keys), 1)
            allowed = (rows == cols) & (key_index <= query_index)
            bias_ref[first:keys, :keys] = jnp.where(allowed, 0.0, NEG_FILL)


def attend_forward_kernel(
    q_ref, k_ref, v_ref, qs_ref, ks_ref, qg_ref, kg_ref, cos_ref, sin_ref, segc_ref, segr_ref,
    qrot_ref, krot_ref, vb_ref, att_ref, log_ref, bias_ref,
):
    fill_mask(bias_ref, segc_ref, segr_ref)
    cosine, sine = cos_ref[...], sin_ref[...]

    def turned(raw, scale, gain):
        norm = raw * scale * gain
        return (norm * cosine + pltpu.roll(norm, HD // 2, 1) * sine).astype(BF16)

    qrot_ref[...] = turned(q_ref[...], qs_ref[...], qg_ref[...])
    krot_ref[...] = turned(k_ref[...], ks_ref[...], kg_ref[...])
    vb_ref[...] = v_ref[...].astype(BF16)
    for first in range(0, LEN, BQ):
        keys = first + BQ
        scores = times_transposed(qrot_ref[first:keys, :], krot_ref[:keys, :]) * SCORE_SCALE
        masked = scores + bias_ref[first:keys, :keys]
        peak = jnp.max(masked, axis=1, keepdims=True)
        weight = jnp.exp(masked - peak)
        total = jnp.sum(weight, axis=1, keepdims=True)
        probs = (weight * (1.0 / total)).astype(BF16)
        att_ref[first:keys, :] = plain_dot(probs, vb_ref[:keys, :]).astype(BF16)
        log_ref[0, first:keys, :] = peak + jnp.log(total)


def attend_backward_kernel(
    q_ref, k_ref, qs_ref, ks_ref, qg_ref, kg_ref, cos_ref, sin_ref, segc_ref, segr_ref,
    qrot_ref, krot_ref, vb_ref, att_ref, log_ref, grad_ref,
    dzq_ref, dzk_ref, gv_ref, dotq_ref, dotk_ref, gainq_ref, gaink_ref,
    dq_acc, dk_acc, dv_acc, bias_ref,
):
    fill_mask(bias_ref, segc_ref, segr_ref)
    dk_acc[...] = jnp.zeros_like(dk_acc)
    dv_acc[...] = jnp.zeros_like(dv_acc)
    for first in range(0, LEN, BQ):
        keys = first + BQ
        queries = qrot_ref[first:keys, :]
        grads = grad_ref[first:keys, :]
        scores = times_transposed(queries, krot_ref[:keys, :]) * SCORE_SCALE
        probs = jnp.exp(scores + bias_ref[first:keys, :keys] - log_ref[0, first:keys, :])
        delta = jnp.sum(
            grads.astype(F32) * att_ref[first:keys, :].astype(F32), axis=1, keepdims=True
        )
        grad_probs = times_transposed(grads, vb_ref[:keys, :])
        grad_scores = (probs * (grad_probs - delta) * SCORE_SCALE).astype(BF16)
        dq_acc[first:keys, :] = plain_dot(grad_scores, krot_ref[:keys, :])
        dk_acc[:keys, :] += left_transposed(grad_scores, queries)
        dv_acc[:keys, :] += left_transposed(probs.astype(BF16), grads)
    gv_ref[...] = dv_acc[...].astype(BF16)
    cosine, sine = cos_ref[...], sin_ref[...]

    def finish(acc, raw_ref, scale_ref, gain_ref, dz_ref, dot_ref, gain_grad_ref):
        grad_rot = acc[...]
        grad_norm = grad_rot * cosine - pltpu.roll(grad_rot, HD // 2, 1) * sine
        unit = raw_ref[...] * scale_ref[...]
        gain_grad_ref[...] = jnp.sum(grad_norm * unit, axis=0, keepdims=True)
        grad_unit = grad_norm * gain_ref[...]
        dz_ref[...] = grad_unit
        part = jnp.sum(grad_unit * unit, axis=1, keepdims=True)

        @pl.when(pl.program_id(0) == 0)
        def _():
            dot_ref[...] = part

        @pl.when(pl.program_id(0) > 0)
        def _():
            dot_ref[...] += part

    finish(dq_acc, q_ref, qs_ref, qg_ref, dzq_ref, dotq_ref, gainq_ref)
    finish(dk_acc, k_ref, ks_ref, kg_ref, dzk_ref, dotk_ref, gaink_ref)


def head_spec(offset):
    return pl.BlockSpec((LEN, HD), lambda h: (0, offset + h))


def whole_spec(shape):
    return pl.BlockSpec(shape, lambda h: (0,) * len(shape))


def gain_spec():
    return pl.BlockSpec((1, HD), lambda h: (0, h))


LOG_SPEC = pl.BlockSpec((1, LEN, 1), lambda h: (h, 0, 0))
COLUMN = (LEN, 1)
TABLE = (LEN, HD)


def attend_forward(qkv, scales, gains, tables, seg_col, seg_row, heads):
    width = heads * HD
    piece = jax.ShapeDtypeStruct((LEN, width), BF16)
    return pl.pallas_call(
        attend_forward_kernel,
        grid=(heads,),
        in_specs=[
            head_spec(0), head_spec(heads), head_spec(2 * heads),
            whole_spec(COLUMN), whole_spec(COLUMN), gain_spec(), gain_spec(),
            whole_spec(TABLE), whole_spec(TABLE), whole_spec(COLUMN), whole_spec((1, LEN)),
        ],
        out_specs=[head_spec(0)] * 4 + [LOG_SPEC],
        out_shape=[piece] * 4 + [jax.ShapeDtypeStruct((heads, LEN, 1), F32)],
        scratch_shapes=[pltpu.VMEM((LEN, LEN), F32)],
        compiler_params=pltpu.CompilerParams(vmem_limit_bytes=VMEM),
        cost_estimate=pl.CostEstimate(
            flops=heads * 4 * LEN * LEN * HD, bytes_accessed=LEN * width * 20, transcendentals=0
        ),
        name="attend_forward",
    )(qkv, qkv, qkv, *scales, *gains, *tables, seg_col, seg_row)


def attend_backward(qkv, scales, gains, tables, seg_col, seg_row, saved, grad_att, heads):
    width = heads * HD
    full = jax.ShapeDtypeStruct((LEN, width), F32)
    column = jax.ShapeDtypeStruct(COLUMN, F32)
    gain_row = jax.ShapeDtypeStruct((1, width), F32)
    return pl.pallas_call(
        attend_backward_kernel,
        grid=(heads,),
        in_specs=[
            head_spec(0), head_spec(heads),
            whole_spec(COLUMN), whole_spec(COLUMN), gain_spec(), gain_spec(),
            whole_spec(TABLE), whole_spec(TABLE), whole_spec(COLUMN), whole_spec((1, LEN)),
            head_spec(0), head_spec(0), head_spec(0), head_spec(0), LOG_SPEC, head_spec(0),
        ],
        out_specs=[
            head_spec(0), head_spec(0), head_spec(0),
            whole_spec(COLUMN), whole_spec(COLUMN), gain_spec(), gain_spec(),
        ],
        out_shape=[
            full, full, jax.ShapeDtypeStruct((LEN, width), BF16), column, column, gain_row, gain_row,
        ],
        scratch_shapes=[pltpu.VMEM((LEN, HD), F32)] * 3 + [pltpu.VMEM((LEN, LEN), F32)],
        compiler_params=pltpu.CompilerParams(vmem_limit_bytes=VMEM),
        cost_estimate=pl.CostEstimate(
            flops=heads * 10 * LEN * LEN * HD, bytes_accessed=LEN * width * 40, transcendentals=0
        ),
        name="attend_backward",
    )(qkv, qkv, *scales, *gains, *tables, seg_col, seg_row, *saved, grad_att)


def fetch_choice(idx_ref, refs, held_ref, sem):
    for number, ref in enumerate(refs):

        @pl.when(idx_ref[2] == number)
        def _():
            copy = pltpu.make_async_copy(ref, held_ref, sem)
            copy.start()
            copy.wait()


def half_tile(step, core, tiles):
    per_half = tiles // 2
    return ((core + step // per_half) % 2) * per_half + step % per_half


def forward_chunk_kernel(
    idx_ref, *refs, out_steps, tiles,
):
    own_ref, left1, left2, left3, right1, right2, right3 = refs[:7]
    wo_own_ref, wo_oth_ref, x_ref, gain_ref, wg_ref, wu_ref, wd_own_ref, wd_oth_ref = refs[7:15]
    raw_ref, scale_ref, hb_ref, gate_ref, up_ref, mixed_ref, part_ref, acc_ref, att_ref = refs[-9:]
    depth, out_tile = wo_own_ref.shape
    blocks, _, block = wd_own_ref.shape
    step = pl.program_id(0)
    core = idx_ref[1]

    @pl.when(step == 0)
    def _():
        quarter = own_ref.shape[1] // 2
        pieces = (
            own_ref[...], right1[...] + left3[...], right2[...] + left2[...], right3[...] + left1[...],
        )
        for half in range(2):
            for number, piece in enumerate(pieces):
                start = half * depth + number * quarter
                att_ref[:, start : start + quarter] = piece[:, half * quarter : (half + 1) * quarter]

    @pl.when(step < out_steps)
    def _():
        own = att_ref[:, pl.ds(pl.multiple_of(core * depth, depth), depth)]
        other = att_ref[:, pl.ds(pl.multiple_of((1 - core) * depth, depth), depth)]
        acc_ref[:, pl.ds(pl.multiple_of(step * out_tile, out_tile), out_tile)] = plain_dot(
            own, wo_own_ref[...]
        ) + plain_dot(other, wo_oth_ref[...])

    @pl.when(step == out_steps - 1)
    def _():
        raw = acc_ref[...]
        scale = lax.rsqrt(jnp.mean(raw * raw, axis=1, keepdims=True) + EPS)
        raw_ref[...] = raw.astype(BF16)
        scale_ref[...] = scale
        hb_ref[...] = (x_ref[...].astype(F32) + raw * scale * gain_ref[...]).astype(BF16)
        acc_ref[...] = jnp.zeros_like(acc_ref)

    def tile_work(wd_ref):
        hidden_b = hb_ref[...]
        gate = plain_dot(hidden_b, wg_ref[...])
        up = plain_dot(hidden_b, wu_ref[...])
        mixed = (gate * jax.nn.sigmoid(gate) * up).astype(BF16)
        gate_ref[...] = gate.astype(BF16)
        up_ref[...] = up.astype(BF16)
        mixed_ref[...] = mixed
        for j in range(blocks):
            acc_ref[:, j * block : (j + 1) * block] += plain_dot(mixed, wd_ref[j])

    @pl.when((step >= out_steps) & (step < out_steps + tiles // 2))
    def _():
        tile_work(wd_own_ref)

    @pl.when(step >= out_steps + tiles // 2)
    def _():
        tile_work(wd_oth_ref)

    @pl.when(step == out_steps + tiles - 1)
    def _():
        part_ref[...] = acc_ref[...].astype(BF16)


TILE = 512


def forward_chunk(index, attended, out_halves, block_input, gain, w_gate_up, down_halves, chunk, before):
    tokens, width = block_input.shape
    hidden = w_gate_up.shape[1] // 2
    depth = out_halves[0].shape[0]
    blocks, _, block = down_halves[0].shape
    tiles = hidden // TILE
    out_steps = width // TILE

    def tile_of(j, idx):
        return half_tile(jnp.maximum(j - out_steps, 0), idx[1], tiles)

    rows = pl.BlockSpec((chunk, width), lambda j, idx: (idx[0], 0))
    out_half = pl.BlockSpec((depth, TILE), lambda j, idx: (0, jnp.minimum(j, out_steps - 1)))
    gate_tile = pl.BlockSpec((width, TILE), lambda j, idx: (0, tile_of(j, idx)))
    up_tile = pl.BlockSpec((width, TILE), lambda j, idx: (0, tiles + tile_of(j, idx)))
    down_own = pl.BlockSpec(
        (blocks, TILE, block), lambda j, idx: (0, jnp.clip(j - out_steps, 0, tiles // 2 - 1), 0)
    )
    down_oth = pl.BlockSpec(
        (blocks, TILE, block), lambda j, idx: (0, jnp.maximum(j - out_steps - tiles // 2, 0), 0)
    )
    act_tile = pl.BlockSpec((chunk, TILE), lambda j, idx: (idx[0], tile_of(j, idx)))
    before = tuple(before)
    return pl.pallas_call(
        functools.partial(forward_chunk_kernel, out_steps=out_steps, tiles=tiles),
        grid_spec=pltpu.PrefetchScalarGridSpec(
            num_scalar_prefetch=1,
            grid=(out_steps + tiles,),
            in_specs=[
                *[pl.BlockSpec((chunk, attended[0].shape[1]), lambda j, idx: (idx[0], 0))] * 7,
                out_half, out_half, rows, pl.BlockSpec((1, width), lambda j, idx: (0, 0)),
                gate_tile, up_tile, down_own, down_oth,
            ] + [pl.BlockSpec(memory_space=pl.ANY)] * len(before),
            out_specs=[
                rows, pl.BlockSpec((chunk, 1), lambda j, idx: (idx[0], 0)), rows, act_tile, act_tile, act_tile,
                pl.BlockSpec((chunk, width), lambda j, idx: (0, 0)),
            ],
            scratch_shapes=[pltpu.VMEM((chunk, width), F32), pltpu.VMEM((chunk, 2 * depth), BF16)],
        ),
        out_shape=[
            jax.ShapeDtypeStruct((tokens, width), BF16),
            jax.ShapeDtypeStruct((tokens, 1), F32),
            jax.ShapeDtypeStruct((tokens, width), BF16),
            jax.ShapeDtypeStruct((tokens, hidden), BF16),
            jax.ShapeDtypeStruct((tokens, hidden), BF16),
            jax.ShapeDtypeStruct((tokens, hidden), BF16),
            jax.ShapeDtypeStruct((chunk, width), BF16),
        ],
        input_output_aliases={16 + i: i for i in range(len(before))},
        compiler_params=pltpu.CompilerParams(vmem_limit_bytes=VMEM),
        cost_estimate=pl.CostEstimate(
            flops=2 * chunk * width * (width + 3 * hidden),
            bytes_accessed=2 * width * (width + 3 * hidden),
            transcendentals=0,
        ),
        name="forward_chunk",
    )(index, *attended, *out_halves, block_input, gain, w_gate_up, w_gate_up, *down_halves, *before)


def backward_chunk_kernel(
    idx_ref, grad_ref, mlp_gain_ref, gate_ref, up_ref, wg_ref, wu_ref, wd_own_ref, wd_oth_ref, *refs, tiles, choices,
):
    gdi_ref, gg_ref, gu_ref, part_ref, gain_grad_ref, acc_ref, down_ref, sem = refs[-8:]
    blocks, _, block = wd_own_ref.shape
    step = pl.program_id(0)

    @pl.when(step == 0)
    def _():
        fetch_choice(idx_ref, refs[:choices], down_ref, sem)
        down_raw = down_ref[...].astype(F32)
        down_scale = lax.rsqrt(jnp.mean(down_raw * down_raw, axis=1, keepdims=True) + EPS)
        unit = down_raw * down_scale
        grad_y = grad_ref[...].astype(F32)
        gain_grad_ref[...] = jnp.sum(grad_y * unit, axis=0, keepdims=True)
        grad_unit = grad_y * mlp_gain_ref[...]
        mean = jnp.mean(grad_unit * unit, axis=1, keepdims=True)
        gdi_ref[...] = (down_scale * (grad_unit - unit * mean)).astype(BF16)
        acc_ref[...] = jnp.zeros_like(acc_ref)

    def tile_work(wd_ref):
        grad_mixed = times_transposed(gdi_ref[:, :block], wd_ref[0])
        for j in range(1, blocks):
            grad_mixed += times_transposed(gdi_ref[:, j * block : (j + 1) * block], wd_ref[j])
        gate = gate_ref[...].astype(F32)
        sig = jax.nn.sigmoid(gate)
        grad_gate = (grad_mixed * up_ref[...].astype(F32) * sig * (1.0 + gate * (1.0 - sig))).astype(BF16)
        grad_up = (grad_mixed * (gate * sig)).astype(BF16)
        gg_ref[...] = grad_gate
        gu_ref[...] = grad_up
        acc_ref[...] += times_transposed(grad_gate, wg_ref[...]) + times_transposed(grad_up, wu_ref[...])

    @pl.when(step < tiles // 2)
    def _():
        tile_work(wd_own_ref)

    @pl.when(step >= tiles // 2)
    def _():
        tile_work(wd_oth_ref)

    @pl.when(step == tiles - 1)
    def _():
        part_ref[...] = acc_ref[...].astype(BF16)


def backward_chunk(
    index, down_rows, grad_output, mlp_gain, gate, up, w_gate_up, down_halves, chunk, before,
):
    tokens, width = grad_output.shape
    hidden = w_gate_up.shape[1] // 2
    blocks, _, block = down_halves[0].shape
    tiles = hidden // TILE

    def tile_of(j, idx):
        return half_tile(j, idx[1], tiles)

    rows = pl.BlockSpec((chunk, width), lambda j, idx: (idx[0], 0))
    gain_row = pl.BlockSpec((1, width), lambda j, idx: (0, 0))
    gate_tile = pl.BlockSpec((width, TILE), lambda j, idx: (0, tile_of(j, idx)))
    up_tile = pl.BlockSpec((width, TILE), lambda j, idx: (0, tiles + tile_of(j, idx)))
    act_tile = pl.BlockSpec((chunk, TILE), lambda j, idx: (idx[0], tile_of(j, idx)))
    before = tuple(before)
    return pl.pallas_call(
        functools.partial(backward_chunk_kernel, tiles=tiles, choices=len(down_rows)),
        grid_spec=pltpu.PrefetchScalarGridSpec(
            num_scalar_prefetch=1,
            grid=(tiles,),
            in_specs=[
                rows, gain_row, act_tile, act_tile, gate_tile, up_tile,
                pl.BlockSpec((blocks, TILE, block), lambda j, idx: (0, jnp.minimum(j, tiles // 2 - 1), 0)),
                pl.BlockSpec((blocks, TILE, block), lambda j, idx: (0, jnp.maximum(j - tiles // 2, 0), 0)),
            ] + [pl.BlockSpec(memory_space=pl.ANY)] * (len(down_rows) + len(before)),
            out_specs=[rows, act_tile, act_tile, pl.BlockSpec((chunk, width), lambda j, idx: (0, 0)), gain_row],
            scratch_shapes=[
                pltpu.VMEM((chunk, width), F32), pltpu.VMEM((chunk, width), BF16), pltpu.SemaphoreType.DMA(()),
            ],
        ),
        out_shape=[
            jax.ShapeDtypeStruct((tokens, width), BF16),
            jax.ShapeDtypeStruct((tokens, hidden), BF16),
            jax.ShapeDtypeStruct((tokens, hidden), BF16),
            jax.ShapeDtypeStruct((chunk, width), BF16),
            jax.ShapeDtypeStruct((1, width), F32),
        ],
        input_output_aliases={9 + len(down_rows) + i: i for i in range(len(before))},
        compiler_params=pltpu.CompilerParams(vmem_limit_bytes=VMEM),
        cost_estimate=pl.CostEstimate(
            flops=6 * chunk * width * hidden, bytes_accessed=6 * width * hidden, transcendentals=0
        ),
        name="backward_chunk",
    )(index, grad_output, mlp_gain, gate, up, w_gate_up, w_gate_up, *down_halves, *down_rows, *before)


PARTS = 4


def attention_chunk_kernel(
    idx_ref, grad_ref, raw_ref, scale_ref, gain_ref, wo_own_ref, wo_oth_ref, *refs, choices,
):
    gai_ref, gatt_ref, gain_grad_ref, held_ref, sem = refs[-5:]
    half = wo_own_ref.shape[0]
    core = idx_ref[1]
    step = pl.program_id(0)

    @pl.when(step == 0)
    def _():
        fetch_choice(idx_ref, refs[:choices], held_ref, sem)
        gain_grad_ref[...] = jnp.zeros_like(gain_grad_ref)

    size = grad_ref.shape[0]
    scale = scale_ref[...]
    unit = raw_ref[...].astype(F32) * scale
    mlp = held_ref[pl.ds(pl.multiple_of(step * size, size), size), :]
    grad_hidden = grad_ref[...].astype(F32) + mlp.astype(F32)
    gain_grad_ref[...] += jnp.sum(grad_hidden * unit, axis=0, keepdims=True)
    grad_unit = grad_hidden * gain_ref[...]
    mean = jnp.mean(grad_unit * unit, axis=1, keepdims=True)
    grad_attn_in = (scale * (grad_unit - unit * mean)).astype(BF16)
    gai_ref[...] = grad_attn_in
    for place, w_ref in ((core, wo_own_ref), (1 - core, wo_oth_ref)):
        gatt_ref[:, pl.ds(pl.multiple_of(place * half, half), half)] = times_transposed(
            grad_attn_in, w_ref[...]
        ).astype(BF16)


def attention_chunk(index, mlp_rows, grad_output, raw, scale, gain, out_halves, half, chunk, before):
    tokens, width = grad_output.shape
    size = chunk
    rows = pl.BlockSpec((size, width), lambda j, idx: (idx[0], 0))
    gain_row = pl.BlockSpec((1, width), lambda j, idx: (0, 0))
    own_heads = pl.BlockSpec((half, width), lambda j, idx: (0, 0))
    before = tuple(before)
    return pl.pallas_call(
        functools.partial(attention_chunk_kernel, choices=len(mlp_rows)),
        grid_spec=pltpu.PrefetchScalarGridSpec(
            num_scalar_prefetch=1,
            grid=(1,),
            in_specs=[
                rows, rows, pl.BlockSpec((size, 1), lambda j, idx: (idx[0], 0)), gain_row,
                own_heads, own_heads,
            ] + [pl.BlockSpec(memory_space=pl.ANY)] * (len(mlp_rows) + len(before)),
            out_specs=[rows, pl.BlockSpec((size, 2 * half), lambda j, idx: (idx[0], 0)), gain_row],
            scratch_shapes=[pltpu.VMEM((chunk, width), BF16), pltpu.SemaphoreType.DMA(())],
        ),
        out_shape=[
            jax.ShapeDtypeStruct((tokens, width), BF16),
            jax.ShapeDtypeStruct((tokens, 2 * half), BF16),
            jax.ShapeDtypeStruct((1, width), F32),
        ],
        input_output_aliases={7 + len(mlp_rows) + i: i for i in range(len(before))},
        compiler_params=pltpu.CompilerParams(vmem_limit_bytes=VMEM),
        cost_estimate=pl.CostEstimate(
            flops=4 * chunk * width * half, bytes_accessed=16 * chunk * width, transcendentals=0
        ),
        name="attention_chunk",
    )(index, grad_output, raw, scale, gain, *out_halves, *mlp_rows, *before)


def output_chunk_kernel(idx_ref, raw_ref, scale_ref, x_ref, attn_gain_ref, mlp_gain_ref, *refs, choices):
    out_ref, held_ref, sem = refs[-3:]
    step = pl.program_id(0)

    @pl.when(step == 0)
    def _():
        fetch_choice(idx_ref, refs[:choices], held_ref, sem)

    size = out_ref.shape[0]
    down_raw = held_ref[pl.ds(pl.multiple_of(step * size, size), size), :].astype(F32)
    down_scale = lax.rsqrt(jnp.mean(down_raw * down_raw, axis=1, keepdims=True) + EPS)
    hidden = x_ref[...].astype(F32) + raw_ref[...].astype(F32) * scale_ref[...] * attn_gain_ref[...]
    out_ref[...] = (hidden + down_raw * down_scale * mlp_gain_ref[...]).astype(BF16)


def output_chunk(index, down_rows, raw, scale, block_input, attn_gain, mlp_gain, chunk, before):
    tokens, width = block_input.shape
    size = chunk // PARTS
    rows = pl.BlockSpec((size, width), lambda j, idx: (PARTS * idx[0] + j, 0))
    gain_row = pl.BlockSpec((1, width), lambda j, idx: (0, 0))
    before = tuple(before)
    return pl.pallas_call(
        functools.partial(output_chunk_kernel, choices=len(down_rows)),
        grid_spec=pltpu.PrefetchScalarGridSpec(
            num_scalar_prefetch=1,
            grid=(PARTS,),
            in_specs=[
                rows, pl.BlockSpec((size, 1), lambda j, idx: (PARTS * idx[0] + j, 0)), rows, gain_row, gain_row,
            ] + [pl.BlockSpec(memory_space=pl.ANY)] * (len(down_rows) + len(before)),
            out_specs=rows,
            scratch_shapes=[pltpu.VMEM((chunk, width), BF16), pltpu.SemaphoreType.DMA(())],
        ),
        out_shape=jax.ShapeDtypeStruct((tokens, width), BF16),
        input_output_aliases={6 + len(down_rows): 0} if before else {},
        compiler_params=pltpu.CompilerParams(vmem_limit_bytes=VMEM),
        cost_estimate=pl.CostEstimate(flops=0, bytes_accessed=8 * chunk * width, transcendentals=0),
        name="output_chunk",
    )(index, raw, scale, block_input, attn_gain, mlp_gain, *down_rows, *before)


def place_rows_kernel(idx_ref, *refs, choices):
    out_ref, held_ref, sem = refs[-3:]
    step = pl.program_id(0)

    @pl.when(step == 0)
    def _():
        fetch_choice(idx_ref, refs[:choices], held_ref, sem)

    size = out_ref.shape[0]
    out_ref[...] = held_ref[pl.ds(pl.multiple_of(step * size, size), size), :].astype(out_ref.dtype)


def place_rows(index, rows_in, tokens, dtype, before):
    chunk, width = rows_in[0].shape
    before = tuple(before)
    return pl.pallas_call(
        functools.partial(place_rows_kernel, choices=len(rows_in)),
        grid_spec=pltpu.PrefetchScalarGridSpec(
            num_scalar_prefetch=1,
            grid=(4,),
            in_specs=[pl.BlockSpec(memory_space=pl.ANY)] * (len(rows_in) + len(before)),
            out_specs=pl.BlockSpec((chunk // 4, width), lambda j, idx: (4 * idx[0] + j, 0)),
            scratch_shapes=[pltpu.VMEM((chunk, width), BF16), pltpu.SemaphoreType.DMA(())],
        ),
        out_shape=jax.ShapeDtypeStruct((tokens, width), dtype),
        input_output_aliases={1 + len(rows_in): 0} if before else {},
        compiler_params=pltpu.CompilerParams(vmem_limit_bytes=VMEM),
        cost_estimate=pl.CostEstimate(flops=0, bytes_accessed=6 * chunk * width, transcendentals=0),
        name="place_rows",
    )(index, *rows_in, *before)


def after(value, *tokens):
    return lax.optimization_barrier((value, tokens))[0]


def unset_kernel(out_ref):
    pass


def unset(shape, dtype):
    return pl.pallas_call(
        unset_kernel,
        out_specs=pl.BlockSpec(memory_space=pl.ANY),
        out_shape=jax.ShapeDtypeStruct(shape, dtype),
        name="unset",
    )()


def shards(
    sizes,
    block_input,
    segment_ids,
    positions,
    w_query,
    w_key,
    w_value,
    w_out,
    w_gate,
    w_up,
    w_down,
    query_gain,
    key_gain,
    attn_gain,
    mlp_gain,
    grad_output,
):
    cores, rows, cols = sizes
    tokens_here, width = block_input.shape
    assert tokens_here == LEN and cores == 2 and cols == 4
    local_width = w_query.shape[1]
    half_width = local_width // 2
    heads = local_width // HD
    chunk = tokens_here // cols
    core = lax.axis_index("dp")
    row = lax.axis_index("row")
    col = lax.axis_index("col")
    swap = [(0, 1), (1, 0)]
    attn_row, mlp_row = attn_gain[None, :], mlp_gain[None, :]

    def own_half(array, axis):
        half = array.shape[axis] // 2
        return lax.dynamic_slice_in_dim(array, core * half, half, axis)

    def other_half(array, axis):
        half = array.shape[axis] // 2
        return lax.dynamic_slice_in_dim(array, (1 - core) * half, half, axis)

    def gather(weight, axis):
        return lax.all_gather(own_half(weight, axis), ("row", "dp"), axis=axis, tiled=True)

    def line_step(from_left, from_right, step):
        from_left = lax.ppermute(from_left, "col", [(i, i + 1) for i in range(step - 1, cols - 1)])
        from_right = lax.ppermute(from_right, "col", [(i + 1, i) for i in range(cols - step)])
        return from_left, from_right

    def sum_step(up, down, step):
        up = lax.ppermute(up, "col", [(i, i + 1) for i in range(step)])
        down = lax.ppermute(down, "col", [(cols - 1 - i, cols - 2 - i) for i in range(step)])
        return up, down

    def pick(at_zero, at_one, at_two, at_three):
        low = jnp.where(col == 0, at_zero, at_one)
        high = jnp.where(col == 2, at_two, at_three)
        return jnp.where(col < 2, low, high)

    slot_chunk = [pick(3, 3, 0, 0), pick(2, 2, 1, 1), pick(1, 0, 3, 2), col]
    slot_index = [
        jnp.stack([one, core, choice]).astype(jnp.int32)
        for one, choice in zip(slot_chunk, (col, col, col % 2, 0 * col))
    ]

    def slot_rows(array, slot):
        return lax.dynamic_slice_in_dim(array, slot_chunk[slot] * chunk, chunk, 0)

    def gather_slots(own, work):
        left, right, token = [own], [own], ()
        arrived = (
            lambda lefts, rights: (lefts[0],),
            lambda lefts, rights: (rights[1], lefts[1]),
            lambda lefts, rights: (rights[2], rights[1], lefts[1], lefts[2]),
            lambda lefts, rights: (rights[3], rights[2], lefts[2], lefts[3]),
        )
        for step in range(1, cols + 1):
            seen = tuple(left), tuple(right)
            if step < cols:
                from_left, from_right = line_step(left[-1], right[-1], step)
                left.append(from_left)
                right.append(from_right)
            token = work(cols - step, arrived[step - 1](*after(seen, token)))

    def sum_slots(make, window=lambda step, gate: ()):
        def at(step, gate):
            window(step, gate)
            return make(step, gate)

        first = make(0, ())
        up, down = sum_step(first, first, 1)
        second = at(1, first)
        up = jnp.where(col == 0, second, first) + up
        down = jnp.where(col == 3, second, first) + down
        gate = (up, down)
        up, down = sum_step(up, down, 2)
        third = at(2, gate)
        up = jnp.where(col == 1, second, third) + up
        down = jnp.where(col == 2, second, third) + down
        gate = (up, down)
        up, down = sum_step(up, down, 3)
        fourth = lax.optimization_barrier(at(3, gate))
        return fourth.astype(F32) + up.astype(F32) + down.astype(F32)

    def both_cores(half, axis):
        other = lax.ppermute(half, "dp", swap)
        first = jnp.where(core == 0, half, other)
        second = jnp.where(core == 0, other, half)
        return jnp.concatenate([first, second], axis=axis).astype(F32)

    def sum_sent(left_mat, right_other):
        return lax.ppermute(left_transposed(left_mat, right_other).astype(BF16), "dp", swap)

    def sum_kept(left_mat, right_own, sent):
        total = (left_transposed(left_mat, right_own) + sent.astype(F32)).astype(BF16)
        return total, lax.psum_scatter(total, "row", scatter_dimension=0, tiled=True)

    by_x = [(0, 1), (1, 0), (2, 3), (3, 2)]
    by_y = [(0, 2), (2, 0), (1, 3), (3, 1)]

    def row_first(half):
        if rows != 4:
            return (half,)
        return half, lax.ppermute(half, "row", by_x), lax.ppermute(half, "row", by_y)

    def row_second(pieces):
        if rows != 4:
            return pieces
        middle = pieces[0].shape[0] // 2
        return (
            *pieces,
            lax.ppermute(pieces[1][:middle], "row", by_y),
            lax.ppermute(pieces[2][middle:], "row", by_x),
        )

    def row_blocks(pieces):
        if rows != 4:
            whole = lax.all_gather(pieces[0], ("row", "dp"), axis=0, tiled=False)
            whole = whole.reshape(rows, cores, *pieces[0].shape)
            return tuple(lax.dynamic_index_in_dim(whole, one, 1, keepdims=False) for one in (core, 1 - core))
        own, by_one, by_two, corner_top, corner_low = pieces
        middle = own.shape[0] // 2
        held = unset((rows, *own.shape), own.dtype)
        for piece, block, start in (
            (own, row, 0), (by_one, row ^ 1, 0), (by_two, row ^ 2, 0),
            (corner_top, row ^ 3, 0), (corner_low, row ^ 3, middle),
        ):
            held = lax.dynamic_update_slice(held, piece[None], (block, start, 0))
        return held, lax.ppermute(held, "dp", swap)

    def row_columns(pieces):
        if rows != 4:
            return lax.all_gather(pieces[0], "row", axis=1, tiled=True)
        own, by_one, by_two, corner_top, corner_low = pieces
        height, block = own.shape
        held = unset((height, rows * block), own.dtype)
        for piece, number, start in (
            (own, row, 0), (by_one, row ^ 1, 0), (by_two, row ^ 2, 0),
            (corner_top, row ^ 3, 0), (corner_low, row ^ 3, height // 2),
        ):
            held = lax.dynamic_update_slice(held, piece, (start, number * block))
        return held

    full_qkv = gather(jnp.concatenate([w_query, w_key, w_value], axis=1), 0)
    full_gate_up = gather(jnp.concatenate([w_gate, w_up], axis=1), 0)
    out_pieces = row_first(own_half(w_out, 0))
    out_pieces = row_second(out_pieces)
    out_own = row_columns(out_pieces)
    out_left, out_right = [out_own], [out_own]
    for step in range(1, cols):
        one, two = line_step(out_left[-1], out_right[-1], step)
        out_left.append(one)
        out_right.append(two)
    down_pieces = row_first(after(own_half(w_down, 0), full_qkv))

    qkv = plain_dot(block_input, full_qkv)
    query_raw, key_raw = qkv[:, :local_width], qkv[:, local_width : 2 * local_width]
    query_sq, key_sq = lax.psum(
        (jnp.sum(query_raw * query_raw, axis=1), jnp.sum(key_raw * key_raw, axis=1)), "col"
    )
    query_scale = lax.rsqrt(query_sq / width + EPS)[:, None]
    key_scale = lax.rsqrt(key_sq / width + EPS)[:, None]
    scales = (query_scale, key_scale)
    gains = (query_gain[None, :], key_gain[None, :])
    tables = rope_tables(positions)
    seg_col, seg_row = segment_ids[:, None], segment_ids[None, :]
    query_rot, key_rot, value_heads, attended, log_total = attend_forward(
        qkv, scales, gains, tables, seg_col, seg_row, heads
    )

    lefts, rights = [attended], [attended]
    for step in range(1, cols):
        from_left, from_right = line_step(lefts[-1], rights[-1], step)
        lefts.append(from_left)
        rights.append(from_right)
        if step == 1:
            out_halves = jnp.concatenate(
                [out_own] + [out_right[k] + out_left[cols - k] for k in range(1, cols)], axis=0
            )
            out_halves = (out_halves, lax.ppermute(out_halves, "dp", swap))
        if step == 2:
            down_pieces = row_second(after(down_pieces, lefts[1], rights[1]))
        if step == 3:
            down_halves = row_blocks(down_pieces)
    attended_all = (attended, *lefts[1:], *rights[1:])

    held = dict(f=(), b=(), a=(), o=(), m=())
    gain_sums = dict(mlp=0.0, attn=0.0)

    def forward_work(slot, gate):
        results = forward_chunk(
            slot_index[slot], after(attended_all, gate), out_halves, block_input, attn_row, full_gate_up,
            down_halves, chunk, held["f"],
        )
        held["f"] = results[:6]
        return results[6]

    down_own = sum_slots(forward_work).astype(BF16)
    attn_raw, attn_scale, hidden_b, gate_proj, up_proj, mixed_act = held["f"]
    mlp_parts = [None] * cols
    down_slots = [None] * cols

    def backward_work(slot, down_rows):
        down_slots[slot] = down_rows
        results = backward_chunk(
            slot_index[slot], down_rows, grad_output, mlp_row, gate_proj, up_proj, full_gate_up,
            down_halves, chunk, held["b"],
        )
        held["b"] = results[:3]
        mlp_parts[slot] = results[3]
        gain_sums["mlp"] = gain_sums["mlp"] + results[4]
        return results[3]

    gather_slots(down_own, backward_work)
    grad_down_in, grad_gate_in, grad_up_in = held["b"]

    blocks = {}
    got = {}

    def mlp_window(step, gate):
        down_left, down_right, hidden_left, gate_right, up_right = after(
            (grad_down_in, mixed_act, hidden_b, grad_gate_in, grad_up_in), gate
        )
        if step == 1:
            got["down"] = sum_sent(down_left, other_half(down_right, 1))
            got["gate"] = sum_sent(hidden_left, other_half(gate_right, 1))
            return got["down"], got["gate"]
        if step == 2:
            blocks["down"] = sum_kept(down_left, own_half(down_right, 1), got["down"])
            got["up"] = sum_sent(hidden_left, other_half(up_right, 1))
            return blocks["down"][0], got["up"]
        blocks["gate"] = sum_kept(hidden_left, own_half(gate_right, 1), got["gate"])
        return blocks["gate"][0]

    mlp_own = sum_slots(lambda slot, gate: mlp_parts[slot], mlp_window).astype(BF16)

    def attention_work(slot, mlp_rows):
        results = attention_chunk(
            slot_index[slot], mlp_rows, grad_output, attn_raw, attn_scale, attn_row, out_halves, half_width,
            chunk, held["a"],
        )
        held["a"] = results[:2]
        gain_sums["attn"] = gain_sums["attn"] + results[2]
        if slot == 3:
            hidden_left, up_right = after((hidden_b, grad_up_in), mlp_rows[0])
            blocks["up"] = sum_kept(hidden_left, own_half(up_right, 1), got["up"])
        for other in {2: (3, 2), 1: (1, 0)}.get(slot, ()):
            output = output_chunk(
                slot_index[other], down_slots[other], after(attn_raw, mlp_rows), attn_scale, block_input, attn_row,
                mlp_row, chunk, held["m"],
            )
            held["m"] = (output,)
        return results[1]

    gather_slots(mlp_own, attention_work)
    grad_attn_in, grad_att = held["a"]
    (block_output,) = held["m"]
    own_grad_hidden = slot_rows(grad_output, 3).astype(F32) + mlp_own.astype(F32)

    query_dz, key_dz, grad_value_in, query_dot, key_dot, grad_query_gain, grad_key_gain = attend_backward(
        qkv, scales, gains, tables, seg_col, seg_row,
        (query_rot, key_rot, value_heads, attended, log_total), grad_att, heads,
    )
    query_dot, key_dot = lax.psum((query_dot[:, 0], key_dot[:, 0]), "col")
    grad_query_in = (
        query_scale * (query_dz - query_raw * query_scale * (query_dot / width)[:, None])
    ).astype(BF16)
    grad_key_in = (
        key_scale * (key_dz - key_raw * key_scale * (key_dot / width)[:, None])
    ).astype(BF16)
    grad_qkv = jnp.concatenate([grad_query_in, grad_key_in, grad_value_in], axis=1)
    gain_pack = jnp.concatenate([grad_query_gain, grad_key_gain, gain_sums["attn"], gain_sums["mlp"]], axis=1)

    def interleaved(picker, pieces_in):
        return jnp.concatenate([picker(one, 1) for one in pieces_in], axis=1)

    def input_window(step, gate):
        nonlocal gain_pack
        pack, *pieces_in, tokens_in, left_out, right_out = after(
            (gain_pack, grad_query_in, grad_key_in, grad_value_in, block_input, grad_attn_in, attended), gate
        )
        if step == 1:
            got["qkv"] = sum_sent(tokens_in, interleaved(other_half, pieces_in))
            got["out"] = sum_sent(left_out, other_half(right_out, 1))
            gain_pack = pack + lax.ppermute(pack, "dp", swap)
            return got["qkv"], got["out"], gain_pack
        if step == 2:
            blocks["out"] = sum_kept(left_out, own_half(right_out, 1), got["out"])
            if rows == 4:
                gain_pack = pack + lax.ppermute(pack, "row", by_x)
            return
        blocks["qkv"] = sum_kept(tokens_in, interleaved(own_half, pieces_in), got["qkv"])
        gain_pack = pack + lax.ppermute(pack, "row", by_y) if rows == 4 else lax.psum(pack, "row")

    def input_work(slot, gate):
        return times_transposed(after(slot_rows(grad_qkv, slot), gate), full_qkv).astype(BF16)

    input_own = sum_slots(input_work, input_window)

    results = {}
    quarter = local_width // 2

    def projection(index):
        pair = both_cores(blocks["qkv"][1][None, :, index * quarter : (index + 1) * quarter], 0)
        return jnp.concatenate([pair[0], pair[1]], axis=1)

    def output_work(slot, rows_in):
        held["o"] = (place_rows(slot_index[slot], rows_in, tokens_here, F32, held["o"]),)
        if slot == 3:
            results["down"] = jnp.transpose(both_cores(blocks["down"][1], 1))
            results["gate"] = both_cores(blocks["gate"][1], 1)
            return held["o"], results["down"], results["gate"]
        if slot == 2:
            results["up"] = both_cores(blocks["up"][1], 1)
            return held["o"], results["up"]
        if slot == 1:
            results["out"] = jnp.transpose(both_cores(blocks["out"][1], 1))
            results["qkv"] = [projection(index) for index in range(3)]
            return held["o"], results["out"], results["qkv"]
        return held["o"]

    gather_slots((own_grad_hidden + input_own).astype(BF16), output_work)
    ends = (local_width, 2 * local_width, 2 * local_width + width)
    gain_grads = jnp.split(gain_pack[0], ends)
    return (
        block_output,
        held["o"][0],
        *results["qkv"],
        results["out"],
        results["gate"],
        results["up"],
        results["down"],
        *gain_grads,
    )


def layer(sizes, *arrays):
    return shards(sizes, *arrays)


def solution(mesh):
    in_specs = (
        P(("dp", "row"), None),
        P(("dp", "row")),
        P(("dp", "row")),
        P("row", "col"),
        P("row", "col"),
        P("row", "col"),
        P("col", "row"),
        P("row", "col"),
        P("row", "col"),
        P("col", "row"),
        P("col"),
        P("col"),
        P(),
        P(),
        P(("dp", "row"), None),
    )
    out_specs = (
        P(("dp", "row"), None),
        P(("dp", "row"), None),
        P("row", "col"),
        P("row", "col"),
        P("row", "col"),
        P("col", "row"),
        P("row", "col"),
        P("row", "col"),
        P("col", "row"),
        P("col"),
        P("col"),
        P(),
        P(),
    )
    sizes = (mesh.shape["dp"], mesh.shape["row"], mesh.shape["col"])
    return jax.shard_map(
        functools.partial(layer, sizes), mesh=mesh, in_specs=in_specs, out_specs=out_specs, check_vma=False
    )
```

```python
import functools

import jax
import jax.numpy as jnp
from jax import lax
from jax.experimental import pallas as pl
from jax.experimental.pallas import tpu as pltpu
from jax.sharding import PartitionSpec as P


HD = 128
LEN = 1024
BQ = 256
VMEM = 60 << 20

EPS = 1e-06
THETA = 500000.0
NEG_FILL = -1e30
SCORE_SCALE = HD ** (-0.5)
F32 = jnp.float32
BF16 = jnp.bfloat16


def plain_dot(left_mat, right_mat):
    return jnp.dot(left_mat, right_mat, preferred_element_type=F32)


def times_transposed(left_mat, right_mat):
    return lax.dot_general(
        left_mat, right_mat, (((1,), (1,)), ((), ())), preferred_element_type=F32
    )


def left_transposed(left_mat, right_mat):
    return lax.dot_general(
        left_mat, right_mat, (((0,), (0,)), ((), ())), preferred_element_type=F32
    )


def rope_tables(positions):
    half_dim = HD // 2
    inv_freq = THETA ** (-(jnp.arange(half_dim, dtype=F32) * 2.0) / HD)
    angles = positions.astype(F32)[:, None] * inv_freq[None, :]
    cos_half, sin_half = jnp.cos(angles), jnp.sin(angles)
    cosine = jnp.concatenate([cos_half, cos_half], axis=-1)
    sine_signed = jnp.concatenate([-sin_half, sin_half], axis=-1)
    return cosine, sine_signed


def fill_mask(bias_ref, seg_col_ref, seg_row_ref):
    @pl.when(pl.program_id(0) == 0)
    def _():
        for first in range(0, LEN, BQ):
            keys = first + BQ
            rows = seg_col_ref[first:keys, :]
            cols = seg_row_ref[:, :keys]
            query_index = first + lax.broadcasted_iota(jnp.int32, (BQ, keys), 0)
            key_index = lax.broadcasted_iota(jnp.int32, (BQ, keys), 1)
            allowed = (rows == cols) & (key_index <= query_index)
            bias_ref[first:keys, :keys] = jnp.where(allowed, 0.0, NEG_FILL)


def attend_forward_kernel(
    q_ref, k_ref, v_ref, qs_ref, ks_ref, qg_ref, kg_ref, cos_ref, sin_ref, segc_ref, segr_ref,
    qrot_ref, krot_ref, vb_ref, att_ref, log_ref, bias_ref,
):
    fill_mask(bias_ref, segc_ref, segr_ref)
    cosine, sine = cos_ref[...], sin_ref[...]

    def turned(raw, scale, gain):
        norm = raw * scale * gain
        return (norm * cosine + pltpu.roll(norm, HD // 2, 1) * sine).astype(BF16)

    qrot_ref[...] = turned(q_ref[...], qs_ref[...], qg_ref[...])
    krot_ref[...] = turned(k_ref[...], ks_ref[...], kg_ref[...])
    vb_ref[...] = v_ref[...].astype(BF16)
    for first in range(0, LEN, BQ):
        keys = first + BQ
        scores = times_transposed(qrot_ref[first:keys, :], krot_ref[:keys, :]) * SCORE_SCALE
        masked = scores + bias_ref[first:keys, :keys]
        peak = jnp.max(masked, axis=1, keepdims=True)
        weight = jnp.exp(masked - peak)
        total = jnp.sum(weight, axis=1, keepdims=True)
        probs = (weight * (1.0 / total)).astype(BF16)
        att_ref[first:keys, :] = plain_dot(probs, vb_ref[:keys, :]).astype(BF16)
        log_ref[0, first:keys, :] = peak + jnp.log(total)


def attend_backward_kernel(
    q_ref, k_ref, qs_ref, ks_ref, qg_ref, kg_ref, cos_ref, sin_ref, segc_ref, segr_ref,
    qrot_ref, krot_ref, vb_ref, att_ref, log_ref, grad_ref,
    dzq_ref, dzk_ref, gv_ref, dotq_ref, dotk_ref, gainq_ref, gaink_ref,
    dq_acc, dk_acc, dv_acc, bias_ref,
):
    fill_mask(bias_ref, segc_ref, segr_ref)
    dk_acc[...] = jnp.zeros_like(dk_acc)
    dv_acc[...] = jnp.zeros_like(dv_acc)
    for first in range(0, LEN, BQ):
        keys = first + BQ
        queries = qrot_ref[first:keys, :]
        grads = grad_ref[first:keys, :]
        scores = times_transposed(queries, krot_ref[:keys, :]) * SCORE_SCALE
        probs = jnp.exp(scores + bias_ref[first:keys, :keys] - log_ref[0, first:keys, :])
        delta = jnp.sum(
            grads.astype(F32) * att_ref[first:keys, :].astype(F32), axis=1, keepdims=True
        )
        grad_probs = times_transposed(grads, vb_ref[:keys, :])
        grad_scores = (probs * (grad_probs - delta) * SCORE_SCALE).astype(BF16)
        dq_acc[first:keys, :] = plain_dot(grad_scores, krot_ref[:keys, :])
        dk_acc[:keys, :] += left_transposed(grad_scores, queries)
        dv_acc[:keys, :] += left_transposed(probs.astype(BF16), grads)
    gv_ref[...] = dv_acc[...].astype(BF16)
    cosine, sine = cos_ref[...], sin_ref[...]

    def finish(acc, raw_ref, scale_ref, gain_ref, dz_ref, dot_ref, gain_grad_ref):
        grad_rot = acc[...]
        grad_norm = grad_rot * cosine - pltpu.roll(grad_rot, HD // 2, 1) * sine
        unit = raw_ref[...] * scale_ref[...]
        gain_grad_ref[...] = jnp.sum(grad_norm * unit, axis=0, keepdims=True)
        grad_unit = grad_norm * gain_ref[...]
        dz_ref[...] = grad_unit
        part = jnp.sum(grad_unit * unit, axis=1, keepdims=True)

        @pl.when(pl.program_id(0) == 0)
        def _():
            dot_ref[...] = part

        @pl.when(pl.program_id(0) > 0)
        def _():
            dot_ref[...] += part

    finish(dq_acc, q_ref, qs_ref, qg_ref, dzq_ref, dotq_ref, gainq_ref)
    finish(dk_acc, k_ref, ks_ref, kg_ref, dzk_ref, dotk_ref, gaink_ref)


def head_spec(offset):
    return pl.BlockSpec((LEN, HD), lambda h: (0, offset + h))


def whole_spec(shape):
    return pl.BlockSpec(shape, lambda h: (0,) * len(shape))


def gain_spec():
    return pl.BlockSpec((1, HD), lambda h: (0, h))


LOG_SPEC = pl.BlockSpec((1, LEN, 1), lambda h: (h, 0, 0))
COLUMN = (LEN, 1)
TABLE = (LEN, HD)


def attend_forward(qkv, scales, gains, tables, seg_col, seg_row, heads):
    width = heads * HD
    piece = jax.ShapeDtypeStruct((LEN, width), BF16)
    return pl.pallas_call(
        attend_forward_kernel,
        grid=(heads,),
        in_specs=[
            head_spec(0), head_spec(heads), head_spec(2 * heads),
            whole_spec(COLUMN), whole_spec(COLUMN), gain_spec(), gain_spec(),
            whole_spec(TABLE), whole_spec(TABLE), whole_spec(COLUMN), whole_spec((1, LEN)),
        ],
        out_specs=[head_spec(0)] * 4 + [LOG_SPEC],
        out_shape=[piece] * 4 + [jax.ShapeDtypeStruct((heads, LEN, 1), F32)],
        scratch_shapes=[pltpu.VMEM((LEN, LEN), F32)],
        compiler_params=pltpu.CompilerParams(vmem_limit_bytes=VMEM),
        cost_estimate=pl.CostEstimate(
            flops=heads * 4 * LEN * LEN * HD, bytes_accessed=LEN * width * 20, transcendentals=0
        ),
        name="attend_forward",
    )(qkv, qkv, qkv, *scales, *gains, *tables, seg_col, seg_row)


def attend_backward(qkv, scales, gains, tables, seg_col, seg_row, saved, grad_att, heads):
    width = heads * HD
    full = jax.ShapeDtypeStruct((LEN, width), F32)
    column = jax.ShapeDtypeStruct(COLUMN, F32)
    gain_row = jax.ShapeDtypeStruct((1, width), F32)
    return pl.pallas_call(
        attend_backward_kernel,
        grid=(heads,),
        in_specs=[
            head_spec(0), head_spec(heads),
            whole_spec(COLUMN), whole_spec(COLUMN), gain_spec(), gain_spec(),
            whole_spec(TABLE), whole_spec(TABLE), whole_spec(COLUMN), whole_spec((1, LEN)),
            head_spec(0), head_spec(0), head_spec(0), head_spec(0), LOG_SPEC, head_spec(0),
        ],
        out_specs=[
            head_spec(0), head_spec(0), head_spec(0),
            whole_spec(COLUMN), whole_spec(COLUMN), gain_spec(), gain_spec(),
        ],
        out_shape=[
            full, full, jax.ShapeDtypeStruct((LEN, width), BF16), column, column, gain_row, gain_row,
        ],
        scratch_shapes=[pltpu.VMEM((LEN, HD), F32)] * 3 + [pltpu.VMEM((LEN, LEN), F32)],
        compiler_params=pltpu.CompilerParams(vmem_limit_bytes=VMEM),
        cost_estimate=pl.CostEstimate(
            flops=heads * 10 * LEN * LEN * HD, bytes_accessed=LEN * width * 40, transcendentals=0
        ),
        name="attend_backward",
    )(qkv, qkv, *scales, *gains, *tables, seg_col, seg_row, *saved, grad_att)


def fetch_choice(idx_ref, refs, held_ref, sem):
    for number, ref in enumerate(refs):

        @pl.when(idx_ref[2] == number)
        def _():
            copy = pltpu.make_async_copy(ref, held_ref, sem)
            copy.start()
            copy.wait()


def half_tile(step, core, tiles):
    per_half = tiles // 2
    return ((core + step // per_half) % 2) * per_half + step % per_half


def forward_chunk_kernel(
    idx_ref, *refs, out_steps, tiles,
):
    own_ref, left1, left2, left3, right1, right2, right3 = refs[:7]
    wo_own_ref, wo_oth_ref, x_ref, gain_ref, wg_ref, wu_ref, wd_own_ref, wd_oth_ref = refs[7:15]
    raw_ref, scale_ref, hb_ref, gate_ref, up_ref, mixed_ref, part_ref, acc_ref, att_ref = refs[-9:]
    depth, out_tile = wo_own_ref.shape
    blocks, _, block = wd_own_ref.shape
    step = pl.program_id(0)
    core = idx_ref[1]

    @pl.when(step == 0)
    def _():
        quarter = own_ref.shape[1] // 2
        pieces = (
            own_ref[...], right1[...] + left3[...], right2[...] + left2[...], right3[...] + left1[...],
        )
        for half in range(2):
            for number, piece in enumerate(pieces):
                start = half * depth + number * quarter
                att_ref[:, start : start + quarter] = piece[:, half * quarter : (half + 1) * quarter]

    @pl.when(step < out_steps)
    def _():
        own = att_ref[:, pl.ds(pl.multiple_of(core * depth, depth), depth)]
        other = att_ref[:, pl.ds(pl.multiple_of((1 - core) * depth, depth), depth)]
        acc_ref[:, pl.ds(pl.multiple_of(step * out_tile, out_tile), out_tile)] = plain_dot(
            own, wo_own_ref[...]
        ) + plain_dot(other, wo_oth_ref[...])

    @pl.when(step == out_steps - 1)
    def _():
        raw = acc_ref[...]
        scale = lax.rsqrt(jnp.mean(raw * raw, axis=1, keepdims=True) + EPS)
        raw_ref[...] = raw.astype(BF16)
        scale_ref[...] = scale
        hb_ref[...] = (x_ref[...].astype(F32) + raw * scale * gain_ref[...]).astype(BF16)
        acc_ref[...] = jnp.zeros_like(acc_ref)

    def tile_work(wd_ref):
        hidden_b = hb_ref[...]
        gate = plain_dot(hidden_b, wg_ref[...])
        up = plain_dot(hidden_b, wu_ref[...])
        mixed = (gate * jax.nn.sigmoid(gate) * up).astype(BF16)
        gate_ref[...] = gate.astype(BF16)
        up_ref[...] = up.astype(BF16)
        mixed_ref[...] = mixed
        for j in range(blocks):
            acc_ref[:, j * block : (j + 1) * block] += plain_dot(mixed, wd_ref[j])

    @pl.when((step >= out_steps) & (step < out_steps + tiles // 2))
    def _():
        tile_work(wd_own_ref)

    @pl.when(step >= out_steps + tiles // 2)
    def _():
        tile_work(wd_oth_ref)

    @pl.when(step == out_steps + tiles - 1)
    def _():
        part_ref[...] = acc_ref[...].astype(BF16)


TILE = 512


def forward_chunk(index, attended, out_halves, block_input, gain, w_gate_up, down_halves, chunk, before):
    tokens, width = block_input.shape
    hidden = w_gate_up.shape[1] // 2
    depth = out_halves[0].shape[0]
    blocks, _, block = down_halves[0].shape
    tiles = hidden // TILE
    out_steps = width // TILE

    def tile_of(j, idx):
        return half_tile(jnp.maximum(j - out_steps, 0), idx[1], tiles)

    rows = pl.BlockSpec((chunk, width), lambda j, idx: (idx[0], 0))
    out_half = pl.BlockSpec((depth, TILE), lambda j, idx: (0, jnp.minimum(j, out_steps - 1)))
    gate_tile = pl.BlockSpec((width, TILE), lambda j, idx: (0, tile_of(j, idx)))
    up_tile = pl.BlockSpec((width, TILE), lambda j, idx: (0, tiles + tile_of(j, idx)))
    down_own = pl.BlockSpec(
        (blocks, TILE, block), lambda j, idx: (0, jnp.clip(j - out_steps, 0, tiles // 2 - 1), 0)
    )
    down_oth = pl.BlockSpec(
        (blocks, TILE, block), lambda j, idx: (0, jnp.maximum(j - out_steps - tiles // 2, 0), 0)
    )
    act_tile = pl.BlockSpec((chunk, TILE), lambda j, idx: (idx[0], tile_of(j, idx)))
    before = tuple(before)
    return pl.pallas_call(
        functools.partial(forward_chunk_kernel, out_steps=out_steps, tiles=tiles),
        grid_spec=pltpu.PrefetchScalarGridSpec(
            num_scalar_prefetch=1,
            grid=(out_steps + tiles,),
            in_specs=[
                *[pl.BlockSpec((chunk, attended[0].shape[1]), lambda j, idx: (idx[0], 0))] * 7,
                out_half, out_half, rows, pl.BlockSpec((1, width), lambda j, idx: (0, 0)),
                gate_tile, up_tile, down_own, down_oth,
            ] + [pl.BlockSpec(memory_space=pl.ANY)] * len(before),
            out_specs=[
                rows, pl.BlockSpec((chunk, 1), lambda j, idx: (idx[0], 0)), rows, act_tile, act_tile, act_tile,
                pl.BlockSpec((chunk, width), lambda j, idx: (0, 0)),
            ],
            scratch_shapes=[pltpu.VMEM((chunk, width), F32), pltpu.VMEM((chunk, 2 * depth), BF16)],
        ),
        out_shape=[
            jax.ShapeDtypeStruct((tokens, width), BF16),
            jax.ShapeDtypeStruct((tokens, 1), F32),
            jax.ShapeDtypeStruct((tokens, width), BF16),
            jax.ShapeDtypeStruct((tokens, hidden), BF16),
            jax.ShapeDtypeStruct((tokens, hidden), BF16),
            jax.ShapeDtypeStruct((tokens, hidden), BF16),
            jax.ShapeDtypeStruct((chunk, width), BF16),
        ],
        input_output_aliases={16 + i: i for i in range(len(before))},
        compiler_params=pltpu.CompilerParams(vmem_limit_bytes=VMEM),
        cost_estimate=pl.CostEstimate(
            flops=2 * chunk * width * (width + 3 * hidden),
            bytes_accessed=2 * width * (width + 3 * hidden),
            transcendentals=0,
        ),
        name="forward_chunk",
    )(index, *attended, *out_halves, block_input, gain, w_gate_up, w_gate_up, *down_halves, *before)


def backward_chunk_kernel(
    idx_ref, grad_ref, mlp_gain_ref, gate_ref, up_ref, wg_ref, wu_ref, wd_own_ref, wd_oth_ref, *refs, tiles, choices,
):
    gdi_ref, gg_ref, gu_ref, part_ref, gain_grad_ref, acc_ref, down_ref, sem = refs[-8:]
    blocks, _, block = wd_own_ref.shape
    step = pl.program_id(0)

    @pl.when(step == 0)
    def _():
        fetch_choice(idx_ref, refs[:choices], down_ref, sem)
        down_raw = down_ref[...].astype(F32)
        down_scale = lax.rsqrt(jnp.mean(down_raw * down_raw, axis=1, keepdims=True) + EPS)
        unit = down_raw * down_scale
        grad_y = grad_ref[...].astype(F32)
        gain_grad_ref[...] = jnp.sum(grad_y * unit, axis=0, keepdims=True)
        grad_unit = grad_y * mlp_gain_ref[...]
        mean = jnp.mean(grad_unit * unit, axis=1, keepdims=True)
        gdi_ref[...] = (down_scale * (grad_unit - unit * mean)).astype(BF16)
        acc_ref[...] = jnp.zeros_like(acc_ref)

    def tile_work(wd_ref):
        grad_mixed = times_transposed(gdi_ref[:, :block], wd_ref[0])
        for j in range(1, blocks):
            grad_mixed += times_transposed(gdi_ref[:, j * block : (j + 1) * block], wd_ref[j])
        gate = gate_ref[...].astype(F32)
        sig = jax.nn.sigmoid(gate)
        grad_gate = (grad_mixed * up_ref[...].astype(F32) * sig * (1.0 + gate * (1.0 - sig))).astype(BF16)
        grad_up = (grad_mixed * (gate * sig)).astype(BF16)
        gg_ref[...] = grad_gate
        gu_ref[...] = grad_up
        acc_ref[...] += times_transposed(grad_gate, wg_ref[...]) + times_transposed(grad_up, wu_ref[...])

    @pl.when(step < tiles // 2)
    def _():
        tile_work(wd_own_ref)

    @pl.when(step >= tiles // 2)
    def _():
        tile_work(wd_oth_ref)

    @pl.when(step == tiles - 1)
    def _():
        part_ref[...] = acc_ref[...].astype(BF16)


def backward_chunk(
    index, down_rows, grad_output, mlp_gain, gate, up, w_gate_up, down_halves, chunk, before,
):
    tokens, width = grad_output.shape
    hidden = w_gate_up.shape[1] // 2
    blocks, _, block = down_halves[0].shape
    tiles = hidden // TILE

    def tile_of(j, idx):
        return half_tile(j, idx[1], tiles)

    rows = pl.BlockSpec((chunk, width), lambda j, idx: (idx[0], 0))
    gain_row = pl.BlockSpec((1, width), lambda j, idx: (0, 0))
    gate_tile = pl.BlockSpec((width, TILE), lambda j, idx: (0, tile_of(j, idx)))
    up_tile = pl.BlockSpec((width, TILE), lambda j, idx: (0, tiles + tile_of(j, idx)))
    act_tile = pl.BlockSpec((chunk, TILE), lambda j, idx: (idx[0], tile_of(j, idx)))
    before = tuple(before)
    return pl.pallas_call(
        functools.partial(backward_chunk_kernel, tiles=tiles, choices=len(down_rows)),
        grid_spec=pltpu.PrefetchScalarGridSpec(
            num_scalar_prefetch=1,
            grid=(tiles,),
            in_specs=[
                rows, gain_row, act_tile, act_tile, gate_tile, up_tile,
                pl.BlockSpec((blocks, TILE, block), lambda j, idx: (0, jnp.minimum(j, tiles // 2 - 1), 0)),
                pl.BlockSpec((blocks, TILE, block), lambda j, idx: (0, jnp.maximum(j - tiles // 2, 0), 0)),
            ] + [pl.BlockSpec(memory_space=pl.ANY)] * (len(down_rows) + len(before)),
            out_specs=[rows, act_tile, act_tile, pl.BlockSpec((chunk, width), lambda j, idx: (0, 0)), gain_row],
            scratch_shapes=[
                pltpu.VMEM((chunk, width), F32), pltpu.VMEM((chunk, width), BF16), pltpu.SemaphoreType.DMA(()),
            ],
        ),
        out_shape=[
            jax.ShapeDtypeStruct((tokens, width), BF16),
            jax.ShapeDtypeStruct((tokens, hidden), BF16),
            jax.ShapeDtypeStruct((tokens, hidden), BF16),
            jax.ShapeDtypeStruct((chunk, width), BF16),
            jax.ShapeDtypeStruct((1, width), F32),
        ],
        input_output_aliases={9 + len(down_rows) + i: i for i in range(len(before))},
        compiler_params=pltpu.CompilerParams(vmem_limit_bytes=VMEM),
        cost_estimate=pl.CostEstimate(
            flops=6 * chunk * width * hidden, bytes_accessed=6 * width * hidden, transcendentals=0
        ),
        name="backward_chunk",
    )(index, grad_output, mlp_gain, gate, up, w_gate_up, w_gate_up, *down_halves, *down_rows, *before)


PARTS = 4


def attention_chunk_kernel(
    idx_ref, grad_ref, raw_ref, scale_ref, gain_ref, wo_own_ref, wo_oth_ref, *refs, choices,
):
    gai_ref, gatt_ref, gain_grad_ref, held_ref, sem = refs[-5:]
    half = wo_own_ref.shape[0]
    core = idx_ref[1]
    step = pl.program_id(0)

    @pl.when(step == 0)
    def _():
        fetch_choice(idx_ref, refs[:choices], held_ref, sem)
        gain_grad_ref[...] = jnp.zeros_like(gain_grad_ref)

    size = grad_ref.shape[0]
    scale = scale_ref[...]
    unit = raw_ref[...].astype(F32) * scale
    mlp = held_ref[pl.ds(pl.multiple_of(step * size, size), size), :]
    grad_hidden = grad_ref[...].astype(F32) + mlp.astype(F32)
    gain_grad_ref[...] += jnp.sum(grad_hidden * unit, axis=0, keepdims=True)
    grad_unit = grad_hidden * gain_ref[...]
    mean = jnp.mean(grad_unit * unit, axis=1, keepdims=True)
    grad_attn_in = (scale * (grad_unit - unit * mean)).astype(BF16)
    gai_ref[...] = grad_attn_in
    for place, w_ref in ((core, wo_own_ref), (1 - core, wo_oth_ref)):
        gatt_ref[:, pl.ds(pl.multiple_of(place * half, half), half)] = times_transposed(
            grad_attn_in, w_ref[...]
        ).astype(BF16)


def attention_chunk(index, mlp_rows, grad_output, raw, scale, gain, out_halves, half, chunk, before):
    tokens, width = grad_output.shape
    size = chunk
    rows = pl.BlockSpec((size, width), lambda j, idx: (idx[0], 0))
    gain_row = pl.BlockSpec((1, width), lambda j, idx: (0, 0))
    own_heads = pl.BlockSpec((half, width), lambda j, idx: (0, 0))
    before = tuple(before)
    return pl.pallas_call(
        functools.partial(attention_chunk_kernel, choices=len(mlp_rows)),
        grid_spec=pltpu.PrefetchScalarGridSpec(
            num_scalar_prefetch=1,
            grid=(1,),
            in_specs=[
                rows, rows, pl.BlockSpec((size, 1), lambda j, idx: (idx[0], 0)), gain_row,
                own_heads, own_heads,
            ] + [pl.BlockSpec(memory_space=pl.ANY)] * (len(mlp_rows) + len(before)),
            out_specs=[rows, pl.BlockSpec((size, 2 * half), lambda j, idx: (idx[0], 0)), gain_row],
            scratch_shapes=[pltpu.VMEM((chunk, width), BF16), pltpu.SemaphoreType.DMA(())],
        ),
        out_shape=[
            jax.ShapeDtypeStruct((tokens, width), BF16),
            jax.ShapeDtypeStruct((tokens, 2 * half), BF16),
            jax.ShapeDtypeStruct((1, width), F32),
        ],
        input_output_aliases={7 + len(mlp_rows) + i: i for i in range(len(before))},
        compiler_params=pltpu.CompilerParams(vmem_limit_bytes=VMEM),
        cost_estimate=pl.CostEstimate(
            flops=4 * chunk * width * half, bytes_accessed=16 * chunk * width, transcendentals=0
        ),
        name="attention_chunk",
    )(index, grad_output, raw, scale, gain, *out_halves, *mlp_rows, *before)


def output_chunk_kernel(idx_ref, raw_ref, scale_ref, x_ref, attn_gain_ref, mlp_gain_ref, *refs, choices):
    out_ref, held_ref, sem = refs[-3:]
    step = pl.program_id(0)

    @pl.when(step == 0)
    def _():
        fetch_choice(idx_ref, refs[:choices], held_ref, sem)

    size = out_ref.shape[0]
    down_raw = held_ref[pl.ds(pl.multiple_of(step * size, size), size), :].astype(F32)
    down_scale = lax.rsqrt(jnp.mean(down_raw * down_raw, axis=1, keepdims=True) + EPS)
    hidden = x_ref[...].astype(F32) + raw_ref[...].astype(F32) * scale_ref[...] * attn_gain_ref[...]
    out_ref[...] = (hidden + down_raw * down_scale * mlp_gain_ref[...]).astype(BF16)


def output_chunk(index, down_rows, raw, scale, block_input, attn_gain, mlp_gain, chunk, before):
    tokens, width = block_input.shape
    size = chunk // PARTS
    rows = pl.BlockSpec((size, width), lambda j, idx: (PARTS * idx[0] + j, 0))
    gain_row = pl.BlockSpec((1, width), lambda j, idx: (0, 0))
    before = tuple(before)
    return pl.pallas_call(
        functools.partial(output_chunk_kernel, choices=len(down_rows)),
        grid_spec=pltpu.PrefetchScalarGridSpec(
            num_scalar_prefetch=1,
            grid=(PARTS,),
            in_specs=[
                rows, pl.BlockSpec((size, 1), lambda j, idx: (PARTS * idx[0] + j, 0)), rows, gain_row, gain_row,
            ] + [pl.BlockSpec(memory_space=pl.ANY)] * (len(down_rows) + len(before)),
            out_specs=rows,
            scratch_shapes=[pltpu.VMEM((chunk, width), BF16), pltpu.SemaphoreType.DMA(())],
        ),
        out_shape=jax.ShapeDtypeStruct((tokens, width), BF16),
        input_output_aliases={6 + len(down_rows): 0} if before else {},
        compiler_params=pltpu.CompilerParams(vmem_limit_bytes=VMEM),
        cost_estimate=pl.CostEstimate(flops=0, bytes_accessed=8 * chunk * width, transcendentals=0),
        name="output_chunk",
    )(index, raw, scale, block_input, attn_gain, mlp_gain, *down_rows, *before)


def place_rows_kernel(idx_ref, *refs, choices):
    out_ref, held_ref, sem = refs[-3:]
    step = pl.program_id(0)

    @pl.when(step == 0)
    def _():
        fetch_choice(idx_ref, refs[:choices], held_ref, sem)

    size = out_ref.shape[0]
    out_ref[...] = held_ref[pl.ds(pl.multiple_of(step * size, size), size), :].astype(out_ref.dtype)


def place_rows(index, rows_in, tokens, dtype, before):
    chunk, width = rows_in[0].shape
    before = tuple(before)
    return pl.pallas_call(
        functools.partial(place_rows_kernel, choices=len(rows_in)),
        grid_spec=pltpu.PrefetchScalarGridSpec(
            num_scalar_prefetch=1,
            grid=(2,),
            in_specs=[pl.BlockSpec(memory_space=pl.ANY)] * (len(rows_in) + len(before)),
            out_specs=pl.BlockSpec((chunk // 2, width), lambda j, idx: (2 * idx[0] + j, 0)),
            scratch_shapes=[pltpu.VMEM((chunk, width), BF16), pltpu.SemaphoreType.DMA(())],
        ),
        out_shape=jax.ShapeDtypeStruct((tokens, width), dtype),
        input_output_aliases={1 + len(rows_in): 0} if before else {},
        compiler_params=pltpu.CompilerParams(vmem_limit_bytes=VMEM),
        cost_estimate=pl.CostEstimate(flops=0, bytes_accessed=6 * chunk * width, transcendentals=0),
        name="place_rows",
    )(index, *rows_in, *before)


def after(value, *tokens):
    return lax.optimization_barrier((value, tokens))[0]


def unset_kernel(out_ref):
    pass


def unset(shape, dtype):
    return pl.pallas_call(
        unset_kernel,
        out_specs=pl.BlockSpec(memory_space=pl.ANY),
        out_shape=jax.ShapeDtypeStruct(shape, dtype),
        name="unset",
    )()


def shards(
    sizes,
    block_input,
    segment_ids,
    positions,
    w_query,
    w_key,
    w_value,
    w_out,
    w_gate,
    w_up,
    w_down,
    query_gain,
    key_gain,
    attn_gain,
    mlp_gain,
    grad_output,
):
    cores, rows, cols = sizes
    tokens_here, width = block_input.shape
    assert tokens_here == LEN and cores == 2 and cols == 4
    local_width = w_query.shape[1]
    half_width = local_width // 2
    heads = local_width // HD
    chunk = tokens_here // cols
    core = lax.axis_index("dp")
    row = lax.axis_index("row")
    col = lax.axis_index("col")
    swap = [(0, 1), (1, 0)]
    attn_row, mlp_row = attn_gain[None, :], mlp_gain[None, :]

    def own_half(array, axis):
        half = array.shape[axis] // 2
        return lax.dynamic_slice_in_dim(array, core * half, half, axis)

    def other_half(array, axis):
        half = array.shape[axis] // 2
        return lax.dynamic_slice_in_dim(array, (1 - core) * half, half, axis)

    def gather(weight, axis):
        return lax.all_gather(own_half(weight, axis), ("row", "dp"), axis=axis, tiled=True)

    def line_step(from_left, from_right, step):
        from_left = lax.ppermute(from_left, "col", [(i, i + 1) for i in range(step - 1, cols - 1)])
        from_right = lax.ppermute(from_right, "col", [(i + 1, i) for i in range(cols - step)])
        return from_left, from_right

    def sum_step(up, down, step):
        up = lax.ppermute(up, "col", [(i, i + 1) for i in range(step)])
        down = lax.ppermute(down, "col", [(cols - 1 - i, cols - 2 - i) for i in range(step)])
        return up, down

    def pick(at_zero, at_one, at_two, at_three):
        low = jnp.where(col == 0, at_zero, at_one)
        high = jnp.where(col == 2, at_two, at_three)
        return jnp.where(col < 2, low, high)

    slot_chunk = [pick(3, 3, 0, 0), pick(2, 2, 1, 1), pick(1, 0, 3, 2), col]
    slot_index = [
        jnp.stack([one, core, choice]).astype(jnp.int32)
        for one, choice in zip(slot_chunk, (col, col, col % 2, 0 * col))
    ]

    def slot_rows(array, slot):
        return lax.dynamic_slice_in_dim(array, slot_chunk[slot] * chunk, chunk, 0)

    def gather_slots(own, work):
        left, right, token = [own], [own], ()
        arrived = (
            lambda lefts, rights: (lefts[0],),
            lambda lefts, rights: (rights[1], lefts[1]),
            lambda lefts, rights: (rights[2], rights[1], lefts[1], lefts[2]),
            lambda lefts, rights: (rights[3], rights[2], lefts[2], lefts[3]),
        )
        for step in range(1, cols + 1):
            seen = tuple(left), tuple(right)
            if step < cols:
                from_left, from_right = line_step(left[-1], right[-1], step)
                left.append(from_left)
                right.append(from_right)
            token = work(cols - step, arrived[step - 1](*after(seen, token)))

    def sum_slots(make, window=lambda step, gate: ()):
        def at(step, gate):
            window(step, gate)
            return make(step, gate)

        first = make(0, ())
        up, down = sum_step(first, first, 1)
        second = at(1, first)
        gate = jnp.where((col == 0) | (col == 3), second, first) + (up + down)
        up, down = sum_step(gate, gate, 2)
        third = at(2, gate)
        up = jnp.where(col == 1, second, third) + up
        down = jnp.where(col == 2, second, third) + down
        gate = (up, down)
        up, down = sum_step(up, down, 3)
        fourth = lax.optimization_barrier(at(3, gate))
        return fourth.astype(F32) + up.astype(F32) + down.astype(F32)

    def both_cores(half, axis):
        other = lax.ppermute(half, "dp", swap)
        first = jnp.where(core == 0, half, other)
        second = jnp.where(core == 0, other, half)
        return jnp.concatenate([first, second], axis=axis).astype(F32)

    def sum_sent(left_mat, right_other):
        return lax.ppermute(left_transposed(left_mat, right_other).astype(BF16), "dp", swap)

    def sum_kept(left_mat, right_own, sent):
        total = (left_transposed(left_mat, right_own) + sent.astype(F32)).astype(BF16)
        return total, lax.psum_scatter(total, "row", scatter_dimension=0, tiled=True)

    by_x = [(0, 1), (1, 0), (2, 3), (3, 2)]
    by_y = [(0, 2), (2, 0), (1, 3), (3, 1)]

    def row_first(half):
        if rows != 4:
            return (half,)
        return half, lax.ppermute(half, "row", by_x), lax.ppermute(half, "row", by_y)

    def row_second(pieces):
        if rows != 4:
            return pieces
        middle = pieces[0].shape[0] // 2
        return (
            *pieces,
            lax.ppermute(pieces[1][:middle], "row", by_y),
            lax.ppermute(pieces[2][middle:], "row", by_x),
        )

    def row_blocks(pieces):
        if rows != 4:
            whole = lax.all_gather(pieces[0], ("row", "dp"), axis=0, tiled=False)
            whole = whole.reshape(rows, cores, *pieces[0].shape)
            return tuple(lax.dynamic_index_in_dim(whole, one, 1, keepdims=False) for one in (core, 1 - core))
        own, by_one, by_two, corner_top, corner_low = pieces
        middle = own.shape[0] // 2
        held = unset((rows, *own.shape), own.dtype)
        for piece, block, start in (
            (own, row, 0), (by_one, row ^ 1, 0), (by_two, row ^ 2, 0),
            (corner_top, row ^ 3, 0), (corner_low, row ^ 3, middle),
        ):
            held = lax.dynamic_update_slice(held, piece[None], (block, start, 0))
        return held, lax.ppermute(held, "dp", swap)

    def row_columns(pieces):
        if rows != 4:
            return lax.all_gather(pieces[0], "row", axis=1, tiled=True)
        own, by_one, by_two, corner_top, corner_low = pieces
        height, block = own.shape
        held = unset((height, rows * block), own.dtype)
        for piece, number, start in (
            (own, row, 0), (by_one, row ^ 1, 0), (by_two, row ^ 2, 0),
            (corner_top, row ^ 3, 0), (corner_low, row ^ 3, height // 2),
        ):
            held = lax.dynamic_update_slice(held, piece, (start, number * block))
        return held

    full_qkv = gather(jnp.concatenate([w_query, w_key, w_value], axis=1), 0)
    full_gate_up = gather(jnp.concatenate([w_gate, w_up], axis=1), 0)
    out_pieces = row_first(own_half(w_out, 0))
    out_pieces = row_second(out_pieces)
    out_own = row_columns(out_pieces)
    out_left, out_right = [out_own], [out_own]
    for step in range(1, cols):
        one, two = line_step(out_left[-1], out_right[-1], step)
        out_left.append(one)
        out_right.append(two)
    down_pieces = row_first(after(own_half(w_down, 0), full_qkv))

    qkv = plain_dot(block_input, full_qkv)
    query_raw, key_raw = qkv[:, :local_width], qkv[:, local_width : 2 * local_width]
    query_sq, key_sq = lax.psum(
        (jnp.sum(query_raw * query_raw, axis=1), jnp.sum(key_raw * key_raw, axis=1)), "col"
    )
    query_scale = lax.rsqrt(query_sq / width + EPS)[:, None]
    key_scale = lax.rsqrt(key_sq / width + EPS)[:, None]
    scales = (query_scale, key_scale)
    gains = (query_gain[None, :], key_gain[None, :])
    tables = rope_tables(positions)
    seg_col, seg_row = segment_ids[:, None], segment_ids[None, :]
    query_rot, key_rot, value_heads, attended, log_total = attend_forward(
        qkv, scales, gains, tables, seg_col, seg_row, heads
    )

    lefts, rights = [attended], [attended]
    for step in range(1, cols):
        from_left, from_right = line_step(lefts[-1], rights[-1], step)
        lefts.append(from_left)
        rights.append(from_right)
        if step == 1:
            out_halves = jnp.concatenate(
                [out_own] + [out_right[k] + out_left[cols - k] for k in range(1, cols)], axis=0
            )
            out_halves = (out_halves, lax.ppermute(out_halves, "dp", swap))
        if step == 2:
            down_pieces = row_second(after(down_pieces, lefts[1], rights[1]))
        if step == 3:
            down_halves = row_blocks(down_pieces)
    attended_all = (attended, *lefts[1:], *rights[1:])

    held = dict(f=(), b=(), a=(), o=(), m=())
    gain_sums = dict(mlp=0.0, attn=0.0)

    def forward_work(slot, gate):
        results = forward_chunk(
            slot_index[slot], after(attended_all, gate), out_halves, block_input, attn_row, full_gate_up,
            down_halves, chunk, held["f"],
        )
        held["f"] = results[:6]
        return results[6]

    down_own = sum_slots(forward_work).astype(BF16)
    attn_raw, attn_scale, hidden_b, gate_proj, up_proj, mixed_act = held["f"]
    mlp_parts = [None] * cols
    down_slots = [None] * cols

    def backward_work(slot, down_rows):
        down_slots[slot] = down_rows
        results = backward_chunk(
            slot_index[slot], down_rows, grad_output, mlp_row, gate_proj, up_proj, full_gate_up,
            down_halves, chunk, held["b"],
        )
        held["b"] = results[:3]
        mlp_parts[slot] = results[3]
        gain_sums["mlp"] = gain_sums["mlp"] + results[4]
        return results[3]

    gather_slots(down_own, backward_work)
    grad_down_in, grad_gate_in, grad_up_in = held["b"]

    blocks = {}
    got = {}

    def mlp_window(step, gate):
        down_left, down_right, hidden_left, gate_right, up_right = after(
            (grad_down_in, mixed_act, hidden_b, grad_gate_in, grad_up_in), gate
        )
        if step == 1:
            got["down"] = sum_sent(down_left, other_half(down_right, 1))
            got["gate"] = sum_sent(hidden_left, other_half(gate_right, 1))
            return got["down"], got["gate"]
        if step == 2:
            blocks["down"] = sum_kept(down_left, own_half(down_right, 1), got["down"])
            got["up"] = sum_sent(hidden_left, other_half(up_right, 1))
            return blocks["down"][0], got["up"]
        blocks["gate"] = sum_kept(hidden_left, own_half(gate_right, 1), got["gate"])
        return blocks["gate"][0]

    mlp_own = sum_slots(lambda slot, gate: mlp_parts[slot], mlp_window).astype(BF16)

    def attention_work(slot, mlp_rows):
        results = attention_chunk(
            slot_index[slot], mlp_rows, grad_output, attn_raw, attn_scale, attn_row, out_halves, half_width,
            chunk, held["a"],
        )
        held["a"] = results[:2]
        gain_sums["attn"] = gain_sums["attn"] + results[2]
        if slot == 3:
            hidden_left, up_right = after((hidden_b, grad_up_in), mlp_rows[0])
            blocks["up"] = sum_kept(hidden_left, own_half(up_right, 1), got["up"])
        for other in {2: (3, 2), 1: (1, 0)}.get(slot, ()):
            output = output_chunk(
                slot_index[other], down_slots[other], after(attn_raw, mlp_rows), attn_scale, block_input, attn_row,
                mlp_row, chunk, held["m"],
            )
            held["m"] = (output,)
        return results[1]

    gather_slots(mlp_own, attention_work)
    grad_attn_in, grad_att = held["a"]
    (block_output,) = held["m"]
    own_grad_hidden = slot_rows(grad_output, 3).astype(F32) + mlp_own.astype(F32)

    query_dz, key_dz, grad_value_in, query_dot, key_dot, grad_query_gain, grad_key_gain = attend_backward(
        qkv, scales, gains, tables, seg_col, seg_row,
        (query_rot, key_rot, value_heads, attended, log_total), grad_att, heads,
    )
    query_dot, key_dot = lax.psum((query_dot[:, 0], key_dot[:, 0]), "col")
    grad_query_in = (
        query_scale * (query_dz - query_raw * query_scale * (query_dot / width)[:, None])
    ).astype(BF16)
    grad_key_in = (
        key_scale * (key_dz - key_raw * key_scale * (key_dot / width)[:, None])
    ).astype(BF16)
    grad_qkv = jnp.concatenate([grad_query_in, grad_key_in, grad_value_in], axis=1)
    gain_pack = jnp.concatenate([grad_query_gain, grad_key_gain, gain_sums["attn"], gain_sums["mlp"]], axis=1)

    def interleaved(picker, pieces_in):
        return jnp.concatenate([picker(one, 1) for one in pieces_in], axis=1)

    def input_window(step, gate):
        nonlocal gain_pack
        pack, *pieces_in, tokens_in, left_out, right_out = after(
            (gain_pack, grad_query_in, grad_key_in, grad_value_in, block_input, grad_attn_in, attended), gate
        )
        if step == 1:
            got["qkv"] = sum_sent(tokens_in, interleaved(other_half, pieces_in))
            got["out"] = sum_sent(left_out, other_half(right_out, 1))
            gain_pack = pack + lax.ppermute(pack, "dp", swap)
            return got["qkv"], got["out"], gain_pack
        if step == 2:
            blocks["out"] = sum_kept(left_out, own_half(right_out, 1), got["out"])
            if rows == 4:
                gain_pack = pack + lax.ppermute(pack, "row", by_x)
            return
        blocks["qkv"] = sum_kept(tokens_in, interleaved(own_half, pieces_in), got["qkv"])
        gain_pack = pack + lax.ppermute(pack, "row", by_y) if rows == 4 else lax.psum(pack, "row")

    def input_work(slot, gate):
        return times_transposed(after(slot_rows(grad_qkv, slot), gate), full_qkv).astype(BF16)

    input_own = sum_slots(input_work, input_window)

    results = {}
    quarter = local_width // 2

    def projection(index):
        pair = both_cores(blocks["qkv"][1][None, :, index * quarter : (index + 1) * quarter], 0)
        return jnp.concatenate([pair[0], pair[1]], axis=1)

    def output_work(slot, rows_in):
        held["o"] = (place_rows(slot_index[slot], rows_in, tokens_here, F32, held["o"]),)
        if slot == 3:
            results["down"] = jnp.transpose(both_cores(blocks["down"][1], 1))
            results["gate"] = both_cores(blocks["gate"][1], 1)
            return held["o"], results["down"], results["gate"]
        if slot == 2:
            results["up"] = both_cores(blocks["up"][1], 1)
            return held["o"], results["up"]
        if slot == 1:
            results["out"] = jnp.transpose(both_cores(blocks["out"][1], 1))
            results["qkv"] = [projection(index) for index in range(3)]
            return held["o"], results["out"], results["qkv"]
        return held["o"]

    gather_slots((own_grad_hidden + input_own).astype(BF16), output_work)
    ends = (local_width, 2 * local_width, 2 * local_width + width)
    gain_grads = jnp.split(gain_pack[0], ends)
    return (
        block_output,
        held["o"][0],
        *results["qkv"],
        results["out"],
        results["gate"],
        results["up"],
        results["down"],
        *gain_grads,
    )


def layer(sizes, *arrays):
    return shards(sizes, *arrays)


def solution(mesh):
    in_specs = (
        P(("dp", "row"), None),
        P(("dp", "row")),
        P(("dp", "row")),
        P("row", "col"),
        P("row", "col"),
        P("row", "col"),
        P("col", "row"),
        P("row", "col"),
        P("row", "col"),
        P("col", "row"),
        P("col"),
        P("col"),
        P(),
        P(),
        P(("dp", "row"), None),
    )
    out_specs = (
        P(("dp", "row"), None),
        P(("dp", "row"), None),
        P("row", "col"),
        P("row", "col"),
        P("row", "col"),
        P("col", "row"),
        P("row", "col"),
        P("row", "col"),
        P("col", "row"),
        P("col"),
        P("col"),
        P(),
        P(),
    )
    sizes = (mesh.shape["dp"], mesh.shape["row"], mesh.shape["col"])
    return jax.shard_map(
        functools.partial(layer, sizes), mesh=mesh, in_specs=in_specs, out_specs=out_specs, check_vma=False
    )
```
